32 devices in a mesh: seq: 4 (over y, x), fsdp: 8 (over z, core).
Axes of the slice: x: 2, y: 2, z: 4, core: 2. Of those that a mesh axis runs over, the one named last changes fastest.
Arguments:
- tokens: bfloat16 [16, 2048, 512], P('fsdp', 'seq'), may hold values from -6 to 6
- encoder_states: bfloat16 [16, 1024, 512], P('fsdp', 'seq'), may hold values from -6 to 6
- lengths: int32 [16, 3], P('fsdp'), may hold values from 256 to 1536, as said below
- timesteps: int32 [16], P('fsdp'), may hold values from 0 to 999
- time_weight: bfloat16 [512, 1024], P('fsdp'), may hold values from -0.1875 to 0.1875
- self_input: bfloat16 [512, 1536], P('fsdp'), may hold values from -0.25 to 0.25
- self_output: bfloat16 [512, 512], P('fsdp'), may hold values from -6 to 6
- cross_query: bfloat16 [512, 512], P('fsdp'), may hold values from -0.25 to 0.25
- cross_memory: bfloat16 [512, 1024], P('fsdp'), may hold values from -0.25 to 0.25
- cross_output: bfloat16 [512, 512], P('fsdp'), may hold values from -4 to 4
- widen_weight: bfloat16 [512, 2048], P('fsdp'), may hold values from -0.25 to 0.25
- narrow_weight: bfloat16 [2048, 512], P('fsdp'), may hold values from -0.125 to 0.125
- norm_gains: bfloat16 [3, 512], P(None, 'fsdp'), may hold values from 0.5 to 1.5
- cotangent: bfloat16 [16, 2048, 512], P('fsdp', 'seq'), may hold values from -6 to 6
Outputs:
- layer_output: bfloat16 [16, 2048, 512], P('fsdp', 'seq')
- grad_tokens: float32 [16, 2048, 512], P('fsdp', 'seq')
- grad_encoder: float32 [16, 1024, 512], P('fsdp', 'seq')
- grad_time_weight: float32 [512, 1024], P('fsdp')
- grad_self_input: float32 [512, 1536], P('fsdp')
- grad_self_output: float32 [512, 512], P('fsdp')
- grad_cross_query: float32 [512, 512], P('fsdp')
- grad_cross_memory: float32 [512, 1024], P('fsdp')
- grad_cross_output: float32 [512, 512], P('fsdp')
- grad_widen: float32 [512, 2048], P('fsdp')
- grad_narrow: float32 [2048, 512], P('fsdp')
- grad_gains: float32 [3, 512], P(None, 'fsdp')
The draws below stay inside these ranges and needn't reach their ends.
Inputs may be any that keep to these rules, and one draw needn't show every extreme that they name: Row g holds the length of group g's prompt, then the lengths of its 2 continuations, each 256 to 512; a row sums to 2048.
All inputs are finite; a program needn't handle non-finite values.
Results may differ from the reference program's by a relative error of at most 0.02.
Values may be sent and summed in bfloat16 or wider, within the bound.
No kernel may reach another device: no remote copies, remote signals or barrier semaphores. Data moves between devices by JAX's collectives and lax.ppermute only.
A program may use at most 128 MiB of HBM per device.

```python
import math
from functools import partial
import jax
import jax.numpy as jnp
from jax import lax

D = 512
HEADS = 8
HEAD_DIM = 64
FF = 2048
ENC = 1024
CONT = 2
GROUP_TOK = 2048
GROUPS = 16


def draw_lengths(key, part):
    tail_key, first_key, second_key = jax.random.split(key, 3)
    longest = GROUP_TOK // 4
    shortest = GROUP_TOK // 8
    continued = jax.random.randint(tail_key, (GROUPS, CONT), shortest, longest + 1)
    chosen = jax.random.randint(first_key, (), 0, GROUPS)
    offset = jax.random.randint(second_key, (), 1, GROUPS)
    second_row = (chosen + offset) % GROUPS
    row_index = jnp.arange(GROUPS)[:, None]
    column_index = jnp.arange(CONT)[None, :]
    continued = jnp.where(row_index == chosen, jnp.where(column_index == 0, longest, shortest), continued)
    continued = jnp.where(row_index == second_row, shortest, continued)
    prompt = GROUP_TOK - jnp.sum(continued, axis=1, keepdims=True)
    return jnp.concatenate([prompt, continued], axis=1).astype(jnp.int32)


def touch_ends(entries, stream_key, smallest, largest):
    spot = [jax.random.randint(jax.random.fold_in(stream_key, axis), (), 0, length) for axis, length in enumerate(entries.shape)]
    widest = entries.shape.index(max(entries.shape))
    neighbour = spot[:widest] + [(spot[widest] + 1) % entries.shape[widest]] + spot[widest + 1:]
    return entries.at[tuple(spot)].set(smallest).at[tuple(neighbour)].set(largest)


def raised(entries, own_key, source, target, parts, factor):
    owner, partner = [(jnp.arange(entries.shape[position]) // (entries.shape[position] // parts)).reshape([-1 if axis == position else 1 for axis in range(entries.ndim)]) for position in (source, target)]
    chosen = jax.random.permutation(own_key, parts)[partner]
    strong = (owner == chosen) | (owner == (partner + parts // 2) % parts)
    return jnp.where(strong, factor * entries, entries)


def levels(rng, shape, pieces, low, largest):
    loudness = 1.0
    for dim, parts in pieces:
        draws = jax.random.uniform(jax.random.fold_in(jax.random.fold_in(rng, 6), dim), (parts,), jnp.float32, low / len(pieces), largest / len(pieces))
        loudness = loudness * jnp.repeat(jnp.exp(draws), shape[dim] // parts).reshape((-1,) + (1,) * (len(shape) - 1 - dim))
    return loudness


def normal_values(rng, extent, width, limit, pieces=(), kind=jnp.bfloat16):
    loudness = levels(rng, extent, pieces, -0.22, 0.18) if pieces else 1.0
    array = jax.random.normal(rng, extent, jnp.float32) * width * loudness
    return jnp.minimum(jnp.maximum(array, -limit), limit).astype(kind)


def bell_draw_with(rng, dims, width, reach, shards, heavy, kind=jnp.bfloat16):
    result = width * jax.random.normal(rng, dims, jnp.float32)
    if shards:
        result = result * levels(rng, dims, shards, -0.22, 0.18)
    return jnp.clip(raised(result, jax.random.fold_in(rng, 3), *heavy), -reach, reach).astype(kind)


def setup_inputs(seed: int = 0) -> dict:
    key_of = jax.random.split(jax.random.key(seed), 15)
    tokens = bell_draw_with(key_of[0], (GROUPS, GROUP_TOK, D), 1.0, 6.0, ((0, 8), (1, 4)), (0, 2, 8, 2.0))
    encoder_states = normal_values(key_of[1], (GROUPS, ENC, D), 1.0, 6.0, ((0, 8), (1, 4)))
    lengths = draw_lengths(jax.random.fold_in(key_of[14], 71), 0)
    timesteps = touch_ends(jax.random.randint(key_of[3], (GROUPS,), 0, 1000), jax.random.fold_in(key_of[3], 1), 0, 999).astype(jnp.int32)
    time_weight = normal_values(key_of[4], (D, 2 * D), (2 * D) ** -0.5, 0.1875, ((0, 8),))
    self_input = normal_values(key_of[5], (D, 3 * D), D ** -0.5, 0.25, ((0, 8),))
    self_output = normal_values(key_of[6], (D, D), (max(1, 4 * D // GROUP_TOK)) ** -0.5, 6.0, ((0, 8),))
    cross_query = normal_values(key_of[7], (D, D), D ** -0.5, 0.25, ((0, 8),))
    cross_memory = normal_values(key_of[8], (D, 2 * D), D ** -0.5, 0.25, ((0, 8),))
    cross_output = normal_values(key_of[9], (D, D), (max(1, 4 * D // ENC)) ** -0.5, 4.0, ((0, 8),))
    widen_weight = normal_values(key_of[10], (D, FF), D ** -0.5, 0.25, ((0, 8),))
    narrow_weight = normal_values(key_of[11], (FF, D), FF ** -0.5, 0.125, ((0, 8),))
    norm_gains = jnp.clip(1.0 + 0.1 * jax.random.normal(key_of[12], (3, D), jnp.float32), 0.5, 1.5).astype(jnp.bfloat16)
    cotangent = normal_values(key_of[13], (GROUPS, GROUP_TOK, D), 1.0, 6.0, ((0, 8), (1, 4)))
    return {"tokens": tokens, "encoder_states": encoder_states, "lengths": lengths, "timesteps": timesteps, "time_weight": time_weight, "self_input": self_input, "self_output": self_output, "cross_query": cross_query, "cross_memory": cross_memory, "cross_output": cross_output, "widen_weight": widen_weight, "narrow_weight": narrow_weight, "norm_gains": norm_gains, "cotangent": cotangent}


@jax.custom_vjp
def low(v):
    return lax.optimization_barrier(v.astype(jnp.bfloat16)).astype(jnp.float32)

@jax.custom_vjp
def low_back(v):
    return v

def low_keep(v):
    return (low(v), None)

def low_pass(kept, grad):
    return (grad,)

def back_keep(v):
    return (v, None)

def back_low(kept, grad):
    return (low(grad),)
low.defvjp(low_keep, low_pass)
low_back.defvjp(back_keep, back_low)
EPS = 1e-05
NEG = -1e+30

def matmul(left, right):
    return jnp.dot(left, right, precision=lax.Precision.HIGHEST, preferred_element_type=jnp.float32)

def normalize(values):
    average = lax.optimization_barrier(jnp.mean(values, axis=-1, keepdims=True))
    centred = values - average
    spread = lax.optimization_barrier(jnp.mean(centred * centred, axis=-1, keepdims=True))
    return centred * lax.rsqrt(spread + EPS)

def time_embedding(step_values, model_width):
    half_width = model_width // 2
    frequency = jnp.exp(-math.log(10000.0) * jnp.arange(half_width, dtype=jnp.float32) / half_width)
    angles = step_values.astype(jnp.float32)[:, None] * frequency[None, :]
    return jnp.concatenate([jnp.sin(angles), jnp.cos(angles)], axis=-1)

def segment_ids(lengths_row, position_count):
    bounds = jnp.cumsum(lengths_row, dtype=jnp.int32)[:-1]
    positions = jnp.arange(position_count, dtype=jnp.int32)
    return lax.optimization_barrier(jnp.sum((positions[:, None] >= bounds[None, :]).astype(jnp.int32), axis=1, dtype=jnp.int32))

def attend(query_rows, key_rows, value_rows, allowed):
    score_scale = HEAD_DIM ** (-0.5)
    scores = low_back(score_scale * jnp.einsum('qhd,khd->hqk', query_rows, key_rows, precision=lax.Precision.HIGHEST))
    if allowed is not None:
        scores = jnp.where(allowed[None], scores, NEG)
    probabilities = low(jax.nn.softmax(scores, axis=-1))
    return jnp.einsum('hqk,khd->qhd', probabilities, value_rows, precision=lax.Precision.HIGHEST)

def sent(values):
    return low_back(low(values))

def group_forward(weights, packed):
    time_weight, self_input, self_output, cross_query, cross_memory, cross_output, widen_weight, narrow_weight, norm_gains = weights
    tokens_rows, encoder_rows, lengths_row, modulation = packed
    group_rows = tokens_rows.shape[0]
    enc_rows = encoder_rows.shape[0]

    def split_heads(flat):
        return flat.reshape(flat.shape[0], HEADS, HEAD_DIM)
    first = low(normalize(tokens_rows) * norm_gains[0] * (1.0 + modulation[:D]) + modulation[D:])
    projected = matmul(first, self_input)
    query_rows = split_heads(sent(projected[:, :D]))
    key_rows = split_heads(sent(projected[:, D:2 * D]))
    value_rows = split_heads(sent(projected[:, 2 * D:]))
    segments = segment_ids(lengths_row, group_rows)
    allowed = (segments[None, :] == 0) | (segments[None, :] == segments[:, None])
    attended = sent(attend(query_rows, key_rows, value_rows, allowed).reshape(group_rows, D))
    second_in = tokens_rows + low_back(matmul(attended, self_output))
    second = low(normalize(second_in) * norm_gains[1])
    cross_rows = split_heads(sent(matmul(second, cross_query)))
    memory = matmul(encoder_rows, cross_memory)
    cross_keys = split_heads(sent(memory[:, :D]))
    cross_values = split_heads(sent(memory[:, D:]))
    cross_attended = sent(attend(cross_rows, cross_keys, cross_values, None).reshape(group_rows, D))
    third_in = second_in + low_back(matmul(cross_attended, cross_output))
    third = low(normalize(third_in) * norm_gains[2])
    pre_act = low_back(matmul(third, widen_weight))
    activated = low(jax.nn.gelu(pre_act, approximate=False))
    return third_in + matmul(activated, narrow_weight)

def reference(tokens, encoder_states, lengths, timesteps, time_weight, self_input, self_output, cross_query, cross_memory, cross_output, widen_weight, narrow_weight, norm_gains, cotangent):
    weights = (time_weight.astype(jnp.float32), self_input.astype(jnp.float32), self_output.astype(jnp.float32), cross_query.astype(jnp.float32), cross_memory.astype(jnp.float32), cross_output.astype(jnp.float32), widen_weight.astype(jnp.float32), narrow_weight.astype(jnp.float32), norm_gains.astype(jnp.float32))

    def forward(tokens_float, encoder_float, weight_tuple):
        embedded = low(time_embedding(timesteps, D))
        modulation = matmul(embedded, weight_tuple[0])
        stepper = jax.checkpoint(partial(group_forward, weight_tuple))
        return lax.map(stepper, (tokens_float, encoder_float, lengths, modulation))
    layer_output, pullback = jax.vjp(forward, tokens.astype(jnp.float32), encoder_states.astype(jnp.float32), weights)
    grad_tokens, grad_encoder, grad_weights = pullback(cotangent.astype(jnp.float32))
    return (layer_output.astype(jnp.bfloat16), grad_tokens, grad_encoder, grad_weights[0], grad_weights[1], grad_weights[2], grad_weights[3], grad_weights[4], grad_weights[5], grad_weights[6], grad_weights[7], grad_weights[8])
```

```python
import math

import jax
import jax.numpy as jnp
from jax import lax
from jax.experimental import pallas as pl
from jax.experimental.pallas import tpu as pltpu
from jax.sharding import PartitionSpec as P


HEAD_DIM = 64
PAIR = 2 * HEAD_DIM
EPS = 1e-05
NEG = -1e30
F32 = jnp.float32
BF16 = jnp.bfloat16
AXES = ("seq", "fsdp")
VMEM_LIMIT = 60 * 2**20
BLOCK = 256


def dot(left, right, left_dim=1, right_dim=0):
    return lax.dot_general(
        left, right, (((left_dim,), (right_dim,)), ((), ())), preferred_element_type=F32
    )


def whole(shape):
    return pl.BlockSpec(shape, lambda *_: (0,) * len(shape))


def rows_of(width, block=BLOCK):
    return pl.BlockSpec((block, width), lambda i, *_: (i, 0))


def params():
    return pltpu.CompilerParams(vmem_limit_bytes=VMEM_LIMIT)


def cost(flops, moved, transcendentals=0):
    return pl.CostEstimate(
        flops=int(flops), bytes_accessed=int(moved), transcendentals=int(transcendentals)
    )


def normalized(values):
    average = jnp.mean(values, axis=-1, keepdims=True)
    centred = values - average
    spread = jnp.mean(centred * centred, axis=-1, keepdims=True)
    scale = lax.rsqrt(spread + EPS)
    return centred * scale, scale


def norm_backward(upstream, normed, scale):
    mean_up = jnp.mean(upstream, axis=-1, keepdims=True)
    mean_both = jnp.mean(upstream * normed, axis=-1, keepdims=True)
    return (upstream - mean_up - normed * mean_both) * scale


def lane_is(part):
    lane = lax.broadcasted_iota(jnp.int32, (1, PAIR), 1)
    return lane < HEAD_DIM if part == 0 else lane >= HEAD_DIM


def half_of(values, part):
    return jnp.where(lane_is(part), values, jnp.zeros_like(values))


def pair_at(index):
    return pl.ds(pl.multiple_of(index * PAIR, PAIR), PAIR)


def project_body(tokens_ref, mod_ref, weight_ref, q_ref, kv_ref, normed_ref):
    width = tokens_ref.shape[1]
    normed, _ = normalized(tokens_ref[...].astype(F32))
    first = (normed * mod_ref[0:1, :] + mod_ref[1:2, :]).astype(BF16)
    normed_ref[...] = first
    projected = dot(first, weight_ref[...])
    q_ref[...] = (projected[:, :width] * HEAD_DIM**-0.5).astype(BF16)
    kv_ref[...] = projected[:, width:].astype(BF16)


def project(tokens, mod, weight):
    rows, width = tokens.shape
    return pl.pallas_call(
        project_body,
        name="project",
        grid=(rows // BLOCK,),
        in_specs=[rows_of(width), whole(mod.shape), whole(weight.shape)],
        out_specs=[rows_of(width), rows_of(2 * width), rows_of(width)],
        out_shape=[
            jax.ShapeDtypeStruct((rows, width), BF16),
            jax.ShapeDtypeStruct((rows, 2 * width), BF16),
            jax.ShapeDtypeStruct((rows, width), BF16),
        ],
        compiler_params=params(),
        cost_estimate=cost(6 * rows * width * width, 10 * rows * width),
    )(tokens, mod, weight)


def memory_body(enc_ref, weight_ref, kv_ref):
    kv_ref[...] = dot(enc_ref[...], weight_ref[...]).astype(BF16)


def project_memory(encoder, weight):
    rows, width = encoder.shape
    return pl.pallas_call(
        memory_body,
        name="project_memory",
        grid=(rows // BLOCK,),
        in_specs=[rows_of(width), whole(weight.shape)],
        out_specs=rows_of(2 * width),
        out_shape=jax.ShapeDtypeStruct((rows, 2 * width), BF16),
        compiler_params=params(),
        cost_estimate=cost(4 * rows * width * width, 8 * rows * width),
    )(encoder, weight)


def block_start(info, block_index, block, quarter):
    per_quarter = quarter // block
    first = block_index < per_quarter
    place = jnp.where(first, info[3], 1 - info[3])
    return (2 * info[2] + place) * quarter + (block_index % per_quarter) * block


def place_keys(info, own, other, scratch, quarter):
    for source, core in ((own, info[2]), (other, 1 - info[2])):
        for part in range(2):
            place = info[3] if part == 0 else 1 - info[3]
            start = pl.multiple_of((2 * core + place) * quarter, quarter)
            scratch[pl.ds(start, quarter), :] = source[part * quarter : (part + 1) * quarter, :]


def self_forward_body(
    info,
    q_ref,
    own_ref,
    other_ref,
    tokens_ref,
    out_weight_ref,
    gain_ref,
    query_weight_ref,
    att_ref,
    lse_ref,
    second_ref,
    cq_ref,
    keys,
    bias,
):
    step = pl.program_id(0)
    block, width = q_ref.shape
    total = keys.shape[0]
    half = total // 2
    quarter = half // 2

    @pl.when(step == 0)
    def _():
        place_keys(info, own_ref, other_ref, keys, quarter)

    start = block_start(info, step, block, quarter)
    qpos = start + lax.broadcasted_iota(jnp.int32, (block, 1), 0)
    first, second = info[0], info[1]
    low = jnp.where((qpos >= first) & (qpos < second), second, first)
    high = jnp.where(qpos >= second, second, total)
    kpos = half + lax.broadcasted_iota(jnp.int32, (1, half), 1)
    bias[...] = jnp.where((kpos >= low) & (kpos < high), NEG, 0.0)

    def pair(index, carry):
        lanes = pair_at(index)
        kk = keys[:, lanes]
        vv = keys[:, pair_at(index + width // PAIR)]
        qq = q_ref[:, lanes]
        outs = []
        sums = []
        for part in range(2):
            qe = half_of(qq, part)
            s0 = dot(qe, kk[:half], 1, 1)
            s1 = dot(qe, kk[half:], 1, 1) + bias[...]
            top = jnp.maximum(
                jnp.max(s0, axis=1, keepdims=True), jnp.max(s1, axis=1, keepdims=True)
            )
            p0 = jnp.exp(s0 - top)
            p1 = jnp.exp(s1 - top)
            norm = jnp.sum(p0, axis=1, keepdims=True) + jnp.sum(p1, axis=1, keepdims=True)
            out = dot(p0.astype(BF16), vv[:half]) + dot(p1.astype(BF16), vv[half:])
            outs.append(out / norm)
            sums.append(top + jnp.log(norm))
        att_ref[:, lanes] = jnp.where(lane_is(0), outs[0], outs[1]).astype(BF16)
        lse_ref[index] = jnp.concatenate(sums, axis=1).T
        return carry

    lax.fori_loop(0, width // PAIR, pair, 0)
    second_in = tokens_ref[...].astype(F32) + dot(att_ref[...], out_weight_ref[...])
    second_ref[...] = second_in
    normed, _ = normalized(second_in)
    normed = (normed * gain_ref[1:2, :]).astype(BF16)
    cq_ref[...] = (dot(normed, query_weight_ref[...]) * HEAD_DIM**-0.5).astype(BF16)


def self_forward(info, q, own, other, tokens, out_weight, gains, query_weight):
    rows, width = q.shape
    pairs = width // PAIR
    return pl.pallas_call(
        self_forward_body,
        name="self_forward",
        grid_spec=pltpu.PrefetchScalarGridSpec(
            num_scalar_prefetch=1,
            grid=(rows // BLOCK,),
            in_specs=[
                rows_of(width),
                whole(own.shape),
                whole(other.shape),
                rows_of(width),
                whole(out_weight.shape),
                whole(gains.shape),
                whole(query_weight.shape),
            ],
            out_specs=[
                rows_of(width),
                pl.BlockSpec((pairs, 2, BLOCK), lambda i, *_: (0, 0, i)),
                rows_of(width),
                rows_of(width),
            ],
            scratch_shapes=[
                pltpu.VMEM((2 * rows, 2 * width), BF16),
                pltpu.VMEM((BLOCK, rows), F32),
            ],
        ),
        out_shape=[
            jax.ShapeDtypeStruct((rows, width), BF16),
            jax.ShapeDtypeStruct((pairs, 2, rows), F32),
            jax.ShapeDtypeStruct((rows, width), F32),
            jax.ShapeDtypeStruct((rows, width), BF16),
        ],
        compiler_params=params(),
        cost_estimate=cost(
            32 * rows * rows * width, 20 * rows * width, 2 * rows * rows * width // HEAD_DIM
        ),
    )(info, q, own, other, tokens, out_weight, gains, query_weight)


def backward_pair(qq, dd, oo, kk, vv, kt, sums, pieces, add_keys, add_values):
    products = (oo.astype(F32) * dd.astype(F32)).T
    row = lax.broadcasted_iota(jnp.int32, (PAIR, 1), 0)
    grads = []
    for part in range(2):
        qe = half_of(qq, part)
        de = half_of(dd, part)
        inner = jnp.sum(
            products[part * HEAD_DIM : (part + 1) * HEAD_DIM], axis=0, keepdims=True
        )
        total = sums[part : part + 1, :]
        grad = None
        for piece, (begin, end, bias) in enumerate(pieces):
            scores = dot(kk(piece), qe, 1, 1)
            if bias is not None:
                scores = scores + bias
            probs = jnp.exp(scores - total)
            dprobs = dot(vv(piece), de, 1, 1)
            dscores = (probs * (dprobs - inner)).astype(BF16)
            add_values(piece, dot(probs.astype(BF16), de))
            add_keys(piece, dot(dscores, qe))
            term = dot(kt(piece), dscores)
            grad = term if grad is None else grad + term
        grads.append(grad)
    return (jnp.where(row < HEAD_DIM, grads[0], grads[1]).T * HEAD_DIM**-0.5).astype(BF16)


def self_backward_body(
    info,
    q_ref,
    own_ref,
    other_ref,
    att_ref,
    dat_ref,
    lse_ref,
    dq_ref,
    down_ref,
    dother_ref,
    keys,
    keys_t,
    acc,
    bias,
):
    step = pl.program_id(0)
    block, width = q_ref.shape
    total = keys.shape[0]
    half = total // 2
    quarter = half // 2

    @pl.when(step == 0)
    def _():
        place_keys(info, own_ref, other_ref, keys, quarter)
        keys_t[...] = keys[:, :width].T
        acc[...] = jnp.zeros_like(acc)

    start = block_start(info, step, block, quarter)
    qpos = start + lax.broadcasted_iota(jnp.int32, (1, block), 1)
    first, second = info[0], info[1]
    low = jnp.where((qpos >= first) & (qpos < second), second, first)
    high = jnp.where(qpos >= second, second, total)
    kpos = half + lax.broadcasted_iota(jnp.int32, (half, 1), 0)
    bias[...] = jnp.where((kpos >= low) & (kpos < high), NEG, 0.0)

    def pair(index, carry):
        lanes = pair_at(index)
        vlanes = pair_at(index + width // PAIR)
        spans = ((0, half), (half, total))

        def add_keys(piece, value):
            begin, end = spans[piece]
            acc[begin:end, lanes] += value

        def add_values(piece, value):
            begin, end = spans[piece]
            acc[begin:end, vlanes] += value

        dq_ref[:, lanes] = backward_pair(
            q_ref[:, lanes],
            dat_ref[:, lanes],
            att_ref[:, lanes],
            lambda piece: keys[spans[piece][0] : spans[piece][1], lanes],
            lambda piece: keys[spans[piece][0] : spans[piece][1], vlanes],
            lambda piece: keys_t[lanes, spans[piece][0] : spans[piece][1]],
            lse_ref[index],
            ((0, half, None), (half, total, bias[...])),
            add_keys,
            add_values,
        )
        return carry

    lax.fori_loop(0, width // PAIR, pair, 0)

    @pl.when(step == pl.num_programs(0) - 1)
    def _():
        for target, core in ((down_ref, info[2]), (dother_ref, 1 - info[2])):
            for part in range(2):
                place = info[3] if part == 0 else 1 - info[3]
                begin = pl.multiple_of((2 * core + place) * quarter, quarter)
                target[part * quarter : (part + 1) * quarter, :] = acc[
                    pl.ds(begin, quarter), :
                ].astype(BF16)


def self_backward(info, q, own, other, att, dat, lse):
    rows, width = q.shape
    pairs = width // PAIR
    return pl.pallas_call(
        self_backward_body,
        name="self_backward",
        grid_spec=pltpu.PrefetchScalarGridSpec(
            num_scalar_prefetch=1,
            grid=(rows // BLOCK,),
            in_specs=[
                rows_of(width),
                whole(own.shape),
                whole(other.shape),
                rows_of(width),
                rows_of(width),
                pl.BlockSpec((pairs, 2, BLOCK), lambda i, *_: (0, 0, i)),
            ],
            out_specs=[rows_of(width), whole(own.shape), whole(other.shape)],
            scratch_shapes=[
                pltpu.VMEM((2 * rows, 2 * width), BF16),
                pltpu.VMEM((width, 2 * rows), BF16),
                pltpu.VMEM((2 * rows, 2 * width), F32),
                pltpu.VMEM((rows, BLOCK), F32),
            ],
        ),
        out_shape=[
            jax.ShapeDtypeStruct((rows, width), BF16),
            jax.ShapeDtypeStruct(own.shape, BF16),
            jax.ShapeDtypeStruct(other.shape, BF16),
        ],
        compiler_params=params(),
        cost_estimate=cost(
            80 * rows * rows * width, 20 * rows * width, 2 * rows * rows * width // HEAD_DIM
        ),
    )(info, q, own, other, att, dat, lse)


def feed_body(
    cq_ref,
    own_ref,
    other_ref,
    second_ref,
    dy_ref,
    cout_ref,
    widen_ref,
    narrow_ref,
    gain_ref,
    out_ref,
    catt_ref,
    lse_ref,
    dthird_ref,
    dca_ref,
    gcout_ref,
    gwiden_ref,
    gnarrow_ref,
    ggain_ref,
    acc_cout,
    acc_widen,
    acc_narrow,
):
    step = pl.program_id(0)
    block, width = cq_ref.shape

    @pl.when(step == 0)
    def _():
        acc_cout[...] = jnp.zeros_like(acc_cout)
        acc_widen[...] = jnp.zeros_like(acc_widen)
        acc_narrow[...] = jnp.zeros_like(acc_narrow)
        ggain_ref[...] = jnp.zeros_like(ggain_ref)

    def pair(index, carry):
        lanes = pair_at(index)
        vlanes = pair_at(index + width // PAIR)
        qq = cq_ref[:, lanes]
        outs = []
        sums = []
        for part in range(2):
            qe = half_of(qq, part)
            s0 = dot(qe, own_ref[:, lanes], 1, 1)
            s1 = dot(qe, other_ref[:, lanes], 1, 1)
            top = jnp.maximum(
                jnp.max(s0, axis=1, keepdims=True), jnp.max(s1, axis=1, keepdims=True)
            )
            p0 = jnp.exp(s0 - top)
            p1 = jnp.exp(s1 - top)
            norm = jnp.sum(p0, axis=1, keepdims=True) + jnp.sum(p1, axis=1, keepdims=True)
            out = dot(p0.astype(BF16), own_ref[:, vlanes]) + dot(
                p1.astype(BF16), other_ref[:, vlanes]
            )
            outs.append(out / norm)
            sums.append(top + jnp.log(norm))
        catt_ref[:, lanes] = jnp.where(lane_is(0), outs[0], outs[1]).astype(BF16)
        lse_ref[index] = jnp.concatenate(sums, axis=1).T
        return carry

    lax.fori_loop(0, width // PAIR, pair, 0)

    catt = catt_ref[...]
    dy = dy_ref[...]
    gain = gain_ref[2:3, :]
    third = second_ref[...] + dot(catt, cout_ref[...])
    normed, scale = normalized(third)
    normed_low = (normed * gain).astype(BF16)
    pre = dot(normed_low, widen_ref[...])
    below = 0.5 * (1.0 + lax.erf(pre * math.sqrt(0.5)))
    bell = jnp.exp(-0.5 * pre * pre) * (1.0 / math.sqrt(2.0 * math.pi))
    act = (pre * below).astype(BF16)
    out_ref[...] = (third + dot(act, narrow_ref[...])).astype(BF16)
    dact = dot(dy, narrow_ref[...], 1, 1)
    dpre = (dact * (below + pre * bell)).astype(BF16)
    acc_narrow[...] += dot(act, dy, 0, 0)
    acc_widen[...] += dot(normed_low, dpre, 0, 0)
    dnormed = dot(dpre, widen_ref[...], 1, 1)
    ggain_ref[...] += jnp.sum(dnormed * normed, axis=0, keepdims=True)
    dthird = dy.astype(F32) + norm_backward(dnormed * gain, normed, scale)
    dthird_ref[...] = dthird
    dc = dthird.astype(BF16)
    dca_ref[...] = dot(dc, cout_ref[...], 1, 1).astype(BF16)
    acc_cout[...] += dot(catt, dc, 0, 0)

    @pl.when(step == pl.num_programs(0) - 1)
    def _():
        gcout_ref[...] = acc_cout[...].astype(BF16)
        gwiden_ref[...] = acc_widen[...].astype(BF16)
        gnarrow_ref[...] = acc_narrow[...].astype(BF16)


def feed(cq, own, other, second_in, dy, cout, widen, narrow, gains):
    rows, width = cq.shape
    hidden = widen.shape[1]
    pairs = width // PAIR
    return pl.pallas_call(
        feed_body,
        name="feed",
        grid=(rows // BLOCK,),
        in_specs=[
            rows_of(width),
            whole(own.shape),
            whole(other.shape),
            rows_of(width),
            rows_of(width),
            whole(cout.shape),
            whole(widen.shape),
            whole(narrow.shape),
            whole(gains.shape),
        ],
        out_specs=[
            rows_of(width),
            rows_of(width),
            pl.BlockSpec((pairs, 2, BLOCK), lambda i: (0, 0, i)),
            rows_of(width),
            rows_of(width),
            whole(cout.shape),
            whole(widen.shape),
            whole(narrow.shape),
            whole((1, width)),
        ],
        out_shape=[
            jax.ShapeDtypeStruct((rows, width), BF16),
            jax.ShapeDtypeStruct((rows, width), BF16),
            jax.ShapeDtypeStruct((pairs, 2, rows), F32),
            jax.ShapeDtypeStruct((rows, width), F32),
            jax.ShapeDtypeStruct((rows, width), BF16),
            jax.ShapeDtypeStruct(cout.shape, BF16),
            jax.ShapeDtypeStruct(widen.shape, BF16),
            jax.ShapeDtypeStruct(narrow.shape, BF16),
            jax.ShapeDtypeStruct((1, width), F32),
        ],
        scratch_shapes=[
            pltpu.VMEM(cout.shape, F32),
            pltpu.VMEM(widen.shape, F32),
            pltpu.VMEM(narrow.shape, F32),
        ],
        compiler_params=params(),
        cost_estimate=cost(
            16 * rows * rows * width + 12 * rows * width * hidden,
            24 * rows * width + 8 * width * hidden,
            rows * rows * width // HEAD_DIM + 2 * rows * hidden,
        ),
    )(cq, own, other, second_in, dy, cout, widen, narrow, gains)


def cross_backward_body(
    cq_ref,
    own_ref,
    other_ref,
    catt_ref,
    dca_ref,
    lse_ref,
    dthird_ref,
    second_ref,
    att_ref,
    query_weight_ref,
    out_weight_ref,
    gain_ref,
    dsecond_ref,
    dat_ref,
    down_ref,
    dother_ref,
    gquery_ref,
    gout_ref,
    ggain_ref,
    dcq,
    keys_t,
    acc,
    acc_query,
    acc_out,
):
    step = pl.program_id(0)
    block, width = cq_ref.shape
    count = own_ref.shape[0]

    @pl.when(step == 0)
    def _():
        keys_t[:, :count] = own_ref[:, :width].T
        keys_t[:, count:] = other_ref[:, :width].T
        acc[...] = jnp.zeros_like(acc)
        acc_query[...] = jnp.zeros_like(acc_query)
        acc_out[...] = jnp.zeros_like(acc_out)
        ggain_ref[...] = jnp.zeros_like(ggain_ref)

    def pair(index, carry):
        lanes = pair_at(index)
        vlanes = pair_at(index + width // PAIR)
        refs = (own_ref, other_ref)

        def add_keys(piece, value):
            acc[piece * count : (piece + 1) * count, lanes] += value

        def add_values(piece, value):
            acc[piece * count : (piece + 1) * count, vlanes] += value

        dcq[:, lanes] = backward_pair(
            cq_ref[:, lanes],
            dca_ref[:, lanes],
            catt_ref[:, lanes],
            lambda piece: refs[piece][:, lanes],
            lambda piece: refs[piece][:, vlanes],
            lambda piece: keys_t[lanes, piece * count : (piece + 1) * count],
            lse_ref[index],
            ((0, count, None), (count, 2 * count, None)),
            add_keys,
            add_values,
        )
        return carry

    lax.fori_loop(0, width // PAIR, pair, 0)

    gain = gain_ref[1:2, :]
    normed, scale = normalized(second_ref[...])
    normed_low = (normed * gain).astype(BF16)
    dnormed = dot(dcq[...], query_weight_ref[...], 1, 1)
    acc_query[...] += dot(normed_low, dcq[...], 0, 0)
    ggain_ref[...] += jnp.sum(dnormed * normed, axis=0, keepdims=True)
    dsecond = dthird_ref[...] + norm_backward(dnormed * gain, normed, scale)
    dsecond_ref[...] = dsecond
    da = dsecond.astype(BF16)
    dat_ref[...] = dot(da, out_weight_ref[...], 1, 1).astype(BF16)
    acc_out[...] += dot(att_ref[...], da, 0, 0)

    @pl.when(step == pl.num_programs(0) - 1)
    def _():
        down_ref[...] = acc[:count, :].astype(BF16)
        dother_ref[...] = acc[count:, :].astype(BF16)
        gquery_ref[...] = acc_query[...].astype(BF16)
        gout_ref[...] = acc_out[...].astype(BF16)


def cross_backward(
    cq, own, other, catt, dca, lse, dthird, second_in, att, query_weight, out_weight, gains
):
    rows, width = cq.shape
    count = own.shape[0]
    pairs = width // PAIR
    return pl.pallas_call(
        cross_backward_body,
        name="cross_backward",
        grid=(rows // BLOCK,),
        in_specs=[
            rows_of(width),
            whole(own.shape),
            whole(other.shape),
            rows_of(width),
            rows_of(width),
            pl.BlockSpec((pairs, 2, BLOCK), lambda i: (0, 0, i)),
            rows_of(width),
            rows_of(width),
            rows_of(width),
            whole(query_weight.shape),
            whole(out_weight.shape),
            whole(gains.shape),
        ],
        out_specs=[
            rows_of(width),
            rows_of(width),
            whole(own.shape),
            whole(other.shape),
            whole(query_weight.shape),
            whole(out_weight.shape),
            whole((1, width)),
        ],
        out_shape=[
            jax.ShapeDtypeStruct((rows, width), F32),
            jax.ShapeDtypeStruct((rows, width), BF16),
            jax.ShapeDtypeStruct(own.shape, BF16),
            jax.ShapeDtypeStruct(other.shape, BF16),
            jax.ShapeDtypeStruct(query_weight.shape, BF16),
            jax.ShapeDtypeStruct(out_weight.shape, BF16),
            jax.ShapeDtypeStruct((1, width), F32),
        ],
        scratch_shapes=[
            pltpu.VMEM((BLOCK, width), BF16),
            pltpu.VMEM((width, 2 * count), BF16),
            pltpu.VMEM((2 * count, 2 * width), F32),
            pltpu.VMEM(query_weight.shape, F32),
            pltpu.VMEM(out_weight.shape, F32),
        ],
        compiler_params=params(),
        cost_estimate=cost(
            40 * rows * rows * width, 30 * rows * width, rows * rows * width // HEAD_DIM
        ),
    )(cq, own, other, catt, dca, lse, dthird, second_in, att, query_weight, out_weight, gains)


def memory_backward_body(enc_ref, own_ref, got_ref, weight_ref, genc_ref, gweight_ref, acc):
    step = pl.program_id(0)

    @pl.when(step == 0)
    def _():
        acc[...] = jnp.zeros_like(acc)

    grads = (own_ref[...].astype(F32) + got_ref[...].astype(F32)).astype(BF16)
    genc_ref[...] = dot(grads, weight_ref[...], 1, 1).astype(BF16)
    acc[...] += dot(enc_ref[...], grads, 0, 0)

    @pl.when(step == pl.num_programs(0) - 1)
    def _():
        gweight_ref[...] = acc[...].astype(BF16)


def memory_backward(encoder, own, got, weight):
    rows, width = encoder.shape
    return pl.pallas_call(
        memory_backward_body,
        name="memory_backward",
        grid=(rows // BLOCK,),
        in_specs=[rows_of(width), rows_of(2 * width), rows_of(2 * width), whole(weight.shape)],
        out_specs=[rows_of(width), whole(weight.shape)],
        out_shape=[
            jax.ShapeDtypeStruct((rows, width), BF16),
            jax.ShapeDtypeStruct(weight.shape, BF16),
        ],
        scratch_shapes=[pltpu.VMEM(weight.shape, F32)],
        compiler_params=params(),
        cost_estimate=cost(8 * rows * width * width, 16 * rows * width),
    )(encoder, own, got, weight)


def project_backward_body(
    tokens_ref,
    normed_ref,
    dq_ref,
    own_ref,
    got_ref,
    dsecond_ref,
    mod_ref,
    weight_ref,
    gtokens_ref,
    gweight_ref,
    sums_ref,
    acc,
):
    step = pl.program_id(0)
    width = tokens_ref.shape[1]

    @pl.when(step == 0)
    def _():
        acc[...] = jnp.zeros_like(acc)
        sums_ref[...] = jnp.zeros_like(sums_ref)

    dq = dq_ref[...]
    dkv = (own_ref[...].astype(F32) + got_ref[...].astype(F32)).astype(BF16)
    first = normed_ref[...]
    acc[:, :width] += dot(first, dq, 0, 0)
    acc[:, width:] += dot(first, dkv, 0, 0)
    dnormed = dot(dq, weight_ref[:, :width], 1, 1) + dot(dkv, weight_ref[:, width:], 1, 1)
    normed, scale = normalized(tokens_ref[...].astype(F32))
    sums_ref[0:1, :] += jnp.sum(dnormed * normed, axis=0, keepdims=True)
    sums_ref[1:2, :] += jnp.sum(dnormed, axis=0, keepdims=True)
    gtokens_ref[...] = (
        dsecond_ref[...] + norm_backward(dnormed * mod_ref[0:1, :], normed, scale)
    ).astype(BF16)

    @pl.when(step == pl.num_programs(0) - 1)
    def _():
        gweight_ref[...] = acc[...].astype(BF16)


def project_backward(tokens, normed, dq, own, got, dsecond, mod, weight):
    rows, width = tokens.shape
    return pl.pallas_call(
        project_backward_body,
        name="project_backward",
        grid=(rows // BLOCK,),
        in_specs=[
            rows_of(width),
            rows_of(width),
            rows_of(width),
            rows_of(2 * width),
            rows_of(2 * width),
            rows_of(width),
            whole(mod.shape),
            whole(weight.shape),
        ],
        out_specs=[rows_of(width), whole(weight.shape), whole((2, width))],
        out_shape=[
            jax.ShapeDtypeStruct((rows, width), BF16),
            jax.ShapeDtypeStruct(weight.shape, BF16),
            jax.ShapeDtypeStruct((2, width), F32),
        ],
        scratch_shapes=[pltpu.VMEM(weight.shape, F32)],
        compiler_params=params(),
        cost_estimate=cost(12 * rows * width * width, 20 * rows * width),
    )(tokens, normed, dq, own, got, dsecond, mod, weight)


def time_embedding(step_values, model_width):
    half_width = model_width // 2
    frequency = jnp.exp(-math.log(10000.0) * jnp.arange(half_width, dtype=F32) / half_width)
    angles = step_values.astype(F32)[:, None] * frequency[None, :]
    return jnp.concatenate([jnp.sin(angles), jnp.cos(angles)], axis=-1).astype(BF16)


def placements(seq_count, fsdp_count):
    def at(seq, fsdp):
        return seq * fsdp_count + fsdp

    same, crossed, swap = [], [], []
    for seq in range(seq_count):
        for fsdp in range(fsdp_count):
            y, x = divmod(seq, 2)
            column, core = divmod(fsdp, 2)
            same.append((at(seq, fsdp), at(2 * core + x, 2 * column + y)))
            crossed.append((at(seq, fsdp), at(2 * core + 1 - x, 2 * column + y)))
            swap.append((at(seq, fsdp), at(seq, fsdp ^ 1)))
    return same, crossed, swap


def reverse(pairs):
    return [(target, source) for source, target in pairs]


def make(seq_count, fsdp_count):
    same, crossed, swap = placements(seq_count, fsdp_count)

    def on_device(
        tokens,
        encoder_states,
        lengths,
        timesteps,
        time_weight,
        self_input,
        self_output,
        cross_query,
        cross_memory,
        cross_output,
        widen_weight,
        narrow_weight,
        norm_gains,
        cotangent,
    ):
        width = tokens.shape[2]
        seq = lax.axis_index("seq")
        fsdp = lax.axis_index("fsdp")
        core = fsdp % 2
        side = seq % 2

        def to_work(values):
            mine = lax.dynamic_index_in_dim(values, side, 0, keepdims=False)
            others = lax.dynamic_index_in_dim(values, 1 - side, 0, keepdims=False)
            return jnp.concatenate(
                [lax.ppermute(mine, AXES, same), lax.ppermute(others, AXES, crossed)], axis=0
            )

        def to_home(values, kind):
            half = values.shape[0] // 2
            mine = lax.ppermute(values[:half], AXES, reverse(same))
            others = lax.ppermute(values[half:], AXES, reverse(crossed))
            first = jnp.where(side == 0, mine, others)
            second = jnp.where(side == 0, others, mine)
            return jnp.stack([first, second], axis=0).astype(kind)

        def gather(weight, axis=0):
            return lax.all_gather(weight, "fsdp", axis=axis, tiled=True)

        work_tokens = to_work(tokens)
        work_encoder = to_work(encoder_states)
        work_dy = to_work(cotangent)

        every = gather(jnp.concatenate([lengths, timesteps[:, None]], axis=1))
        group = 2 * (fsdp - core) + seq
        own_row = lax.dynamic_index_in_dim(every, group, 0, keepdims=False)
        info = jnp.stack([own_row[0], own_row[0] + own_row[1], core, side])
        embedded = time_embedding(every[:, 3], width)
        own_embedded = lax.dynamic_slice_in_dim(embedded, group, 1, 0)
        modulation = dot(own_embedded, gather(time_weight))
        gains = gather(norm_gains, 1).astype(F32)
        plus = 1.0 + modulation[:, :width]
        mod = jnp.concatenate([gains[0:1] * plus, modulation[:, width:]], axis=0)

        input_weight = gather(self_input)
        output_weight = gather(self_output)
        query_weight = gather(cross_query)
        memory_weight = gather(cross_memory)
        cout_weight = gather(cross_output)
        widen = gather(widen_weight)
        narrow = gather(narrow_weight)

        q, kv, normed_first = project(work_tokens, mod, input_weight)
        kv_other = lax.ppermute(kv, AXES, swap)
        ckv = project_memory(work_encoder, memory_weight)
        ckv_other = lax.ppermute(ckv, AXES, swap)
        att, lse, second_in, cq = self_forward(
            info, q, kv, kv_other, work_tokens, output_weight, gains, query_weight
        )
        (layer_out, catt, cross_lse, dthird, dca, gcout, gwiden, gnarrow, ggain_third) = feed(
            cq, ckv, ckv_other, second_in, work_dy, cout_weight, widen, narrow, gains
        )
        (dsecond, dat, dckv, dckv_other, gquery, gout, ggain_second) = cross_backward(
            cq,
            ckv,
            ckv_other,
            catt,
            dca,
            cross_lse,
            dthird,
            second_in,
            att,
            query_weight,
            output_weight,
            gains,
        )
        dckv_got = lax.ppermute(dckv_other, AXES, swap)
        genc, gmemory = memory_backward(work_encoder, dckv, dckv_got, memory_weight)
        dq, dkv, dkv_other = self_backward(info, q, kv, kv_other, att, dat, lse)
        dkv_got = lax.ppermute(dkv_other, AXES, swap)
        gtokens, ginput, sums = project_backward(
            work_tokens, normed_first, dq, dkv, dkv_got, dsecond, mod, input_weight
        )

        def reduce_rows(grad):
            part = lax.psum_scatter(grad, "fsdp", scatter_dimension=0, tiled=True)
            return lax.psum(part, "seq").astype(F32)

        dmodulation = jnp.concatenate([gains[0:1] * sums[0:1], sums[1:2]], axis=1)
        every_dmod = lax.all_gather(dmodulation, AXES, axis=0, tiled=True)
        rows = time_weight.shape[0]
        own_columns = lax.dynamic_slice_in_dim(embedded, fsdp * rows, rows, 1)
        by_group = every_dmod.reshape(seq_count, fsdp_count // 2, 2, 2 * width).sum(axis=2)
        by_group = by_group.transpose(1, 0, 2).reshape(-1, 2 * width)
        gtime = lax.dot_general(
            own_columns.astype(F32),
            by_group,
            (((0,), (0,)), ((), ())),
            precision=lax.Precision.HIGHEST,
            preferred_element_type=F32,
        )
        ggains = jnp.concatenate([plus * sums[0:1], ggain_second, ggain_third], axis=0)
        ggains = lax.psum(ggains, AXES)
        gain_width = norm_gains.shape[1]
        ggains = lax.dynamic_slice_in_dim(ggains, fsdp * gain_width, gain_width, 1)
        return (
            to_home(layer_out, BF16),
            to_home(gtokens, F32),
            to_home(genc, F32),
            gtime,
            reduce_rows(ginput),
            reduce_rows(gout),
            reduce_rows(gquery),
            reduce_rows(gmemory),
            reduce_rows(gcout),
            reduce_rows(gwiden),
            reduce_rows(gnarrow),
            ggains,
        )

    return on_device


def solution(mesh):
    rows = P("fsdp", "seq", None)
    weight = P("fsdp", None)
    in_specs = (rows, rows, P("fsdp", None), P("fsdp")) + (weight,) * 8 + (P(None, "fsdp"), rows)
    out_specs = (rows,) * 3 + (weight,) * 8 + (P(None, "fsdp"),)
    return jax.shard_map(
        make(mesh.shape["seq"], mesh.shape["fsdp"]),
        mesh=mesh,
        in_specs=in_specs,
        out_specs=out_specs,
        check_vma=False,
    )
```

```python
import math

import jax
import jax.numpy as jnp
from jax import lax
from jax.experimental import pallas as pl
from jax.experimental.pallas import tpu as pltpu
from jax.sharding import PartitionSpec as P


HEAD_DIM = 64
PAIR = 2 * HEAD_DIM
EPS = 1e-05
NEG = -1e30
F32 = jnp.float32
BF16 = jnp.bfloat16
AXES = ("seq", "fsdp")
VMEM_LIMIT = 60 * 2**20
BLOCK = 256


def dot(left, right, left_dim=1, right_dim=0):
    return lax.dot_general(
        left, right, (((left_dim,), (right_dim,)), ((), ())), preferred_element_type=F32
    )


def whole(shape):
    return pl.BlockSpec(shape, lambda *_: (0,) * len(shape))


def rows_of(width, block=BLOCK):
    return pl.BlockSpec((block, width), lambda i, *_: (i, 0))


def params():
    return pltpu.CompilerParams(vmem_limit_bytes=VMEM_LIMIT)


def cost(flops, moved, transcendentals=0):
    return pl.CostEstimate(
        flops=int(flops), bytes_accessed=int(moved), transcendentals=int(transcendentals)
    )


def normalized(values):
    average = jnp.mean(values, axis=-1, keepdims=True)
    centred = values - average
    spread = jnp.mean(centred * centred, axis=-1, keepdims=True)
    scale = lax.rsqrt(spread + EPS)
    return centred * scale, scale


def norm_backward(upstream, normed, scale):
    mean_up = jnp.mean(upstream, axis=-1, keepdims=True)
    mean_both = jnp.mean(upstream * normed, axis=-1, keepdims=True)
    return (upstream - mean_up - normed * mean_both) * scale


def lane_is(part):
    lane = lax.broadcasted_iota(jnp.int32, (1, PAIR), 1)
    return lane < HEAD_DIM if part == 0 else lane >= HEAD_DIM


def half_of(values, part):
    return jnp.where(lane_is(part), values, jnp.zeros_like(values))


def pair_at(index):
    return pl.ds(pl.multiple_of(index * PAIR, PAIR), PAIR)


class Weight:
    def __init__(self, arrays, start, width):
        self.arrays = arrays
        self.start = start
        self.width = width

    def columns(self, start, width):
        return Weight(self.arrays, self.start + start, width)

    @property
    def split(self):
        return len(self.arrays) == 2

    @property
    def rows(self):
        first = self.arrays[0]
        return 2 * first.shape[0] * first.shape[1] if self.split else first.shape[0]

    def specs(self):
        place = self.start // self.width
        if self.split:
            nz, shard, _ = self.arrays[0].shape
            return [pl.BlockSpec((nz, shard, self.width), lambda *_: (0, 0, place))] * 2
        return [pl.BlockSpec((self.rows, self.width), lambda *_: (0, place))]

    def scratch(self):
        return pltpu.VMEM((self.rows, self.width) if self.split else (8, 128), BF16)

    def load(self, info, refs, scratch):
        if not self.split:
            return refs[0]

        @pl.when(pl.program_id(0) == 0)
        def _():
            count, shard, _ = refs[0].shape
            for core, ref in ((info[2], refs[0]), (1 - info[2], refs[1])):
                for shift in range(count):
                    owner = lax.rem(info[4] - shift + count, count)
                    start = pl.multiple_of((2 * owner + core) * shard, shard)
                    scratch[pl.ds(start, shard), :] = ref[shift]

        return scratch


class FeedWeights:
    def __init__(self, arrays, hidden):
        self.arrays = arrays
        self.hidden = hidden

    @property
    def split(self):
        return len(self.arrays[0].shape) == 4

    def specs(self):
        return [
            pl.BlockSpec(a.shape, lambda *_, rank=len(a.shape): (0,) * rank) for a in self.arrays
        ]

    def scratch(self):
        if not self.split:
            return [pltpu.VMEM((8, 128), BF16)] * 2
        width = self.arrays[0].shape[3]
        return [pltpu.VMEM((width, self.hidden), BF16), pltpu.VMEM((self.hidden, width), BF16)]

    def load(self, info, refs, scratch):
        if not self.split:
            return refs
        widen, narrow = scratch

        @pl.when(pl.program_id(0) == 0)
        def _():
            seqs, count, rows, width = refs[0].shape
            blocks = self.hidden // width
            short = rows // (2 * blocks)
            tall = rows // 2
            for core, ref in ((info[2], refs[0]), (1 - info[2], refs[1])):
                for turn in range(seqs):
                    seq = lax.bitwise_xor(info[5], turn)
                    for shift in range(count):
                        owner = 2 * lax.rem(info[4] - shift + count, count) + core
                        start = pl.multiple_of((owner * seqs + seq) * short, short)
                        for block in range(blocks):
                            widen[pl.ds(start, short), block * width : (block + 1) * width] = ref[
                                turn, shift, block * short : (block + 1) * short, :
                            ]
                        start = pl.multiple_of((owner * seqs + seq) * tall, tall)
                        narrow[pl.ds(start, tall), :] = ref[turn, shift, tall:, :]

        return widen, narrow


def pack_rows(packed_ref, offset, grad_ref):
    count = packed_ref.shape[0]
    width = packed_ref.shape[2]
    rows = grad_ref.shape[0] // count
    for shard in range(count):
        for block in range(grad_ref.shape[1] // width):
            packed_ref[shard, offset + block * rows : offset + (block + 1) * rows, :] = grad_ref[
                shard * rows : (shard + 1) * rows, block * width : (block + 1) * width
            ].astype(packed_ref.dtype)
    return offset + rows * (grad_ref.shape[1] // width)


def unpack_rows(packed, offset, rows, columns):
    width = packed.shape[1]
    blocks = columns // width
    parts = [packed[offset + b * rows : offset + (b + 1) * rows] for b in range(blocks)]
    return jnp.concatenate(parts, axis=1) if blocks > 1 else parts[0]


def call(body, name, info, grid, inputs, outputs, scratch, estimate):
    return pl.pallas_call(
        body,
        name=name,
        grid_spec=pltpu.PrefetchScalarGridSpec(
            num_scalar_prefetch=1,
            grid=(grid,),
            in_specs=[spec for _, spec in inputs],
            out_specs=[spec for _, _, spec in outputs],
            scratch_shapes=scratch,
        ),
        out_shape=[jax.ShapeDtypeStruct(shape, kind) for shape, kind, _ in outputs],
        compiler_params=params(),
        cost_estimate=estimate,
    )(info, *[array for array, _ in inputs])


def project(info, tokens, mod, weight):
    rows, width = tokens.shape

    def body(info_ref, tokens_ref, mod_ref, *refs):
        weight_refs, (q_ref, kv_ref, normed_ref, scratch) = refs[:-4], refs[-4:]
        full = weight.load(info_ref, weight_refs, scratch)
        normed, _ = normalized(tokens_ref[...].astype(F32))
        first = (normed * mod_ref[0:1, :] + mod_ref[1:2, :]).astype(BF16)
        normed_ref[...] = first
        projected = dot(first, full[...])
        q_ref[...] = (projected[:, :width] * HEAD_DIM**-0.5).astype(BF16)
        kv_ref[...] = projected[:, width:].astype(BF16)

    return call(
        body,
        "project",
        info,
        rows // BLOCK,
        [(tokens, rows_of(width)), (mod, whole(mod.shape))]
        + list(zip(weight.arrays, weight.specs())),
        [
            ((rows, width), BF16, rows_of(width)),
            ((rows, 2 * width), BF16, rows_of(2 * width)),
            ((rows, width), BF16, rows_of(width)),
        ],
        [weight.scratch()],
        cost(6 * rows * width * width, 10 * rows * width),
    )


def project_memory(info, encoder, weight):
    rows, width = encoder.shape

    def body(info_ref, enc_ref, *refs):
        weight_refs, (kv_ref, scratch) = refs[:-2], refs[-2:]
        full = weight.load(info_ref, weight_refs, scratch)
        kv_ref[...] = dot(enc_ref[...], full[...]).astype(BF16)

    return call(
        body,
        "project_memory",
        info,
        rows // BLOCK,
        [(encoder, rows_of(width))] + list(zip(weight.arrays, weight.specs())),
        [((rows, 2 * width), BF16, rows_of(2 * width))],
        [weight.scratch()],
        cost(4 * rows * width * width, 8 * rows * width),
    )[0]


def block_start(info, block_index, block, quarter):
    per_quarter = quarter // block
    first = block_index < per_quarter
    place = jnp.where(first, info[3], 1 - info[3])
    return (2 * info[2] + place) * quarter + lax.rem(block_index, per_quarter) * block


def place_keys(info, own, other, scratch, lanes, quarter):
    for source, core in ((own, info[2]), (other, 1 - info[2])):
        for part in range(2):
            place = info[3] if part == 0 else 1 - info[3]
            start = pl.multiple_of((2 * core + place) * quarter, quarter)
            scratch[pl.ds(start, quarter), lanes] = source[
                part * quarter : (part + 1) * quarter, :
            ]


def forbidden(info, start, block, half, queries_dim):
    keys_dim = 1 - queries_dim
    qshape = [1, 1]
    qshape[queries_dim] = block
    kshape = [1, 1]
    kshape[keys_dim] = half
    qpos = start + lax.broadcasted_iota(jnp.int32, tuple(qshape), queries_dim)
    kpos = half + lax.broadcasted_iota(jnp.int32, tuple(kshape), keys_dim)
    first, second = info[0], info[1]
    low = jnp.where((qpos >= first) & (qpos < second), second, first)
    high = jnp.where(qpos >= second, second, 2 * half)
    return jnp.where((kpos >= low) & (kpos < high), NEG, 0.0)


def key_specs(array, lanes, split, width):
    rows = array.shape[0]
    count = width // lanes
    return [
        (array, pl.BlockSpec((rows, lanes), lambda *_: (0, split))),
        (array, pl.BlockSpec((rows, lanes), lambda *_: (0, count + split))),
    ]


def split_rows(lanes, split, block=BLOCK):
    return pl.BlockSpec((block, lanes), lambda i, *_: (i, split))


def forward_pair(qq, kk, vv, pieces):
    outs = []
    sums = []
    for part in range(2):
        qe = half_of(qq, part)
        scores = []
        for piece, bias in enumerate(pieces):
            s = dot(qe, kk(piece), 1, 1)
            scores.append(s if bias is None else s + bias)
        top = jnp.max(scores[0], axis=1, keepdims=True)
        for s in scores[1:]:
            top = jnp.maximum(top, jnp.max(s, axis=1, keepdims=True))
        norm = None
        out = None
        for piece, s in enumerate(scores):
            p = jnp.exp(s - top)
            total = jnp.sum(p, axis=1, keepdims=True)
            term = dot(p.astype(BF16), vv(piece))
            norm = total if norm is None else norm + total
            out = term if out is None else out + term
        outs.append(out / norm)
        sums.append(top + jnp.log(norm))
    joined = jnp.where(lane_is(0), outs[0], outs[1]).astype(BF16)
    return joined, jnp.concatenate(sums, axis=1).T


def self_forward(info, q, own, other, splits, split):
    rows, width = q.shape
    lanes = width // splits
    pairs = lanes // PAIR
    quarter = rows // 2

    def body(info_ref, q_ref, ok_ref, ov_ref, tk_ref, tv_ref, att_ref, lse_ref, keys, bias):
        step = pl.program_id(0)

        @pl.when(step == 0)
        def _():
            place_keys(info_ref, ok_ref, tk_ref, keys, slice(0, lanes), quarter)
            place_keys(info_ref, ov_ref, tv_ref, keys, slice(lanes, 2 * lanes), quarter)

        start = block_start(info_ref, step, BLOCK, quarter)
        bias[...] = forbidden(info_ref, start, BLOCK, rows, 0)

        def pair(index, carry):
            at = pair_at(index)
            vat = pair_at(index + pairs)
            att_ref[:, at], lse_ref[index] = forward_pair(
                q_ref[:, at],
                lambda piece: keys[piece * rows : (piece + 1) * rows, at],
                lambda piece: keys[piece * rows : (piece + 1) * rows, vat],
                (None, bias[...]),
            )
            return carry

        lax.fori_loop(0, pairs, pair, 0)

    return call(
        body,
        "self_forward",
        info,
        rows // BLOCK,
        [(q, split_rows(lanes, split))]
        + key_specs(own, lanes, split, width)
        + key_specs(other, lanes, split, width),
        [
            ((rows, lanes), BF16, rows_of(lanes)),
            ((pairs, 2, rows), F32, pl.BlockSpec((pairs, 2, BLOCK), lambda i, *_: (0, 0, i))),
        ],
        [pltpu.VMEM((2 * rows, 2 * lanes), BF16), pltpu.VMEM((BLOCK, rows), F32)],
        cost(32 * rows * rows * lanes, 12 * rows * lanes, 2 * rows * rows * lanes // HEAD_DIM),
    )


def middle(info, atts, tokens, out_weight, gains, query_weight):
    rows, width = tokens.shape
    count = len(atts)

    def body(info_ref, *refs):
        att_refs = refs[:count]
        tokens_ref, gain_ref = refs[count : count + 2]
        rest = refs[count + 2 : -4]
        out_refs, query_refs = rest[: len(rest) // 2], rest[len(rest) // 2 :]
        second_ref, cq_ref, out_scratch, query_scratch = refs[-4:]
        out_full = out_weight.load(info_ref, out_refs, out_scratch)
        query_full = query_weight.load(info_ref, query_refs, query_scratch)
        att = jnp.concatenate([ref[...] for ref in att_refs], axis=1)
        second_in = tokens_ref[...].astype(F32) + dot(att, out_full[...])
        second_ref[...] = second_in
        normed, _ = normalized(second_in)
        normed = (normed * gain_ref[1:2, :]).astype(BF16)
        cq_ref[...] = (dot(normed, query_full[...]) * HEAD_DIM**-0.5).astype(BF16)

    return call(
        body,
        "middle",
        info,
        rows // BLOCK,
        [(att, rows_of(att.shape[1])) for att in atts]
        + [(tokens, rows_of(width)), (gains, whole(gains.shape))]
        + list(zip(out_weight.arrays, out_weight.specs()))
        + list(zip(query_weight.arrays, query_weight.specs())),
        [((rows, width), F32, rows_of(width)), ((rows, width), BF16, rows_of(width))],
        [out_weight.scratch(), query_weight.scratch()],
        cost(4 * rows * width * width, 10 * rows * width),
    )


def backward_pair(qq, dd, oo, kk, vv, kt, sums, pieces, add_keys, add_values):
    products = (oo.astype(F32) * dd.astype(F32)).T
    row = lax.broadcasted_iota(jnp.int32, (PAIR, 1), 0)
    grads = []
    for part in range(2):
        qe = half_of(qq, part)
        de = half_of(dd, part)
        inner = jnp.sum(
            products[part * HEAD_DIM : (part + 1) * HEAD_DIM], axis=0, keepdims=True
        )
        total = sums[part : part + 1, :]
        grad = None
        for piece, bias in enumerate(pieces):
            scores = dot(kk(piece), qe, 1, 1)
            if bias is not None:
                scores = scores + bias
            probs = jnp.exp(scores - total)
            dprobs = dot(vv(piece), de, 1, 1)
            dscores = (probs * (dprobs - inner)).astype(BF16)
            add_values(piece, dot(probs.astype(BF16), de))
            add_keys(piece, dot(dscores, qe))
            term = dot(kt(piece), dscores)
            grad = term if grad is None else grad + term
        grads.append(grad)
    return (jnp.where(row < HEAD_DIM, grads[0], grads[1]).T * HEAD_DIM**-0.5).astype(BF16)


def self_backward(info, q, own, other, att, dat, lse, splits, split):
    rows, width = q.shape
    lanes = width // splits
    pairs = lanes // PAIR
    quarter = rows // 2

    def body(
        info_ref,
        q_ref,
        ok_ref,
        ov_ref,
        tk_ref,
        tv_ref,
        att_ref,
        dat_ref,
        lse_ref,
        dq_ref,
        down_ref,
        dother_ref,
        keys,
        keys_t,
        acc,
        bias,
    ):
        step = pl.program_id(0)

        @pl.when(step == 0)
        def _():
            place_keys(info_ref, ok_ref, tk_ref, keys, slice(0, lanes), quarter)
            place_keys(info_ref, ov_ref, tv_ref, keys, slice(lanes, 2 * lanes), quarter)
            keys_t[...] = keys[:, :lanes].T
            acc[...] = jnp.zeros_like(acc)

        start = block_start(info_ref, step, BLOCK, quarter)
        bias[...] = forbidden(info_ref, start, BLOCK, rows, 1)

        def pair(index, carry):
            at = pair_at(index)
            vat = pair_at(index + pairs)

            def add_keys(piece, value):
                acc[piece * rows : (piece + 1) * rows, at] += value

            def add_values(piece, value):
                acc[piece * rows : (piece + 1) * rows, vat] += value

            dq_ref[:, at] = backward_pair(
                q_ref[:, at],
                dat_ref[:, at],
                att_ref[:, at],
                lambda piece: keys[piece * rows : (piece + 1) * rows, at],
                lambda piece: keys[piece * rows : (piece + 1) * rows, vat],
                lambda piece: keys_t[at, piece * rows : (piece + 1) * rows],
                lse_ref[index],
                (None, bias[...]),
                add_keys,
                add_values,
            )
            return carry

        lax.fori_loop(0, pairs, pair, 0)

        @pl.when(step == pl.num_programs(0) - 1)
        def _():
            for target, core in ((down_ref, info_ref[2]), (dother_ref, 1 - info_ref[2])):
                for part in range(2):
                    place = info_ref[3] if part == 0 else 1 - info_ref[3]
                    begin = pl.multiple_of((2 * core + place) * quarter, quarter)
                    target[part * quarter : (part + 1) * quarter, :] = acc[
                        pl.ds(begin, quarter), :
                    ].astype(BF16)

    return call(
        body,
        "self_backward",
        info,
        rows // BLOCK,
        [(q, split_rows(lanes, split))]
        + key_specs(own, lanes, split, width)
        + key_specs(other, lanes, split, width)
        + [
            (att, rows_of(lanes)),
            (dat, split_rows(lanes, split)),
            (lse, pl.BlockSpec((pairs, 2, BLOCK), lambda i, *_: (0, 0, i))),
        ],
        [
            ((rows, lanes), BF16, rows_of(lanes)),
            ((rows, 2 * lanes), BF16, whole((rows, 2 * lanes))),
            ((rows, 2 * lanes), BF16, whole((rows, 2 * lanes))),
        ],
        [
            pltpu.VMEM((2 * rows, 2 * lanes), BF16),
            pltpu.VMEM((lanes, 2 * rows), BF16),
            pltpu.VMEM((2 * rows, 2 * lanes), F32),
            pltpu.VMEM((rows, BLOCK), F32),
        ],
        cost(80 * rows * rows * lanes, 20 * rows * lanes, 2 * rows * rows * lanes // HEAD_DIM),
    )


def feed(info, cq, own, other, second_in, dy, cout, weights, gains, shards):
    rows, width = cq.shape
    hidden = weights.hidden
    pairs = width // PAIR
    cout_count = len(cout.arrays)
    packed_rows = (width + width * (hidden // width) + hidden) // shards

    def body(info_ref, cq_ref, own_ref, other_ref, second_ref, dy_ref, gain_ref, *refs):
        cout_refs, feed_refs = refs[:cout_count], refs[cout_count : cout_count + 2]
        (
            out_ref,
            catt_ref,
            lse_ref,
            dthird_ref,
            dca_ref,
            packed_ref,
            ggain_ref,
            acc_cout,
            acc_widen,
            acc_narrow,
            cout_scratch,
            widen_scratch,
            narrow_scratch,
        ) = refs[cout_count + 2 :]
        cout_full = cout.load(info_ref, cout_refs, cout_scratch)
        widen_full, narrow_full = weights.load(info_ref, feed_refs, (widen_scratch, narrow_scratch))
        step = pl.program_id(0)

        @pl.when(step == 0)
        def _():
            acc_cout[...] = jnp.zeros_like(acc_cout)
            acc_widen[...] = jnp.zeros_like(acc_widen)
            acc_narrow[...] = jnp.zeros_like(acc_narrow)
            ggain_ref[...] = jnp.zeros_like(ggain_ref)

        key_refs = (own_ref, other_ref)

        def pair(index, carry):
            at = pair_at(index)
            vat = pair_at(index + pairs)
            catt_ref[:, at], lse_ref[index] = forward_pair(
                cq_ref[:, at],
                lambda piece: key_refs[piece][:, at],
                lambda piece: key_refs[piece][:, vat],
                (None, None),
            )
            return carry

        lax.fori_loop(0, pairs, pair, 0)

        catt = catt_ref[...]
        dy_low = dy_ref[...]
        gain = gain_ref[2:3, :]
        third = second_ref[...] + dot(catt, cout_full[...])
        normed, scale = normalized(third)
        normed_low = (normed * gain).astype(BF16)
        pre = dot(normed_low, widen_full[...])
        below = 0.5 * (1.0 + lax.erf(pre * math.sqrt(0.5)))
        bell = jnp.exp(-0.5 * pre * pre) * (1.0 / math.sqrt(2.0 * math.pi))
        act = (pre * below).astype(BF16)
        out_ref[...] = (third + dot(act, narrow_full[...])).astype(BF16)
        dact = dot(dy_low, narrow_full[...], 1, 1)
        dpre = (dact * (below + pre * bell)).astype(BF16)
        acc_narrow[...] += dot(act, dy_low, 0, 0)
        acc_widen[...] += dot(normed_low, dpre, 0, 0)
        dnormed = dot(dpre, widen_full[...], 1, 1)
        ggain_ref[...] += jnp.sum(dnormed * normed, axis=0, keepdims=True)
        dthird = dy_low.astype(F32) + norm_backward(dnormed * gain, normed, scale)
        dthird_ref[...] = dthird
        dc = dthird.astype(BF16)
        dca_ref[...] = dot(dc, cout_full[...], 1, 1).astype(BF16)
        acc_cout[...] += dot(catt, dc, 0, 0)

        @pl.when(step == pl.num_programs(0) - 1)
        def _():
            offset = pack_rows(packed_ref, 0, acc_cout)
            offset = pack_rows(packed_ref, offset, acc_widen)
            pack_rows(packed_ref, offset, acc_narrow)

    return call(
        body,
        "feed",
        info,
        rows // BLOCK,
        [
            (cq, rows_of(width)),
            (own, whole(own.shape)),
            (other, whole(other.shape)),
            (second_in, rows_of(width)),
            (dy, rows_of(width)),
            (gains, whole(gains.shape)),
        ]
        + list(zip(cout.arrays, cout.specs()))
        + list(zip(weights.arrays, weights.specs())),
        [
            ((rows, width), BF16, rows_of(width)),
            ((rows, width), BF16, rows_of(width)),
            ((pairs, 2, rows), F32, pl.BlockSpec((pairs, 2, BLOCK), lambda i, *_: (0, 0, i))),
            ((rows, width), F32, rows_of(width)),
            ((rows, width), BF16, rows_of(width)),
            ((shards, packed_rows, width), BF16, whole((shards, packed_rows, width))),
            ((1, width), F32, whole((1, width))),
        ],
        [
            pltpu.VMEM((width, width), F32),
            pltpu.VMEM((width, hidden), F32),
            pltpu.VMEM((hidden, width), F32),
            cout.scratch(),
        ]
        + weights.scratch(),
        cost(
            16 * rows * rows * width + 12 * rows * width * hidden,
            24 * rows * width + 8 * width * hidden,
            rows * rows * width // HEAD_DIM + 2 * rows * hidden,
        ),
    )


def cross_backward(info, cq, own, other, catt, dca, lse, splits, split):
    rows, width = cq.shape
    count = own.shape[0]
    lanes = width // splits
    pairs = lanes // PAIR

    def body(
        info_ref,
        cq_ref,
        ok_ref,
        ov_ref,
        tk_ref,
        tv_ref,
        catt_ref,
        dca_ref,
        lse_ref,
        dcq_ref,
        down_ref,
        dother_ref,
        keys_t,
        acc,
    ):
        step = pl.program_id(0)

        @pl.when(step == 0)
        def _():
            keys_t[:, :count] = ok_ref[...].T
            keys_t[:, count:] = tk_ref[...].T
            acc[...] = jnp.zeros_like(acc)

        key_refs = (ok_ref, tk_ref)
        value_refs = (ov_ref, tv_ref)

        def pair(index, carry):
            at = pair_at(index)
            vat = pair_at(index + pairs)

            def add_keys(piece, value):
                acc[piece * count : (piece + 1) * count, at] += value

            def add_values(piece, value):
                acc[piece * count : (piece + 1) * count, vat] += value

            dcq_ref[:, at] = backward_pair(
                cq_ref[:, at],
                dca_ref[:, at],
                catt_ref[:, at],
                lambda piece: key_refs[piece][:, at],
                lambda piece: value_refs[piece][:, at],
                lambda piece: keys_t[at, piece * count : (piece + 1) * count],
                lse_ref[index],
                (None, None),
                add_keys,
                add_values,
            )
            return carry

        lax.fori_loop(0, pairs, pair, 0)

        @pl.when(step == pl.num_programs(0) - 1)
        def _():
            down_ref[...] = acc[:count, :].astype(BF16)
            dother_ref[...] = acc[count:, :].astype(BF16)

    return call(
        body,
        "cross_backward",
        info,
        rows // BLOCK,
        [(cq, split_rows(lanes, split))]
        + key_specs(own, lanes, split, width)
        + key_specs(other, lanes, split, width)
        + [
            (catt, split_rows(lanes, split)),
            (dca, split_rows(lanes, split)),
            (lse, pl.BlockSpec((pairs, 2, BLOCK), lambda i, *_: (split, 0, i))),
        ],
        [
            ((rows, lanes), BF16, rows_of(lanes)),
            ((count, 2 * lanes), BF16, whole((count, 2 * lanes))),
            ((count, 2 * lanes), BF16, whole((count, 2 * lanes))),
        ],
        [pltpu.VMEM((lanes, 2 * count), BF16), pltpu.VMEM((2 * count, 2 * lanes), F32)],
        cost(40 * rows * rows * lanes, 20 * rows * lanes, rows * rows * lanes // HEAD_DIM),
    )


def middle_backward(info, dcqs, second_in, dthird, atts, out_weight, query_weight, gains, shards):
    rows, width = second_in.shape
    count = len(dcqs)
    packed_rows = 2 * width // shards

    def body(info_ref, *refs):
        dcq_refs, att_refs = refs[:count], refs[count : 2 * count]
        second_ref, dthird_ref, gain_ref = refs[2 * count : 2 * count + 3]
        rest = refs[2 * count + 3 : -8]
        out_refs, query_refs = rest[: len(rest) // 2], rest[len(rest) // 2 :]
        (
            dsecond_ref,
            dat_ref,
            packed_ref,
            ggain_ref,
            acc_query,
            acc_out,
            out_scratch,
            query_scratch,
        ) = refs[-8:]
        out_full = out_weight.load(info_ref, out_refs, out_scratch)
        query_full = query_weight.load(info_ref, query_refs, query_scratch)
        step = pl.program_id(0)

        @pl.when(step == 0)
        def _():
            acc_query[...] = jnp.zeros_like(acc_query)
            acc_out[...] = jnp.zeros_like(acc_out)
            ggain_ref[...] = jnp.zeros_like(ggain_ref)

        dcq = jnp.concatenate([ref[...] for ref in dcq_refs], axis=1)
        att = jnp.concatenate([ref[...] for ref in att_refs], axis=1)
        gain = gain_ref[1:2, :]
        normed, scale = normalized(second_ref[...])
        normed_low = (normed * gain).astype(BF16)
        dnormed = dot(dcq, query_full[...], 1, 1)
        acc_query[...] += dot(normed_low, dcq, 0, 0)
        ggain_ref[...] += jnp.sum(dnormed * normed, axis=0, keepdims=True)
        dsecond = dthird_ref[...] + norm_backward(dnormed * gain, normed, scale)
        dsecond_ref[...] = dsecond
        da = dsecond.astype(BF16)
        dat_ref[...] = dot(da, out_full[...], 1, 1).astype(BF16)
        acc_out[...] += dot(att, da, 0, 0)

        @pl.when(step == pl.num_programs(0) - 1)
        def _():
            offset = pack_rows(packed_ref, 0, acc_query)
            pack_rows(packed_ref, offset, acc_out)

    return call(
        body,
        "middle_backward",
        info,
        rows // BLOCK,
        [(a, rows_of(a.shape[1])) for a in dcqs]
        + [(a, rows_of(a.shape[1])) for a in atts]
        + [
            (second_in, rows_of(width)),
            (dthird, rows_of(width)),
            (gains, whole(gains.shape)),
        ]
        + list(zip(out_weight.arrays, out_weight.specs()))
        + list(zip(query_weight.arrays, query_weight.specs())),
        [
            ((rows, width), F32, rows_of(width)),
            ((rows, width), BF16, rows_of(width)),
            ((shards, packed_rows, width), BF16, whole((shards, packed_rows, width))),
            ((1, width), F32, whole((1, width))),
        ],
        [
            pltpu.VMEM((width, width), F32),
            pltpu.VMEM((width, width), F32),
            out_weight.scratch(),
            query_weight.scratch(),
        ],
        cost(8 * rows * width * width, 20 * rows * width),
    )


def sum_low(own_ref, got_ref):
    return (own_ref[...].astype(F32) + got_ref[...].astype(F32)).astype(BF16)


def memory_backward(info, encoder, owns, gots, weight, shards):
    rows, width = encoder.shape
    count = len(owns)
    lanes = width // count
    packed_rows = 2 * width // shards

    def body(info_ref, enc_ref, *refs):
        own_refs, got_refs = refs[:count], refs[count : 2 * count]
        weight_refs = refs[2 * count : -4]
        genc_ref, packed_ref, acc, scratch = refs[-4:]
        full = weight.load(info_ref, weight_refs, scratch)
        step = pl.program_id(0)

        @pl.when(step == 0)
        def _():
            acc[...] = jnp.zeros_like(acc)

        enc = enc_ref[...]
        total = None
        for split in range(count):
            grads = sum_low(own_refs[split], got_refs[split])
            for kind in range(2):
                at = slice(kind * width + split * lanes, kind * width + (split + 1) * lanes)
                piece = grads[:, kind * lanes : (kind + 1) * lanes]
                term = dot(piece, full[:, at], 1, 1)
                total = term if total is None else total + term
                acc[:, at] += dot(enc, piece, 0, 0)
        genc_ref[...] = total.astype(BF16)

        @pl.when(step == pl.num_programs(0) - 1)
        def _():
            pack_rows(packed_ref, 0, acc)

    return call(
        body,
        "memory_backward",
        info,
        rows // BLOCK,
        [(encoder, rows_of(width))]
        + [(a, rows_of(2 * lanes)) for a in owns]
        + [(a, rows_of(2 * lanes)) for a in gots]
        + list(zip(weight.arrays, weight.specs())),
        [
            ((rows, width), BF16, rows_of(width)),
            ((shards, packed_rows, width), BF16, whole((shards, packed_rows, width))),
        ],
        [pltpu.VMEM((width, 2 * width), F32), weight.scratch()],
        cost(8 * rows * width * width, 16 * rows * width),
    )


def project_backward(info, tokens, normed, dqs, owns, gots, dsecond, mod, weight, shards):
    rows, width = tokens.shape
    count = len(dqs)
    lanes = width // count
    packed_rows = 3 * width // shards

    def body(info_ref, tokens_ref, normed_ref, dsecond_ref, mod_ref, *refs):
        dq_refs, own_refs = refs[:count], refs[count : 2 * count]
        got_refs = refs[2 * count : 3 * count]
        weight_refs = refs[3 * count : -5]
        gtokens_ref, packed_ref, sums_ref, acc, scratch = refs[-5:]
        full = weight.load(info_ref, weight_refs, scratch)
        step = pl.program_id(0)

        @pl.when(step == 0)
        def _():
            acc[...] = jnp.zeros_like(acc)
            sums_ref[...] = jnp.zeros_like(sums_ref)

        first = normed_ref[...]
        dnormed = None
        for split in range(count):
            grads = sum_low(own_refs[split], got_refs[split])
            pieces = (dq_refs[split][...], grads[:, :lanes], grads[:, lanes:])
            for kind, piece in enumerate(pieces):
                at = slice(kind * width + split * lanes, kind * width + (split + 1) * lanes)
                acc[:, at] += dot(first, piece, 0, 0)
                term = dot(piece, full[:, at], 1, 1)
                dnormed = term if dnormed is None else dnormed + term
        unit, scale = normalized(tokens_ref[...].astype(F32))
        sums_ref[0:1, :] += jnp.sum(dnormed * unit, axis=0, keepdims=True)
        sums_ref[1:2, :] += jnp.sum(dnormed, axis=0, keepdims=True)
        gtokens_ref[...] = (
            dsecond_ref[...] + norm_backward(dnormed * mod_ref[0:1, :], unit, scale)
        ).astype(BF16)

        @pl.when(step == pl.num_programs(0) - 1)
        def _():
            pack_rows(packed_ref, 0, acc)

    return call(
        body,
        "project_backward",
        info,
        rows // BLOCK,
        [
            (tokens, rows_of(width)),
            (normed, rows_of(width)),
            (dsecond, rows_of(width)),
            (mod, whole(mod.shape)),
        ]
        + [(a, rows_of(lanes)) for a in dqs]
        + [(a, rows_of(2 * lanes)) for a in owns]
        + [(a, rows_of(2 * lanes)) for a in gots]
        + list(zip(weight.arrays, weight.specs())),
        [
            ((rows, width), BF16, rows_of(width)),
            ((shards, packed_rows, width), BF16, whole((shards, packed_rows, width))),
            ((2, width), F32, whole((2, width))),
        ],
        [pltpu.VMEM((width, 3 * width), F32), weight.scratch()],
        cost(12 * rows * width * width, 20 * rows * width),
    )


def permutations(seq_count, fsdp_count):
    columns = fsdp_count // 2

    def at(seq, fsdp):
        return seq * fsdp_count + fsdp

    def pairs(move):
        return [
            (at(seq, fsdp), at(*move(seq, fsdp)))
            for seq in range(seq_count)
            for fsdp in range(fsdp_count)
        ]

    def home(turn):
        def move(seq, fsdp):
            y, x = divmod(seq, 2)
            column, core = divmod(fsdp, 2)
            return 2 * core + (x ^ turn), 2 * column + y

        return move

    shift = {
        r: pairs(lambda seq, fsdp, r=r: (seq, (fsdp + 2 * r) % fsdp_count))
        for r in range(1, columns)
    }
    cross = {t: pairs(lambda seq, fsdp, t=t: (seq ^ t, fsdp)) for t in range(1, seq_count)}
    swap = pairs(lambda seq, fsdp: (seq, fsdp ^ 1))
    return pairs(home(0)), pairs(home(1)), swap, shift, cross


def reverse(pairs):
    return [(target, source) for source, target in pairs]


def after(values, signal):
    return lax.optimization_barrier((values, signal))[0]


class Direct:
    def __init__(self, perms, seq, fsdp, columns):
        self.same, self.crossed, self.swap_pairs, self.shifts, self.crosses = perms
        self.seq = seq
        self.core = fsdp % 2
        self.z = fsdp // 2
        self.columns = columns

    def permute(self, values, pairs):
        return lax.ppermute(values, AXES, pairs)

    def swap(self, values):
        return self.permute(values, self.swap_pairs)

    def along_z(self, values):
        parts = [values] + [
            self.permute(values, self.shifts[r]) for r in range(1, self.columns)
        ]
        return jnp.stack(parts, axis=0)

    def over_seq(self, values):
        return [values] + [self.permute(values, self.crosses[t]) for t in sorted(self.crosses)]

    def in_z_order(self, values, axis):
        count = self.columns
        turned = jnp.flip(values, axis)
        twice = jnp.concatenate([turned, turned], axis=axis)
        return lax.dynamic_slice_in_dim(twice, count - 1 - self.z, count, axis)

    def in_seq_order(self, parts):
        for bit in range(2):
            odd = (self.seq >> bit) % 2 == 1
            parts = [
                jnp.where(odd, parts[t ^ (1 << bit)], parts[t]) for t in range(len(parts))
            ]
        return parts

    def of_z(self, values, shift):
        return lax.dynamic_index_in_dim(
            values, lax.rem(self.z + shift, self.columns), 0, keepdims=False
        )

    def core_sum(self, packed):
        shards = packed.reshape((self.columns, 2) + packed.shape[1:])
        away = lax.dynamic_index_in_dim(shards, 1 - self.core, 1, keepdims=False)
        mine = lax.dynamic_index_in_dim(shards, self.core, 1, keepdims=False)
        return (mine.astype(F32) + self.swap(away).astype(F32)).astype(BF16)

    def z_sum(self, shards):
        total = self.of_z(shards, 0).astype(F32)
        for r in range(1, self.columns):
            total = total + self.permute(self.of_z(shards, r), self.shifts[r]).astype(F32)
        return lax.optimization_barrier(total.astype(BF16))

    def seq_sum(self, values):
        parts = [part.astype(F32) for part in self.over_seq(values)]
        return (parts[0] + parts[1]) + (parts[2] + parts[3])

    def reduce(self, packed):
        return self.seq_sum(self.z_sum(self.core_sum(packed)))


SPLITS = 2


def time_embedding(step_values, model_width):
    half_width = model_width // 2
    frequency = jnp.exp(-math.log(10000.0) * jnp.arange(half_width, dtype=F32) / half_width)
    angles = step_values.astype(F32)[:, None] * frequency[None, :]
    return jnp.concatenate([jnp.sin(angles), jnp.cos(angles)], axis=-1).astype(BF16)


def exact_dot(left, right):
    return lax.dot_general(
        left,
        right,
        (((0,), (0,)), ((), ())),
        precision=lax.Precision.HIGHEST,
        preferred_element_type=F32,
    )


def make(seq_count, fsdp_count):
    perms = permutations(seq_count, fsdp_count)
    same, crossed = perms[:2]
    columns = fsdp_count // 2
    shards = fsdp_count

    def on_device(
        tokens,
        encoder_states,
        lengths,
        timesteps,
        time_weight,
        self_input,
        self_output,
        cross_query,
        cross_memory,
        cross_output,
        widen_weight,
        narrow_weight,
        norm_gains,
        cotangent,
    ):
        width = tokens.shape[2]
        hidden = widen_weight.shape[1]
        shard = time_weight.shape[0]
        seq = lax.axis_index("seq")
        fsdp = lax.axis_index("fsdp")
        core = fsdp % 2
        side = seq % 2
        direct = Direct(perms, seq, fsdp, columns) if columns == 4 else None

        def to_work(values):
            mine = lax.dynamic_index_in_dim(values, side, 0, keepdims=False)
            others = lax.dynamic_index_in_dim(values, 1 - side, 0, keepdims=False)
            return jnp.concatenate(
                [lax.ppermute(mine, AXES, same), lax.ppermute(others, AXES, crossed)], axis=0
            )

        def to_home(values, kind):
            half = values.shape[0] // 2
            mine = lax.ppermute(values[:half], AXES, reverse(same))
            others = lax.ppermute(values[half:], AXES, reverse(crossed))
            first = jnp.where(side == 0, mine, others)
            second = jnp.where(side == 0, others, mine)
            return jnp.stack([first, second], axis=0).astype(kind)

        def gather(weight, axis=0):
            return lax.all_gather(weight, "fsdp", axis=axis, tiled=True)

        work_tokens = to_work(tokens)
        later = after((encoder_states, cotangent), work_tokens)
        work_encoder, work_dy = to_work(later[0]), to_work(later[1])

        group = 2 * (fsdp - core) + seq
        if direct:
            numbers = jnp.concatenate([timesteps.astype(F32), lengths.astype(F32).reshape(-1)])
            count = numbers.shape[0]
            small = jnp.concatenate(
                [
                    jnp.pad(norm_gains.astype(F32), ((0, 0), (0, 128 - norm_gains.shape[1]))),
                    jnp.pad(numbers[None], ((0, 4), (0, 128 - count))),
                ],
                axis=0,
            )
            small = direct.along_z(small)
            input_mine = direct.along_z(self_input)
            small_other = direct.swap(small)
            both = jnp.stack(
                [
                    jnp.where(core == 0, small, small_other),
                    jnp.where(core == 0, small_other, small),
                ],
                axis=1,
            )
            both = direct.in_z_order(both, 0)
            gains = both[:, :, :3, : norm_gains.shape[1]].transpose(2, 0, 1, 3).reshape(3, width)
            numbers = both[:, :, 3, :count].astype(jnp.int32)
            times = numbers[..., :2].reshape(-1)
            sizes = numbers[..., 2:].reshape(-1, 3)
            embedded = time_embedding(times, width)
            selected = lax.dynamic_index_in_dim(
                embedded.reshape(columns, seq_count, width), seq, 1, keepdims=False
            )
            selected = lax.dynamic_slice_in_dim(selected, fsdp * shard, shard, 1)
            partial = dot(selected, time_weight).reshape(columns, -1, 128)
            partial = partial + direct.swap(partial)
            modulation = direct.of_z(partial, 0)
            for r in range(1, columns):
                modulation = modulation + direct.permute(
                    direct.of_z(partial, r), direct.shifts[r]
                )
            modulation = modulation.reshape(1, 2 * width)
            input_weight = Weight([input_mine, direct.swap(input_mine)], 0, 3 * width)

            thin = widen_weight.shape[0] // seq_count
            tall = narrow_weight.shape[0] // seq_count
            wide = lax.dynamic_slice_in_dim(widen_weight, seq * thin, thin, 0)
            wide = wide.reshape(thin, hidden // width, width).transpose(1, 0, 2)
            high = lax.dynamic_slice_in_dim(narrow_weight, seq * tall, tall, 0)
            quarter = jnp.concatenate([wide.reshape(-1, width), high], axis=0)
            rest = jnp.concatenate([self_output, cross_query, cross_memory, cross_output], axis=1)
            quarter, rest = after((quarter, rest), partial)
            quarter = jnp.stack(direct.over_seq(direct.along_z(quarter)), axis=0)
            feed_weights = FeedWeights([quarter, direct.swap(quarter)], hidden)
            rest = direct.along_z(rest)
            rest = [rest, direct.swap(rest)]
            output_weight = Weight(rest, 0, width)
            query_weight = Weight(rest, width, width)
            memory_weight = Weight(rest, 2 * width, 2 * width)
            cout_weight = Weight(rest, 4 * width, width)
        else:
            times = gather(timesteps)
            sizes = gather(lengths)
            gains = gather(norm_gains, 1).astype(F32)
            embedded = time_embedding(times, width)
            own_embedded = lax.dynamic_slice_in_dim(embedded, group, 1, 0)
            modulation = dot(own_embedded, gather(time_weight))
            input_weight = Weight([gather(self_input)], 0, 3 * width)
            output_weight = Weight([gather(self_output)], 0, width)
            query_weight = Weight([gather(cross_query)], 0, width)
            memory_weight = Weight([gather(cross_memory)], 0, 2 * width)
            cout_weight = Weight([gather(cross_output)], 0, width)
            feed_weights = FeedWeights([gather(widen_weight), gather(narrow_weight)], hidden)

        own_row = lax.dynamic_index_in_dim(sizes, group, 0, keepdims=False)
        info = jnp.stack([own_row[0], own_row[0] + own_row[1], core, side, fsdp // 2, seq])
        plus = 1.0 + modulation[:, :width]
        mod = jnp.concatenate([gains[0:1] * plus, modulation[:, width:]], axis=0)

        def swap(values):
            return lax.ppermute(values, AXES, perms[2])

        def reduce(packed):
            if direct:
                return direct.reduce(packed)
            part = lax.psum_scatter(packed, "fsdp", scatter_dimension=0, tiled=True)
            return lax.psum(part[0], "seq").astype(F32)

        splits = range(SPLITS)
        q, kv, normed_first = project(info, work_tokens, mod, input_weight)
        kv_other = swap(kv)
        atts, lses = zip(*[self_forward(info, q, kv, kv_other, SPLITS, i) for i in splits])
        ckv = project_memory(info, work_encoder, memory_weight)
        ckv_other = swap(ckv)
        second_in, cq = middle(info, atts, work_tokens, output_weight, gains, query_weight)
        (layer_out, catt, cross_lse, dthird, dca, packed_feed, ggain_third) = feed(
            info, cq, ckv, ckv_other, second_in, work_dy, cout_weight, feed_weights, gains, shards
        )
        dcqs, dckvs, dckv_others = zip(
            *[
                cross_backward(info, cq, ckv, ckv_other, catt, dca, cross_lse, SPLITS, i)
                for i in splits
            ]
        )
        dckv_gots = [swap(a) for a in dckv_others]
        dsecond, dat, packed_middle, ggain_second = middle_backward(
            info, dcqs, second_in, dthird, atts, output_weight, query_weight, gains, shards
        )
        genc, packed_memory = memory_backward(
            info, work_encoder, dckvs, dckv_gots, memory_weight, shards
        )
        dqs, dkvs, dkv_others = zip(
            *[
                self_backward(info, q, kv, kv_other, atts[i], dat, lses[i], SPLITS, i)
                for i in splits
            ]
        )
        dkv_gots = [swap(a) for a in dkv_others]
        gtokens, packed_input, sums = project_backward(
            info,
            work_tokens,
            normed_first,
            dqs,
            dkvs,
            dkv_gots,
            dsecond,
            mod,
            input_weight,
            shards,
        )

        reduced_feed = reduce(packed_feed)
        reduced_middle = reduce(jnp.concatenate([packed_middle, packed_memory], axis=1))
        ggains = jnp.concatenate([plus * sums[0:1], ggain_second, ggain_third], axis=0)
        dmodulation = jnp.concatenate([gains[0:1] * sums[0:1], sums[1:2]], axis=0)
        if direct:
            vectors = jnp.pad(jnp.concatenate([ggains, dmodulation], axis=0), ((0, 11), (0, 0)))
            vectors = (vectors + direct.swap(vectors)).astype(BF16)
            chip = direct.core_sum(packed_input)
            size = chip.shape[1]
            total = direct.of_z(chip, 0).astype(F32)
            columns_vectors = [vectors]
            for r in range(1, columns):
                got = direct.permute(
                    jnp.concatenate([direct.of_z(chip, r), vectors], axis=0), direct.shifts[r]
                )
                total = total + got[:size].astype(F32)
                columns_vectors.append(got[size:])
            joined = jnp.concatenate([total.astype(BF16)] + columns_vectors, axis=0)
            joined = lax.optimization_barrier(joined)
            parts = [part.astype(F32) for part in direct.over_seq(joined)]
            summed = [part[:size] for part in parts]
            reduced_input = (summed[0] + summed[1]) + (summed[2] + summed[3])
            rows = jnp.stack(direct.in_seq_order([part[size:] for part in parts]), axis=0)
            rows = rows.reshape(seq_count, columns, 16, width)[:, :, :5]
            ggains = rows[:, :, :3].sum(axis=(0, 1))
            by_group = direct.in_z_order(rows[:, :, 3:], 1).transpose(1, 0, 2, 3)
            by_group = by_group.reshape(columns * seq_count, 2 * width)
        else:
            reduced_input = reduce(packed_input)
            ggains = lax.psum(ggains, AXES)
            by_group = lax.all_gather(dmodulation, AXES, axis=0)
            by_group = by_group.reshape(seq_count, columns, 2, 2 * width).sum(axis=2)
            by_group = by_group.transpose(1, 0, 2).reshape(-1, 2 * width)
        own_columns = lax.dynamic_slice_in_dim(embedded, fsdp * shard, shard, 1)
        gtime = exact_dot(own_columns.astype(F32), by_group)
        gain_width = norm_gains.shape[1]
        ggains = lax.dynamic_slice_in_dim(ggains, fsdp * gain_width, gain_width, 1)

        tall = narrow_weight.shape[0]
        return (
            to_home(layer_out, BF16),
            to_home(gtokens, F32),
            to_home(genc, F32),
            gtime,
            unpack_rows(reduced_input, 0, shard, 3 * width),
            unpack_rows(reduced_middle, shard, shard, width),
            unpack_rows(reduced_middle, 0, shard, width),
            unpack_rows(reduced_middle, 2 * shard, shard, 2 * width),
            unpack_rows(reduced_feed, 0, shard, width),
            unpack_rows(reduced_feed, shard, shard, hidden),
            unpack_rows(reduced_feed, shard * (1 + hidden // width), tall, width),
            ggains,
        )

    return on_device


def solution(mesh):
    rows = P("fsdp", "seq", None)
    weight = P("fsdp", None)
    in_specs = (rows, rows, P("fsdp", None), P("fsdp")) + (weight,) * 8 + (P(None, "fsdp"), rows)
    out_specs = (rows,) * 3 + (weight,) * 8 + (P(None, "fsdp"),)
    return jax.shard_map(
        make(mesh.shape["seq"], mesh.shape["fsdp"]),
        mesh=mesh,
        in_specs=in_specs,
        out_specs=out_specs,
        check_vma=False,
    )
```

```python
import math

import jax
import jax.numpy as jnp
from jax import lax
from jax.experimental import pallas as pl
from jax.experimental.pallas import tpu as pltpu
from jax.sharding import PartitionSpec as P


HEAD_DIM = 64
PAIR = 2 * HEAD_DIM
EPS = 1e-05
NEG = -1e30
F32 = jnp.float32
BF16 = jnp.bfloat16
AXES = ("seq", "fsdp")
VMEM_LIMIT = 60 * 2**20
BLOCK = 256


def dot(left, right, left_dim=1, right_dim=0):
    return lax.dot_general(
        left, right, (((left_dim,), (right_dim,)), ((), ())), preferred_element_type=F32
    )


def whole(shape):
    return pl.BlockSpec(shape, lambda *_: (0,) * len(shape))


def rows_of(width, block=BLOCK):
    return pl.BlockSpec((block, width), lambda i, *_: (i, 0))


def params():
    return pltpu.CompilerParams(vmem_limit_bytes=VMEM_LIMIT)


def cost(flops, moved, transcendentals=0):
    return pl.CostEstimate(
        flops=int(flops), bytes_accessed=int(moved), transcendentals=int(transcendentals)
    )


def normalized(values):
    average = jnp.mean(values, axis=-1, keepdims=True)
    centred = values - average
    spread = jnp.mean(centred * centred, axis=-1, keepdims=True)
    scale = lax.rsqrt(spread + EPS)
    return centred * scale, scale


def norm_backward(upstream, normed, scale):
    mean_up = jnp.mean(upstream, axis=-1, keepdims=True)
    mean_both = jnp.mean(upstream * normed, axis=-1, keepdims=True)
    return (upstream - mean_up - normed * mean_both) * scale


def lane_is(part):
    lane = lax.broadcasted_iota(jnp.int32, (1, PAIR), 1)
    return lane < HEAD_DIM if part == 0 else lane >= HEAD_DIM


def half_of(values, part):
    return jnp.where(lane_is(part), values, jnp.zeros_like(values))


def pair_at(index):
    return pl.ds(pl.multiple_of(index * PAIR, PAIR), PAIR)


class Weight:
    def __init__(self, pieces, start, width):
        self.arrays = pieces
        self.start = start
        self.width = width

    @property
    def split(self):
        return len(self.arrays) > 1

    @property
    def rows(self):
        return len(self.arrays) * self.arrays[0].shape[0]

    @property
    def aligned(self):
        return self.start % self.width == 0

    def inputs(self):
        if not self.aligned:
            return [(array, whole(array.shape)) for array in self.arrays]
        place = self.start // self.width
        shape = (self.arrays[0].shape[0], self.width)
        return [(array, pl.BlockSpec(shape, lambda *_: (0, place))) for array in self.arrays]

    def scratch(self):
        return pltpu.VMEM((self.rows, self.width) if self.split else (16, 128), BF16)

    def load(self, info, refs, scratch):
        if not self.split:
            return refs[0]
        columns = slice(0, self.width) if self.aligned else slice(self.start, self.start + self.width)

        @pl.when(pl.program_id(0) == 0)
        def _():
            count = len(refs) // 2
            shard = refs[0].shape[0]
            for index, ref in enumerate(refs):
                turn, shift = divmod(index, count)
                core = info[2] if turn == 0 else 1 - info[2]
                owner = lax.rem(info[4] - shift + count, count)
                start = pl.multiple_of((2 * owner + core) * shard, shard)
                scratch[pl.ds(start, shard), :] = ref[:, columns]

        return scratch


class Halves:
    def __init__(self, arrays, start, rows):
        self.arrays = arrays
        self.start = start
        self.rows = rows
        self.shape = (2 * rows, arrays[0].shape[1])

    def inputs(self, block):
        width = self.shape[1]
        count = self.rows // block
        base = self.start // block
        return [
            (
                self.arrays[0],
                pl.BlockSpec((block, width), lambda i, *_: (base + jnp.minimum(i, count - 1), 0)),
            ),
            (
                self.arrays[1],
                pl.BlockSpec((block, width), lambda i, *_: (base + jnp.maximum(i - count, 0), 0)),
            ),
        ]

    def resident(self):
        place = self.start // self.rows
        spec = pl.BlockSpec((self.rows, self.shape[1]), lambda *_: (place, 0))
        return [(array, spec) for array in self.arrays]

    def load(self, first_ref, second_ref):
        half = pl.num_programs(0) // 2
        return jnp.where(pl.program_id(0) < half, first_ref[...], second_ref[...])


def half_outputs(rows, width, block):
    count = rows // block // 2
    half = (rows // 2, width)
    return [
        (half, BF16, pl.BlockSpec((block, width), lambda i, *_: (jnp.minimum(i, count - 1), 0))),
        (half, BF16, pl.BlockSpec((block, width), lambda i, *_: (jnp.maximum(i - count, 0), 0))),
    ]


def store_half(refs, value):
    first = pl.program_id(0) < pl.num_programs(0) // 2

    @pl.when(first)
    def _():
        refs[0][...] = value

    @pl.when(jnp.logical_not(first))
    def _():
        refs[1][...] = value


class FeedWeights:
    def __init__(self, arrays, hidden):
        self.arrays = arrays
        self.hidden = hidden

    @property
    def split(self):
        return len(self.arrays) > 2

    def inputs(self):
        return [(array, whole(array.shape)) for array in self.arrays]

    def scratch(self):
        if not self.split:
            return [pltpu.VMEM((16, 128), BF16)] * 2
        width = self.arrays[0].shape[1]
        return [pltpu.VMEM((width, self.hidden), BF16), pltpu.VMEM((self.hidden, width), BF16)]

    def load(self, info, refs, scratch):
        if not self.split:
            return refs
        widen, narrow = scratch

        @pl.when(pl.program_id(0) == 0)
        def _():
            count = len(refs) // 2
            rows, width = refs[0].shape
            blocks = self.hidden // width
            tall = rows // 2
            short = tall // blocks
            for index, ref in enumerate(refs):
                turn, shift = divmod(index, count)
                core = info[2] if turn == 0 else 1 - info[2]
                owner = 2 * lax.rem(info[4] - shift + count, count) + core
                start = pl.multiple_of(owner * short, short)
                for block in range(blocks):
                    widen[pl.ds(start, short), block * width : (block + 1) * width] = ref[
                        block * short : (block + 1) * short, :
                    ]
                start = pl.multiple_of(owner * tall, tall)
                narrow[pl.ds(start, tall), :] = ref[tall:, :]

        return widen, narrow


class Packing:
    def __init__(self, shards, direct, width):
        self.shards = shards
        self.direct = direct
        self.width = width

    def outputs(self, elements, extra=0):
        rows = elements // (self.shards * self.width)
        if self.direct:
            rows += extra
        if self.direct:
            shape = (self.shards // 2, rows, self.width)
            return [(shape, BF16, whole(shape))] * 2
        shape = (self.shards, rows, self.width)
        return [(shape, BF16, whole(shape))]

    def store(self, info, packed, grads):
        offset = 0
        for grad in grads:
            rows = grad.shape[0] // self.shards
            for block in range(grad.shape[1] // self.width):
                columns = slice(block * self.width, (block + 1) * self.width)
                into = slice(offset, offset + rows)
                if self.direct:
                    count = self.shards // 2
                    for ref, core in ((packed[0], info[2]), (packed[1], 1 - info[2])):
                        for shift in range(count):
                            owner = 2 * lax.rem(info[4] + shift, count) + core
                            start = pl.multiple_of(owner * rows, rows)
                            ref[shift, into, :] = grad[pl.ds(start, rows), columns].astype(BF16)
                else:
                    for shard in range(self.shards):
                        packed[0][shard, into, :] = grad[
                            shard * rows : (shard + 1) * rows, columns
                        ].astype(BF16)
                offset += rows


def unpack_rows(packed, offset, rows, columns):
    width = packed.shape[1]
    blocks = columns // width
    parts = [packed[offset + b * rows : offset + (b + 1) * rows] for b in range(blocks)]
    return jnp.concatenate(parts, axis=1) if blocks > 1 else parts[0]


def call(body, name, info, grid, inputs, outputs, scratch, estimate):
    return pl.pallas_call(
        body,
        name=name,
        grid_spec=pltpu.PrefetchScalarGridSpec(
            num_scalar_prefetch=1,
            grid=(grid,),
            in_specs=[spec for _, spec in inputs],
            out_specs=[spec for _, _, spec in outputs],
            scratch_shapes=scratch,
        ),
        out_shape=[jax.ShapeDtypeStruct(shape, kind) for shape, kind, _ in outputs],
        compiler_params=params(),
        cost_estimate=estimate,
    )(info, *[array for array, _ in inputs])


def block_start(info, block_index, block, quarter):
    per_quarter = quarter // block
    first = block_index < per_quarter
    place = jnp.where(first, info[3], 1 - info[3])
    return (2 * info[2] + place) * quarter + lax.rem(block_index, per_quarter) * block


def forbidden(info, start, block, half, queries_dim):
    keys_dim = 1 - queries_dim
    qshape = [1, 1]
    qshape[queries_dim] = block
    kshape = [1, 1]
    kshape[keys_dim] = half
    qpos = start + lax.broadcasted_iota(jnp.int32, tuple(qshape), queries_dim)
    kpos = half + lax.broadcasted_iota(jnp.int32, tuple(kshape), keys_dim)
    first, second = info[0], info[1]
    low = jnp.where((qpos >= first) & (qpos < second), second, first)
    high = jnp.where(qpos >= second, second, 2 * half)
    return jnp.where((kpos >= low) & (kpos < high), NEG, 0.0)


def key_specs(array, lanes, split, width):
    rows = array.shape[0]
    count = width // lanes
    return [
        (array, pl.BlockSpec((rows, lanes), lambda *_: (0, split))),
        (array, pl.BlockSpec((rows, lanes), lambda *_: (0, count + split))),
    ]


def split_rows(lanes, split, block=BLOCK):
    return pl.BlockSpec((block, lanes), lambda i, *_: (i, split))


def forward_pair(qq, kk, vv, pieces):
    outs = []
    sums = []
    for part in range(2):
        qe = half_of(qq, part)
        scores = []
        for piece, bias in enumerate(pieces):
            s = dot(qe, kk(piece), 1, 1)
            scores.append(s if bias is None else s + bias)
        top = jnp.max(scores[0], axis=1, keepdims=True)
        for s in scores[1:]:
            top = jnp.maximum(top, jnp.max(s, axis=1, keepdims=True))
        norm = None
        out = None
        for piece, s in enumerate(scores):
            p = jnp.exp(s - top)
            total = jnp.sum(p, axis=1, keepdims=True)
            term = dot(p.astype(BF16), vv(piece))
            norm = total if norm is None else norm + total
            out = term if out is None else out + term
        outs.append(out / norm)
        sums.append(top + jnp.log(norm))
    joined = jnp.where(lane_is(0), outs[0], outs[1]).astype(BF16)
    return joined, jnp.concatenate(sums, axis=1).T


def place_of(info, core, part):
    return 2 * core + (info[3] if part == 0 else 1 - info[3])


def self_forward(info, own, other, embedded, time, turned_gains, weight):
    rows, width = own.shape
    pairs = width // PAIR
    quarter = rows // 2
    weights = (weight, time, turned_gains)
    pieces = [len(w.arrays) for w in weights]

    def body(info_ref, embedded_ref, *refs):
        token_refs, refs = refs[:4], refs[4:]
        weight_refs = []
        for number in pieces:
            weight_refs.append(refs[:number])
            refs = refs[number:]
        (
            mod_ref,
            q_out,
            kv_out,
            normed_out,
            att_ref,
            lse_ref,
            queries,
            keys,
            normed,
            bias,
            *scratch,
            sems,
        ) = refs
        step = pl.program_id(0)
        full, time_full, gains_full = [
            w.load(info_ref, r, s) for w, r, s in zip(weights, weight_refs, scratch)
        ]
        copies = [
            pltpu.make_async_copy(queries, q_out, sems.at[0]),
            pltpu.make_async_copy(keys, kv_out, sems.at[1]),
            pltpu.make_async_copy(normed, normed_out, sems.at[2]),
        ]

        @pl.when(step == 0)
        def _():
            modulation = dot(embedded_ref[...], time_full[...])
            gains = gains_full[...].astype(F32).T[:3, :]
            plus = 1.0 + modulation[0:1, :width]
            shift = modulation[0:1, width:]
            mod_ref[...] = jnp.concatenate(
                [gains[0:1] * plus, shift, plus, gains, jnp.zeros((2, width), F32)], axis=0
            )
            for index, ref in enumerate(token_refs):
                turn, part = divmod(index, 2)
                core = info_ref[2] if turn == 0 else 1 - info_ref[2]
                begin = place_of(info_ref, core, part) * quarter
                for block in range(quarter // BLOCK):
                    into = slice(block * BLOCK, (block + 1) * BLOCK)
                    unit, _ = normalized(ref[into, :].astype(F32))
                    first = (unit * mod_ref[0:1, :] + mod_ref[1:2, :]).astype(BF16)
                    at = pl.ds(pl.multiple_of(begin + block * BLOCK, BLOCK), BLOCK)
                    keys[at, :] = dot(first, full[:, width:]).astype(BF16)
                    if turn == 0:
                        here = slice(part * quarter + block * BLOCK, part * quarter + (block + 1) * BLOCK)
                        normed[here, :] = first
                        queries[here, :] = (dot(first, full[:, :width]) * HEAD_DIM**-0.5).astype(BF16)
            for copy in copies:
                copy.start()

        start = block_start(info_ref, step, BLOCK, quarter)
        bias[...] = forbidden(info_ref, start, BLOCK, rows, 0)
        mine = pl.ds(pl.multiple_of(step * BLOCK, BLOCK), BLOCK)

        def pair(index, carry):
            at = pair_at(index)
            vat = pair_at(index + pairs)
            att_ref[:, at], lse_ref[index] = forward_pair(
                queries[mine, at],
                lambda piece: keys[piece * rows : (piece + 1) * rows, at],
                lambda piece: keys[piece * rows : (piece + 1) * rows, vat],
                (None, bias[...]),
            )
            return carry

        lax.fori_loop(0, pairs, pair, 0)

        @pl.when(step == pl.num_programs(0) - 1)
        def _():
            for copy in copies:
                copy.wait()

    anywhere = pl.BlockSpec(memory_space=pl.ANY)
    return call(
        body,
        "self_forward",
        info,
        rows // BLOCK,
        [(embedded, whole(embedded.shape))]
        + own.resident()
        + other.resident()
        + [entry for w in weights for entry in w.inputs()],
        [
            ((8, width), F32, whole((8, width))),
            ((rows, width), BF16, anywhere),
            ((2 * rows, 2 * width), BF16, anywhere),
            ((rows, width), BF16, anywhere),
            ((rows, width), BF16, rows_of(width)),
            ((pairs, 2, rows), F32, pl.BlockSpec((pairs, 2, BLOCK), lambda i, *_: (0, 0, i))),
        ],
        [
            pltpu.VMEM((rows, width), BF16),
            pltpu.VMEM((2 * rows, 2 * width), BF16),
            pltpu.VMEM((rows, width), BF16),
            pltpu.VMEM((BLOCK, rows), F32),
        ]
        + [w.scratch() for w in weights]
        + [pltpu.SemaphoreType.DMA((3,))],
        cost(32 * rows * rows * width, 12 * rows * width, 2 * rows * rows * width // HEAD_DIM),
    )


def cross_forward(info, att, tokens, own, other, out_weight, gains, query_weight, memory_weight):
    rows, width = att.shape
    pairs = width // PAIR
    count = own.rows
    weights = (out_weight, query_weight, memory_weight)
    pieces = [len(w.arrays) for w in weights]

    def body(info_ref, att_ref, first_ref, last_ref, gain_ref, *refs):
        enc_refs, refs = refs[:4], refs[4:]
        weight_refs = []
        for number in pieces:
            weight_refs.append(refs[:number])
            refs = refs[number:]
        second_ref, cq_ref, ckv_out, catt_ref, lse_ref, memory, *scratch, sem = refs
        out_full, query_full, memory_full = [
            w.load(info_ref, r, s) for w, r, s in zip(weights, weight_refs, scratch)
        ]
        step = pl.program_id(0)
        copy = pltpu.make_async_copy(memory, ckv_out, sem)

        @pl.when(step == 0)
        def _():
            for index, ref in enumerate(enc_refs):
                memory[index * count : (index + 1) * count, :] = dot(
                    ref[...], memory_full[...]
                ).astype(BF16)
            copy.start()

        second_in = tokens.load(first_ref, last_ref).astype(F32) + dot(att_ref[...], out_full[...])
        second_ref[...] = second_in
        normed, _ = normalized(second_in)
        normed = (normed * gain_ref[4:5, :]).astype(BF16)
        cq_ref[...] = (dot(normed, query_full[...]) * HEAD_DIM**-0.5).astype(BF16)

        def pair(index, carry):
            at = pair_at(index)
            vat = pair_at(index + pairs)
            catt_ref[:, at], lse_ref[index] = forward_pair(
                cq_ref[:, at],
                lambda piece: memory[:, at],
                lambda piece: memory[:, vat],
                (None,),
            )
            return carry

        lax.fori_loop(0, pairs, pair, 0)

        @pl.when(step == pl.num_programs(0) - 1)
        def _():
            copy.wait()

    return call(
        body,
        "cross_forward",
        info,
        rows // BLOCK,
        [(att, rows_of(width))]
        + tokens.inputs(BLOCK)
        + [(gains, whole(gains.shape))]
        + own.resident()
        + other.resident()
        + [entry for w in weights for entry in w.inputs()],
        [
            ((rows, width), F32, rows_of(width)),
            ((rows, width), BF16, rows_of(width)),
            ((4 * count, 2 * width), BF16, pl.BlockSpec(memory_space=pl.ANY)),
            ((rows, width), BF16, rows_of(width)),
            ((pairs, 2, rows), F32, pl.BlockSpec((pairs, 2, BLOCK), lambda i, *_: (0, 0, i))),
        ],
        [pltpu.VMEM((4 * count, 2 * width), BF16)]
        + [w.scratch() for w in weights]
        + [pltpu.SemaphoreType.DMA],
        cost(16 * rows * rows * width, 12 * rows * width, rows * rows * width // HEAD_DIM),
    )


def backward_pair(qq, dd, oo, kk, vv, kt, sums, pieces, add_keys, add_values):
    products = (oo.astype(F32) * dd.astype(F32)).T
    row_head = lax.broadcasted_iota(jnp.int32, (PAIR, 1), 0) // HEAD_DIM
    lane_head = lax.broadcasted_iota(jnp.int32, (1, PAIR), 1) // HEAD_DIM

    def head(part, total_grad):
        qe = jnp.where(lane_head == part, qq, jnp.zeros_like(qq))
        de = jnp.where(lane_head == part, dd, jnp.zeros_like(dd))
        inner = jnp.sum(jnp.where(row_head == part, products, 0.0), axis=0, keepdims=True)
        total = sums(part)
        grad = None
        for piece, bias in enumerate(pieces):
            scores = dot(kk(piece), qe, 1, 1)
            if bias is not None:
                scores = scores + bias
            probs = jnp.exp(scores - total)
            dprobs = dot(vv(piece), de, 1, 1)
            dscores = (probs * (dprobs - inner)).astype(BF16)
            add_values(piece, dot(probs.astype(BF16), de))
            add_keys(piece, dot(dscores, qe))
            term = dot(kt(piece), dscores)
            grad = term if grad is None else grad + term
        return total_grad + jnp.where(row_head == part, grad, 0.0)

    grad = lax.fori_loop(0, 2, head, jnp.zeros((PAIR, qq.shape[0]), F32))
    return (grad.T * HEAD_DIM**-0.5).astype(BF16)


def self_backward(info, q, kv, att, dat, lse, splits, split):
    rows, width = q.shape
    lanes = width // splits
    pairs = lanes // PAIR
    quarter = rows // 2

    def body(
        info_ref,
        q_ref,
        k_ref,
        v_ref,
        att_ref,
        dat_ref,
        lse_ref,
        dq_ref,
        down_ref,
        dother_ref,
        keys_t,
        acc,
        bias,
    ):
        step = pl.program_id(0)

        @pl.when(step == 0)
        def _():
            keys_t[...] = k_ref[...].T
            acc[...] = jnp.zeros_like(acc)

        start = block_start(info_ref, step, BLOCK, quarter)
        bias[...] = forbidden(info_ref, start, BLOCK, rows, 1)

        def pair(index, carry):
            at = pair_at(index)
            vat = pair_at(index + pairs)

            def add_keys(piece, value):
                acc[piece * rows : (piece + 1) * rows, at] += value

            def add_values(piece, value):
                acc[piece * rows : (piece + 1) * rows, vat] += value

            dq_ref[:, at] = backward_pair(
                q_ref[:, at],
                dat_ref[:, at],
                att_ref[:, at],
                lambda piece: k_ref[piece * rows : (piece + 1) * rows, at],
                lambda piece: v_ref[piece * rows : (piece + 1) * rows, at],
                lambda piece: keys_t[at, piece * rows : (piece + 1) * rows],
                lambda part: lse_ref[index, pl.ds(part, 1), :],
                (None, bias[...]),
                add_keys,
                add_values,
            )
            return carry

        lax.fori_loop(0, pairs, pair, 0)

        @pl.when(step == pl.num_programs(0) - 1)
        def _():
            for target, core in ((down_ref, info_ref[2]), (dother_ref, 1 - info_ref[2])):
                for part in range(2):
                    begin = pl.multiple_of(place_of(info_ref, core, part) * quarter, quarter)
                    target[part * quarter : (part + 1) * quarter, :] = acc[
                        pl.ds(begin, quarter), :
                    ].astype(BF16)

    return call(
        body,
        "self_backward",
        info,
        rows // BLOCK,
        [(q, split_rows(lanes, split))]
        + key_specs(kv, lanes, split, width)
        + [
            (att, split_rows(lanes, split)),
            (dat, split_rows(lanes, split)),
            (lse, pl.BlockSpec((pairs, 2, BLOCK), lambda i, *_: (split, 0, i))),
        ],
        [
            ((rows, lanes), BF16, rows_of(lanes)),
            ((rows, 2 * lanes), BF16, whole((rows, 2 * lanes))),
            ((rows, 2 * lanes), BF16, whole((rows, 2 * lanes))),
        ],
        [
            pltpu.VMEM((lanes, 2 * rows), BF16),
            pltpu.VMEM((2 * rows, 2 * lanes), F32),
            pltpu.VMEM((rows, BLOCK), F32),
        ],
        cost(80 * rows * rows * lanes, 20 * rows * lanes, 2 * rows * rows * lanes // HEAD_DIM),
    )


def feed(info, catt, second_in, dy, cout, weights, gains, packing):
    rows, width = catt.shape
    hidden = weights.hidden
    cout_count = len(cout.arrays)
    feed_count = len(weights.arrays)
    packed = packing.outputs(width * width + 2 * width * hidden)

    def body(info_ref, catt_ref, second_ref, dy_first, dy_last, gain_ref, *refs):
        cout_refs, refs = refs[:cout_count], refs[cout_count:]
        feed_refs, refs = refs[:feed_count], refs[feed_count:]
        (
            out_first,
            out_last,
            dthird_ref,
            dca_ref,
            ggain_ref,
            *packed_refs,
            acc_cout,
            acc_widen,
            acc_narrow,
            cout_scratch,
            widen_scratch,
            narrow_scratch,
        ) = refs
        cout_full = cout.load(info_ref, cout_refs, cout_scratch)
        widen_full, narrow_full = weights.load(info_ref, feed_refs, (widen_scratch, narrow_scratch))
        step = pl.program_id(0)

        @pl.when(step == 0)
        def _():
            acc_cout[...] = jnp.zeros_like(acc_cout)
            acc_widen[...] = jnp.zeros_like(acc_widen)
            acc_narrow[...] = jnp.zeros_like(acc_narrow)
            ggain_ref[...] = jnp.zeros_like(ggain_ref)

        catt = catt_ref[...]
        dy_low = dy.load(dy_first, dy_last)
        gain = gain_ref[5:6, :]
        third = second_ref[...] + dot(catt, cout_full[...])
        normed, scale = normalized(third)
        normed_low = (normed * gain).astype(BF16)
        pre = dot(normed_low, widen_full[...])
        below = 0.5 * (1.0 + lax.erf(pre * math.sqrt(0.5)))
        bell = jnp.exp(-0.5 * pre * pre) * (1.0 / math.sqrt(2.0 * math.pi))
        act = (pre * below).astype(BF16)
        store_half(
            (out_first, out_last), (third + dot(act, narrow_full[...])).astype(BF16)
        )
        dact = dot(dy_low, narrow_full[...], 1, 1)
        dpre = (dact * (below + pre * bell)).astype(BF16)
        acc_narrow[...] += dot(act, dy_low, 0, 0)
        acc_widen[...] += dot(normed_low, dpre, 0, 0)
        dnormed = dot(dpre, widen_full[...], 1, 1)
        ggain_ref[...] += jnp.sum(dnormed * normed, axis=0, keepdims=True)
        dthird = dy_low.astype(F32) + norm_backward(dnormed * gain, normed, scale)
        dthird_ref[...] = dthird
        dc = dthird.astype(BF16)
        dca_ref[...] = dot(dc, cout_full[...], 1, 1).astype(BF16)
        acc_cout[...] += dot(catt, dc, 0, 0)

        @pl.when(step == pl.num_programs(0) - 1)
        def _():
            packing.store(info_ref, packed_refs, (acc_cout, acc_widen, acc_narrow))

    return call(
        body,
        "feed",
        info,
        rows // BLOCK,
        [(catt, rows_of(width)), (second_in, rows_of(width))]
        + dy.inputs(BLOCK)
        + [(gains, whole(gains.shape))]
        + cout.inputs()
        + weights.inputs(),
        half_outputs(rows, width, BLOCK)
        + [
            ((rows, width), F32, rows_of(width)),
            ((rows, width), BF16, rows_of(width)),
            ((1, width), F32, whole((1, width))),
        ]
        + packed,
        [
            pltpu.VMEM((width, width), F32),
            pltpu.VMEM((width, hidden), F32),
            pltpu.VMEM((hidden, width), F32),
            cout.scratch(),
        ]
        + weights.scratch(),
        cost(
            12 * rows * width * hidden, 24 * rows * width + 8 * width * hidden, 2 * rows * hidden
        ),
    )


def cross_backward(info, cq, ckv, catt, dca, lse, splits, split):
    rows, width = cq.shape
    count = ckv.shape[0]
    lanes = width // splits
    pairs = lanes // PAIR

    def body(
        info_ref,
        cq_ref,
        k_ref,
        v_ref,
        catt_ref,
        dca_ref,
        lse_ref,
        dcq_ref,
        down_ref,
        dother_ref,
        keys_t,
        acc,
    ):
        step = pl.program_id(0)

        @pl.when(step == 0)
        def _():
            keys_t[...] = k_ref[...].T
            acc[...] = jnp.zeros_like(acc)

        def pair(index, carry):
            at = pair_at(index)
            vat = pair_at(index + pairs)

            def add_keys(piece, value):
                acc[:, at] += value

            def add_values(piece, value):
                acc[:, vat] += value

            dcq_ref[:, at] = backward_pair(
                cq_ref[:, at],
                dca_ref[:, at],
                catt_ref[:, at],
                lambda piece: k_ref[:, at],
                lambda piece: v_ref[:, at],
                lambda piece: keys_t[at, :],
                lambda part: lse_ref[index, pl.ds(part, 1), :],
                (None,),
                add_keys,
                add_values,
            )
            return carry

        lax.fori_loop(0, pairs, pair, 0)

        @pl.when(step == pl.num_programs(0) - 1)
        def _():
            down_ref[...] = acc[: count // 2, :].astype(BF16)
            dother_ref[...] = acc[count // 2 :, :].astype(BF16)

    half = (count // 2, 2 * lanes)
    return call(
        body,
        "cross_backward",
        info,
        rows // BLOCK,
        [(cq, split_rows(lanes, split))]
        + key_specs(ckv, lanes, split, width)
        + [
            (catt, split_rows(lanes, split)),
            (dca, split_rows(lanes, split)),
            (lse, pl.BlockSpec((pairs, 2, BLOCK), lambda i, *_: (split, 0, i))),
        ],
        [
            ((rows, lanes), BF16, rows_of(lanes)),
            (half, BF16, whole(half)),
            (half, BF16, whole(half)),
        ],
        [pltpu.VMEM((lanes, count), BF16), pltpu.VMEM((count, 2 * lanes), F32)],
        cost(40 * rows * rows * lanes, 20 * rows * lanes, rows * rows * lanes // HEAD_DIM),
    )


def sum_low(own_ref, got_ref):
    return (own_ref[...].astype(F32) + got_ref[...].astype(F32)).astype(BF16)


def middle_backward(
    info, dcqs, second_in, dthird, att, owns, gots, encoder, weights, gains, packing
):
    rows, width = second_in.shape
    count = len(dcqs)
    lanes = width // count
    packed = packing.outputs(4 * width * width)
    pieces = [len(w.arrays) for w in weights]
    short = encoder.shape[0] // (rows // BLOCK)

    def body(info_ref, att_ref, second_ref, dthird_ref, gain_ref, enc_first, enc_last, *refs):
        dcq_refs, refs = refs[:count], refs[count:]
        own_refs, refs = refs[:count], refs[count:]
        got_refs, refs = refs[:count], refs[count:]
        weight_refs = []
        for number in pieces:
            weight_refs.append(refs[:number])
            refs = refs[number:]
        dsecond_ref, dat_ref, ggain_ref, *genc_refs = refs[:5]
        refs = refs[5:]
        packed_refs, refs = refs[: len(packed)], refs[len(packed) :]
        acc_query, acc_out, acc_memory, *scratch = refs
        out_full, query_full, memory_full = [
            w.load(info_ref, r, s) for w, r, s in zip(weights, weight_refs, scratch)
        ]
        step = pl.program_id(0)

        @pl.when(step == 0)
        def _():
            acc_query[...] = jnp.zeros_like(acc_query)
            acc_out[...] = jnp.zeros_like(acc_out)
            acc_memory[...] = jnp.zeros_like(acc_memory)
            ggain_ref[...] = jnp.zeros_like(ggain_ref)

        dcq = jnp.concatenate([ref[...] for ref in dcq_refs], axis=1)
        gain = gain_ref[4:5, :]
        normed, scale = normalized(second_ref[...])
        normed_low = (normed * gain).astype(BF16)
        dnormed = dot(dcq, query_full[...], 1, 1)
        acc_query[...] += dot(normed_low, dcq, 0, 0)
        ggain_ref[...] += jnp.sum(dnormed * normed, axis=0, keepdims=True)
        dsecond = dthird_ref[...] + norm_backward(dnormed * gain, normed, scale)
        dsecond_ref[...] = dsecond
        da = dsecond.astype(BF16)
        dat_ref[...] = dot(da, out_full[...], 1, 1).astype(BF16)
        acc_out[...] += dot(att_ref[...], da, 0, 0)

        turned = encoder.load(enc_first, enc_last).T
        grads = [sum_low(own, got) for own, got in zip(own_refs, got_refs)]
        dckv = jnp.concatenate(
            [g[:, :lanes] for g in grads] + [g[:, lanes:] for g in grads], axis=1
        )
        store_half(genc_refs, dot(dckv, memory_full[...], 1, 1).astype(BF16))
        acc_memory[...] += dot(turned, dckv)

        @pl.when(step == pl.num_programs(0) - 1)
        def _():
            packing.store(info_ref, packed_refs, (acc_query, acc_out, acc_memory))

    return call(
        body,
        "middle_backward",
        info,
        rows // BLOCK,
        [
            (att, rows_of(width)),
            (second_in, rows_of(width)),
            (dthird, rows_of(width)),
            (gains, whole(gains.shape)),
        ]
        + encoder.inputs(short)
        + [(a, rows_of(lanes)) for a in dcqs]
        + [(a, rows_of(2 * lanes, short)) for a in owns]
        + [(a, rows_of(2 * lanes, short)) for a in gots]
        + [entry for w in weights for entry in w.inputs()],
        [
            ((rows, width), F32, rows_of(width)),
            ((rows, width), BF16, rows_of(width)),
            ((1, width), F32, whole((1, width))),
        ]
        + half_outputs(encoder.shape[0], width, short)
        + packed,
        [
            pltpu.VMEM((width, width), F32),
            pltpu.VMEM((width, width), F32),
            pltpu.VMEM((width, 2 * width), F32),
        ]
        + [w.scratch() for w in weights],
        cost(16 * rows * width * width, 20 * rows * width),
    )


VECTORS = 16


def project_backward(
    info, tokens, normed, dqs, owns, gots, dsecond, mods, ggains, embedded, weight, packing
):
    rows, width = tokens.shape
    count = len(dqs)
    lanes = width // count
    packed = packing.outputs(3 * width * width, VECTORS)
    pieces = len(weight.arrays)

    def body(info_ref, first_ref, last_ref, normed_ref, dsecond_ref, mod_ref, *refs):
        second_gain, third_gain, embedded_ref, *refs = refs
        dq_refs, refs = refs[:count], refs[count:]
        own_refs, refs = refs[:count], refs[count:]
        got_refs, refs = refs[:count], refs[count:]
        weight_refs, refs = refs[:pieces], refs[pieces:]
        gfirst_ref, glast_ref, vectors_ref, *packed_refs, acc, sums, scratch = refs
        full = weight.load(info_ref, weight_refs, scratch)
        step = pl.program_id(0)

        @pl.when(step == 0)
        def _():
            acc[...] = jnp.zeros_like(acc)
            sums[...] = jnp.zeros_like(sums)

        turned = normed_ref[...].T
        dkvs = [sum_low(own, got) for own, got in zip(own_refs, got_refs)]
        grads = jnp.concatenate(
            [ref[...] for ref in dq_refs]
            + [dkv[:, :lanes] for dkv in dkvs]
            + [dkv[:, lanes:] for dkv in dkvs],
            axis=1,
        )
        acc[...] += dot(turned, grads)
        dnormed = dot(grads, full[...], 1, 1)
        unit, scale = normalized(tokens.load(first_ref, last_ref).astype(F32))
        sums[0:1, :] += jnp.sum(dnormed * unit, axis=0, keepdims=True)
        sums[1:2, :] += jnp.sum(dnormed, axis=0, keepdims=True)
        store_half(
            (gfirst_ref, glast_ref),
            (
                dsecond_ref[...] + norm_backward(dnormed * mod_ref[0:1, :], unit, scale)
            ).astype(BF16),
        )

        @pl.when(step == pl.num_programs(0) - 1)
        def _():
            vectors = jnp.concatenate(
                [
                    sums[0:1, :] * mod_ref[2:3, :],
                    second_gain[...],
                    third_gain[...],
                    sums[0:1, :] * mod_ref[3:4, :],
                    sums[1:2, :],
                    embedded_ref[0:1, :].astype(F32),
                    jnp.zeros((VECTORS - 6, width), F32),
                ],
                axis=0,
            )
            vectors_ref[...] = vectors
            packing.store(info_ref, packed_refs, (acc,))
            if packing.direct:
                for ref in packed_refs:
                    for shift in range(ref.shape[0]):
                        ref[shift, ref.shape[1] - VECTORS :, :] = vectors.astype(BF16)

    return call(
        body,
        "project_backward",
        info,
        rows // BLOCK,
        tokens.inputs(BLOCK)
        + [
            (normed, rows_of(width)),
            (dsecond, rows_of(width)),
            (mods, whole(mods.shape)),
            (ggains[0], whole((1, width))),
            (ggains[1], whole((1, width))),
            (embedded, whole(embedded.shape)),
        ]
        + [(a, rows_of(lanes)) for a in dqs]
        + [(a, rows_of(2 * lanes)) for a in owns]
        + [(a, rows_of(2 * lanes)) for a in gots]
        + weight.inputs(),
        half_outputs(rows, width, BLOCK)
        + [((VECTORS, width), F32, whole((VECTORS, width)))]
        + packed,
        [pltpu.VMEM((width, 3 * width), F32), pltpu.VMEM((8, width), F32), weight.scratch()],
        cost(12 * rows * width * width, 20 * rows * width),
    )


def join_columns(info, parts):
    size = parts[0].shape[0] - VECTORS
    shape = (size + len(parts) * VECTORS, parts[0].shape[1])

    def body(info_ref, *refs):
        *part_refs, out_ref = refs
        total = part_refs[0][:size, :].astype(F32)
        for ref in part_refs[1:]:
            total = total + ref[:size, :].astype(F32)
        out_ref[:size, :] = total.astype(BF16)
        for index, ref in enumerate(part_refs):
            begin = size + index * VECTORS
            out_ref[begin : begin + VECTORS, :] = ref[size:, :]

    return call(
        body,
        "join_columns",
        info,
        1,
        [(part, whole(part.shape)) for part in parts],
        [(shape, BF16, whole(shape))],
        [],
        cost(0, 4 * size * shape[1]),
    )[0]


def in_seq_order(info, own, got, bit, out_ref, begin):
    rows = own.shape[0]
    own_place = (info[5] >> bit) % 2
    for part, place in ((own, own_place), (got, 1 - own_place)):
        at = pl.ds(pl.multiple_of(begin + place * rows, VECTORS), rows)
        out_ref[at, :] = part


def join_rows(info, own, got, size):
    count = own.shape[0] - size
    shape = (size + 2 * count, own.shape[1])

    def body(info_ref, own_ref, got_ref, out_ref):
        total = own_ref[:size, :].astype(F32) + got_ref[:size, :].astype(F32)
        out_ref[:size, :] = total.astype(BF16)
        in_seq_order(info_ref, own_ref[size:, :], got_ref[size:, :], 0, out_ref, size)

    return call(
        body,
        "join_rows",
        info,
        1,
        [(own, whole(own.shape)), (got, whole(got.shape))],
        [(shape, BF16, whole(shape))],
        [],
        cost(0, 6 * size * shape[1]),
    )[0]


def finish(info, own, got, size, shard):
    width = own.shape[1]
    count = own.shape[0] - size
    devices = 2 * count // VECTORS

    def body(info_ref, own_ref, got_ref, ginput_ref, gtime_ref, ggains_ref, listed, turned):
        for block in range(size // shard):
            rows = slice(block * shard, (block + 1) * shard)
            ginput_ref[:, block * width : (block + 1) * width] = own_ref[rows, :].astype(
                F32
            ) + got_ref[rows, :].astype(F32)
        in_seq_order(info_ref, own_ref[size:, :], got_ref[size:, :], 1, listed, 0)
        vectors = listed[...]
        column = lax.broadcasted_iota(jnp.int32, (devices, 2 * count), 1)
        row = lax.broadcasted_iota(jnp.int32, (devices, 2 * count), 0)

        def pick(kind):
            chosen = jnp.where(column == row * VECTORS + kind, 1.0, 0.0).astype(BF16)
            return dot(chosen, vectors)

        chosen = jnp.where(lax.rem(column, VECTORS) == row, 1.0, 0.0).astype(BF16)
        turned[...] = jnp.concatenate([0.5 * pick(5), dot(chosen, vectors)], axis=0).T
        place = (2 * info_ref[4] + info_ref[2]) * shard
        part = turned[pl.ds(pl.multiple_of(place, shard), shard), :]
        grads = jnp.concatenate([pick(3), pick(4)], axis=1).astype(BF16)
        gtime_ref[...] = dot(part[:, :devices].astype(BF16), grads)
        ggains_ref[...] = part.T[devices : devices + 3, :]

    return call(
        body,
        "finish",
        info,
        1,
        [(own, whole(own.shape)), (got, whole(got.shape))],
        [
            ((shard, 3 * width), F32, whole((shard, 3 * width))),
            ((shard, 2 * width), F32, whole((shard, 2 * width))),
            ((3, shard), F32, whole((3, shard))),
        ],
        [pltpu.VMEM((2 * count, width), BF16), pltpu.VMEM((width, 2 * devices), F32)],
        cost(4 * devices * count * width, 8 * size * width),
    )


def permutations(seq_count, fsdp_count):
    columns = fsdp_count // 2

    def at(seq, fsdp):
        return seq * fsdp_count + fsdp

    def pairs(move):
        return [
            (at(seq, fsdp), at(*move(seq, fsdp)))
            for seq in range(seq_count)
            for fsdp in range(fsdp_count)
        ]

    def home(turn):
        def move(seq, fsdp):
            y, x = divmod(seq, 2)
            column, core = divmod(fsdp, 2)
            return 2 * core + (x ^ turn), 2 * column + y

        return move

    shift = {
        r: pairs(lambda seq, fsdp, r=r: (seq, (fsdp + 2 * r) % fsdp_count))
        for r in range(1, columns)
    }
    cross = {t: pairs(lambda seq, fsdp, t=t: (seq ^ t, fsdp)) for t in range(1, seq_count)}
    swap = pairs(lambda seq, fsdp: (seq, fsdp ^ 1))
    return pairs(home(0)), pairs(home(1)), swap, shift, cross


def reverse(pairs):
    return [(target, source) for source, target in pairs]


def after(values, signal):
    return lax.optimization_barrier((values, signal))[0]


class Direct:
    def __init__(self, perms, seq, fsdp, columns):
        self.same, self.crossed, self.swap_pairs, self.shifts, self.crosses = perms
        self.seq = seq
        self.core = fsdp % 2
        self.z = fsdp // 2
        self.columns = columns

    def permute(self, values, pairs):
        return lax.ppermute(values, AXES, pairs)

    def swap(self, values):
        return self.permute(values, self.swap_pairs)

    def along_z(self, values):
        return [values] + [
            self.permute(values, self.shifts[r]) for r in range(1, self.columns)
        ]

    def both_cores(self, pieces):
        return pieces + [self.swap(piece) for piece in pieces]

    def core_sum(self, mine, away, signal=()):
        got = after(self.swap(away), signal)
        return [
            (mine[r].astype(F32) + got[r].astype(F32)).astype(BF16) for r in range(self.columns)
        ]

    def z_parts(self, shards):
        return [self.permute(shards[r], self.shifts[r]) for r in range(1, self.columns)]

    def z_sum(self, shards, got, signal=()):
        total = shards[0].astype(F32)
        for part in after(got, signal):
            total = total + part.astype(F32)
        return lax.optimization_barrier(total.astype(BF16))

    def add(self, first, second):
        return lax.optimization_barrier((first.astype(F32) + second.astype(F32)).astype(BF16))

    def cross(self, values, turn):
        return self.permute(values, self.crosses[turn])


SPLITS = 2


def time_embedding(step_values, model_width):
    half_width = model_width // 2
    frequency = jnp.exp(-math.log(10000.0) * jnp.arange(half_width, dtype=F32) / half_width)
    angles = step_values.astype(F32)[:, None] * frequency[None, :]
    return jnp.concatenate([jnp.sin(angles), jnp.cos(angles)], axis=-1).astype(BF16)


def exact_dot(left, right):
    return lax.dot_general(
        left,
        right,
        (((0,), (0,)), ((), ())),
        precision=lax.Precision.HIGHEST,
        preferred_element_type=F32,
    )


def make(seq_count, fsdp_count):
    perms = permutations(seq_count, fsdp_count)
    same, crossed = perms[:2]
    columns = fsdp_count // 2

    def on_device(
        tokens,
        encoder_states,
        lengths,
        timesteps,
        time_weight,
        self_input,
        self_output,
        cross_query,
        cross_memory,
        cross_output,
        widen_weight,
        narrow_weight,
        norm_gains,
        cotangent,
    ):
        width = tokens.shape[2]
        hidden = widen_weight.shape[1]
        shard = time_weight.shape[0]
        seq = lax.axis_index("seq")
        fsdp = lax.axis_index("fsdp")
        core = fsdp % 2
        side = seq % 2
        direct = Direct(perms, seq, fsdp, columns) if columns == 4 else None

        def send_work(values):
            mine = lax.dynamic_index_in_dim(values, side, 0, keepdims=False)
            others = lax.dynamic_index_in_dim(values, 1 - side, 0, keepdims=False)
            return [lax.ppermute(mine, AXES, same), lax.ppermute(others, AXES, crossed)]

        def send_home(halves):
            return [
                lax.ppermute(halves[0], AXES, reverse(same)),
                lax.ppermute(halves[1], AXES, reverse(crossed)),
            ]

        def at_home(parts, kind):
            first = jnp.where(side == 0, parts[0], parts[1])
            second = jnp.where(side == 0, parts[1], parts[0])
            return jnp.stack([first, second], axis=0).astype(kind)

        def gather(weight, axis=0):
            return lax.all_gather(weight, "fsdp", axis=axis, tiled=True)

        def swap(values):
            return lax.ppermute(values, AXES, perms[2])

        packing = Packing(fsdp_count, direct is not None, width)
        token_rows, encoder_rows = tokens.shape[1], encoder_states.shape[1]
        turned = jnp.pad(norm_gains.T, ((0, 0), (0, 128 - norm_gains.shape[0])))
        first = jnp.concatenate([self_input, time_weight, turned], axis=1)
        first_mine = direct.along_z(first) if direct else [(), ()]
        own = send_work(tokens)
        other = [swap(part) for part in after(own, first_mine[-1])]
        work_tokens = Halves(own, 0, token_rows)
        other_tokens = Halves(other, 0, token_rows)

        numbers = jnp.concatenate([lengths, timesteps[:, None]], axis=1)
        numbers_other = swap(numbers)
        own_row = jnp.where(core == seq // 2, numbers, numbers_other)
        own_row = lax.dynamic_index_in_dim(own_row, side, 0, keepdims=False)
        info = jnp.stack([own_row[0], own_row[0] + own_row[1], core, side, fsdp // 2, seq])
        step_value = own_row[3:4]
        embedded = jnp.pad(time_embedding(step_value, width), ((0, 15), (0, 0)))
        if direct:
            first = direct.both_cores(first_mine)
            rest = jnp.concatenate([self_output, cross_query, cross_memory, cross_output], axis=1)
            wide = widen_weight.reshape(shard, hidden // width, width).transpose(1, 0, 2)
            large = jnp.concatenate([wide.reshape(-1, width), narrow_weight], axis=0)
            rest, large = after((rest, large), own)
            rest_mine = direct.along_z(rest)
            large_mine = direct.along_z(large)
            input_weight = Weight(first, 0, 3 * width)
            time_full = Weight(first, 3 * width, 2 * width)
            turned_gains = Weight(first, 5 * width, 128)
        else:
            input_weight = Weight([gather(self_input)], 0, 3 * width)
            time_full = Weight([gather(time_weight)], 0, 2 * width)
            turned_gains = Weight([gather(turned)], 0, 128)
            output_weight = Weight([gather(self_output)], 0, width)
            query_weight = Weight([gather(cross_query)], 0, width)
            memory_weight = Weight([gather(cross_memory)], 0, 2 * width)
            cout_weight = Weight([gather(cross_output)], 0, width)
            feed_weights = FeedWeights([gather(widen_weight), gather(narrow_weight)], hidden)

        second_own = send_work(
            after(jnp.concatenate([encoder_states, cotangent], axis=1), own)
        )

        ready = after(info, second_own)

        mods, q, kv, normed_first, att, lse = self_forward(
            ready, work_tokens, other_tokens, embedded, time_full, turned_gains, input_weight
        )
        ready = info
        if direct:
            rest_mine[1:], large_mine[:2] = after((rest_mine[1:], large_mine[:2]), att)
            rest = direct.both_cores(rest_mine)
            large_other = [swap(part) for part in large_mine[:2]]
            ready = after(info, large_other)
            output_weight = Weight(rest, 0, width)
            query_weight = Weight(rest, width, width)
            memory_weight = Weight(rest, 2 * width, 2 * width)
            cout_weight = Weight(rest, 4 * width, width)
        second_other = [swap(part[:encoder_rows]) for part in second_own]
        work_encoder = Halves(second_own, 0, encoder_rows)
        other_encoder = Halves(second_other, 0, encoder_rows)
        work_dy = Halves(second_own, encoder_rows, token_rows)
        second_in, cq, ckv, catt, cross_lse = cross_forward(
            ready,
            att,
            work_tokens,
            work_encoder,
            other_encoder,
            output_weight,
            mods,
            query_weight,
            memory_weight,
        )
        if direct:
            large_mine[2:] = after(large_mine[2:], catt)
            large_other += [swap(part) for part in large_mine[2:]]
            feed_weights = FeedWeights(large_mine + large_other, hidden)
        out_first, out_last, dthird, dca, ggain_third, *packed_feed = feed(
            info, catt, second_in, work_dy, cout_weight, feed_weights, mods, packing
        )
        layer_out = (out_first, out_last)
        out_parts = send_home(layer_out)

        def backward_cross(split, ready):
            return cross_backward(ready, cq, ckv, catt, dca, cross_lse, SPLITS, split)

        def backward_self(split, ready):
            return self_backward(ready, q, kv, att, dat, lse, SPLITS, split)

        crosses = [backward_cross(0, info)]
        out_parts = after(out_parts, crosses[0][0])
        chip_feed = direct.core_sum(*packed_feed, crosses[0][0]) if direct else ()
        crosses.append(backward_cross(1, after(info, (chip_feed, out_parts))))
        dcqs, dckvs, dckv_others = zip(*crosses)
        dckv_gots = [swap(a) for a in dckv_others]
        feed_parts = direct.z_parts(chip_feed) if direct else [()]
        dsecond, dat, ggain_second, *genc = middle_backward(
            after(info, (feed_parts[0], dcqs)),
            dcqs,
            second_in,
            dthird,
            att,
            dckvs,
            dckv_gots,
            work_encoder,
            (output_weight, query_weight, memory_weight),
            mods,
            packing,
        )
        genc, packed_middle = genc[:2], genc[2:]
        selfs = [backward_self(0, after(info, packed_middle))]
        if direct:
            column_feed = direct.z_sum(chip_feed, feed_parts, selfs[0][0])
            chip_middle = direct.core_sum(*packed_middle, selfs[0][0])
            selfs.append(backward_self(1, after(info, (column_feed, chip_middle))))
            middle_parts = after(direct.z_parts(chip_middle), selfs[1][0])
            row_feed = after(direct.cross(column_feed, 1), selfs[1][0])
            row_feed = direct.add(column_feed, row_feed)
            column_middle = direct.z_sum(chip_middle, middle_parts)
        else:
            selfs.append(backward_self(1, info))
        dqs, dkvs, dkv_others = zip(*selfs)
        dkv_others = list(dkv_others)
        if direct:
            dkv_others[1] = after(dkv_others[1], (column_middle, row_feed))
        dkv_gots = [swap(a) for a in dkv_others]
        first_grad, last_grad, vectors, *packed_input = project_backward(
            info,
            work_tokens,
            normed_first,
            dqs,
            dkvs,
            dkv_gots,
            dsecond,
            mods,
            (ggain_second, ggain_third),
            embedded,
            input_weight,
            packing,
        )
        gtokens = (first_grad, last_grad)
        if direct:
            chip = direct.core_sum(*packed_input)
            got_row = after(direct.cross(row_feed, 2), gtokens)
            row_middle = after(direct.cross(column_middle, 1), gtokens)
            row_middle = direct.add(column_middle, row_middle)
            enc_parts = after(send_home(genc), gtokens)
            gots = direct.z_parts(chip)
            token_parts = after(send_home(after(gtokens, chip)), gots)
            reduced_feed = row_feed.astype(F32) + got_row.astype(F32)
            size = chip[0].shape[0] - VECTORS
            joined = join_columns(info, [chip[0]] + gots)
            got = direct.cross(joined, 1)
            got_row = direct.cross(after(row_middle, joined), 2)
            joined = join_rows(info, joined, got, size)
            got = direct.cross(joined, 2)
            reduced_middle = row_middle.astype(F32) + got_row.astype(F32)
            reduced_input, gtime, ggains = finish(info, joined, got, size, shard)
        else:

            def reduce(packed):
                part = lax.psum_scatter(packed[0], "fsdp", scatter_dimension=0, tiled=True)
                return lax.psum(part[0], "seq").astype(F32)

            reduced_input = reduce(packed_input)
            reduced_input = unpack_rows(reduced_input, 0, shard, 3 * width)
            reduced_middle = reduce(packed_middle)
            reduced_feed = reduce(packed_feed)
            token_parts, enc_parts = send_home(gtokens), send_home(genc)
            ggains = lax.psum(vectors[:3], AXES)
            ggains = lax.dynamic_slice_in_dim(ggains, fsdp * shard, shard, 1)
            by_group = lax.all_gather(vectors[3:5], AXES, axis=0)
            by_group = by_group.reshape(seq_count, columns, 2, 2 * width).sum(axis=2)
            by_group = by_group.transpose(1, 0, 2).reshape(-1, 2 * width)
            every = time_embedding(gather(timesteps), width)
            own_columns = lax.dynamic_slice_in_dim(every, fsdp * shard, shard, 1)
            gtime = exact_dot(own_columns.astype(F32), by_group)

        tall = narrow_weight.shape[0]
        return (
            at_home(out_parts, BF16),
            at_home(token_parts, F32),
            at_home(enc_parts, F32),
            gtime,
            reduced_input,
            unpack_rows(reduced_middle, shard, shard, width),
            unpack_rows(reduced_middle, 0, shard, width),
            unpack_rows(reduced_middle, 2 * shard, shard, 2 * width),
            unpack_rows(reduced_feed, 0, shard, width),
            unpack_rows(reduced_feed, shard, shard, hidden),
            unpack_rows(reduced_feed, shard * (1 + hidden // width), tall, width),
            ggains,
        )

    return on_device


def solution(mesh):
    rows = P("fsdp", "seq", None)
    weight = P("fsdp", None)
    in_specs = (rows, rows, P("fsdp", None), P("fsdp")) + (weight,) * 8 + (P(None, "fsdp"), rows)
    out_specs = (rows,) * 3 + (weight,) * 8 + (P(None, "fsdp"),)
    return jax.shard_map(
        make(mesh.shape["seq"], mesh.shape["fsdp"]),
        mesh=mesh,
        in_specs=in_specs,
        out_specs=out_specs,
        check_vma=False,
    )
```

```python
import math

import jax
import jax.numpy as jnp
from jax import lax
from jax.experimental import pallas as pl
from jax.experimental.pallas import tpu as pltpu
from jax.sharding import PartitionSpec as P


HEAD_DIM = 64
PAIR = 2 * HEAD_DIM
EPS = 1e-05
NEG = -1e30
F32 = jnp.float32
BF16 = jnp.bfloat16
AXES = ("seq", "fsdp")
VMEM_LIMIT = 60 * 2**20
BLOCK = 256
WIDE = 512


def dot(left, right, left_dim=1, right_dim=0):
    return lax.dot_general(
        left, right, (((left_dim,), (right_dim,)), ((), ())), preferred_element_type=F32
    )


def whole(shape):
    return pl.BlockSpec(shape, lambda *_: (0,) * len(shape))


def rows_of(width, block=BLOCK):
    return pl.BlockSpec((block, width), lambda i, *_: (i, 0))


def params():
    return pltpu.CompilerParams(vmem_limit_bytes=VMEM_LIMIT)


def cost(flops, moved, transcendentals=0):
    return pl.CostEstimate(
        flops=int(flops), bytes_accessed=int(moved), transcendentals=int(transcendentals)
    )


def normalized(values):
    average = jnp.mean(values, axis=-1, keepdims=True)
    centred = values - average
    spread = jnp.mean(centred * centred, axis=-1, keepdims=True)
    scale = lax.rsqrt(spread + EPS)
    return centred * scale, scale


def norm_backward(upstream, normed, scale):
    mean_up = jnp.mean(upstream, axis=-1, keepdims=True)
    mean_both = jnp.mean(upstream * normed, axis=-1, keepdims=True)
    return (upstream - mean_up - normed * mean_both) * scale


def lane_is(part):
    lane = lax.broadcasted_iota(jnp.int32, (1, PAIR), 1)
    return lane < HEAD_DIM if part == 0 else lane >= HEAD_DIM


def half_of(values, part):
    return jnp.where(lane_is(part), values, jnp.zeros_like(values))


def pair_at(index):
    return pl.ds(pl.multiple_of(index * PAIR, PAIR), PAIR)


def first_step(dims=1):
    first = pl.program_id(0) == 0
    return first if dims == 1 else first & (pl.program_id(1) == 0)


class Weight:
    def __init__(self, pieces, start, width):
        self.arrays = pieces
        self.start = start
        self.width = width

    @property
    def split(self):
        return len(self.arrays) > 1

    @property
    def rows(self):
        return len(self.arrays) * self.arrays[0].shape[0]

    @property
    def aligned(self):
        return self.start % self.width == 0

    def inputs(self):
        if not self.aligned:
            return [(array, whole(array.shape)) for array in self.arrays]
        place = self.start // self.width
        shape = (self.arrays[0].shape[0], self.width)
        return [(array, pl.BlockSpec(shape, lambda *_: (0, place))) for array in self.arrays]

    def scratch(self):
        return pltpu.VMEM((self.rows, self.width) if self.split else (16, 128), BF16)

    def load(self, info, refs, scratch, dims=1):
        if not self.split:
            return refs[0]
        columns = slice(0, self.width) if self.aligned else slice(self.start, self.start + self.width)

        @pl.when(first_step(dims))
        def _():
            count = len(refs) // 2
            shard = refs[0].shape[0]
            for index, ref in enumerate(refs):
                turn, shift = divmod(index, count)
                core = info[2] if turn == 0 else 1 - info[2]
                owner = lax.rem(info[4] - shift + count, count)
                start = pl.multiple_of((2 * owner + core) * shard, shard)
                scratch[pl.ds(start, shard), :] = ref[:, columns]

        return scratch


class Halves:
    def __init__(self, arrays, start, rows):
        self.arrays = arrays
        self.start = start
        self.rows = rows
        self.shape = (2 * rows, arrays[0].shape[1])

    def inputs(self, block):
        width = self.shape[1]
        count = self.rows // block
        base = self.start // block
        return [
            (
                self.arrays[0],
                pl.BlockSpec((block, width), lambda i, *_: (base + jnp.minimum(i, count - 1), 0)),
            ),
            (
                self.arrays[1],
                pl.BlockSpec((block, width), lambda i, *_: (base + jnp.maximum(i - count, 0), 0)),
            ),
        ]

    def resident(self):
        place = self.start // self.rows
        spec = pl.BlockSpec((self.rows, self.shape[1]), lambda *_: (place, 0))
        return [(array, spec) for array in self.arrays]

    def load(self, first_ref, second_ref):
        half = pl.num_programs(0) // 2
        return jnp.where(pl.program_id(0) < half, first_ref[...], second_ref[...])


def half_outputs(rows, width, block):
    count = rows // block // 2
    half = (rows // 2, width)
    return [
        (half, BF16, pl.BlockSpec((block, width), lambda i, *_: (jnp.minimum(i, count - 1), 0))),
        (half, BF16, pl.BlockSpec((block, width), lambda i, *_: (jnp.maximum(i - count, 0), 0))),
    ]


def store_half(refs, value):
    first = pl.program_id(0) < pl.num_programs(0) // 2

    @pl.when(first)
    def _():
        refs[0][...] = value

    @pl.when(jnp.logical_not(first))
    def _():
        refs[1][...] = value


class FeedWeights:
    def __init__(self, arrays, hidden):
        self.arrays = arrays
        self.hidden = hidden

    @property
    def split(self):
        return len(self.arrays) > 2

    def inputs(self):
        return [(array, whole(array.shape)) for array in self.arrays]

    def scratch(self):
        if not self.split:
            return [pltpu.VMEM((16, 128), BF16)] * 2
        width = self.arrays[0].shape[1]
        return [pltpu.VMEM((width, self.hidden), BF16), pltpu.VMEM((self.hidden, width), BF16)]

    def load(self, info, refs, scratch):
        if not self.split:
            return refs
        widen, narrow = scratch

        @pl.when(pl.program_id(0) == 0)
        def _():
            count = len(refs) // 2
            rows, width = refs[0].shape
            blocks = self.hidden // width
            tall = rows // 2
            short = tall // blocks
            for index, ref in enumerate(refs):
                turn, shift = divmod(index, count)
                core = info[2] if turn == 0 else 1 - info[2]
                owner = 2 * lax.rem(info[4] - shift + count, count) + core
                start = pl.multiple_of(owner * short, short)
                for block in range(blocks):
                    widen[pl.ds(start, short), block * width : (block + 1) * width] = ref[
                        block * short : (block + 1) * short, :
                    ]
                start = pl.multiple_of(owner * tall, tall)
                narrow[pl.ds(start, tall), :] = ref[tall:, :]

        return widen, narrow


class Packing:
    def __init__(self, shards, direct, width):
        self.shards = shards
        self.direct = direct
        self.width = width

    def outputs(self, elements, extra=0):
        rows = elements // (self.shards * self.width)
        if self.direct:
            rows += extra
        if self.direct:
            shape = (self.shards // 2, rows, self.width)
            return [(shape, BF16, whole(shape))] * 2
        shape = (self.shards, rows, self.width)
        return [(shape, BF16, whole(shape))]

    def store(self, info, packed, grads, vectors=None):
        def put(ref, slot, owner):
            offset = 0
            for grad in grads:
                rows = grad.shape[0] // self.shards
                for block in range(grad.shape[1] // self.width):
                    columns = slice(block * self.width, (block + 1) * self.width)
                    if isinstance(owner, int):
                        part = grad[owner * rows : (owner + 1) * rows, columns]
                    else:
                        part = grad[pl.ds(pl.multiple_of(owner * rows, rows), rows), columns]
                    ref[slot, offset : offset + rows, :] = part.astype(BF16)
                    offset += rows
            if vectors is not None and self.direct:
                ref[slot, offset:, :] = vectors.astype(BF16)

        if self.direct:
            count = self.shards // 2
            for ref, core in ((packed[0], info[2]), (packed[1], 1 - info[2])):

                def one(shift, carry, ref=ref, core=core):
                    put(ref, shift, 2 * lax.rem(info[4] + shift, count) + core)
                    return carry

                lax.fori_loop(0, count, one, 0)
        else:
            for shard in range(self.shards):
                put(packed[0], shard, shard)


def unpack_rows(packed, offset, rows, columns):
    width = packed.shape[1]
    blocks = columns // width
    parts = [packed[offset + b * rows : offset + (b + 1) * rows] for b in range(blocks)]
    return jnp.concatenate(parts, axis=1) if blocks > 1 else parts[0]


def call(body, name, info, grid, inputs, outputs, scratch, estimate):
    return pl.pallas_call(
        body,
        name=name,
        grid_spec=pltpu.PrefetchScalarGridSpec(
            num_scalar_prefetch=1,
            grid=grid if isinstance(grid, tuple) else (grid,),
            in_specs=[spec for _, spec in inputs],
            out_specs=[spec for _, _, spec in outputs],
            scratch_shapes=scratch,
        ),
        out_shape=[jax.ShapeDtypeStruct(shape, kind) for shape, kind, _ in outputs],
        compiler_params=params(),
        cost_estimate=estimate,
    )(info, *[array for array, _ in inputs])


def block_start(info, block_index, block, quarter):
    per_quarter = quarter // block
    first = block_index < per_quarter
    place = jnp.where(first, info[3], 1 - info[3])
    return (2 * info[2] + place) * quarter + lax.rem(block_index, per_quarter) * block


def forbidden(info, start, block, half, queries_dim):
    keys_dim = 1 - queries_dim
    qshape = [1, 1]
    qshape[queries_dim] = block
    kshape = [1, 1]
    kshape[keys_dim] = half
    qpos = start + lax.broadcasted_iota(jnp.int32, tuple(qshape), queries_dim)
    kpos = half + lax.broadcasted_iota(jnp.int32, tuple(kshape), keys_dim)
    first, second = info[0], info[1]
    low = jnp.where((qpos >= first) & (qpos < second), second, first)
    high = jnp.where(qpos >= second, second, 2 * half)
    return jnp.where((kpos >= low) & (kpos < high), NEG, 0.0)


def key_specs(array, lanes, split, width):
    rows = array.shape[0]
    count = width // lanes
    return [
        (array, pl.BlockSpec((rows, lanes), lambda *_: (0, split))),
        (array, pl.BlockSpec((rows, lanes), lambda *_: (0, count + split))),
    ]


def attention_sums(low, high):
    return (low > 1e-20) & (high < 1e30)


def attend_pair(qq, keys_at, turned_values, free, bias, att_ref, inverse_ref, probs_ref):
    count = probs_ref.shape[1]
    row_head = lax.broadcasted_iota(jnp.int32, (PAIR, 1), 0) // HEAD_DIM
    lane_head = lax.broadcasted_iota(jnp.int32, (1, PAIR), 1) // HEAD_DIM
    turned_at = turned_values(slice(0, count))

    def head(part):
        qe = jnp.where(lane_head == part, qq, jnp.zeros_like(qq))
        total = None
        out = None
        for piece in (slice(0, free), slice(free, count)):
            if piece.start == piece.stop:
                continue
            s = dot(keys_at(piece), qe, 1, 1)
            p = jnp.exp(s if piece.start == 0 else s + bias[...])
            low = p.astype(BF16)
            probs_ref[part, piece, :] = low
            term = jnp.sum(p, axis=0, keepdims=True)
            attended = dot(turned_at[:, piece], low)
            total = term if total is None else total + term
            out = attended if out is None else out + attended
        return out, total

    outs, totals = zip(head(0), head(1))
    inverses = [1.0 / total for total in totals]
    out = jnp.where(row_head == 0, outs[0] * inverses[0], outs[1] * inverses[1])
    att_ref[...] = out.T.astype(BF16)
    for part in range(2):
        inverse_ref[0, part : part + 1, :] = inverses[part]
    low = jnp.min(jnp.minimum(totals[0], totals[1]))
    high = jnp.max(jnp.maximum(totals[0], totals[1]))

    @pl.when(jnp.logical_not((low > 1e-20) & (high < 1e30)))
    def _():
        chunk = BLOCK // 2
        queries = qq.shape[0]

        def again(part, carry):
            qe = jnp.where(lane_head == part, qq, jnp.zeros_like(qq))

            def scores(index):
                at = pl.ds(pl.multiple_of(index * chunk, chunk), chunk)
                s = dot(keys_at(at), qe, 1, 1)
                if free == count:
                    return at, s
                begin = jnp.maximum(index * chunk - free, 0)
                part_bias = bias[pl.ds(pl.multiple_of(begin, chunk), chunk), :]
                return at, s + jnp.where(index * chunk >= free, part_bias, 0.0)

            def largest(index, top):
                return jnp.maximum(top, jnp.max(scores(index)[1], axis=0, keepdims=True))

            top = lax.fori_loop(
                0, count // chunk, largest, jnp.full((1, queries), -jnp.inf, F32)
            )

            def add(index, sums):
                at, s = scores(index)
                p = jnp.exp(s - top)
                low = p.astype(BF16)
                probs_ref[part, at, :] = low
                return (
                    sums[0] + jnp.sum(p, axis=0, keepdims=True),
                    sums[1] + dot(turned_values(at), low),
                )

            total, out = lax.fori_loop(
                0,
                count // chunk,
                add,
                (jnp.zeros((1, queries), F32), jnp.zeros((PAIR, queries), F32)),
            )
            inverse = 1.0 / total
            inverse_ref[0, pl.ds(part, 1), :] = inverse
            return carry + jnp.where(row_head == part, out * inverse, 0.0)

        out = lax.fori_loop(0, 2, again, jnp.zeros((PAIR, queries), F32))
        att_ref[...] = out.T.astype(BF16)


def attention_outputs(rows, width, count):
    pairs = width // PAIR
    return [
        ((rows, width), BF16, pl.BlockSpec((WIDE, PAIR), lambda i, h, *_: (i, h))),
        ((pairs, 2, rows), F32, pl.BlockSpec((1, 2, WIDE), lambda i, h, *_: (h, 0, i))),
        ((2 * pairs, count, rows), BF16, pl.BlockSpec((2, count, WIDE), lambda i, h, *_: (h, 0, i))),
    ]


def place_of(info, core, part):
    return 2 * core + (info[3] if part == 0 else 1 - info[3])


def self_forward(info, own, other, embedded, time, turned_gains, weight):
    rows, width = own.shape
    pairs = width // PAIR
    quarter = rows // 2
    weights = (weight, time, turned_gains)
    pieces = [len(w.arrays) for w in weights]

    def body(info_ref, embedded_ref, *refs):
        token_refs, refs = refs[:4], refs[4:]
        weight_refs = []
        for number in pieces:
            weight_refs.append(refs[:number])
            refs = refs[number:]
        (
            mod_ref,
            q_out,
            kv_out,
            normed_out,
            att_ref,
            inverse_ref,
            probs_ref,
            queries,
            keys,
            normed,
            turned_values,
            staged,
            bias,
            *scratch,
            sems,
        ) = refs
        step = pl.program_id(0)
        index = pl.program_id(1)
        full, time_full, gains_full = [
            w.load(info_ref, r, s, 2) for w, r, s in zip(weights, weight_refs, scratch)
        ]
        copies = [
            pltpu.make_async_copy(queries, q_out, sems.at[0]),
            pltpu.make_async_copy(keys, kv_out, sems.at[1]),
            pltpu.make_async_copy(normed, normed_out, sems.at[2]),
        ]

        @pl.when(first_step(2))
        def _():
            modulation = dot(embedded_ref[...], time_full[...])
            gains = gains_full[...].astype(F32).T[:3, :]
            plus = 1.0 + modulation[0:1, :width]
            shift = modulation[0:1, width:]
            mod_ref[...] = jnp.concatenate(
                [gains[0:1] * plus, shift, plus, gains, jnp.zeros((2, width), F32)], axis=0
            )
            for number, ref in enumerate(token_refs):
                turn, part = divmod(number, 2)
                holder = info_ref[2] if turn == 0 else 1 - info_ref[2]
                begin = place_of(info_ref, holder, part) * quarter
                staged[pl.ds(pl.multiple_of(begin, quarter), quarter), :] = ref[...]

            def project(place, carry):
                at = pl.ds(pl.multiple_of(place * quarter, quarter), quarter)
                unit, _ = normalized(staged[at, :].astype(F32))
                first = (unit * mod_ref[0:1, :] + mod_ref[1:2, :]).astype(BF16)
                keys[at, :] = dot(first, full[:, width:]).astype(BF16)

                @pl.when(place // 2 == info_ref[2])
                def _():
                    begin = lax.bitwise_xor(lax.rem(place, 2), info_ref[3]) * quarter
                    here = pl.ds(pl.multiple_of(begin, quarter), quarter)
                    normed[here, :] = first
                    queries[here, :] = (dot(first, full[:, :width]) * HEAD_DIM**-0.5).astype(BF16)

                return carry

            lax.fori_loop(0, 4, project, 0)
            for copy in copies:
                copy.start()

            turned_values[...] = keys[:, width:].T

        @pl.when(index == 0)
        def _():
            start = block_start(info_ref, step, WIDE, quarter)
            bias[...] = forbidden(info_ref, start, WIDE, rows, 1)

        mine = pl.ds(pl.multiple_of(step * WIDE, WIDE), WIDE)
        at = pair_at(index)
        attend_pair(
            queries[mine, at],
            lambda piece: keys[piece, at],
            lambda piece: turned_values[at, piece],
            rows,
            bias,
            att_ref,
            inverse_ref,
            probs_ref,
        )

        @pl.when((step == pl.num_programs(0) - 1) & (index == pairs - 1))
        def _():
            for copy in copies:
                copy.wait()

    anywhere = pl.BlockSpec(memory_space=pl.ANY)
    return call(
        body,
        "self_forward",
        info,
        (rows // WIDE, pairs),
        [(embedded, whole(embedded.shape))]
        + own.resident()
        + other.resident()
        + [entry for w in weights for entry in w.inputs()],
        [
            ((8, width), F32, whole((8, width))),
            ((rows, width), BF16, anywhere),
            ((2 * rows, 2 * width), BF16, anywhere),
            ((rows, width), BF16, anywhere),
        ]
        + attention_outputs(rows, width, 2 * rows),
        [
            pltpu.VMEM((rows, width), BF16),
            pltpu.VMEM((2 * rows, 2 * width), BF16),
            pltpu.VMEM((rows, width), BF16),
            pltpu.VMEM((width, 2 * rows), BF16),
            pltpu.VMEM((2 * rows, width), BF16),
            pltpu.VMEM((rows, WIDE), F32),
        ]
        + [w.scratch() for w in weights]
        + [pltpu.SemaphoreType.DMA((3,))],
        cost(32 * rows * rows * width, 12 * rows * width, 2 * rows * rows * width // HEAD_DIM),
    )


def cross_forward(info, att, tokens, own, other, out_weight, gains, query_weight, memory_weight):
    rows, width = att.shape
    pairs = width // PAIR
    count = own.rows
    weights = (out_weight, query_weight, memory_weight)
    pieces = [len(w.arrays) for w in weights]

    def body(info_ref, att_ref, first_ref, last_ref, gain_ref, *refs):
        enc_refs, refs = refs[:4], refs[4:]
        weight_refs = []
        for number in pieces:
            weight_refs.append(refs[:number])
            refs = refs[number:]
        second_ref, cq_ref, ckv_out, catt_ref, inverse_ref, probs_ref, *refs = refs
        memory, turned_values, staged, *scratch, sem = refs
        out_full, query_full, memory_full = [
            w.load(info_ref, r, s, 2) for w, r, s in zip(weights, weight_refs, scratch)
        ]
        step = pl.program_id(0)
        index = pl.program_id(1)
        copy = pltpu.make_async_copy(memory, ckv_out, sem)

        @pl.when(first_step(2))
        def _():
            for part, ref in enumerate(enc_refs):
                staged[part * count : (part + 1) * count, :] = ref[...]

            def project(part, carry):
                at = pl.ds(pl.multiple_of(part * count, count), count)
                memory[at, :] = dot(staged[at, :], memory_full[...]).astype(BF16)
                return carry

            lax.fori_loop(0, 4, project, 0)
            copy.start()
            turned_values[...] = memory[:, width:].T

        @pl.when(index == 0)
        def _():
            second_in = tokens.load(first_ref, last_ref).astype(F32) + dot(
                att_ref[...], out_full[...]
            )
            second_ref[...] = second_in
            normed, _ = normalized(second_in)
            normed = (normed * gain_ref[4:5, :]).astype(BF16)
            cq_ref[...] = (dot(normed, query_full[...]) * HEAD_DIM**-0.5).astype(BF16)

        at = pair_at(index)
        attend_pair(
            cq_ref[:, at],
            lambda piece: memory[piece, at],
            lambda piece: turned_values[at, piece],
            4 * count,
            None,
            catt_ref,
            inverse_ref,
            probs_ref,
        )

        @pl.when((step == pl.num_programs(0) - 1) & (index == pairs - 1))
        def _():
            copy.wait()

    return call(
        body,
        "cross_forward",
        info,
        (rows // WIDE, pairs),
        [(att, rows_of(width, WIDE))]
        + tokens.inputs(WIDE)
        + [(gains, whole(gains.shape))]
        + own.resident()
        + other.resident()
        + [entry for w in weights for entry in w.inputs()],
        [
            ((rows, width), F32, rows_of(width, WIDE)),
            ((rows, width), BF16, rows_of(width, WIDE)),
            ((4 * count, 2 * width), BF16, pl.BlockSpec(memory_space=pl.ANY)),
        ]
        + attention_outputs(rows, width, 4 * count),
        [
            pltpu.VMEM((4 * count, 2 * width), BF16),
            pltpu.VMEM((width, 4 * count), BF16),
            pltpu.VMEM((4 * count, width), BF16),
        ]
        + [w.scratch() for w in weights]
        + [pltpu.SemaphoreType.DMA],
        cost(16 * rows * rows * width, 12 * rows * width, rows * rows * width // HEAD_DIM),
    )


def backward_pair(qq, dd, oo, keys, values, turned_keys, inverses, probs, size, add_keys, add_values):
    products = (oo.astype(F32) * dd.astype(F32)).T
    row_head = lax.broadcasted_iota(jnp.int32, (PAIR, 1), 0) // HEAD_DIM
    lane_head = lax.broadcasted_iota(jnp.int32, (1, PAIR), 1) // HEAD_DIM

    def head(part, total_grad):
        qe = jnp.where(lane_head == part, qq, jnp.zeros_like(qq))
        de = jnp.where(lane_head == part, dd, jnp.zeros_like(dd))
        inner = jnp.sum(jnp.where(row_head == part, products, 0.0), axis=0, keepdims=True)
        inverse = inverses(part)
        column = jnp.broadcast_to(inverse, (8, inverse.shape[1])).T[:, 0:1]
        scaled = (de.astype(F32) * column).astype(BF16)
        grad = None
        for begin in range(0, keys.shape[0], size):
            into = slice(begin, begin + size)
            p = probs(part, into)
            dprobs = dot(values[into, :], de, 1, 1)
            dscores = (p.astype(F32) * ((dprobs - inner) * inverse)).astype(BF16)
            add_values(into, dot(p, scaled))
            add_keys(into, dot(dscores, qe))
            term = dot(turned_keys[:, into], dscores)
            grad = term if grad is None else grad + term
        return total_grad + jnp.where(row_head == part, grad, 0.0)

    grad = lax.fori_loop(0, 2, head, jnp.zeros((PAIR, qq.shape[0]), F32))
    return (grad.T * HEAD_DIM**-0.5).astype(BF16)


def attention_backward(name, info, q, kv, att, datt, inverses, probs, splits, split, stores):
    rows, width = q.shape
    count = kv.shape[0]
    lanes = width // splits
    pairs = lanes // PAIR
    all_pairs = width // PAIR
    base = split * pairs

    def body(info_ref, q_ref, k_ref, v_ref, att_ref, datt_ref, inverse_ref, probs_ref, *refs):
        dq_ref, down_ref, dother_ref, turned_keys, acc = refs
        step = pl.program_id(0)
        index = pl.program_id(1)
        at = pair_at(index)
        vat = pair_at(index + pairs)

        @pl.when(step == 0)
        def _():
            turned_keys[at, :] = k_ref[...].T
            acc[:, at] = jnp.zeros((count, PAIR), F32)
            acc[:, vat] = jnp.zeros((count, PAIR), F32)

        def add_keys(into, value):
            acc[into, at] += value

        def add_values(into, value):
            acc[into, vat] += value

        dq_ref[...] = backward_pair(
            q_ref[...],
            datt_ref[...],
            att_ref[...],
            k_ref,
            v_ref,
            turned_keys[at, :],
            lambda part: inverse_ref[0, pl.ds(part, 1), :],
            lambda part, into: probs_ref[part, into, :],
            1024,
            add_keys,
            add_values,
        )

        @pl.when((step == pl.num_programs(0) - 1) & (index == pairs - 1))
        def _():
            stores(info_ref, acc, down_ref, dother_ref)

    pair_rows = pl.BlockSpec((WIDE, PAIR), lambda i, h, *_: (i, base + h))
    half = (count // 2, 2 * lanes)
    return call(
        body,
        name,
        info,
        (rows // WIDE, pairs),
        [
            (q, pair_rows),
            (kv, pl.BlockSpec((count, PAIR), lambda i, h, *_: (0, base + h))),
            (kv, pl.BlockSpec((count, PAIR), lambda i, h, *_: (0, all_pairs + base + h))),
            (att, pair_rows),
            (datt, pair_rows),
            (inverses, pl.BlockSpec((1, 2, WIDE), lambda i, h, *_: (base + h, 0, i))),
            (probs, pl.BlockSpec((2, count, WIDE), lambda i, h, *_: (base + h, 0, i))),
        ],
        [
            ((rows, lanes), BF16, pl.BlockSpec((WIDE, PAIR), lambda i, h, *_: (i, h))),
            (half, BF16, whole(half)),
            (half, BF16, whole(half)),
        ],
        [pltpu.VMEM((lanes, count), BF16), pltpu.VMEM((count, 2 * lanes), F32)],
        cost(32 * rows * count * lanes, 20 * rows * lanes + 2 * rows * count),
    )


def self_backward(info, q, kv, att, dat, inverses, probs, splits, split):
    quarter = q.shape[0] // 2

    def stores(info_ref, acc, down_ref, dother_ref):
        for target, core in ((down_ref, info_ref[2]), (dother_ref, 1 - info_ref[2])):
            for part in range(2):
                begin = pl.multiple_of(place_of(info_ref, core, part) * quarter, quarter)
                target[part * quarter : (part + 1) * quarter, :] = acc[
                    pl.ds(begin, quarter), :
                ].astype(BF16)

    return attention_backward(
        "self_backward", info, q, kv, att, dat, inverses, probs, splits, split, stores
    )


def cross_backward(info, cq, ckv, catt, dca, inverses, probs, splits, split):
    count = ckv.shape[0]

    def stores(info_ref, acc, down_ref, dother_ref):
        down_ref[...] = acc[: count // 2, :].astype(BF16)
        dother_ref[...] = acc[count // 2 :, :].astype(BF16)

    return attention_backward(
        "cross_backward", info, cq, ckv, catt, dca, inverses, probs, splits, split, stores
    )


def feed(info, catt, second_in, dy, cout, weights, gains, packing):
    rows, width = catt.shape
    hidden = weights.hidden
    cout_count = len(cout.arrays)
    feed_count = len(weights.arrays)
    packed = packing.outputs(width * width + 2 * width * hidden)

    def body(info_ref, catt_ref, second_ref, dy_first, dy_last, gain_ref, *refs):
        cout_refs, refs = refs[:cout_count], refs[cout_count:]
        feed_refs, refs = refs[:feed_count], refs[feed_count:]
        (
            out_first,
            out_last,
            dthird_ref,
            dca_ref,
            ggain_ref,
            *packed_refs,
            acc_cout,
            acc_widen,
            acc_narrow,
            cout_scratch,
            widen_scratch,
            narrow_scratch,
        ) = refs
        cout_full = cout.load(info_ref, cout_refs, cout_scratch)
        widen_full, narrow_full = weights.load(info_ref, feed_refs, (widen_scratch, narrow_scratch))
        step = pl.program_id(0)

        @pl.when(step == 0)
        def _():
            acc_cout[...] = jnp.zeros_like(acc_cout)
            acc_widen[...] = jnp.zeros_like(acc_widen)
            acc_narrow[...] = jnp.zeros_like(acc_narrow)
            ggain_ref[...] = jnp.zeros_like(ggain_ref)

        catt = catt_ref[...]
        dy_low = dy.load(dy_first, dy_last)
        gain = gain_ref[5:6, :]
        third = second_ref[...] + dot(catt, cout_full[...])
        normed, scale = normalized(third)
        normed_low = (normed * gain).astype(BF16)
        pre = dot(normed_low, widen_full[...])
        below = 0.5 * (1.0 + lax.erf(pre * math.sqrt(0.5)))
        bell = jnp.exp(-0.5 * pre * pre) * (1.0 / math.sqrt(2.0 * math.pi))
        act = (pre * below).astype(BF16)
        store_half(
            (out_first, out_last), (third + dot(act, narrow_full[...])).astype(BF16)
        )
        dact = dot(dy_low, narrow_full[...], 1, 1)
        dpre = (dact * (below + pre * bell)).astype(BF16)
        acc_narrow[...] += dot(act, dy_low, 0, 0)
        acc_widen[...] += dot(normed_low, dpre, 0, 0)
        dnormed = dot(dpre, widen_full[...], 1, 1)
        ggain_ref[...] += jnp.sum(dnormed * normed, axis=0, keepdims=True)
        dthird = dy_low.astype(F32) + norm_backward(dnormed * gain, normed, scale)
        dthird_ref[...] = dthird
        dc = dthird.astype(BF16)
        dca_ref[...] = dot(dc, cout_full[...], 1, 1).astype(BF16)
        acc_cout[...] += dot(catt, dc, 0, 0)

        @pl.when(step == pl.num_programs(0) - 1)
        def _():
            packing.store(info_ref, packed_refs, (acc_cout, acc_widen, acc_narrow))

    return call(
        body,
        "feed",
        info,
        rows // BLOCK,
        [(catt, rows_of(width)), (second_in, rows_of(width))]
        + dy.inputs(BLOCK)
        + [(gains, whole(gains.shape))]
        + cout.inputs()
        + weights.inputs(),
        half_outputs(rows, width, BLOCK)
        + [
            ((rows, width), F32, rows_of(width)),
            ((rows, width), BF16, rows_of(width)),
            ((1, width), F32, whole((1, width))),
        ]
        + packed,
        [
            pltpu.VMEM((width, width), F32),
            pltpu.VMEM((width, hidden), F32),
            pltpu.VMEM((hidden, width), F32),
            cout.scratch(),
        ]
        + weights.scratch(),
        cost(
            12 * rows * width * hidden, 24 * rows * width + 8 * width * hidden, 2 * rows * hidden
        ),
    )


def sum_low(own_ref, got_ref):
    return (own_ref[...].astype(F32) + got_ref[...].astype(F32)).astype(BF16)


def middle_backward(
    info, dcqs, second_in, dthird, att, owns, gots, encoder, weights, gains, packing
):
    rows, width = second_in.shape
    count = len(dcqs)
    lanes = width // count
    packed = packing.outputs(4 * width * width)
    pieces = [len(w.arrays) for w in weights]
    short = encoder.shape[0] // (rows // BLOCK)

    def body(info_ref, att_ref, second_ref, dthird_ref, gain_ref, enc_first, enc_last, *refs):
        dcq_refs, refs = refs[:count], refs[count:]
        own_refs, refs = refs[:count], refs[count:]
        got_refs, refs = refs[:count], refs[count:]
        weight_refs = []
        for number in pieces:
            weight_refs.append(refs[:number])
            refs = refs[number:]
        dsecond_ref, dat_ref, ggain_ref, *genc_refs = refs[:5]
        refs = refs[5:]
        packed_refs, refs = refs[: len(packed)], refs[len(packed) :]
        acc_query, acc_out, acc_memory, *scratch = refs
        out_full, query_full, memory_full = [
            w.load(info_ref, r, s) for w, r, s in zip(weights, weight_refs, scratch)
        ]
        step = pl.program_id(0)

        @pl.when(step == 0)
        def _():
            acc_query[...] = jnp.zeros_like(acc_query)
            acc_out[...] = jnp.zeros_like(acc_out)
            acc_memory[...] = jnp.zeros_like(acc_memory)
            ggain_ref[...] = jnp.zeros_like(ggain_ref)

        dcq = jnp.concatenate([ref[...] for ref in dcq_refs], axis=1)
        gain = gain_ref[4:5, :]
        normed, scale = normalized(second_ref[...])
        normed_low = (normed * gain).astype(BF16)
        dnormed = dot(dcq, query_full[...], 1, 1)
        acc_query[...] += dot(normed_low, dcq, 0, 0)
        ggain_ref[...] += jnp.sum(dnormed * normed, axis=0, keepdims=True)
        dsecond = dthird_ref[...] + norm_backward(dnormed * gain, normed, scale)
        dsecond_ref[...] = dsecond
        da = dsecond.astype(BF16)
        dat_ref[...] = dot(da, out_full[...], 1, 1).astype(BF16)
        acc_out[...] += dot(att_ref[...], da, 0, 0)

        turned = encoder.load(enc_first, enc_last).T
        grads = [sum_low(own, got) for own, got in zip(own_refs, got_refs)]
        dckv = jnp.concatenate(
            [g[:, :lanes] for g in grads] + [g[:, lanes:] for g in grads], axis=1
        )
        store_half(genc_refs, dot(dckv, memory_full[...], 1, 1).astype(BF16))
        acc_memory[...] += dot(turned, dckv)

        @pl.when(step == pl.num_programs(0) - 1)
        def _():
            packing.store(info_ref, packed_refs, (acc_query, acc_out, acc_memory))

    return call(
        body,
        "middle_backward",
        info,
        rows // BLOCK,
        [
            (att, rows_of(width)),
            (second_in, rows_of(width)),
            (dthird, rows_of(width)),
            (gains, whole(gains.shape)),
        ]
        + encoder.inputs(short)
        + [(a, rows_of(lanes)) for a in dcqs]
        + [(a, rows_of(2 * lanes, short)) for a in owns]
        + [(a, rows_of(2 * lanes, short)) for a in gots]
        + [entry for w in weights for entry in w.inputs()],
        [
            ((rows, width), F32, rows_of(width)),
            ((rows, width), BF16, rows_of(width)),
            ((1, width), F32, whole((1, width))),
        ]
        + half_outputs(encoder.shape[0], width, short)
        + packed,
        [
            pltpu.VMEM((width, width), F32),
            pltpu.VMEM((width, width), F32),
            pltpu.VMEM((width, 2 * width), F32),
        ]
        + [w.scratch() for w in weights],
        cost(16 * rows * width * width, 20 * rows * width),
    )


VECTORS = 16


def project_backward(
    info, tokens, normed, dqs, owns, gots, dsecond, mods, ggains, embedded, weight, packing
):
    rows, width = tokens.shape
    count = len(dqs)
    lanes = width // count
    packed = packing.outputs(3 * width * width, VECTORS)
    pieces = len(weight.arrays)

    def body(info_ref, first_ref, last_ref, normed_ref, dsecond_ref, mod_ref, *refs):
        second_gain, third_gain, embedded_ref, *refs = refs
        dq_refs, refs = refs[:count], refs[count:]
        own_refs, refs = refs[:count], refs[count:]
        got_refs, refs = refs[:count], refs[count:]
        weight_refs, refs = refs[:pieces], refs[pieces:]
        gfirst_ref, glast_ref, vectors_ref, *packed_refs, acc, sums, scratch = refs
        full = weight.load(info_ref, weight_refs, scratch)
        step = pl.program_id(0)

        @pl.when(step == 0)
        def _():
            acc[...] = jnp.zeros_like(acc)
            sums[...] = jnp.zeros_like(sums)

        turned = normed_ref[...].T
        dkvs = [sum_low(own, got) for own, got in zip(own_refs, got_refs)]
        grads = jnp.concatenate(
            [ref[...] for ref in dq_refs]
            + [dkv[:, :lanes] for dkv in dkvs]
            + [dkv[:, lanes:] for dkv in dkvs],
            axis=1,
        )
        acc[...] += dot(turned, grads)
        dnormed = dot(grads, full[...], 1, 1)
        unit, scale = normalized(tokens.load(first_ref, last_ref).astype(F32))
        sums[0:1, :] += jnp.sum(dnormed * unit, axis=0, keepdims=True)
        sums[1:2, :] += jnp.sum(dnormed, axis=0, keepdims=True)
        store_half(
            (gfirst_ref, glast_ref),
            (
                dsecond_ref[...] + norm_backward(dnormed * mod_ref[0:1, :], unit, scale)
            ).astype(BF16),
        )

        @pl.when(step == pl.num_programs(0) - 1)
        def _():
            vectors = jnp.concatenate(
                [
                    sums[0:1, :] * mod_ref[2:3, :],
                    second_gain[...],
                    third_gain[...],
                    sums[0:1, :] * mod_ref[3:4, :],
                    sums[1:2, :],
                    embedded_ref[0:1, :].astype(F32),
                    jnp.zeros((VECTORS - 6, width), F32),
                ],
                axis=0,
            )
            vectors_ref[...] = vectors
            packing.store(info_ref, packed_refs, (acc,), vectors)

    return call(
        body,
        "project_backward",
        info,
        rows // BLOCK,
        tokens.inputs(BLOCK)
        + [
            (normed, rows_of(width)),
            (dsecond, rows_of(width)),
            (mods, whole(mods.shape)),
            (ggains[0], whole((1, width))),
            (ggains[1], whole((1, width))),
            (embedded, whole(embedded.shape)),
        ]
        + [(a, rows_of(lanes)) for a in dqs]
        + [(a, rows_of(2 * lanes)) for a in owns]
        + [(a, rows_of(2 * lanes)) for a in gots]
        + weight.inputs(),
        half_outputs(rows, width, BLOCK)
        + [((VECTORS, width), F32, whole((VECTORS, width)))]
        + packed,
        [pltpu.VMEM((width, 3 * width), F32), pltpu.VMEM((8, width), F32), weight.scratch()],
        cost(12 * rows * width * width, 20 * rows * width),
    )


def join_columns(info, parts):
    size = parts[0].shape[0] - VECTORS
    shape = (size + len(parts) * VECTORS, parts[0].shape[1])

    def body(info_ref, *refs):
        *part_refs, out_ref = refs
        total = part_refs[0][:size, :].astype(F32)
        for ref in part_refs[1:]:
            total = total + ref[:size, :].astype(F32)
        out_ref[:size, :] = total.astype(BF16)
        for index, ref in enumerate(part_refs):
            begin = size + index * VECTORS
            out_ref[begin : begin + VECTORS, :] = ref[size:, :]

    return call(
        body,
        "join_columns",
        info,
        1,
        [(part, whole(part.shape)) for part in parts],
        [(shape, BF16, whole(shape))],
        [],
        cost(0, 4 * size * shape[1]),
    )[0]


def in_seq_order(info, own, got, bit, out_ref, begin):
    rows = own.shape[0]
    own_place = (info[5] >> bit) % 2
    for part, place in ((own, own_place), (got, 1 - own_place)):
        at = pl.ds(pl.multiple_of(begin + place * rows, VECTORS), rows)
        out_ref[at, :] = part


def join_rows(info, own, got, size):
    count = own.shape[0] - size
    shape = (size + 2 * count, own.shape[1])

    def body(info_ref, own_ref, got_ref, out_ref):
        total = own_ref[:size, :].astype(F32) + got_ref[:size, :].astype(F32)
        out_ref[:size, :] = total.astype(BF16)
        in_seq_order(info_ref, own_ref[size:, :], got_ref[size:, :], 0, out_ref, size)

    return call(
        body,
        "join_rows",
        info,
        1,
        [(own, whole(own.shape)), (got, whole(got.shape))],
        [(shape, BF16, whole(shape))],
        [],
        cost(0, 6 * size * shape[1]),
    )[0]


def finish(info, own, got, size, shard):
    width = own.shape[1]
    count = own.shape[0] - size
    devices = 2 * count // VECTORS

    def body(info_ref, own_ref, got_ref, ginput_ref, gtime_ref, ggains_ref, listed, turned):
        for block in range(size // shard):
            rows = slice(block * shard, (block + 1) * shard)
            ginput_ref[:, block * width : (block + 1) * width] = own_ref[rows, :].astype(
                F32
            ) + got_ref[rows, :].astype(F32)
        in_seq_order(info_ref, own_ref[size:, :], got_ref[size:, :], 1, listed, 0)
        vectors = listed[...]
        column = lax.broadcasted_iota(jnp.int32, (devices, 2 * count), 1)
        row = lax.broadcasted_iota(jnp.int32, (devices, 2 * count), 0)

        def pick(kind):
            chosen = jnp.where(column == row * VECTORS + kind, 1.0, 0.0).astype(BF16)
            return dot(chosen, vectors)

        chosen = jnp.where(lax.rem(column, VECTORS) == row, 1.0, 0.0).astype(BF16)
        turned[...] = jnp.concatenate([0.5 * pick(5), dot(chosen, vectors)], axis=0).T
        place = (2 * info_ref[4] + info_ref[2]) * shard
        part = turned[pl.ds(pl.multiple_of(place, shard), shard), :]
        grads = jnp.concatenate([pick(3), pick(4)], axis=1).astype(BF16)
        gtime_ref[...] = dot(part[:, :devices].astype(BF16), grads)
        ggains_ref[...] = part.T[devices : devices + 3, :]

    return call(
        body,
        "finish",
        info,
        1,
        [(own, whole(own.shape)), (got, whole(got.shape))],
        [
            ((shard, 3 * width), F32, whole((shard, 3 * width))),
            ((shard, 2 * width), F32, whole((shard, 2 * width))),
            ((3, shard), F32, whole((3, shard))),
        ],
        [pltpu.VMEM((2 * count, width), BF16), pltpu.VMEM((width, 2 * devices), F32)],
        cost(4 * devices * count * width, 8 * size * width),
    )


def permutations(seq_count, fsdp_count):
    columns = fsdp_count // 2

    def at(seq, fsdp):
        return seq * fsdp_count + fsdp

    def pairs(move):
        return [
            (at(seq, fsdp), at(*move(seq, fsdp)))
            for seq in range(seq_count)
            for fsdp in range(fsdp_count)
        ]

    def home(turn):
        def move(seq, fsdp):
            y, x = divmod(seq, 2)
            column, core = divmod(fsdp, 2)
            return 2 * core + (x ^ turn), 2 * column + y

        return move

    shift = {
        r: pairs(lambda seq, fsdp, r=r: (seq, (fsdp + 2 * r) % fsdp_count))
        for r in range(1, columns)
    }
    cross = {t: pairs(lambda seq, fsdp, t=t: (seq ^ t, fsdp)) for t in range(1, seq_count)}
    swap = pairs(lambda seq, fsdp: (seq, fsdp ^ 1))
    return pairs(home(0)), pairs(home(1)), swap, shift, cross


def reverse(pairs):
    return [(target, source) for source, target in pairs]


def after(values, signal):
    return lax.optimization_barrier((values, signal))[0]


class Direct:
    def __init__(self, perms, seq, fsdp, columns):
        self.same, self.crossed, self.swap_pairs, self.shifts, self.crosses = perms
        self.seq = seq
        self.core = fsdp % 2
        self.z = fsdp // 2
        self.columns = columns

    def permute(self, values, pairs):
        return lax.ppermute(values, AXES, pairs)

    def swap(self, values):
        return self.permute(values, self.swap_pairs)

    def along_z(self, values):
        return [values] + [
            self.permute(values, self.shifts[r]) for r in range(1, self.columns)
        ]

    def both_cores(self, pieces):
        return pieces + [self.swap(piece) for piece in pieces]

    def core_sum(self, mine, away, signal=()):
        got = after(self.swap(away), signal)
        return [
            (mine[r].astype(F32) + got[r].astype(F32)).astype(BF16) for r in range(self.columns)
        ]

    def z_parts(self, shards):
        return [self.permute(shards[r], self.shifts[r]) for r in range(1, self.columns)]

    def z_sum(self, shards, got, signal=()):
        total = shards[0].astype(F32)
        for part in after(got, signal):
            total = total + part.astype(F32)
        return lax.optimization_barrier(total.astype(BF16))

    def add(self, first, second):
        return lax.optimization_barrier((first.astype(F32) + second.astype(F32)).astype(BF16))

    def cross(self, values, turn):
        return self.permute(values, self.crosses[turn])


SPLITS = 2


def time_embedding(step_values, model_width):
    half_width = model_width // 2
    frequency = jnp.exp(-math.log(10000.0) * jnp.arange(half_width, dtype=F32) / half_width)
    angles = step_values.astype(F32)[:, None] * frequency[None, :]
    return jnp.concatenate([jnp.sin(angles), jnp.cos(angles)], axis=-1).astype(BF16)


def exact_dot(left, right):
    return lax.dot_general(
        left,
        right,
        (((0,), (0,)), ((), ())),
        precision=lax.Precision.HIGHEST,
        preferred_element_type=F32,
    )


def make(seq_count, fsdp_count):
    perms = permutations(seq_count, fsdp_count)
    same, crossed = perms[:2]
    columns = fsdp_count // 2

    def on_device(
        tokens,
        encoder_states,
        lengths,
        timesteps,
        time_weight,
        self_input,
        self_output,
        cross_query,
        cross_memory,
        cross_output,
        widen_weight,
        narrow_weight,
        norm_gains,
        cotangent,
    ):
        width = tokens.shape[2]
        hidden = widen_weight.shape[1]
        shard = time_weight.shape[0]
        seq = lax.axis_index("seq")
        fsdp = lax.axis_index("fsdp")
        core = fsdp % 2
        side = seq % 2
        direct = Direct(perms, seq, fsdp, columns) if columns == 4 else None

        def send_work(values):
            mine = lax.dynamic_index_in_dim(values, side, 0, keepdims=False)
            others = lax.dynamic_index_in_dim(values, 1 - side, 0, keepdims=False)
            return [lax.ppermute(mine, AXES, same), lax.ppermute(others, AXES, crossed)]

        def send_home(halves):
            return [
                lax.ppermute(halves[0], AXES, reverse(same)),
                lax.ppermute(halves[1], AXES, reverse(crossed)),
            ]

        def at_home(parts, kind):
            first = jnp.where(side == 0, parts[0], parts[1])
            second = jnp.where(side == 0, parts[1], parts[0])
            return jnp.stack([first, second], axis=0).astype(kind)

        def gather(weight, axis=0):
            return lax.all_gather(weight, "fsdp", axis=axis, tiled=True)

        def swap(values):
            return lax.ppermute(values, AXES, perms[2])

        packing = Packing(fsdp_count, direct is not None, width)
        token_rows, encoder_rows = tokens.shape[1], encoder_states.shape[1]
        numbers = jnp.concatenate([lengths, timesteps[:, None]], axis=1)
        numbers_other = swap(numbers)
        own_row = jnp.where(core == seq // 2, numbers, numbers_other)
        own_row = lax.dynamic_slice_in_dim(own_row, side, 1, 0)
        step_value = own_row[0, 3:4]
        place = lax.broadcasted_iota(jnp.int32, (8,), 0)
        info = jnp.where(place == 1, own_row[0, 1], 0) + jnp.where(place <= 1, own_row[0, 0], 0)
        for index, value in enumerate((core, side, fsdp // 2, seq)):
            info = jnp.where(place == index + 2, value, info)
        embedded = jnp.pad(time_embedding(step_value, width), ((0, 15), (0, 0)))

        turned = jnp.pad(norm_gains.T, ((0, 0), (0, 128 - norm_gains.shape[0])))
        first = jnp.concatenate([self_input, time_weight, turned], axis=1)
        first_mine = direct.along_z(first) if direct else [(), ()]
        own = send_work(jnp.concatenate([tokens, encoder_states, cotangent], axis=1))
        inputs = token_rows + encoder_rows
        other = [swap(part[:inputs]) for part in after(own, first_mine[1:])]
        work_tokens = Halves(own, 0, token_rows)
        other_tokens = Halves(other, 0, token_rows)
        work_encoder = Halves(own, token_rows, encoder_rows)
        other_encoder = Halves(other, token_rows, encoder_rows)
        work_dy = Halves(own, inputs, token_rows)

        ready = info
        if direct:
            first_mine[0] = after(first_mine[0], (info, embedded))
            first = direct.both_cores(first_mine)
            rest = jnp.concatenate([self_output, cross_query, cross_memory, cross_output], axis=1)
            wide = widen_weight.reshape(shard, hidden // width, width).transpose(1, 0, 2)
            large = jnp.concatenate([wide.reshape(-1, width), narrow_weight], axis=0)
            rest, large = after((rest, large), own)
            rest_mine = direct.along_z(rest)
            rest_other = [swap(rest)]
            large_mine = direct.along_z(large)
            large_other = [swap(large)]
            ready = after(info, (rest_other, large_other))
            input_weight = Weight(first, 0, 3 * width)
            time_full = Weight(first, 3 * width, 2 * width)
            turned_gains = Weight(first, 5 * width, 128)
        else:
            input_weight = Weight([gather(self_input)], 0, 3 * width)
            time_full = Weight([gather(time_weight)], 0, 2 * width)
            turned_gains = Weight([gather(turned)], 0, 128)
            output_weight = Weight([gather(self_output)], 0, width)
            query_weight = Weight([gather(cross_query)], 0, width)
            memory_weight = Weight([gather(cross_memory)], 0, 2 * width)
            cout_weight = Weight([gather(cross_output)], 0, width)
            feed_weights = FeedWeights([gather(widen_weight), gather(narrow_weight)], hidden)

        mods, q, kv, normed_first, att, inverses, probs = self_forward(
            ready, work_tokens, other_tokens, embedded, time_full, turned_gains, input_weight
        )
        ready = info
        if direct:
            rest_mine[1:], large_mine[:2] = after((rest_mine[1:], large_mine[:2]), att)
            rest_other += [swap(part) for part in rest_mine[1:]]
            rest = rest_mine + rest_other
            large_other.append(swap(large_mine[1]))
            ready = after(info, large_other)
            output_weight = Weight(rest, 0, width)
            query_weight = Weight(rest, width, width)
            memory_weight = Weight(rest, 2 * width, 2 * width)
            cout_weight = Weight(rest, 4 * width, width)
        second_in, cq, ckv, catt, cross_inverses, cross_probs = cross_forward(
            ready,
            att,
            work_tokens,
            work_encoder,
            other_encoder,
            output_weight,
            mods,
            query_weight,
            memory_weight,
        )
        if direct:
            large_mine[2:] = after(large_mine[2:], catt)
            large_other += [swap(part) for part in large_mine[2:]]
            feed_weights = FeedWeights(large_mine + large_other, hidden)
        out_first, out_last, dthird, dca, ggain_third, *packed_feed = feed(
            info, catt, second_in, work_dy, cout_weight, feed_weights, mods, packing
        )
        layer_out = (out_first, out_last)
        out_parts = send_home(layer_out)

        def backward_cross(split, ready):
            return cross_backward(
                ready, cq, ckv, catt, dca, cross_inverses, cross_probs, SPLITS, split
            )

        def backward_self(split, ready):
            return self_backward(ready, q, kv, att, dat, inverses, probs, SPLITS, split)

        crosses = [backward_cross(0, info)]
        out_parts = after(out_parts, crosses[0][0])
        chip_feed = direct.core_sum(*packed_feed, crosses[0][0]) if direct else ()
        crosses.append(backward_cross(1, after(info, (chip_feed, out_parts))))
        dcqs, dckvs, dckv_others = zip(*crosses)
        dckv_gots = [swap(a) for a in dckv_others]
        feed_parts = direct.z_parts(chip_feed) if direct else [()]
        dsecond, dat, ggain_second, *genc = middle_backward(
            after(info, (feed_parts[0], dcqs)),
            dcqs,
            second_in,
            dthird,
            att,
            dckvs,
            dckv_gots,
            work_encoder,
            (output_weight, query_weight, memory_weight),
            mods,
            packing,
        )
        genc, packed_middle = genc[:2], genc[2:]
        selfs = [backward_self(0, after(info, packed_middle))]
        if direct:
            column_feed = direct.z_sum(chip_feed, feed_parts, selfs[0][0])
            chip_middle = direct.core_sum(*packed_middle, selfs[0][0])
            selfs.append(backward_self(1, after(info, (column_feed, chip_middle))))
            middle_parts = after(direct.z_parts(chip_middle), selfs[1][0])
            row_feed = after(direct.cross(column_feed, 1), selfs[1][0])
            row_feed = direct.add(column_feed, row_feed)
            column_middle = direct.z_sum(chip_middle, middle_parts)
        else:
            selfs.append(backward_self(1, info))
        dqs, dkvs, dkv_others = zip(*selfs)
        dkv_others = list(dkv_others)
        if direct:
            dkv_others[1] = after(dkv_others[1], (column_middle, row_feed))
        dkv_gots = [swap(a) for a in dkv_others]
        first_grad, last_grad, vectors, *packed_input = project_backward(
            info,
            work_tokens,
            normed_first,
            dqs,
            dkvs,
            dkv_gots,
            dsecond,
            mods,
            (ggain_second, ggain_third),
            embedded,
            input_weight,
            packing,
        )
        gtokens = (first_grad, last_grad)
        if direct:
            chip = direct.core_sum(*packed_input)
            got_row = after(direct.cross(row_feed, 2), gtokens)
            row_middle = after(direct.cross(column_middle, 1), gtokens)
            row_middle = direct.add(column_middle, row_middle)
            enc_parts = after(send_home(genc), gtokens)
            gots = direct.z_parts(chip)
            token_parts = after(send_home(after(gtokens, chip)), gots)
            ready = after(info, token_parts)
            reduced_feed = row_feed.astype(F32) + got_row.astype(F32)
            size = chip[0].shape[0] - VECTORS
            joined = join_columns(ready, [chip[0]] + gots)
            got = direct.cross(joined, 1)
            got_row = direct.cross(after(row_middle, joined), 2)
            joined = join_rows(info, joined, got, size)
            got = direct.cross(joined, 2)
            reduced_middle = row_middle.astype(F32) + got_row.astype(F32)
            reduced_input, gtime, ggains = finish(info, joined, got, size, shard)
        else:

            def reduce(packed):
                part = lax.psum_scatter(packed[0], "fsdp", scatter_dimension=0, tiled=True)
                return lax.psum(part[0], "seq").astype(F32)

            reduced_input = reduce(packed_input)
            reduced_input = unpack_rows(reduced_input, 0, shard, 3 * width)
            reduced_middle = reduce(packed_middle)
            reduced_feed = reduce(packed_feed)
            token_parts, enc_parts = send_home(gtokens), send_home(genc)
            ggains = lax.psum(vectors[:3], AXES)
            ggains = lax.dynamic_slice_in_dim(ggains, fsdp * shard, shard, 1)
            by_group = lax.all_gather(vectors[3:5], AXES, axis=0)
            by_group = by_group.reshape(seq_count, columns, 2, 2 * width).sum(axis=2)
            by_group = by_group.transpose(1, 0, 2).reshape(-1, 2 * width)
            every = time_embedding(gather(timesteps), width)
            own_columns = lax.dynamic_slice_in_dim(every, fsdp * shard, shard, 1)
            gtime = exact_dot(own_columns.astype(F32), by_group)

        tall = narrow_weight.shape[0]
        return (
            at_home(out_parts, BF16),
            at_home(token_parts, F32),
            at_home(enc_parts, F32),
            gtime,
            reduced_input,
            unpack_rows(reduced_middle, shard, shard, width),
            unpack_rows(reduced_middle, 0, shard, width),
            unpack_rows(reduced_middle, 2 * shard, shard, 2 * width),
            unpack_rows(reduced_feed, 0, shard, width),
            unpack_rows(reduced_feed, shard, shard, hidden),
            unpack_rows(reduced_feed, shard * (1 + hidden // width), tall, width),
            ggains,
        )

    return on_device


def solution(mesh):
    rows = P("fsdp", "seq", None)
    weight = P("fsdp", None)
    in_specs = (rows, rows, P("fsdp", None), P("fsdp")) + (weight,) * 8 + (P(None, "fsdp"), rows)
    out_specs = (rows,) * 3 + (weight,) * 8 + (P(None, "fsdp"),)
    return jax.shard_map(
        make(mesh.shape["seq"], mesh.shape["fsdp"]),
        mesh=mesh,
        in_specs=in_specs,
        out_specs=out_specs,
        check_vma=False,
    )
```

```python
import math

import jax
import jax.numpy as jnp
from jax import lax
from jax.experimental import pallas as pl
from jax.experimental.pallas import tpu as pltpu
from jax.sharding import PartitionSpec as P


HEAD_DIM = 64
PAIR = 2 * HEAD_DIM
EPS = 1e-05
NEG = -1e30
F32 = jnp.float32
BF16 = jnp.bfloat16
AXES = ("seq", "fsdp")
VMEM_LIMIT = 60 * 2**20
BLOCK = 256
WIDE = 512


def dot(left, right, left_dim=1, right_dim=0):
    return lax.dot_general(
        left, right, (((left_dim,), (right_dim,)), ((), ())), preferred_element_type=F32
    )


def whole(shape):
    return pl.BlockSpec(shape, lambda *_: (0,) * len(shape))


def rows_of(width, block=BLOCK):
    return pl.BlockSpec((block, width), lambda i, *_: (i, 0))


def params():
    return pltpu.CompilerParams(vmem_limit_bytes=VMEM_LIMIT)


def cost(flops, moved, transcendentals=0):
    return pl.CostEstimate(
        flops=int(flops), bytes_accessed=int(moved), transcendentals=int(transcendentals)
    )


def normalized(values):
    average = jnp.mean(values, axis=-1, keepdims=True)
    centred = values - average
    spread = jnp.mean(centred * centred, axis=-1, keepdims=True)
    scale = lax.rsqrt(spread + EPS)
    return centred * scale, scale


def norm_backward(upstream, normed, scale):
    mean_up = jnp.mean(upstream, axis=-1, keepdims=True)
    mean_both = jnp.mean(upstream * normed, axis=-1, keepdims=True)
    return (upstream - mean_up - normed * mean_both) * scale


def lane_is(part):
    lane = lax.broadcasted_iota(jnp.int32, (1, PAIR), 1)
    return lane < HEAD_DIM if part == 0 else lane >= HEAD_DIM


def half_of(values, part):
    return jnp.where(lane_is(part), values, jnp.zeros_like(values))


def pair_at(index):
    return pl.ds(pl.multiple_of(index * PAIR, PAIR), PAIR)


def first_step(dims=1):
    first = pl.program_id(0) == 0
    return first if dims == 1 else first & (pl.program_id(1) == 0)


class Weight:
    def __init__(self, pieces, start, width):
        self.arrays = pieces
        self.start = start
        self.width = width

    @property
    def split(self):
        return len(self.arrays) > 1

    @property
    def rows(self):
        return len(self.arrays) * self.arrays[0].shape[0]

    @property
    def aligned(self):
        return self.start % self.width == 0

    def inputs(self):
        if not self.aligned:
            return [(array, whole(array.shape)) for array in self.arrays]
        place = self.start // self.width
        shape = (self.arrays[0].shape[0], self.width)
        return [(array, pl.BlockSpec(shape, lambda *_: (0, place))) for array in self.arrays]

    def scratch(self):
        return pltpu.VMEM((self.rows, self.width) if self.split else (16, 128), BF16)

    def load(self, info, refs, scratch, dims=1):
        if not self.split:
            return refs[0]
        columns = slice(0, self.width) if self.aligned else slice(self.start, self.start + self.width)

        @pl.when(first_step(dims))
        def _():
            count = len(refs) // 2
            shard = refs[0].shape[0]
            for index, ref in enumerate(refs):
                turn, shift = divmod(index, count)
                core = info[2] if turn == 0 else 1 - info[2]
                owner = lax.rem(info[4] - shift + count, count)
                start = pl.multiple_of((2 * owner + core) * shard, shard)
                scratch[pl.ds(start, shard), :] = ref[:, columns]

        return scratch


class Halves:
    def __init__(self, arrays, start, rows):
        self.arrays = arrays
        self.start = start
        self.rows = rows
        self.shape = (2 * rows, arrays[0].shape[1])

    def inputs(self, block):
        width = self.shape[1]
        count = self.rows // block
        base = self.start // block
        return [
            (
                self.arrays[0],
                pl.BlockSpec((block, width), lambda i, *_: (base + jnp.minimum(i, count - 1), 0)),
            ),
            (
                self.arrays[1],
                pl.BlockSpec((block, width), lambda i, *_: (base + jnp.maximum(i - count, 0), 0)),
            ),
        ]

    def resident(self):
        place = self.start // self.rows
        spec = pl.BlockSpec((self.rows, self.shape[1]), lambda *_: (place, 0))
        return [(array, spec) for array in self.arrays]

    def load(self, first_ref, second_ref):
        half = pl.num_programs(0) // 2
        return jnp.where(pl.program_id(0) < half, first_ref[...], second_ref[...])


def half_outputs(rows, width, block):
    count = rows // block // 2
    half = (rows // 2, width)
    return [
        (half, BF16, pl.BlockSpec((block, width), lambda i, *_: (jnp.minimum(i, count - 1), 0))),
        (half, BF16, pl.BlockSpec((block, width), lambda i, *_: (jnp.maximum(i - count, 0), 0))),
    ]


def store_half(refs, value):
    first = pl.program_id(0) < pl.num_programs(0) // 2

    @pl.when(first)
    def _():
        refs[0][...] = value

    @pl.when(jnp.logical_not(first))
    def _():
        refs[1][...] = value


class FeedWeights:
    def __init__(self, arrays, hidden):
        self.arrays = arrays
        self.hidden = hidden

    @property
    def split(self):
        return len(self.arrays) > 2

    def inputs(self):
        return [(array, whole(array.shape)) for array in self.arrays]

    def scratch(self):
        if not self.split:
            return [pltpu.VMEM((16, 128), BF16)] * 2
        width = self.arrays[0].shape[1]
        return [pltpu.VMEM((width, self.hidden), BF16), pltpu.VMEM((self.hidden, width), BF16)]

    def load(self, info, refs, scratch):
        if not self.split:
            return refs
        widen, narrow = scratch

        @pl.when(pl.program_id(0) == 0)
        def _():
            count = len(refs) // 2
            rows, width = refs[0].shape
            blocks = self.hidden // width
            tall = rows // 2
            short = tall // blocks
            for index, ref in enumerate(refs):
                turn, shift = divmod(index, count)
                core = info[2] if turn == 0 else 1 - info[2]
                owner = 2 * lax.rem(info[4] - shift + count, count) + core
                start = pl.multiple_of(owner * short, short)
                for block in range(blocks):
                    widen[pl.ds(start, short), block * width : (block + 1) * width] = ref[
                        block * short : (block + 1) * short, :
                    ]
                start = pl.multiple_of(owner * tall, tall)
                narrow[pl.ds(start, tall), :] = ref[tall:, :]

        return widen, narrow


class Packing:
    def __init__(self, shards, direct, width):
        self.shards = shards
        self.direct = direct
        self.width = width

    def outputs(self, elements, extra=0):
        rows = elements // (self.shards * self.width)
        if self.direct:
            rows += extra
        if self.direct:
            shape = (self.shards // 2, rows, self.width)
            return [(shape, BF16, whole(shape))] * 2
        shape = (self.shards, rows, self.width)
        return [(shape, BF16, whole(shape))]

    def store(self, info, packed, grads, vectors=None, unroll=False):
        def put(ref, slot, owner):
            offset = 0
            for grad in grads:
                rows = grad.shape[0] // self.shards
                start = owner * rows
                if not isinstance(owner, int):
                    start = pl.multiple_of(start, rows)
                for block in range(grad.shape[1] // self.width):
                    columns = slice(block * self.width, (block + 1) * self.width)
                    ref[slot, offset : offset + rows, :] = grad[pl.ds(start, rows), columns].astype(
                        BF16
                    )
                    offset += rows
            if vectors is not None and self.direct:
                ref[slot, offset:, :] = vectors.astype(BF16)

        if self.direct:
            count = self.shards // 2
            for ref, core in ((packed[0], info[2]), (packed[1], 1 - info[2])):

                def one(shift, carry, ref=ref, core=core):
                    put(ref, shift, 2 * lax.rem(info[4] + shift, count) + core)
                    return carry

                if unroll:
                    for shift in range(count):
                        one(shift, 0)
                else:
                    lax.fori_loop(0, count, one, 0)
        else:
            for shard in range(self.shards):
                put(packed[0], shard, shard)


def unpack_rows(packed, offset, rows, columns):
    width = packed.shape[1]
    blocks = columns // width
    parts = [packed[offset + b * rows : offset + (b + 1) * rows] for b in range(blocks)]
    return jnp.concatenate(parts, axis=1) if blocks > 1 else parts[0]


def call(body, name, info, grid, inputs, outputs, scratch, estimate):
    return pl.pallas_call(
        body,
        name=name,
        grid_spec=pltpu.PrefetchScalarGridSpec(
            num_scalar_prefetch=1,
            grid=grid if isinstance(grid, tuple) else (grid,),
            in_specs=[spec for _, spec in inputs],
            out_specs=[spec for _, _, spec in outputs],
            scratch_shapes=scratch,
        ),
        out_shape=[jax.ShapeDtypeStruct(shape, kind) for shape, kind, _ in outputs],
        compiler_params=params(),
        cost_estimate=estimate,
    )(info, *[array for array, _ in inputs])


def block_start(info, block_index, block, quarter):
    per_quarter = quarter // block
    first = block_index < per_quarter
    place = jnp.where(first, info[3], 1 - info[3])
    return (2 * info[2] + place) * quarter + lax.rem(block_index, per_quarter) * block


def forbidden(info, start, block, half, queries_dim):
    keys_dim = 1 - queries_dim
    qshape = [1, 1]
    qshape[queries_dim] = block
    kshape = [1, 1]
    kshape[keys_dim] = half
    qpos = start + lax.broadcasted_iota(jnp.int32, tuple(qshape), queries_dim)
    kpos = half + lax.broadcasted_iota(jnp.int32, tuple(kshape), keys_dim)
    first, second = info[0], info[1]
    low = jnp.where((qpos >= first) & (qpos < second), second, first)
    high = jnp.where(qpos >= second, second, 2 * half)
    return jnp.where((kpos >= low) & (kpos < high), NEG, 0.0)


def key_specs(array, lanes, split, width):
    rows = array.shape[0]
    count = width // lanes
    return [
        (array, pl.BlockSpec((rows, lanes), lambda *_: (0, split))),
        (array, pl.BlockSpec((rows, lanes), lambda *_: (0, count + split))),
    ]


def attention_sums(low, high):
    return (low > 1e-20) & (high < 1e30)


def attend_pair(qq, keys_at, turned_values, free, bias, att_ref, inverse_ref, probs_ref):
    count = probs_ref.shape[1]
    row_head = lax.broadcasted_iota(jnp.int32, (PAIR, 1), 0) // HEAD_DIM
    lane_head = lax.broadcasted_iota(jnp.int32, (1, PAIR), 1) // HEAD_DIM
    turned_at = turned_values(slice(0, count))

    def head(part):
        qe = jnp.where(lane_head == part, qq, jnp.zeros_like(qq))
        total = None
        out = None
        for piece in (slice(0, free), slice(free, count)):
            if piece.start == piece.stop:
                continue
            s = dot(keys_at(piece), qe, 1, 1)
            p = jnp.exp(s if piece.start == 0 else s + bias[...])
            low = p.astype(BF16)
            probs_ref[part, piece, :] = low
            term = jnp.sum(p, axis=0, keepdims=True)
            attended = dot(turned_at[:, piece], low)
            total = term if total is None else total + term
            out = attended if out is None else out + attended
        return out, total

    outs, totals = zip(head(0), head(1))
    inverses = [1.0 / total for total in totals]
    out = jnp.where(row_head == 0, outs[0] * inverses[0], outs[1] * inverses[1])
    att_ref[...] = out.T.astype(BF16)
    for part in range(2):
        inverse_ref[0, part : part + 1, :] = inverses[part]
    low = jnp.min(jnp.minimum(totals[0], totals[1]))
    high = jnp.max(jnp.maximum(totals[0], totals[1]))

    @pl.when(jnp.logical_not((low > 1e-20) & (high < 1e30)))
    def _():
        chunk = BLOCK // 2
        queries = qq.shape[0]

        def again(part, carry):
            qe = jnp.where(lane_head == part, qq, jnp.zeros_like(qq))

            def scores(index):
                at = pl.ds(pl.multiple_of(index * chunk, chunk), chunk)
                s = dot(keys_at(at), qe, 1, 1)
                if free == count:
                    return at, s
                begin = jnp.maximum(index * chunk - free, 0)
                part_bias = bias[pl.ds(pl.multiple_of(begin, chunk), chunk), :]
                return at, s + jnp.where(index * chunk >= free, part_bias, 0.0)

            def largest(index, top):
                return jnp.maximum(top, jnp.max(scores(index)[1], axis=0, keepdims=True))

            top = lax.fori_loop(
                0, count // chunk, largest, jnp.full((1, queries), -jnp.inf, F32)
            )

            def add(index, sums):
                at, s = scores(index)
                p = jnp.exp(s - top)
                low = p.astype(BF16)
                probs_ref[part, at, :] = low
                return (
                    sums[0] + jnp.sum(p, axis=0, keepdims=True),
                    sums[1] + dot(turned_values(at), low),
                )

            total, out = lax.fori_loop(
                0,
                count // chunk,
                add,
                (jnp.zeros((1, queries), F32), jnp.zeros((PAIR, queries), F32)),
            )
            inverse = 1.0 / total
            inverse_ref[0, pl.ds(part, 1), :] = inverse
            return carry + jnp.where(row_head == part, out * inverse, 0.0)

        out = lax.fori_loop(0, 2, again, jnp.zeros((PAIR, queries), F32))
        att_ref[...] = out.T.astype(BF16)


def attention_outputs(rows, width, count):
    pairs = width // PAIR
    return [
        ((rows, width), BF16, pl.BlockSpec((WIDE, PAIR), lambda i, h, *_: (i, h))),
        ((pairs, 2, rows), F32, pl.BlockSpec((1, 2, WIDE), lambda i, h, *_: (h, 0, i))),
        ((2 * pairs, count, rows), BF16, pl.BlockSpec((2, count, WIDE), lambda i, h, *_: (h, 0, i))),
    ]


def place_of(info, core, part):
    return 2 * core + (info[3] if part == 0 else 1 - info[3])


def self_forward(info, own, other, embedded, time, turned_gains, weight):
    rows, width = own.shape
    pairs = width // PAIR
    quarter = rows // 2
    weights = (weight, time, turned_gains)
    pieces = [len(w.arrays) for w in weights]

    def body(info_ref, embedded_ref, *refs):
        token_refs, refs = refs[:4], refs[4:]
        weight_refs = []
        for number in pieces:
            weight_refs.append(refs[:number])
            refs = refs[number:]
        (
            mod_ref,
            q_out,
            kv_out,
            normed_out,
            att_ref,
            inverse_ref,
            probs_ref,
            queries,
            keys,
            normed,
            turned_values,
            staged,
            bias,
            *scratch,
            sems,
        ) = refs
        step = pl.program_id(0)
        index = pl.program_id(1)
        full, time_full, gains_full = [
            w.load(info_ref, r, s, 2) for w, r, s in zip(weights, weight_refs, scratch)
        ]
        copies = [
            pltpu.make_async_copy(queries, q_out, sems.at[0]),
            pltpu.make_async_copy(keys, kv_out, sems.at[1]),
            pltpu.make_async_copy(normed, normed_out, sems.at[2]),
        ]

        @pl.when(first_step(2))
        def _():
            modulation = dot(embedded_ref[...], time_full[...])
            gains = gains_full[...].astype(F32).T[:3, :]
            plus = 1.0 + modulation[0:1, :width]
            shift = modulation[0:1, width:]
            mod_ref[...] = jnp.concatenate(
                [gains[0:1] * plus, shift, plus, gains, jnp.zeros((2, width), F32)], axis=0
            )
            for number, ref in enumerate(token_refs):
                turn, part = divmod(number, 2)
                holder = info_ref[2] if turn == 0 else 1 - info_ref[2]
                begin = place_of(info_ref, holder, part) * quarter
                staged[pl.ds(pl.multiple_of(begin, quarter), quarter), :] = ref[...]

            def project(block, carry):
                at = pl.ds(pl.multiple_of(block * BLOCK, BLOCK), BLOCK)
                unit, _ = normalized(staged[at, :].astype(F32))
                first = (unit * mod_ref[0:1, :] + mod_ref[1:2, :]).astype(BF16)
                keys[at, :] = dot(first, full[:, width:]).astype(BF16)
                per_quarter = quarter // BLOCK
                place = block // per_quarter

                @pl.when(place // 2 == info_ref[2])
                def _():
                    part = lax.bitwise_xor(lax.rem(place, 2), info_ref[3])
                    begin = part * quarter + lax.rem(block, per_quarter) * BLOCK
                    here = pl.ds(pl.multiple_of(begin, BLOCK), BLOCK)
                    normed[here, :] = first
                    queries[here, :] = (dot(first, full[:, :width]) * HEAD_DIM**-0.5).astype(BF16)

                return carry

            lax.fori_loop(0, 2 * rows // BLOCK, project, 0)
            for copy in copies:
                copy.start()

            turned_values[...] = keys[:, width:].T

        @pl.when(index == 0)
        def _():
            start = block_start(info_ref, step, WIDE, quarter)
            bias[...] = forbidden(info_ref, start, WIDE, rows, 1)

        mine = pl.ds(pl.multiple_of(step * WIDE, WIDE), WIDE)
        at = pair_at(index)
        attend_pair(
            queries[mine, at],
            lambda piece: keys[piece, at],
            lambda piece: turned_values[at, piece],
            rows,
            bias,
            att_ref,
            inverse_ref,
            probs_ref,
        )

        @pl.when((step == pl.num_programs(0) - 1) & (index == pairs - 1))
        def _():
            for copy in copies:
                copy.wait()

    anywhere = pl.BlockSpec(memory_space=pl.ANY)
    return call(
        body,
        "self_forward",
        info,
        (rows // WIDE, pairs),
        [(embedded, whole(embedded.shape))]
        + own.resident()
        + other.resident()
        + [entry for w in weights for entry in w.inputs()],
        [
            ((8, width), F32, whole((8, width))),
            ((rows, width), BF16, anywhere),
            ((2 * rows, 2 * width), BF16, anywhere),
            ((rows, width), BF16, anywhere),
        ]
        + attention_outputs(rows, width, 2 * rows),
        [
            pltpu.VMEM((rows, width), BF16),
            pltpu.VMEM((2 * rows, 2 * width), BF16),
            pltpu.VMEM((rows, width), BF16),
            pltpu.VMEM((width, 2 * rows), BF16),
            pltpu.VMEM((2 * rows, width), BF16),
            pltpu.VMEM((rows, WIDE), F32),
        ]
        + [w.scratch() for w in weights]
        + [pltpu.SemaphoreType.DMA((3,))],
        cost(32 * rows * rows * width, 12 * rows * width, 2 * rows * rows * width // HEAD_DIM),
    )


def cross_forward(info, att, tokens, own, other, out_weight, gains, query_weight, memory_weight):
    rows, width = att.shape
    pairs = width // PAIR
    count = own.rows
    weights = (out_weight, query_weight, memory_weight)
    pieces = [len(w.arrays) for w in weights]

    def body(info_ref, att_ref, first_ref, last_ref, gain_ref, *refs):
        enc_refs, refs = refs[:4], refs[4:]
        weight_refs = []
        for number in pieces:
            weight_refs.append(refs[:number])
            refs = refs[number:]
        second_ref, cq_ref, ckv_out, catt_ref, inverse_ref, probs_ref, *refs = refs
        memory, turned_values, staged, *scratch, sem = refs
        out_full, query_full, memory_full = [
            w.load(info_ref, r, s, 2) for w, r, s in zip(weights, weight_refs, scratch)
        ]
        step = pl.program_id(0)
        index = pl.program_id(1)
        copy = pltpu.make_async_copy(memory, ckv_out, sem)

        @pl.when(first_step(2))
        def _():
            for part, ref in enumerate(enc_refs):
                staged[part * count : (part + 1) * count, :] = ref[...]

            def project(part, carry):
                at = pl.ds(pl.multiple_of(part * count, count), count)
                memory[at, :] = dot(staged[at, :], memory_full[...]).astype(BF16)
                return carry

            lax.fori_loop(0, 4, project, 0)
            copy.start()
            turned_values[...] = memory[:, width:].T

        @pl.when(index == 0)
        def _():
            second_in = tokens.load(first_ref, last_ref).astype(F32) + dot(
                att_ref[...], out_full[...]
            )
            second_ref[...] = second_in
            normed, _ = normalized(second_in)
            normed = (normed * gain_ref[4:5, :]).astype(BF16)
            cq_ref[...] = (dot(normed, query_full[...]) * HEAD_DIM**-0.5).astype(BF16)

        at = pair_at(index)
        attend_pair(
            cq_ref[:, at],
            lambda piece: memory[piece, at],
            lambda piece: turned_values[at, piece],
            4 * count,
            None,
            catt_ref,
            inverse_ref,
            probs_ref,
        )

        @pl.when((step == pl.num_programs(0) - 1) & (index == pairs - 1))
        def _():
            copy.wait()

    return call(
        body,
        "cross_forward",
        info,
        (rows // WIDE, pairs),
        [(att, rows_of(width, WIDE))]
        + tokens.inputs(WIDE)
        + [(gains, whole(gains.shape))]
        + own.resident()
        + other.resident()
        + [entry for w in weights for entry in w.inputs()],
        [
            ((rows, width), F32, rows_of(width, WIDE)),
            ((rows, width), BF16, rows_of(width, WIDE)),
            ((4 * count, 2 * width), BF16, pl.BlockSpec(memory_space=pl.ANY)),
        ]
        + attention_outputs(rows, width, 4 * count),
        [
            pltpu.VMEM((4 * count, 2 * width), BF16),
            pltpu.VMEM((width, 4 * count), BF16),
            pltpu.VMEM((4 * count, width), BF16),
        ]
        + [w.scratch() for w in weights]
        + [pltpu.SemaphoreType.DMA],
        cost(16 * rows * rows * width, 12 * rows * width, rows * rows * width // HEAD_DIM),
    )


def backward_pair(qq, dd, oo, keys, values, turned_keys, inverses, probs, size, add_keys, add_values):
    products = (oo.astype(F32) * dd.astype(F32)).T
    row_head = lax.broadcasted_iota(jnp.int32, (PAIR, 1), 0) // HEAD_DIM
    lane_head = lax.broadcasted_iota(jnp.int32, (1, PAIR), 1) // HEAD_DIM

    def head(part, total_grad):
        qe = jnp.where(lane_head == part, qq, jnp.zeros_like(qq))
        de = jnp.where(lane_head == part, dd, jnp.zeros_like(dd))
        inner = jnp.sum(jnp.where(row_head == part, products, 0.0), axis=0, keepdims=True)
        inverse = inverses(part)
        column = jnp.broadcast_to(inverse, (8, inverse.shape[1])).T[:, 0:1]
        scaled = (de.astype(F32) * column).astype(BF16)
        grad = None
        for begin in range(0, keys.shape[0], size):
            into = slice(begin, min(begin + size, keys.shape[0]))
            p = probs(part, into)
            dprobs = dot(values[into, :], de, 1, 1)
            dscores = (p.astype(F32) * ((dprobs - inner) * inverse)).astype(BF16)
            add_values(into, dot(p, scaled))
            add_keys(into, dot(dscores, qe))
            term = dot(turned_keys[:, into], dscores)
            grad = term if grad is None else grad + term
        return total_grad + jnp.where(row_head == part, grad, 0.0)

    grad = lax.fori_loop(0, 2, head, jnp.zeros((PAIR, qq.shape[0]), F32))
    return (grad.T * HEAD_DIM**-0.5).astype(BF16)


def attention_backward(name, info, q, kv, att, datt, inverses, probs, splits, split, stores):
    rows, width = q.shape
    count = kv.shape[0]
    lanes = width // splits
    pairs = lanes // PAIR
    all_pairs = width // PAIR
    base = split * pairs

    def body(info_ref, q_ref, k_ref, v_ref, att_ref, datt_ref, inverse_ref, probs_ref, *refs):
        dq_ref, down_ref, dother_ref, turned_keys, acc = refs
        step = pl.program_id(0)
        index = pl.program_id(1)
        at = pair_at(index)
        vat = pair_at(index + pairs)

        @pl.when(step == 0)
        def _():
            turned_keys[at, :] = k_ref[...].T
            acc[:, at] = jnp.zeros((count, PAIR), F32)
            acc[:, vat] = jnp.zeros((count, PAIR), F32)

        def add_keys(into, value):
            acc[into, at] += value

        def add_values(into, value):
            acc[into, vat] += value

        dq_ref[...] = backward_pair(
            q_ref[...],
            datt_ref[...],
            att_ref[...],
            k_ref,
            v_ref,
            turned_keys[at, :],
            lambda part: inverse_ref[0, pl.ds(part, 1), :],
            lambda part, into: probs_ref[part, into, :],
            2048,
            add_keys,
            add_values,
        )

        @pl.when((step == pl.num_programs(0) - 1) & (index == pairs - 1))
        def _():
            stores(info_ref, acc, down_ref, dother_ref)

    pair_rows = pl.BlockSpec((WIDE, PAIR), lambda i, h, *_: (i, base + h))
    half = (count // 2, 2 * lanes)
    return call(
        body,
        name,
        info,
        (rows // WIDE, pairs),
        [
            (q, pair_rows),
            (kv, pl.BlockSpec((count, PAIR), lambda i, h, *_: (0, base + h))),
            (kv, pl.BlockSpec((count, PAIR), lambda i, h, *_: (0, all_pairs + base + h))),
            (att, pair_rows),
            (datt, pair_rows),
            (inverses, pl.BlockSpec((1, 2, WIDE), lambda i, h, *_: (base + h, 0, i))),
            (probs, pl.BlockSpec((2, count, WIDE), lambda i, h, *_: (base + h, 0, i))),
        ],
        [
            ((rows, lanes), BF16, pl.BlockSpec((WIDE, PAIR), lambda i, h, *_: (i, h))),
            (half, BF16, whole(half)),
            (half, BF16, whole(half)),
        ],
        [pltpu.VMEM((lanes, count), BF16), pltpu.VMEM((count, 2 * lanes), F32)],
        cost(32 * rows * count * lanes, 20 * rows * lanes + 2 * rows * count),
    )


def self_backward(info, q, kv, att, dat, inverses, probs, splits, split):
    quarter = q.shape[0] // 2

    def stores(info_ref, acc, down_ref, dother_ref):
        for target, core in ((down_ref, info_ref[2]), (dother_ref, 1 - info_ref[2])):
            for part in range(2):
                begin = pl.multiple_of(place_of(info_ref, core, part) * quarter, quarter)
                target[part * quarter : (part + 1) * quarter, :] = acc[
                    pl.ds(begin, quarter), :
                ].astype(BF16)

    return attention_backward(
        "self_backward", info, q, kv, att, dat, inverses, probs, splits, split, stores
    )


def cross_backward(info, cq, ckv, catt, dca, inverses, probs, splits, split):
    count = ckv.shape[0]

    def stores(info_ref, acc, down_ref, dother_ref):
        down_ref[...] = acc[: count // 2, :].astype(BF16)
        dother_ref[...] = acc[count // 2 :, :].astype(BF16)

    return attention_backward(
        "cross_backward", info, cq, ckv, catt, dca, inverses, probs, splits, split, stores
    )


def feed(info, catt, second_in, dy, cout, weights, gains, packing):
    rows, width = catt.shape
    hidden = weights.hidden
    cout_count = len(cout.arrays)
    feed_count = len(weights.arrays)
    packed = packing.outputs(width * width + 2 * width * hidden)

    def body(info_ref, catt_ref, second_ref, dy_first, dy_last, gain_ref, *refs):
        cout_refs, refs = refs[:cout_count], refs[cout_count:]
        feed_refs, refs = refs[:feed_count], refs[feed_count:]
        (
            out_first,
            out_last,
            dthird_ref,
            dca_ref,
            ggain_ref,
            *packed_refs,
            acc_cout,
            acc_widen,
            acc_narrow,
            cout_scratch,
            widen_scratch,
            narrow_scratch,
        ) = refs
        cout_full = cout.load(info_ref, cout_refs, cout_scratch)
        widen_full, narrow_full = weights.load(info_ref, feed_refs, (widen_scratch, narrow_scratch))
        step = pl.program_id(0)

        @pl.when(step == 0)
        def _():
            acc_cout[...] = jnp.zeros_like(acc_cout)
            acc_widen[...] = jnp.zeros_like(acc_widen)
            acc_narrow[...] = jnp.zeros_like(acc_narrow)
            ggain_ref[...] = jnp.zeros_like(ggain_ref)

        catt = catt_ref[...]
        dy_low = dy.load(dy_first, dy_last)
        gain = gain_ref[5:6, :]
        third = second_ref[...] + dot(catt, cout_full[...])
        normed, scale = normalized(third)
        normed_low = (normed * gain).astype(BF16)
        pre = dot(normed_low, widen_full[...])
        below = 0.5 * (1.0 + lax.erf(pre * math.sqrt(0.5)))
        bell = jnp.exp(-0.5 * pre * pre) * (1.0 / math.sqrt(2.0 * math.pi))
        act = (pre * below).astype(BF16)
        store_half(
            (out_first, out_last), (third + dot(act, narrow_full[...])).astype(BF16)
        )
        dact = dot(dy_low, narrow_full[...], 1, 1)
        dpre = (dact * (below + pre * bell)).astype(BF16)
        acc_narrow[...] += dot(act, dy_low, 0, 0)
        acc_widen[...] += dot(normed_low, dpre, 0, 0)
        dnormed = dot(dpre, widen_full[...], 1, 1)
        ggain_ref[...] += jnp.sum(dnormed * normed, axis=0, keepdims=True)
        dthird = dy_low.astype(F32) + norm_backward(dnormed * gain, normed, scale)
        dthird_ref[...] = dthird
        dc = dthird.astype(BF16)
        dca_ref[...] = dot(dc, cout_full[...], 1, 1).astype(BF16)
        acc_cout[...] += dot(catt, dc, 0, 0)

        @pl.when(step == pl.num_programs(0) - 1)
        def _():
            packing.store(
                info_ref, packed_refs, (acc_cout, acc_widen, acc_narrow), unroll=True
            )

    return call(
        body,
        "feed",
        info,
        rows // BLOCK,
        [(catt, rows_of(width)), (second_in, rows_of(width))]
        + dy.inputs(BLOCK)
        + [(gains, whole(gains.shape))]
        + cout.inputs()
        + weights.inputs(),
        half_outputs(rows, width, BLOCK)
        + [
            ((rows, width), F32, rows_of(width)),
            ((rows, width), BF16, rows_of(width)),
            ((1, width), F32, whole((1, width))),
        ]
        + packed,
        [
            pltpu.VMEM((width, width), F32),
            pltpu.VMEM((width, hidden), F32),
            pltpu.VMEM((hidden, width), F32),
            cout.scratch(),
        ]
        + weights.scratch(),
        cost(
            12 * rows * width * hidden, 24 * rows * width + 8 * width * hidden, 2 * rows * hidden
        ),
    )


def sum_low(own_ref, got_ref):
    return (own_ref[...].astype(F32) + got_ref[...].astype(F32)).astype(BF16)


def middle_backward(
    info, dcqs, second_in, dthird, att, owns, gots, encoder, weights, gains, packing
):
    rows, width = second_in.shape
    count = len(dcqs)
    lanes = width // count
    packed = packing.outputs(4 * width * width)
    pieces = [len(w.arrays) for w in weights]
    short = encoder.shape[0] // (rows // BLOCK)

    def body(info_ref, att_ref, second_ref, dthird_ref, gain_ref, enc_first, enc_last, *refs):
        dcq_refs, refs = refs[:count], refs[count:]
        own_refs, refs = refs[:count], refs[count:]
        got_refs, refs = refs[:count], refs[count:]
        weight_refs = []
        for number in pieces:
            weight_refs.append(refs[:number])
            refs = refs[number:]
        dsecond_ref, dat_ref, ggain_ref, *genc_refs = refs[:5]
        refs = refs[5:]
        packed_refs, refs = refs[: len(packed)], refs[len(packed) :]
        acc_query, acc_out, acc_memory, *scratch = refs
        out_full, query_full, memory_full = [
            w.load(info_ref, r, s) for w, r, s in zip(weights, weight_refs, scratch)
        ]
        step = pl.program_id(0)

        @pl.when(step == 0)
        def _():
            acc_query[...] = jnp.zeros_like(acc_query)
            acc_out[...] = jnp.zeros_like(acc_out)
            acc_memory[...] = jnp.zeros_like(acc_memory)
            ggain_ref[...] = jnp.zeros_like(ggain_ref)

        dcq = jnp.concatenate([ref[...] for ref in dcq_refs], axis=1)
        gain = gain_ref[4:5, :]
        normed, scale = normalized(second_ref[...])
        normed_low = (normed * gain).astype(BF16)
        dnormed = dot(dcq, query_full[...], 1, 1)
        acc_query[...] += dot(normed_low, dcq, 0, 0)
        ggain_ref[...] += jnp.sum(dnormed * normed, axis=0, keepdims=True)
        dsecond = dthird_ref[...] + norm_backward(dnormed * gain, normed, scale)
        dsecond_ref[...] = dsecond
        da = dsecond.astype(BF16)
        dat_ref[...] = dot(da, out_full[...], 1, 1).astype(BF16)
        acc_out[...] += dot(att_ref[...], da, 0, 0)

        turned = encoder.load(enc_first, enc_last).T
        grads = [sum_low(own, got) for own, got in zip(own_refs, got_refs)]
        dckv = jnp.concatenate(
            [g[:, :lanes] for g in grads] + [g[:, lanes:] for g in grads], axis=1
        )
        store_half(genc_refs, dot(dckv, memory_full[...], 1, 1).astype(BF16))
        acc_memory[...] += dot(turned, dckv)

        @pl.when(step == pl.num_programs(0) - 1)
        def _():
            packing.store(info_ref, packed_refs, (acc_query, acc_out, acc_memory))

    return call(
        body,
        "middle_backward",
        info,
        rows // BLOCK,
        [
            (att, rows_of(width)),
            (second_in, rows_of(width)),
            (dthird, rows_of(width)),
            (gains, whole(gains.shape)),
        ]
        + encoder.inputs(short)
        + [(a, rows_of(lanes)) for a in dcqs]
        + [(a, rows_of(2 * lanes, short)) for a in owns]
        + [(a, rows_of(2 * lanes, short)) for a in gots]
        + [entry for w in weights for entry in w.inputs()],
        [
            ((rows, width), F32, rows_of(width)),
            ((rows, width), BF16, rows_of(width)),
            ((1, width), F32, whole((1, width))),
        ]
        + half_outputs(encoder.shape[0], width, short)
        + packed,
        [
            pltpu.VMEM((width, width), F32),
            pltpu.VMEM((width, width), F32),
            pltpu.VMEM((width, 2 * width), F32),
        ]
        + [w.scratch() for w in weights],
        cost(16 * rows * width * width, 20 * rows * width),
    )


VECTORS = 8


def project_backward(
    info, tokens, normed, dqs, owns, gots, dsecond, mods, ggains, embedded, gencs, weight, packing
):
    rows, width = tokens.shape
    count = len(dqs)
    lanes = width // count
    packed = packing.outputs(3 * width * width, VECTORS)
    sent = (rows // 2 + gencs[0].shape[0], width)
    pieces = len(weight.arrays)

    def body(info_ref, first_ref, last_ref, normed_ref, dsecond_ref, mod_ref, *refs):
        second_gain, third_gain, embedded_ref, *genc_refs = refs[:5]
        refs = refs[5:]
        dq_refs, refs = refs[:count], refs[count:]
        own_refs, refs = refs[:count], refs[count:]
        got_refs, refs = refs[:count], refs[count:]
        weight_refs, refs = refs[:pieces], refs[pieces:]
        gfirst_ref, glast_ref, vectors_ref, *packed_refs, acc, sums, scratch = refs
        full = weight.load(info_ref, weight_refs, scratch)
        step = pl.program_id(0)

        @pl.when(step == 0)
        def _():
            acc[...] = jnp.zeros_like(acc)
            sums[...] = jnp.zeros_like(sums)

        turned = normed_ref[...].T
        dkvs = [sum_low(own, got) for own, got in zip(own_refs, got_refs)]
        grads = jnp.concatenate(
            [ref[...] for ref in dq_refs]
            + [dkv[:, :lanes] for dkv in dkvs]
            + [dkv[:, lanes:] for dkv in dkvs],
            axis=1,
        )
        acc[...] += dot(turned, grads)
        dnormed = dot(grads, full[...], 1, 1)
        unit, scale = normalized(tokens.load(first_ref, last_ref).astype(F32))
        sums[0:1, :] += jnp.sum(dnormed * unit, axis=0, keepdims=True)
        sums[1:2, :] += jnp.sum(dnormed, axis=0, keepdims=True)
        gtokens = (
            dsecond_ref[...] + norm_backward(dnormed * mod_ref[0:1, :], unit, scale)
        ).astype(BF16)
        steps = rows // BLOCK // 2
        at = pl.ds(pl.multiple_of(lax.rem(step, steps) * BLOCK, BLOCK), BLOCK)
        for half, ref in enumerate((gfirst_ref, glast_ref)):

            @pl.when(step // steps == half)
            def _(half=half, ref=ref):
                ref[at, :] = gtokens
                ref[rows // 2 :, :] = genc_refs[half][...]

        @pl.when(step == pl.num_programs(0) - 1)
        def _():
            vectors = jnp.concatenate(
                [
                    sums[0:1, :] * mod_ref[2:3, :],
                    second_gain[...],
                    third_gain[...],
                    sums[0:1, :] * mod_ref[3:4, :],
                    sums[1:2, :],
                    embedded_ref[0:1, :].astype(F32),
                    jnp.zeros((VECTORS - 6, width), F32),
                ],
                axis=0,
            )
            vectors_ref[...] = vectors
            packing.store(info_ref, packed_refs, (acc,), vectors)

    return call(
        body,
        "project_backward",
        info,
        rows // BLOCK,
        tokens.inputs(BLOCK)
        + [
            (normed, rows_of(width)),
            (dsecond, rows_of(width)),
            (mods, whole(mods.shape)),
            (ggains[0], whole((1, width))),
            (ggains[1], whole((1, width))),
            (embedded, whole(embedded.shape)),
            (gencs[0], whole(gencs[0].shape)),
            (gencs[1], whole(gencs[1].shape)),
        ]
        + [(a, rows_of(lanes)) for a in dqs]
        + [(a, rows_of(2 * lanes)) for a in owns]
        + [(a, rows_of(2 * lanes)) for a in gots]
        + weight.inputs(),
        [(sent, BF16, whole(sent))] * 2
        + [((VECTORS, width), F32, whole((VECTORS, width)))]
        + packed,
        [pltpu.VMEM((width, 3 * width), F32), pltpu.VMEM((8, width), F32), weight.scratch()],
        cost(12 * rows * width * width, 20 * rows * width),
    )


def join_columns(info, parts):
    size = parts[0].shape[0] - VECTORS
    shape = (size + len(parts) * VECTORS, parts[0].shape[1])

    def body(info_ref, *refs):
        *part_refs, out_ref = refs
        total = part_refs[0][:size, :].astype(F32)
        for ref in part_refs[1:]:
            total = total + ref[:size, :].astype(F32)
        out_ref[:size, :] = total.astype(BF16)
        for index, ref in enumerate(part_refs):
            begin = size + index * VECTORS
            out_ref[begin : begin + VECTORS, :] = ref[size:, :]

    return call(
        body,
        "join_columns",
        info,
        1,
        [(part, whole(part.shape)) for part in parts],
        [(shape, BF16, whole(shape))],
        [],
        cost(0, 4 * size * shape[1]),
    )[0]


def in_seq_order(info, own, got, bit, out_ref, begin):
    rows = own.shape[0]
    own_place = (info[5] >> bit) % 2
    for part, place in ((own, own_place), (got, 1 - own_place)):
        at = pl.ds(pl.multiple_of(begin + place * rows, VECTORS), rows)
        out_ref[at, :] = part


def join_rows(info, own, got, size):
    count = own.shape[0] - size
    shape = (size + 2 * count, own.shape[1])

    def body(info_ref, own_ref, got_ref, out_ref):
        total = own_ref[:size, :].astype(F32) + got_ref[:size, :].astype(F32)
        out_ref[:size, :] = total.astype(BF16)
        in_seq_order(info_ref, own_ref[size:, :], got_ref[size:, :], 0, out_ref, size)

    return call(
        body,
        "join_rows",
        info,
        1,
        [(own, whole(own.shape)), (got, whole(got.shape))],
        [(shape, BF16, whole(shape))],
        [],
        cost(0, 6 * size * shape[1]),
    )[0]


def finish(info, own, got, size, shard):
    width = own.shape[1]
    count = own.shape[0] - size
    devices = 2 * count // VECTORS

    def body(info_ref, own_ref, got_ref, ginput_ref, gtime_ref, ggains_ref, listed, turned):
        for block in range(size // shard):
            rows = slice(block * shard, (block + 1) * shard)
            ginput_ref[:, block * width : (block + 1) * width] = own_ref[rows, :].astype(
                F32
            ) + got_ref[rows, :].astype(F32)
        in_seq_order(info_ref, own_ref[size:, :], got_ref[size:, :], 1, listed, 0)
        vectors = listed[...]
        column = lax.broadcasted_iota(jnp.int32, (devices, 2 * count), 1)
        row = lax.broadcasted_iota(jnp.int32, (devices, 2 * count), 0)

        def pick(kind):
            chosen = jnp.where(column == row * VECTORS + kind, 1.0, 0.0).astype(BF16)
            return dot(chosen, vectors)

        chosen = jnp.where(lax.rem(column, VECTORS) == row, 1.0, 0.0).astype(BF16)
        turned[...] = jnp.concatenate([0.5 * pick(5), dot(chosen, vectors)], axis=0).T
        place = (2 * info_ref[4] + info_ref[2]) * shard
        part = turned[pl.ds(pl.multiple_of(place, shard), shard), :]
        grads = jnp.concatenate([pick(3), pick(4)], axis=1).astype(BF16)
        gtime_ref[...] = dot(part[:, :devices].astype(BF16), grads)
        ggains_ref[...] = part.T[devices : devices + 3, :]

    return call(
        body,
        "finish",
        info,
        1,
        [(own, whole(own.shape)), (got, whole(got.shape))],
        [
            ((shard, 3 * width), F32, whole((shard, 3 * width))),
            ((shard, 2 * width), F32, whole((shard, 2 * width))),
            ((3, shard), F32, whole((3, shard))),
        ],
        [pltpu.VMEM((2 * count, width), BF16), pltpu.VMEM((width, 2 * devices), F32)],
        cost(4 * devices * count * width, 8 * size * width),
    )


def permutations(seq_count, fsdp_count):
    columns = fsdp_count // 2

    def at(seq, fsdp):
        return seq * fsdp_count + fsdp

    def pairs(move):
        return [
            (at(seq, fsdp), at(*move(seq, fsdp)))
            for seq in range(seq_count)
            for fsdp in range(fsdp_count)
        ]

    def home(turn):
        def move(seq, fsdp):
            y, x = divmod(seq, 2)
            column, core = divmod(fsdp, 2)
            return 2 * core + (x ^ turn), 2 * column + y

        return move

    shift = {
        r: pairs(lambda seq, fsdp, r=r: (seq, (fsdp + 2 * r) % fsdp_count))
        for r in range(1, columns)
    }
    cross = {t: pairs(lambda seq, fsdp, t=t: (seq ^ t, fsdp)) for t in range(1, seq_count)}
    swap = pairs(lambda seq, fsdp: (seq, fsdp ^ 1))
    return pairs(home(0)), pairs(home(1)), swap, shift, cross


def reverse(pairs):
    return [(target, source) for source, target in pairs]


def after(values, signal):
    return lax.optimization_barrier((values, signal))[0]


class Direct:
    def __init__(self, perms, seq, fsdp, columns):
        self.same, self.crossed, self.swap_pairs, self.shifts, self.crosses = perms
        self.seq = seq
        self.core = fsdp % 2
        self.z = fsdp // 2
        self.columns = columns

    def permute(self, values, pairs):
        return lax.ppermute(values, AXES, pairs)

    def swap(self, values):
        return self.permute(values, self.swap_pairs)

    def along_z(self, values):
        return [values] + [
            self.permute(values, self.shifts[r]) for r in range(1, self.columns)
        ]

    def both_cores(self, pieces):
        return pieces + [self.swap(piece) for piece in pieces]

    def core_sum(self, mine, away, signal=()):
        got = after(self.swap(away), signal)
        return [
            (mine[r].astype(F32) + got[r].astype(F32)).astype(BF16) for r in range(self.columns)
        ]

    def z_parts(self, shards):
        return [self.permute(shards[r], self.shifts[r]) for r in range(1, self.columns)]

    def z_sum(self, shards, got, signal=()):
        total = shards[0].astype(F32)
        for part in after(got, signal):
            total = total + part.astype(F32)
        return lax.optimization_barrier(total.astype(BF16))

    def add(self, first, second):
        return lax.optimization_barrier((first.astype(F32) + second.astype(F32)).astype(BF16))

    def cross(self, values, turn):
        return self.permute(values, self.crosses[turn])


SPLITS = 2


def time_embedding(step_values, model_width):
    half_width = model_width // 2
    frequency = jnp.exp(-math.log(10000.0) * jnp.arange(half_width, dtype=F32) / half_width)
    angles = step_values.astype(F32)[:, None] * frequency[None, :]
    return jnp.concatenate([jnp.sin(angles), jnp.cos(angles)], axis=-1).astype(BF16)


def exact_dot(left, right):
    return lax.dot_general(
        left,
        right,
        (((0,), (0,)), ((), ())),
        precision=lax.Precision.HIGHEST,
        preferred_element_type=F32,
    )


def make(seq_count, fsdp_count):
    perms = permutations(seq_count, fsdp_count)
    same, crossed = perms[:2]
    columns = fsdp_count // 2

    def on_device(
        tokens,
        encoder_states,
        lengths,
        timesteps,
        time_weight,
        self_input,
        self_output,
        cross_query,
        cross_memory,
        cross_output,
        widen_weight,
        narrow_weight,
        norm_gains,
        cotangent,
    ):
        width = tokens.shape[2]
        hidden = widen_weight.shape[1]
        shard = time_weight.shape[0]
        seq = lax.axis_index("seq")
        fsdp = lax.axis_index("fsdp")
        core = fsdp % 2
        side = seq % 2
        direct = Direct(perms, seq, fsdp, columns) if columns == 4 else None

        def send_work(values):
            mine = lax.dynamic_index_in_dim(values, side, 0, keepdims=False)
            others = lax.dynamic_index_in_dim(values, 1 - side, 0, keepdims=False)
            return [lax.ppermute(mine, AXES, same), lax.ppermute(others, AXES, crossed)]

        def send_home(halves):
            return [
                lax.ppermute(halves[0], AXES, reverse(same)),
                lax.ppermute(halves[1], AXES, reverse(crossed)),
            ]

        def at_home(parts, kind):
            first = jnp.where(side == 0, parts[0], parts[1])
            second = jnp.where(side == 0, parts[1], parts[0])
            return jnp.stack([first, second], axis=0).astype(kind)

        def gather(weight, axis=0):
            return lax.all_gather(weight, "fsdp", axis=axis, tiled=True)

        def swap(values):
            return lax.ppermute(values, AXES, perms[2])

        packing = Packing(fsdp_count, direct is not None, width)
        token_rows, encoder_rows = tokens.shape[1], encoder_states.shape[1]
        numbers = jnp.concatenate([lengths, timesteps[:, None]], axis=1)
        numbers_other = swap(numbers)
        own_row = jnp.where(core == seq // 2, numbers, numbers_other)
        own_row = lax.dynamic_slice_in_dim(own_row, side, 1, 0)
        step_value = own_row[0, 3:4]
        place = lax.broadcasted_iota(jnp.int32, (8,), 0)
        info = jnp.where(place == 1, own_row[0, 1], 0) + jnp.where(place <= 1, own_row[0, 0], 0)
        for index, value in enumerate((core, side, fsdp // 2, seq)):
            info = jnp.where(place == index + 2, value, info)
        embedded = jnp.pad(time_embedding(step_value, width), ((0, 15), (0, 0)))

        turned = jnp.pad(norm_gains.T, ((0, 0), (0, 128 - norm_gains.shape[0])))
        first = jnp.concatenate([self_input, time_weight, turned], axis=1)
        first_mine = direct.along_z(first) if direct else [(), ()]
        own = send_work(jnp.concatenate([tokens, encoder_states], axis=1))
        other = [swap(part) for part in after(own, first_mine[1:])]
        work_tokens = Halves(own, 0, token_rows)
        other_tokens = Halves(other, 0, token_rows)
        work_encoder = Halves(own, token_rows, encoder_rows)
        other_encoder = Halves(other, token_rows, encoder_rows)

        ready = info
        if direct:
            first = direct.both_cores(first_mine)
            rest = jnp.concatenate([self_output, cross_query, cross_memory, cross_output], axis=1)
            wide = widen_weight.reshape(shard, hidden // width, width).transpose(1, 0, 2)
            large = jnp.concatenate([wide.reshape(-1, width), narrow_weight], axis=0)
            rest, large = after((rest, large), (own, info, embedded))
            rest_mine = direct.along_z(rest)
            small_other = [swap(rest)]
            large_mine = direct.along_z(large)
            large_other = [swap(large)]
            ready = after(info, (small_other, large_other))
            input_weight = Weight(first, 0, 3 * width)
            time_full = Weight(first, 3 * width, 2 * width)
            turned_gains = Weight(first, 5 * width, 128)
        else:
            input_weight = Weight([gather(self_input)], 0, 3 * width)
            time_full = Weight([gather(time_weight)], 0, 2 * width)
            turned_gains = Weight([gather(turned)], 0, 128)
            output_weight = Weight([gather(self_output)], 0, width)
            query_weight = Weight([gather(cross_query)], 0, width)
            memory_weight = Weight([gather(cross_memory)], 0, 2 * width)
            cout_weight = Weight([gather(cross_output)], 0, width)
            feed_weights = FeedWeights([gather(widen_weight), gather(narrow_weight)], hidden)

        mods, q, kv, normed_first, att, inverses, probs = self_forward(
            ready, work_tokens, other_tokens, embedded, time_full, turned_gains, input_weight
        )
        ready = info
        if direct:
            rest_mine[1:], large_mine[:2] = after((rest_mine[1:], large_mine[:2]), att)
            small_other += [swap(part) for part in rest_mine[1:]]
            rest = rest_mine + small_other
            large_other.append(swap(large_mine[1]))
            ready = after(info, large_other)
            output_weight = Weight(rest, 0, width)
            query_weight = Weight(rest, width, width)
            memory_weight = Weight(rest, 2 * width, 2 * width)
            cout_weight = Weight(rest, 4 * width, width)
        dy_parts = send_work(after(cotangent, att))
        second_in, cq, ckv, catt, cross_inverses, cross_probs = cross_forward(
            ready,
            att,
            work_tokens,
            work_encoder,
            other_encoder,
            output_weight,
            mods,
            query_weight,
            memory_weight,
        )
        work_dy = Halves(after(dy_parts, catt), 0, token_rows)
        if direct:
            large_mine[2:] = after(large_mine[2:], catt)
            large_other += [swap(part) for part in large_mine[2:]]
            feed_weights = FeedWeights(large_mine + large_other, hidden)
        out_first, out_last, dthird, dca, ggain_third, *packed_feed = feed(
            info, catt, second_in, work_dy, cout_weight, feed_weights, mods, packing
        )
        layer_out = (out_first, out_last)
        out_parts = send_home(layer_out)

        def backward_cross(split, ready):
            return cross_backward(
                ready, cq, ckv, catt, dca, cross_inverses, cross_probs, SPLITS, split
            )

        def backward_self(split, ready):
            return self_backward(ready, q, kv, att, dat, inverses, probs, SPLITS, split)

        crosses = [backward_cross(0, info)]
        out_parts = after(out_parts, crosses[0][0])
        chip_feed = direct.core_sum(*packed_feed, crosses[0][0]) if direct else ()
        crosses.append(backward_cross(1, after(info, (chip_feed, out_parts))))
        dcqs, dckvs, dckv_others = zip(*crosses)
        dckv_gots = [swap(a) for a in dckv_others]
        feed_parts = direct.z_parts(chip_feed) if direct else [()]
        dsecond, dat, ggain_second, *genc = middle_backward(
            after(info, (feed_parts[0], dcqs)),
            dcqs,
            second_in,
            dthird,
            att,
            dckvs,
            dckv_gots,
            work_encoder,
            (output_weight, query_weight, memory_weight),
            mods,
            packing,
        )
        genc, packed_middle = genc[:2], genc[2:]
        selfs = [backward_self(0, after(info, packed_middle))]
        if direct:
            column_feed = direct.z_sum(chip_feed, feed_parts, selfs[0][0])
            chip_middle = direct.core_sum(*packed_middle, selfs[0][0])
            selfs.append(backward_self(1, after(info, (column_feed, chip_middle))))
            middle_parts = after(direct.z_parts(chip_middle), selfs[1][0])
            row_feed = after(direct.cross(column_feed, 1), selfs[1][0])
            row_feed = direct.add(column_feed, row_feed)
            column_middle = direct.z_sum(chip_middle, middle_parts)
        else:
            selfs.append(backward_self(1, info))
        dqs, dkvs, dkv_others = zip(*selfs)
        dkv_others = list(dkv_others)
        if direct:
            dkv_others[1] = after(dkv_others[1], (column_middle, row_feed))
        dkv_gots = [swap(a) for a in dkv_others]
        first_grad, last_grad, vectors, *packed_input = project_backward(
            info,
            work_tokens,
            normed_first,
            dqs,
            dkvs,
            dkv_gots,
            dsecond,
            mods,
            (ggain_second, ggain_third),
            embedded,
            genc,
            input_weight,
            packing,
        )
        gtokens = (first_grad, last_grad)
        if direct:
            got_row = after(direct.cross(row_feed, 2), gtokens)
            row_middle = after(direct.cross(column_middle, 1), gtokens)
            away = after(packed_input[1], (got_row, row_middle))
            chip = direct.core_sum(packed_input[0], away)
            row_middle = direct.add(column_middle, row_middle)
            gots = direct.z_parts(chip)
            token_parts = after(send_home(after(gtokens, chip)), gots)
            ready = after(info, token_parts)
            reduced_feed = row_feed.astype(F32) + got_row.astype(F32)
            size = chip[0].shape[0] - VECTORS
            joined = join_columns(ready, [chip[0]] + gots)
            got = direct.cross(joined, 1)
            got_row = direct.cross(after(row_middle, joined), 2)
            joined = join_rows(info, joined, got, size)
            got = direct.cross(joined, 2)
            reduced_middle = row_middle.astype(F32) + got_row.astype(F32)
            reduced_input, gtime, ggains = finish(info, joined, got, size, shard)
        else:

            def reduce(packed):
                part = lax.psum_scatter(packed[0], "fsdp", scatter_dimension=0, tiled=True)
                return lax.psum(part[0], "seq").astype(F32)

            reduced_input = reduce(packed_input)
            reduced_input = unpack_rows(reduced_input, 0, shard, 3 * width)
            reduced_middle = reduce(packed_middle)
            reduced_feed = reduce(packed_feed)
            token_parts = send_home(gtokens)
            ggains = lax.psum(vectors[:3], AXES)
            ggains = lax.dynamic_slice_in_dim(ggains, fsdp * shard, shard, 1)
            by_group = lax.all_gather(vectors[3:5], AXES, axis=0)
            by_group = by_group.reshape(seq_count, columns, 2, 2 * width).sum(axis=2)
            by_group = by_group.transpose(1, 0, 2).reshape(-1, 2 * width)
            every = time_embedding(gather(timesteps), width)
            own_columns = lax.dynamic_slice_in_dim(every, fsdp * shard, shard, 1)
            gtime = exact_dot(own_columns.astype(F32), by_group)

        tall = narrow_weight.shape[0]
        return (
            at_home(out_parts, BF16),
            at_home([part[:token_rows] for part in token_parts], F32),
            at_home([part[token_rows:] for part in token_parts], F32),
            gtime,
            reduced_input,
            unpack_rows(reduced_middle, shard, shard, width),
            unpack_rows(reduced_middle, 0, shard, width),
            unpack_rows(reduced_middle, 2 * shard, shard, 2 * width),
            unpack_rows(reduced_feed, 0, shard, width),
            unpack_rows(reduced_feed, shard, shard, hidden),
            unpack_rows(reduced_feed, shard * (1 + hidden // width), tall, width),
            ggains,
        )

    return on_device


def solution(mesh):
    rows = P("fsdp", "seq", None)
    weight = P("fsdp", None)
    in_specs = (rows, rows, P("fsdp", None), P("fsdp")) + (weight,) * 8 + (P(None, "fsdp"), rows)
    out_specs = (rows,) * 3 + (weight,) * 8 + (P(None, "fsdp"),)
    return jax.shard_map(
        make(mesh.shape["seq"], mesh.shape["fsdp"]),
        mesh=mesh,
        in_specs=in_specs,
        out_specs=out_specs,
        check_vma=False,
    )
```

```python
import math

import jax
import jax.numpy as jnp
from jax import lax
from jax.experimental import pallas as pl
from jax.experimental.pallas import tpu as pltpu
from jax.sharding import PartitionSpec as P


HEAD_DIM = 64
PAIR = 2 * HEAD_DIM
EPS = 1e-05
NEG = -1e30
F32 = jnp.float32
BF16 = jnp.bfloat16
AXES = ("seq", "fsdp")
VMEM_LIMIT = 60 * 2**20
BLOCK = 256
WIDE = 512


def dot(left, right, left_dim=1, right_dim=0):
    return lax.dot_general(
        left, right, (((left_dim,), (right_dim,)), ((), ())), preferred_element_type=F32
    )


def whole(shape):
    return pl.BlockSpec(shape, lambda *_: (0,) * len(shape))


def rows_of(width, block=BLOCK):
    return pl.BlockSpec((block, width), lambda i, *_: (i, 0))


def params():
    return pltpu.CompilerParams(vmem_limit_bytes=VMEM_LIMIT)


def cost(flops, moved, transcendentals=0):
    return pl.CostEstimate(
        flops=int(flops), bytes_accessed=int(moved), transcendentals=int(transcendentals)
    )


def normalized(values):
    average = jnp.mean(values, axis=-1, keepdims=True)
    centred = values - average
    spread = jnp.mean(centred * centred, axis=-1, keepdims=True)
    scale = lax.rsqrt(spread + EPS)
    return centred * scale, scale


def norm_backward(upstream, normed, scale):
    mean_up = jnp.mean(upstream, axis=-1, keepdims=True)
    mean_both = jnp.mean(upstream * normed, axis=-1, keepdims=True)
    return (upstream - mean_up - normed * mean_both) * scale


def lane_is(part):
    lane = lax.broadcasted_iota(jnp.int32, (1, PAIR), 1)
    return lane < HEAD_DIM if part == 0 else lane >= HEAD_DIM


def half_of(values, part):
    return jnp.where(lane_is(part), values, jnp.zeros_like(values))


def pair_at(index):
    return pl.ds(pl.multiple_of(index * PAIR, PAIR), PAIR)


def first_step(dims=1):
    first = pl.program_id(0) == 0
    return first if dims == 1 else first & (pl.program_id(1) == 0)


class Weight:
    def __init__(self, pieces, start, width):
        self.arrays = pieces
        self.start = start
        self.width = width

    @property
    def split(self):
        return len(self.arrays) > 1

    @property
    def rows(self):
        return len(self.arrays) * self.arrays[0].shape[0]

    @property
    def aligned(self):
        return self.start % self.width == 0

    def inputs(self):
        if not self.aligned:
            return [(array, whole(array.shape)) for array in self.arrays]
        place = self.start // self.width
        shape = (self.arrays[0].shape[0], self.width)
        return [(array, pl.BlockSpec(shape, lambda *_: (0, place))) for array in self.arrays]

    def scratch(self):
        return pltpu.VMEM((self.rows, self.width) if self.split else (16, 128), BF16)

    def load(self, info, refs, scratch, dims=1):
        if not self.split:
            return refs[0]
        columns = slice(0, self.width) if self.aligned else slice(self.start, self.start + self.width)

        @pl.when(first_step(dims))
        def _():
            count = len(refs) // 2
            shard = refs[0].shape[0]
            for index, ref in enumerate(refs):
                turn, shift = divmod(index, count)
                core = info[2] if turn == 0 else 1 - info[2]
                owner = lax.rem(info[4] - shift + count, count)
                start = pl.multiple_of((2 * owner + core) * shard, shard)
                scratch[pl.ds(start, shard), :] = ref[:, columns]

        return scratch


class Halves:
    def __init__(self, arrays, start, rows):
        self.arrays = arrays
        self.start = start
        self.rows = rows
        self.shape = (2 * rows, arrays[0].shape[1])

    def inputs(self, block):
        width = self.shape[1]
        count = self.rows // block
        base = self.start // block
        return [
            (
                self.arrays[0],
                pl.BlockSpec((block, width), lambda i, *_: (base + jnp.minimum(i, count - 1), 0)),
            ),
            (
                self.arrays[1],
                pl.BlockSpec((block, width), lambda i, *_: (base + jnp.maximum(i - count, 0), 0)),
            ),
        ]

    def resident(self):
        place = self.start // self.rows
        spec = pl.BlockSpec((self.rows, self.shape[1]), lambda *_: (place, 0))
        return [(array, spec) for array in self.arrays]

    def load(self, first_ref, second_ref):
        half = pl.num_programs(0) // 2
        return jnp.where(pl.program_id(0) < half, first_ref[...], second_ref[...])


def half_outputs(rows, width, block):
    count = rows // block // 2
    half = (rows // 2, width)
    return [
        (half, BF16, pl.BlockSpec((block, width), lambda i, *_: (jnp.minimum(i, count - 1), 0))),
        (half, BF16, pl.BlockSpec((block, width), lambda i, *_: (jnp.maximum(i - count, 0), 0))),
    ]


def store_half(refs, value):
    first = pl.program_id(0) < pl.num_programs(0) // 2

    @pl.when(first)
    def _():
        refs[0][...] = value

    @pl.when(jnp.logical_not(first))
    def _():
        refs[1][...] = value


class FeedWeights:
    def __init__(self, arrays, hidden):
        self.arrays = arrays
        self.hidden = hidden

    @property
    def split(self):
        return len(self.arrays) > 2

    def inputs(self):
        return [(array, whole(array.shape)) for array in self.arrays]

    def scratch(self):
        if not self.split:
            return [pltpu.VMEM((16, 128), BF16)] * 2
        width = self.arrays[0].shape[1]
        return [pltpu.VMEM((width, self.hidden), BF16), pltpu.VMEM((self.hidden, width), BF16)]

    def load(self, info, refs, scratch):
        if not self.split:
            return refs
        widen, narrow = scratch

        @pl.when(pl.program_id(0) == 0)
        def _():
            count = len(refs) // 2
            rows, width = refs[0].shape
            blocks = self.hidden // width
            tall = rows // 2
            short = tall // blocks
            for index, ref in enumerate(refs):
                turn, shift = divmod(index, count)
                core = info[2] if turn == 0 else 1 - info[2]
                owner = 2 * lax.rem(info[4] - shift + count, count) + core
                start = pl.multiple_of(owner * short, short)
                for block in range(blocks):
                    widen[pl.ds(start, short), block * width : (block + 1) * width] = ref[
                        block * short : (block + 1) * short, :
                    ]
                start = pl.multiple_of(owner * tall, tall)
                narrow[pl.ds(start, tall), :] = ref[tall:, :]

        return widen, narrow


class Packing:
    def __init__(self, shards, direct, width):
        self.shards = shards
        self.direct = direct
        self.width = width

    def outputs(self, elements, extra=0):
        rows = elements // (self.shards * self.width)
        if self.direct:
            rows += extra
        if self.direct:
            shape = (self.shards // 2, rows, self.width)
            return [(shape, BF16, whole(shape))] * 2
        shape = (self.shards, rows, self.width)
        return [(shape, BF16, whole(shape))]

    def store(self, info, packed, grads, vectors=None, unroll=False):
        def put(ref, slot, owner):
            offset = 0
            for grad in grads:
                rows = grad.shape[0] // self.shards
                start = owner * rows
                if not isinstance(owner, int):
                    start = pl.multiple_of(start, rows)
                for block in range(grad.shape[1] // self.width):
                    columns = slice(block * self.width, (block + 1) * self.width)
                    ref[slot, offset : offset + rows, :] = grad[pl.ds(start, rows), columns].astype(
                        BF16
                    )
                    offset += rows
            if vectors is not None and self.direct:
                ref[slot, offset:, :] = vectors.astype(BF16)

        if self.direct:
            count = self.shards // 2
            for ref, core in ((packed[0], info[2]), (packed[1], 1 - info[2])):

                def one(shift, carry, ref=ref, core=core):
                    put(ref, shift, 2 * lax.rem(info[4] + shift, count) + core)
                    return carry

                if unroll:
                    for shift in range(count):
                        one(shift, 0)
                else:
                    lax.fori_loop(0, count, one, 0)
        else:
            for shard in range(self.shards):
                put(packed[0], shard, shard)


def unpack_rows(packed, offset, rows, columns):
    width = packed.shape[1]
    blocks = columns // width
    parts = [packed[offset + b * rows : offset + (b + 1) * rows] for b in range(blocks)]
    return jnp.concatenate(parts, axis=1) if blocks > 1 else parts[0]


def call(body, name, info, grid, inputs, outputs, scratch, estimate):
    return pl.pallas_call(
        body,
        name=name,
        grid_spec=pltpu.PrefetchScalarGridSpec(
            num_scalar_prefetch=1,
            grid=grid if isinstance(grid, tuple) else (grid,),
            in_specs=[spec for _, spec in inputs],
            out_specs=[spec for _, _, spec in outputs],
            scratch_shapes=scratch,
        ),
        out_shape=[jax.ShapeDtypeStruct(shape, kind) for shape, kind, _ in outputs],
        compiler_params=params(),
        cost_estimate=estimate,
    )(info, *[array for array, _ in inputs])


def block_start(info, block_index, block, quarter):
    per_quarter = quarter // block
    first = block_index < per_quarter
    place = jnp.where(first, info[3], 1 - info[3])
    return (2 * info[2] + place) * quarter + lax.rem(block_index, per_quarter) * block


def forbidden(info, start, block, half, queries_dim):
    keys_dim = 1 - queries_dim
    qshape = [1, 1]
    qshape[queries_dim] = block
    kshape = [1, 1]
    kshape[keys_dim] = half
    qpos = start + lax.broadcasted_iota(jnp.int32, tuple(qshape), queries_dim)
    kpos = half + lax.broadcasted_iota(jnp.int32, tuple(kshape), keys_dim)
    first, second = info[0], info[1]
    low = jnp.where((qpos >= first) & (qpos < second), second, first)
    high = jnp.where(qpos >= second, second, 2 * half)
    return jnp.where((kpos >= low) & (kpos < high), NEG, 0.0)


def key_specs(array, lanes, split, width):
    rows = array.shape[0]
    count = width // lanes
    return [
        (array, pl.BlockSpec((rows, lanes), lambda *_: (0, split))),
        (array, pl.BlockSpec((rows, lanes), lambda *_: (0, count + split))),
    ]


def attention_sums(low, high):
    return (low > 1e-20) & (high < 1e30)


def attend_pair(qq, keys_at, turned_values, free, bias, att_ref, inverse_ref, probs_ref):
    count = probs_ref.shape[1]
    row_head = lax.broadcasted_iota(jnp.int32, (PAIR, 1), 0) // HEAD_DIM
    lane_head = lax.broadcasted_iota(jnp.int32, (1, PAIR), 1) // HEAD_DIM
    turned_at = turned_values(slice(0, count))

    def head(part):
        qe = jnp.where(lane_head == part, qq, jnp.zeros_like(qq))
        total = None
        out = None
        for piece in (slice(0, free), slice(free, count)):
            if piece.start == piece.stop:
                continue
            s = dot(keys_at(piece), qe, 1, 1)
            p = jnp.exp(s if piece.start == 0 else s + bias[...])
            low = p.astype(BF16)
            probs_ref[part, piece, :] = low
            term = jnp.sum(p, axis=0, keepdims=True)
            attended = dot(turned_at[:, piece], low)
            total = term if total is None else total + term
            out = attended if out is None else out + attended
        return out, total

    def one(part, carry):
        out, total = head(part)
        inverse = 1.0 / total
        inverse_ref[0, pl.ds(part, 1), :] = inverse
        joined, low, high = carry
        joined = joined + jnp.where(row_head == part, out * inverse, 0.0)
        return joined, jnp.minimum(low, total), jnp.maximum(high, total)

    ones = jnp.ones((1, qq.shape[0]), F32)
    out, low, high = lax.fori_loop(0, 2, one, (jnp.zeros((PAIR, qq.shape[0]), F32), ones, ones))
    att_ref[...] = out.T.astype(BF16)
    low, high = jnp.min(low), jnp.max(high)

    @pl.when(jnp.logical_not((low > 1e-20) & (high < 1e30)))
    def _():
        chunk = BLOCK // 2
        queries = qq.shape[0]

        def again(part, carry):
            qe = jnp.where(lane_head == part, qq, jnp.zeros_like(qq))

            def scores(index):
                at = pl.ds(pl.multiple_of(index * chunk, chunk), chunk)
                s = dot(keys_at(at), qe, 1, 1)
                if free == count:
                    return at, s
                begin = jnp.maximum(index * chunk - free, 0)
                part_bias = bias[pl.ds(pl.multiple_of(begin, chunk), chunk), :]
                return at, s + jnp.where(index * chunk >= free, part_bias, 0.0)

            def largest(index, top):
                return jnp.maximum(top, jnp.max(scores(index)[1], axis=0, keepdims=True))

            top = lax.fori_loop(
                0, count // chunk, largest, jnp.full((1, queries), -jnp.inf, F32)
            )

            def add(index, sums):
                at, s = scores(index)
                p = jnp.exp(s - top)
                low = p.astype(BF16)
                probs_ref[part, at, :] = low
                return (
                    sums[0] + jnp.sum(p, axis=0, keepdims=True),
                    sums[1] + dot(turned_values(at), low),
                )

            total, out = lax.fori_loop(
                0,
                count // chunk,
                add,
                (jnp.zeros((1, queries), F32), jnp.zeros((PAIR, queries), F32)),
            )
            inverse = 1.0 / total
            inverse_ref[0, pl.ds(part, 1), :] = inverse
            return carry + jnp.where(row_head == part, out * inverse, 0.0)

        out = lax.fori_loop(0, 2, again, jnp.zeros((PAIR, queries), F32))
        att_ref[...] = out.T.astype(BF16)


def attention_outputs(rows, width, count):
    pairs = width // PAIR
    return [
        ((rows, width), BF16, pl.BlockSpec((WIDE, PAIR), lambda i, h, *_: (i, h))),
        ((pairs, 2, rows), F32, pl.BlockSpec((1, 2, WIDE), lambda i, h, *_: (h, 0, i))),
        ((2 * pairs, count, rows), BF16, pl.BlockSpec((2, count, WIDE), lambda i, h, *_: (h, 0, i))),
    ]


def place_of(info, core, part):
    return 2 * core + (info[3] if part == 0 else 1 - info[3])


def self_forward(info, own, other, embedded, weight):
    rows, width = own.shape
    pairs = width // PAIR
    quarter = rows // 2
    pieces = len(weight.arrays)

    def body(info_ref, embedded_ref, *refs):
        token_refs, refs = refs[:4], refs[4:]
        weight_refs, refs = refs[:pieces], refs[pieces:]
        (
            mod_ref,
            q_out,
            kv_out,
            normed_out,
            att_ref,
            inverse_ref,
            probs_ref,
            queries,
            keys,
            normed,
            turned_values,
            staged,
            bias,
            scratch,
            sems,
        ) = refs
        step = pl.program_id(0)
        index = pl.program_id(1)
        full = weight.load(info_ref, weight_refs, scratch, 2)
        time_at = slice(3 * width, 5 * width)
        copies = [
            pltpu.make_async_copy(queries, q_out, sems.at[0]),
            pltpu.make_async_copy(keys, kv_out, sems.at[1]),
            pltpu.make_async_copy(normed, normed_out, sems.at[2]),
        ]

        @pl.when(first_step(2))
        def _():
            modulation = dot(embedded_ref[...], full[:, time_at])
            gains = full[:, 5 * width :].astype(F32).T[:3, :]
            plus = 1.0 + modulation[0:1, :width]
            shift = modulation[0:1, width:]
            mod_ref[...] = jnp.concatenate(
                [gains[0:1] * plus, shift, plus, gains, jnp.zeros((2, width), F32)], axis=0
            )
            for number, ref in enumerate(token_refs):
                turn, part = divmod(number, 2)
                holder = info_ref[2] if turn == 0 else 1 - info_ref[2]
                begin = place_of(info_ref, holder, part) * quarter
                staged[pl.ds(pl.multiple_of(begin, quarter), quarter), :] = ref[...]

            def project(block, carry):
                at = pl.ds(pl.multiple_of(block * BLOCK, BLOCK), BLOCK)
                unit, _ = normalized(staged[at, :].astype(F32))
                first = (unit * mod_ref[0:1, :] + mod_ref[1:2, :]).astype(BF16)
                keys[at, :] = dot(first, full[:, width : 3 * width]).astype(BF16)
                per_quarter = quarter // BLOCK
                place = block // per_quarter

                @pl.when(place // 2 == info_ref[2])
                def _():
                    part = lax.bitwise_xor(lax.rem(place, 2), info_ref[3])
                    begin = part * quarter + lax.rem(block, per_quarter) * BLOCK
                    here = pl.ds(pl.multiple_of(begin, BLOCK), BLOCK)
                    normed[here, :] = first
                    queries[here, :] = (dot(first, full[:, :width]) * HEAD_DIM**-0.5).astype(BF16)

                return carry

            lax.fori_loop(0, 2 * rows // BLOCK, project, 0)
            for copy in copies:
                copy.start()

            turned_values[...] = keys[:, width:].T

        @pl.when(index == 0)
        def _():
            start = block_start(info_ref, step, WIDE, quarter)
            bias[...] = forbidden(info_ref, start, WIDE, rows, 1)

        mine = pl.ds(pl.multiple_of(step * WIDE, WIDE), WIDE)
        at = pair_at(index)
        attend_pair(
            queries[mine, at],
            lambda piece: keys[piece, at],
            lambda piece: turned_values[at, piece],
            rows,
            bias,
            att_ref,
            inverse_ref,
            probs_ref,
        )

        @pl.when((step == pl.num_programs(0) - 1) & (index == pairs - 1))
        def _():
            for copy in copies:
                copy.wait()

    anywhere = pl.BlockSpec(memory_space=pl.ANY)
    return call(
        body,
        "self_forward",
        info,
        (rows // WIDE, pairs),
        [(embedded, whole(embedded.shape))]
        + own.resident()
        + other.resident()
        + weight.inputs(),
        [
            ((8, width), F32, whole((8, width))),
            ((rows, width), BF16, anywhere),
            ((2 * rows, 2 * width), BF16, anywhere),
            ((rows, width), BF16, anywhere),
        ]
        + attention_outputs(rows, width, 2 * rows),
        [
            pltpu.VMEM((rows, width), BF16),
            pltpu.VMEM((2 * rows, 2 * width), BF16),
            pltpu.VMEM((rows, width), BF16),
            pltpu.VMEM((width, 2 * rows), BF16),
            pltpu.VMEM((2 * rows, width), BF16),
            pltpu.VMEM((rows, WIDE), F32),
            weight.scratch(),
            pltpu.SemaphoreType.DMA((3,)),
        ],
        cost(32 * rows * rows * width, 12 * rows * width, 2 * rows * rows * width // HEAD_DIM),
    )


def cross_forward(info, att, tokens, own, other, weight, gains):
    rows, width = att.shape
    pairs = width // PAIR
    count = own.rows
    pieces = len(weight.arrays)

    def body(info_ref, att_ref, first_ref, last_ref, gain_ref, *refs):
        enc_refs, refs = refs[:4], refs[4:]
        weight_refs, refs = refs[:pieces], refs[pieces:]
        second_ref, cq_ref, ckv_out, catt_ref, inverse_ref, probs_ref, *refs = refs
        memory, turned_values, staged, scratch, sem = refs
        full = weight.load(info_ref, weight_refs, scratch, 2)
        step = pl.program_id(0)
        index = pl.program_id(1)
        copy = pltpu.make_async_copy(memory, ckv_out, sem)

        @pl.when(first_step(2))
        def _():
            for part, ref in enumerate(enc_refs):
                staged[part * count : (part + 1) * count, :] = ref[...]

            def project(part, carry):
                at = pl.ds(pl.multiple_of(part * count, count), count)
                memory[at, :] = dot(staged[at, :], full[:, 2 * width :]).astype(BF16)
                return carry

            lax.fori_loop(0, 4, project, 0)
            copy.start()
            turned_values[...] = memory[:, width:].T

        @pl.when(index == 0)
        def _():
            second_in = tokens.load(first_ref, last_ref).astype(F32) + dot(
                att_ref[...], full[:, :width]
            )
            second_ref[...] = second_in
            normed, _ = normalized(second_in)
            normed = (normed * gain_ref[4:5, :]).astype(BF16)
            cq_ref[...] = (dot(normed, full[:, width : 2 * width]) * HEAD_DIM**-0.5).astype(BF16)

        at = pair_at(index)
        attend_pair(
            cq_ref[:, at],
            lambda piece: memory[piece, at],
            lambda piece: turned_values[at, piece],
            4 * count,
            None,
            catt_ref,
            inverse_ref,
            probs_ref,
        )

        @pl.when((step == pl.num_programs(0) - 1) & (index == pairs - 1))
        def _():
            copy.wait()

    return call(
        body,
        "cross_forward",
        info,
        (rows // WIDE, pairs),
        [(att, rows_of(width, WIDE))]
        + tokens.inputs(WIDE)
        + [(gains, whole(gains.shape))]
        + own.resident()
        + other.resident()
        + weight.inputs(),
        [
            ((rows, width), F32, rows_of(width, WIDE)),
            ((rows, width), BF16, rows_of(width, WIDE)),
            ((4 * count, 2 * width), BF16, pl.BlockSpec(memory_space=pl.ANY)),
        ]
        + attention_outputs(rows, width, 4 * count),
        [
            pltpu.VMEM((4 * count, 2 * width), BF16),
            pltpu.VMEM((width, 4 * count), BF16),
            pltpu.VMEM((4 * count, width), BF16),
            weight.scratch(),
            pltpu.SemaphoreType.DMA,
        ],
        cost(16 * rows * rows * width, 12 * rows * width, rows * rows * width // HEAD_DIM),
    )


def backward_pair(qq, dd, oo, keys, values, turned_keys, inverses, probs, size, add_keys, add_values):
    products = (oo.astype(F32) * dd.astype(F32)).T
    row_head = lax.broadcasted_iota(jnp.int32, (PAIR, 1), 0) // HEAD_DIM
    lane_head = lax.broadcasted_iota(jnp.int32, (1, PAIR), 1) // HEAD_DIM

    def head(part, total_grad):
        qe = jnp.where(lane_head == part, qq, jnp.zeros_like(qq))
        de = jnp.where(lane_head == part, dd, jnp.zeros_like(dd))
        inner = jnp.sum(jnp.where(row_head == part, products, 0.0), axis=0, keepdims=True)
        inverse = inverses(part)
        column = jnp.broadcast_to(inverse, (8, inverse.shape[1])).T[:, 0:1]
        scaled = (de.astype(F32) * column).astype(BF16)
        grad = None
        for begin in range(0, keys.shape[0], size):
            into = slice(begin, min(begin + size, keys.shape[0]))
            p = probs(part, into)
            dprobs = dot(values[into, :], de, 1, 1)
            dscores = (p.astype(F32) * ((dprobs - inner) * inverse)).astype(BF16)
            add_values(into, dot(p, scaled))
            add_keys(into, dot(dscores, qe))
            term = dot(turned_keys[:, into], dscores)
            grad = term if grad is None else grad + term
        return total_grad + jnp.where(row_head == part, grad, 0.0)

    grad = lax.fori_loop(0, 2, head, jnp.zeros((PAIR, qq.shape[0]), F32))
    return (grad.T * HEAD_DIM**-0.5).astype(BF16)


def attention_backward(name, info, q, kv, att, datt, inverses, probs, splits, split, stores):
    rows, width = q.shape
    count = kv.shape[0]
    lanes = width // splits
    pairs = lanes // PAIR
    all_pairs = width // PAIR
    base = split * pairs

    def body(info_ref, q_ref, k_ref, v_ref, att_ref, datt_ref, inverse_ref, probs_ref, *refs):
        dq_ref, down_ref, dother_ref, turned_keys, acc = refs
        step = pl.program_id(0)
        index = pl.program_id(1)
        at = pair_at(index)
        vat = pair_at(index + pairs)

        @pl.when(step == 0)
        def _():
            turned_keys[at, :] = k_ref[...].T
            acc[:, at] = jnp.zeros((count, PAIR), F32)
            acc[:, vat] = jnp.zeros((count, PAIR), F32)

        def add_keys(into, value):
            acc[into, at] += value

        def add_values(into, value):
            acc[into, vat] += value

        dq_ref[...] = backward_pair(
            q_ref[...],
            datt_ref[...],
            att_ref[...],
            k_ref,
            v_ref,
            turned_keys[at, :],
            lambda part: inverse_ref[0, pl.ds(part, 1), :],
            lambda part, into: probs_ref[part, into, :],
            2048,
            add_keys,
            add_values,
        )

        @pl.when((step == pl.num_programs(0) - 1) & (index == pairs - 1))
        def _():
            stores(info_ref, acc, down_ref, dother_ref)

    pair_rows = pl.BlockSpec((WIDE, PAIR), lambda i, h, *_: (i, base + h))
    half = (count // 2, 2 * lanes)
    return call(
        body,
        name,
        info,
        (rows // WIDE, pairs),
        [
            (q, pair_rows),
            (kv, pl.BlockSpec((count, PAIR), lambda i, h, *_: (0, base + h))),
            (kv, pl.BlockSpec((count, PAIR), lambda i, h, *_: (0, all_pairs + base + h))),
            (att, pair_rows),
            (datt, pair_rows),
            (inverses, pl.BlockSpec((1, 2, WIDE), lambda i, h, *_: (base + h, 0, i))),
            (probs, pl.BlockSpec((2, count, WIDE), lambda i, h, *_: (base + h, 0, i))),
        ],
        [
            ((rows, lanes), BF16, pl.BlockSpec((WIDE, PAIR), lambda i, h, *_: (i, h))),
            (half, BF16, whole(half)),
            (half, BF16, whole(half)),
        ],
        [pltpu.VMEM((lanes, count), BF16), pltpu.VMEM((count, 2 * lanes), F32)],
        cost(32 * rows * count * lanes, 20 * rows * lanes + 2 * rows * count),
    )


def self_backward(info, q, kv, att, dat, inverses, probs, splits, split):
    quarter = q.shape[0] // 2

    def stores(info_ref, acc, down_ref, dother_ref):
        for target, core in ((down_ref, info_ref[2]), (dother_ref, 1 - info_ref[2])):
            for part in range(2):
                begin = pl.multiple_of(place_of(info_ref, core, part) * quarter, quarter)
                target[part * quarter : (part + 1) * quarter, :] = acc[
                    pl.ds(begin, quarter), :
                ].astype(BF16)

    return attention_backward(
        "self_backward", info, q, kv, att, dat, inverses, probs, splits, split, stores
    )


def cross_backward(info, cq, ckv, catt, dca, inverses, probs, splits, split):
    count = ckv.shape[0]

    def stores(info_ref, acc, down_ref, dother_ref):
        down_ref[...] = acc[: count // 2, :].astype(BF16)
        dother_ref[...] = acc[count // 2 :, :].astype(BF16)

    return attention_backward(
        "cross_backward", info, cq, ckv, catt, dca, inverses, probs, splits, split, stores
    )


def feed(info, catt, second_in, dy, cout, weights, gains, packing):
    rows, width = catt.shape
    hidden = weights.hidden
    cout_count = len(cout.arrays)
    feed_count = len(weights.arrays)
    packed = packing.outputs(width * width + 2 * width * hidden)

    def body(info_ref, catt_ref, second_ref, dy_first, dy_last, gain_ref, *refs):
        cout_refs, refs = refs[:cout_count], refs[cout_count:]
        feed_refs, refs = refs[:feed_count], refs[feed_count:]
        (
            out_first,
            out_last,
            dthird_ref,
            dca_ref,
            ggain_ref,
            *packed_refs,
            acc_cout,
            acc_widen,
            acc_narrow,
            cout_scratch,
            widen_scratch,
            narrow_scratch,
        ) = refs
        cout_full = cout.load(info_ref, cout_refs, cout_scratch)
        widen_full, narrow_full = weights.load(info_ref, feed_refs, (widen_scratch, narrow_scratch))
        step = pl.program_id(0)

        @pl.when(step == 0)
        def _():
            acc_cout[...] = jnp.zeros_like(acc_cout)
            acc_widen[...] = jnp.zeros_like(acc_widen)
            acc_narrow[...] = jnp.zeros_like(acc_narrow)
            ggain_ref[...] = jnp.zeros_like(ggain_ref)

        catt = catt_ref[...]
        dy_low = dy.load(dy_first, dy_last)
        gain = gain_ref[5:6, :]
        third = second_ref[...] + dot(catt, cout_full[...])
        normed, scale = normalized(third)
        normed_low = (normed * gain).astype(BF16)
        pre = dot(normed_low, widen_full[...])
        below = 0.5 * (1.0 + lax.erf(pre * math.sqrt(0.5)))
        bell = jnp.exp(-0.5 * pre * pre) * (1.0 / math.sqrt(2.0 * math.pi))
        act = (pre * below).astype(BF16)
        store_half(
            (out_first, out_last), (third + dot(act, narrow_full[...])).astype(BF16)
        )
        dact = dot(dy_low, narrow_full[...], 1, 1)
        dpre = (dact * (below + pre * bell)).astype(BF16)
        acc_narrow[...] += dot(act, dy_low, 0, 0)
        acc_widen[...] += dot(normed_low, dpre, 0, 0)
        dnormed = dot(dpre, widen_full[...], 1, 1)
        ggain_ref[...] += jnp.sum(dnormed * normed, axis=0, keepdims=True)
        dthird = dy_low.astype(F32) + norm_backward(dnormed * gain, normed, scale)
        dthird_ref[...] = dthird
        dc = dthird.astype(BF16)
        dca_ref[...] = dot(dc, cout_full[...], 1, 1).astype(BF16)
        acc_cout[...] += dot(catt, dc, 0, 0)

        @pl.when(step == pl.num_programs(0) - 1)
        def _():
            packing.store(
                info_ref, packed_refs, (acc_cout, acc_widen, acc_narrow), unroll=True
            )

    return call(
        body,
        "feed",
        info,
        rows // BLOCK,
        [(catt, rows_of(width)), (second_in, rows_of(width))]
        + dy.inputs(BLOCK)
        + [(gains, whole(gains.shape))]
        + cout.inputs()
        + weights.inputs(),
        half_outputs(rows, width, BLOCK)
        + [
            ((rows, width), F32, rows_of(width)),
            ((rows, width), BF16, rows_of(width)),
            ((1, width), F32, whole((1, width))),
        ]
        + packed,
        [
            pltpu.VMEM((width, width), F32),
            pltpu.VMEM((width, hidden), F32),
            pltpu.VMEM((hidden, width), F32),
            cout.scratch(),
        ]
        + weights.scratch(),
        cost(
            12 * rows * width * hidden, 24 * rows * width + 8 * width * hidden, 2 * rows * hidden
        ),
    )


def sum_low(own_ref, got_ref):
    return (own_ref[...].astype(F32) + got_ref[...].astype(F32)).astype(BF16)


def middle_backward(
    info, dcqs, second_in, dthird, att, owns, gots, encoder, weight, gains, packing
):
    rows, width = second_in.shape
    count = len(dcqs)
    lanes = width // count
    packed = packing.outputs(4 * width * width)
    pieces = len(weight.arrays)
    short = encoder.shape[0] // (rows // BLOCK)

    def body(info_ref, att_ref, second_ref, dthird_ref, gain_ref, enc_first, enc_last, *refs):
        dcq_refs, refs = refs[:count], refs[count:]
        own_refs, refs = refs[:count], refs[count:]
        got_refs, refs = refs[:count], refs[count:]
        weight_refs, refs = refs[:pieces], refs[pieces:]
        dsecond_ref, dat_ref, ggain_ref, *genc_refs = refs[:5]
        refs = refs[5:]
        packed_refs, refs = refs[: len(packed)], refs[len(packed) :]
        acc_query, acc_out, acc_memory, scratch = refs
        full = weight.load(info_ref, weight_refs, scratch)
        step = pl.program_id(0)

        @pl.when(step == 0)
        def _():
            acc_query[...] = jnp.zeros_like(acc_query)
            acc_out[...] = jnp.zeros_like(acc_out)
            acc_memory[...] = jnp.zeros_like(acc_memory)
            ggain_ref[...] = jnp.zeros_like(ggain_ref)

        dcq = jnp.concatenate([ref[...] for ref in dcq_refs], axis=1)
        gain = gain_ref[4:5, :]
        normed, scale = normalized(second_ref[...])
        normed_low = (normed * gain).astype(BF16)
        dnormed = dot(dcq, full[:, width : 2 * width], 1, 1)
        acc_query[...] += dot(normed_low, dcq, 0, 0)
        ggain_ref[...] += jnp.sum(dnormed * normed, axis=0, keepdims=True)
        dsecond = dthird_ref[...] + norm_backward(dnormed * gain, normed, scale)
        dsecond_ref[...] = dsecond
        da = dsecond.astype(BF16)
        dat_ref[...] = dot(da, full[:, :width], 1, 1).astype(BF16)
        acc_out[...] += dot(att_ref[...], da, 0, 0)

        turned = encoder.load(enc_first, enc_last).T
        grads = [sum_low(own, got) for own, got in zip(own_refs, got_refs)]
        dckv = jnp.concatenate(
            [g[:, :lanes] for g in grads] + [g[:, lanes:] for g in grads], axis=1
        )
        store_half(genc_refs, dot(dckv, full[:, 2 * width :], 1, 1).astype(BF16))
        acc_memory[...] += dot(turned, dckv)

        @pl.when(step == pl.num_programs(0) - 1)
        def _():
            packing.store(info_ref, packed_refs, (acc_query, acc_out, acc_memory))

    return call(
        body,
        "middle_backward",
        info,
        rows // BLOCK,
        [
            (att, rows_of(width)),
            (second_in, rows_of(width)),
            (dthird, rows_of(width)),
            (gains, whole(gains.shape)),
        ]
        + encoder.inputs(short)
        + [(a, rows_of(lanes)) for a in dcqs]
        + [(a, rows_of(2 * lanes, short)) for a in owns]
        + [(a, rows_of(2 * lanes, short)) for a in gots]
        + weight.inputs(),
        [
            ((rows, width), F32, rows_of(width)),
            ((rows, width), BF16, rows_of(width)),
            ((1, width), F32, whole((1, width))),
        ]
        + half_outputs(encoder.shape[0], width, short)
        + packed,
        [
            pltpu.VMEM((width, width), F32),
            pltpu.VMEM((width, width), F32),
            pltpu.VMEM((width, 2 * width), F32),
            weight.scratch(),
        ],
        cost(16 * rows * width * width, 20 * rows * width),
    )


VECTORS = 8


def project_backward(
    info, tokens, normed, dqs, owns, gots, dsecond, mods, ggains, embedded, gencs, weight, packing
):
    rows, width = tokens.shape
    count = len(dqs)
    lanes = width // count
    packed = packing.outputs(3 * width * width, VECTORS)
    sent = (rows // 2 + gencs[0].shape[0], width)
    pieces = len(weight.arrays)

    def body(info_ref, first_ref, last_ref, normed_ref, dsecond_ref, mod_ref, *refs):
        second_gain, third_gain, embedded_ref, *genc_refs = refs[:5]
        refs = refs[5:]
        dq_refs, refs = refs[:count], refs[count:]
        own_refs, refs = refs[:count], refs[count:]
        got_refs, refs = refs[:count], refs[count:]
        weight_refs, refs = refs[:pieces], refs[pieces:]
        gfirst_ref, glast_ref, vectors_ref, *packed_refs, acc, sums, scratch = refs
        full = weight.load(info_ref, weight_refs, scratch)
        step = pl.program_id(0)

        @pl.when(step == 0)
        def _():
            acc[...] = jnp.zeros_like(acc)
            sums[...] = jnp.zeros_like(sums)

        turned = normed_ref[...].T
        dkvs = [sum_low(own, got) for own, got in zip(own_refs, got_refs)]
        grads = jnp.concatenate(
            [ref[...] for ref in dq_refs]
            + [dkv[:, :lanes] for dkv in dkvs]
            + [dkv[:, lanes:] for dkv in dkvs],
            axis=1,
        )
        acc[...] += dot(turned, grads)
        dnormed = dot(grads, full[...], 1, 1)
        unit, scale = normalized(tokens.load(first_ref, last_ref).astype(F32))
        sums[0:1, :] += jnp.sum(dnormed * unit, axis=0, keepdims=True)
        sums[1:2, :] += jnp.sum(dnormed, axis=0, keepdims=True)
        gtokens = (
            dsecond_ref[...] + norm_backward(dnormed * mod_ref[0:1, :], unit, scale)
        ).astype(BF16)
        steps = rows // BLOCK // 2
        at = pl.ds(pl.multiple_of(lax.rem(step, steps) * BLOCK, BLOCK), BLOCK)
        for half, ref in enumerate((gfirst_ref, glast_ref)):

            @pl.when(step // steps == half)
            def _(half=half, ref=ref):
                ref[at, :] = gtokens
                ref[rows // 2 :, :] = genc_refs[half][...]

        @pl.when(step == pl.num_programs(0) - 1)
        def _():
            vectors = jnp.concatenate(
                [
                    sums[0:1, :] * mod_ref[2:3, :],
                    second_gain[...],
                    third_gain[...],
                    sums[0:1, :] * mod_ref[3:4, :],
                    sums[1:2, :],
                    embedded_ref[0:1, :].astype(F32),
                    jnp.zeros((VECTORS - 6, width), F32),
                ],
                axis=0,
            )
            vectors_ref[...] = vectors
            packing.store(info_ref, packed_refs, (acc,), vectors)

    return call(
        body,
        "project_backward",
        info,
        rows // BLOCK,
        tokens.inputs(BLOCK)
        + [
            (normed, rows_of(width)),
            (dsecond, rows_of(width)),
            (mods, whole(mods.shape)),
            (ggains[0], whole((1, width))),
            (ggains[1], whole((1, width))),
            (embedded, whole(embedded.shape)),
            (gencs[0], whole(gencs[0].shape)),
            (gencs[1], whole(gencs[1].shape)),
        ]
        + [(a, rows_of(lanes)) for a in dqs]
        + [(a, rows_of(2 * lanes)) for a in owns]
        + [(a, rows_of(2 * lanes)) for a in gots]
        + weight.inputs(),
        [(sent, BF16, whole(sent))] * 2
        + [((VECTORS, width), F32, whole((VECTORS, width)))]
        + packed,
        [pltpu.VMEM((width, 3 * width), F32), pltpu.VMEM((8, width), F32), weight.scratch()],
        cost(12 * rows * width * width, 20 * rows * width),
    )


def join_columns(info, parts):
    size = parts[0].shape[0] - VECTORS
    shape = (size + len(parts) * VECTORS, parts[0].shape[1])

    def body(info_ref, *refs):
        *part_refs, out_ref = refs
        total = part_refs[0][:size, :].astype(F32)
        for ref in part_refs[1:]:
            total = total + ref[:size, :].astype(F32)
        out_ref[:size, :] = total.astype(BF16)
        for index, ref in enumerate(part_refs):
            begin = size + index * VECTORS
            out_ref[begin : begin + VECTORS, :] = ref[size:, :]

    return call(
        body,
        "join_columns",
        info,
        1,
        [(part, whole(part.shape)) for part in parts],
        [(shape, BF16, whole(shape))],
        [],
        cost(0, 4 * size * shape[1]),
    )[0]


def finish(info, parts, size, shard):
    width = parts[0].shape[1]
    count = parts[0].shape[0] - size
    devices = len(parts) * count // VECTORS

    def body(info_ref, *refs):
        part_refs = refs[: len(parts)]
        ginput_ref, gtime_ref, ggains_ref, listed, turned = refs[len(parts) :]
        for block in range(size // shard):
            rows = slice(block * shard, (block + 1) * shard)
            terms = [ref[rows, :].astype(F32) for ref in part_refs]
            ginput_ref[:, block * width : (block + 1) * width] = (terms[0] + terms[1]) + (
                terms[2] + terms[3]
            )
        for turn, ref in enumerate(part_refs):
            place = lax.bitwise_xor(info_ref[5], turn)
            listed[pl.ds(pl.multiple_of(place * count, count), count), :] = ref[size:, :]
        vectors = listed[...]
        column = lax.broadcasted_iota(jnp.int32, (devices, devices * VECTORS), 1)
        row = lax.broadcasted_iota(jnp.int32, (devices, devices * VECTORS), 0)

        def pick(kind):
            chosen = jnp.where(column == row * VECTORS + kind, 1.0, 0.0).astype(BF16)
            return dot(chosen, vectors)

        chosen = jnp.where(lax.rem(column, VECTORS) == row, 1.0, 0.0).astype(BF16)
        turned[...] = jnp.concatenate([0.5 * pick(5), dot(chosen, vectors)], axis=0).T
        place = (2 * info_ref[4] + info_ref[2]) * shard
        part = turned[pl.ds(pl.multiple_of(place, shard), shard), :]
        grads = jnp.concatenate([pick(3), pick(4)], axis=1).astype(BF16)
        gtime_ref[...] = dot(part[:, :devices].astype(BF16), grads)
        ggains_ref[...] = part.T[devices : devices + 3, :]

    return call(
        body,
        "finish",
        info,
        1,
        [(part, whole(part.shape)) for part in parts],
        [
            ((shard, 3 * width), F32, whole((shard, 3 * width))),
            ((shard, 2 * width), F32, whole((shard, 2 * width))),
            ((3, shard), F32, whole((3, shard))),
        ],
        [pltpu.VMEM((devices * VECTORS, width), BF16), pltpu.VMEM((width, 2 * devices), F32)],
        cost(8 * devices * count * width, 12 * size * width),
    )


def permutations(seq_count, fsdp_count):
    columns = fsdp_count // 2

    def at(seq, fsdp):
        return seq * fsdp_count + fsdp

    def pairs(move):
        return [
            (at(seq, fsdp), at(*move(seq, fsdp)))
            for seq in range(seq_count)
            for fsdp in range(fsdp_count)
        ]

    def home(turn):
        def move(seq, fsdp):
            y, x = divmod(seq, 2)
            column, core = divmod(fsdp, 2)
            return 2 * core + (x ^ turn), 2 * column + y

        return move

    shift = {
        r: pairs(lambda seq, fsdp, r=r: (seq, (fsdp + 2 * r) % fsdp_count))
        for r in range(1, columns)
    }
    cross = {t: pairs(lambda seq, fsdp, t=t: (seq ^ t, fsdp)) for t in range(1, seq_count)}
    swap = pairs(lambda seq, fsdp: (seq, fsdp ^ 1))
    return pairs(home(0)), pairs(home(1)), swap, shift, cross


def reverse(pairs):
    return [(target, source) for source, target in pairs]


def after(values, signal):
    return lax.optimization_barrier((values, signal))[0]


class Direct:
    def __init__(self, perms, seq, fsdp, columns):
        self.same, self.crossed, self.swap_pairs, self.shifts, self.crosses = perms
        self.seq = seq
        self.core = fsdp % 2
        self.z = fsdp // 2
        self.columns = columns

    def permute(self, values, pairs):
        return lax.ppermute(values, AXES, pairs)

    def swap(self, values):
        return self.permute(values, self.swap_pairs)

    def along_z(self, values):
        return [values] + [
            self.permute(values, self.shifts[r]) for r in range(1, self.columns)
        ]

    def both_cores(self, pieces):
        return pieces + [self.swap(piece) for piece in pieces]

    def core_sum(self, mine, away, signal=()):
        got = after(self.swap(away), signal)
        return [
            (mine[r].astype(F32) + got[r].astype(F32)).astype(BF16) for r in range(self.columns)
        ]

    def z_parts(self, shards):
        return [self.permute(shards[r], self.shifts[r]) for r in range(1, self.columns)]

    def z_sum(self, shards, got, signal=()):
        total = shards[0].astype(F32)
        for part in after(got, signal):
            total = total + part.astype(F32)
        return lax.optimization_barrier(total.astype(BF16))

    def add(self, first, second):
        return lax.optimization_barrier((first.astype(F32) + second.astype(F32)).astype(BF16))

    def cross(self, values, turn):
        return self.permute(values, self.crosses[turn])


SPLITS = 2


def time_embedding(step_values, model_width):
    half_width = model_width // 2
    frequency = jnp.exp(-math.log(10000.0) * jnp.arange(half_width, dtype=F32) / half_width)
    angles = step_values.astype(F32)[:, None] * frequency[None, :]
    return jnp.concatenate([jnp.sin(angles), jnp.cos(angles)], axis=-1).astype(BF16)


def exact_dot(left, right):
    return lax.dot_general(
        left,
        right,
        (((0,), (0,)), ((), ())),
        precision=lax.Precision.HIGHEST,
        preferred_element_type=F32,
    )


def make(seq_count, fsdp_count):
    perms = permutations(seq_count, fsdp_count)
    same, crossed = perms[:2]
    columns = fsdp_count // 2

    def on_device(
        tokens,
        encoder_states,
        lengths,
        timesteps,
        time_weight,
        self_input,
        self_output,
        cross_query,
        cross_memory,
        cross_output,
        widen_weight,
        narrow_weight,
        norm_gains,
        cotangent,
    ):
        width = tokens.shape[2]
        hidden = widen_weight.shape[1]
        shard = time_weight.shape[0]
        seq = lax.axis_index("seq")
        fsdp = lax.axis_index("fsdp")
        core = fsdp % 2
        side = seq % 2
        direct = Direct(perms, seq, fsdp, columns) if columns == 4 else None

        def send_work(values):
            mine = lax.dynamic_index_in_dim(values, side, 0, keepdims=False)
            others = lax.dynamic_index_in_dim(values, 1 - side, 0, keepdims=False)
            return [lax.ppermute(mine, AXES, same), lax.ppermute(others, AXES, crossed)]

        def send_home(halves):
            return [
                lax.ppermute(halves[0], AXES, reverse(same)),
                lax.ppermute(halves[1], AXES, reverse(crossed)),
            ]

        def at_home(parts, kind):
            first = jnp.where(side == 0, parts[0], parts[1])
            second = jnp.where(side == 0, parts[1], parts[0])
            return jnp.stack([first, second], axis=0).astype(kind)

        def gather(weight, axis=0):
            return lax.all_gather(weight, "fsdp", axis=axis, tiled=True)

        def swap(values):
            return lax.ppermute(values, AXES, perms[2])

        packing = Packing(fsdp_count, direct is not None, width)
        token_rows, encoder_rows = tokens.shape[1], encoder_states.shape[1]
        numbers = jnp.concatenate([lengths, timesteps[:, None]], axis=1)
        numbers_other = swap(numbers)
        own_row = jnp.where(core == seq // 2, numbers, numbers_other)
        own_row = lax.dynamic_slice_in_dim(own_row, side, 1, 0)
        step_value = own_row[0, 3:4]
        place = lax.broadcasted_iota(jnp.int32, (8,), 0)
        info = jnp.where(place == 1, own_row[0, 1], 0) + jnp.where(place <= 1, own_row[0, 0], 0)
        for index, value in enumerate((core, side, fsdp // 2, seq)):
            info = jnp.where(place == index + 2, value, info)
        embedded = jnp.pad(time_embedding(step_value, width), ((0, 15), (0, 0)))

        turned = jnp.pad(norm_gains.T, ((0, 0), (0, 128 - norm_gains.shape[0])))
        first = jnp.concatenate([self_input, time_weight, turned], axis=1)
        first_mine = direct.along_z(first) if direct else [(), ()]
        own = send_work(jnp.concatenate([tokens, encoder_states], axis=1))
        other = [swap(part) for part in after(own, first_mine[1:])]
        work_tokens = Halves(own, 0, token_rows)
        other_tokens = Halves(other, 0, token_rows)
        work_encoder = Halves(own, token_rows, encoder_rows)
        other_encoder = Halves(other, token_rows, encoder_rows)

        ready = info
        rest = jnp.concatenate([self_output, cross_query, cross_memory, cross_output], axis=1)
        if direct:
            first = direct.both_cores(first_mine)
            wide = widen_weight.reshape(shard, hidden // width, width).transpose(1, 0, 2)
            large = jnp.concatenate([wide.reshape(-1, width), narrow_weight], axis=0)
            rest, large = after((rest, large), (own, info, embedded))
            rest_mine = direct.along_z(rest)
            small_other = [swap(rest)]
            large_mine = direct.along_z(large)
            large_other = [swap(large)]
            ready = after(info, (small_other, large_other))
        else:
            first = [gather(first)]
            rest = [gather(rest)]
            feed_weights = FeedWeights([gather(widen_weight), gather(narrow_weight)], hidden)

        mods, q, kv, normed_first, att, inverses, probs = self_forward(
            ready, work_tokens, other_tokens, embedded, Weight(first, 0, first[0].shape[1])
        )
        ready = info
        if direct:
            rest_mine[1:], large_mine[:2] = after((rest_mine[1:], large_mine[:2]), att)
            small_other += [swap(part) for part in rest_mine[1:]]
            rest = rest_mine + small_other
            large_other.append(swap(large_mine[1]))
            ready = after(info, large_other)
        input_weight = Weight(first, 0, 3 * width)
        cross_weight = Weight(rest, 0, 4 * width)
        cout_weight = Weight(rest, 4 * width, width)
        dy_parts = send_work(after(cotangent, att))
        second_in, cq, ckv, catt, cross_inverses, cross_probs = cross_forward(
            ready, att, work_tokens, work_encoder, other_encoder, cross_weight, mods
        )
        work_dy = Halves(after(dy_parts, catt), 0, token_rows)
        if direct:
            large_mine[2:] = after(large_mine[2:], catt)
            large_other += [swap(part) for part in large_mine[2:]]
            feed_weights = FeedWeights(large_mine + large_other, hidden)
        out_first, out_last, dthird, dca, ggain_third, *packed_feed = feed(
            info, catt, second_in, work_dy, cout_weight, feed_weights, mods, packing
        )
        layer_out = (out_first, out_last)
        out_parts = send_home(layer_out)

        def backward_cross(split, ready):
            return cross_backward(
                ready, cq, ckv, catt, dca, cross_inverses, cross_probs, SPLITS, split
            )

        def backward_self(split, ready):
            return self_backward(ready, q, kv, att, dat, inverses, probs, SPLITS, split)

        crosses = [backward_cross(0, info)]
        out_parts = after(out_parts, crosses[0][0])
        chip_feed = direct.core_sum(*packed_feed, crosses[0][0]) if direct else ()
        crosses.append(backward_cross(1, after(info, (chip_feed, out_parts))))
        dcqs, dckvs, dckv_others = zip(*crosses)
        dckv_gots = [swap(a) for a in dckv_others]
        feed_parts = direct.z_parts(chip_feed) if direct else [()]
        dsecond, dat, ggain_second, *genc = middle_backward(
            after(info, (feed_parts[0], dcqs)),
            dcqs,
            second_in,
            dthird,
            att,
            dckvs,
            dckv_gots,
            work_encoder,
            cross_weight,
            mods,
            packing,
        )
        genc, packed_middle = genc[:2], genc[2:]
        selfs = [backward_self(0, after(info, packed_middle))]
        if direct:
            column_feed = direct.z_sum(chip_feed, feed_parts, selfs[0][0])
            chip_middle = direct.core_sum(*packed_middle, selfs[0][0])
            selfs.append(backward_self(1, after(info, (column_feed, chip_middle))))
            middle_parts = after(direct.z_parts(chip_middle), selfs[1][0])
            row_feed = after(direct.cross(column_feed, 1), selfs[1][0])
            row_feed = direct.add(column_feed, row_feed)
            column_middle = direct.z_sum(chip_middle, middle_parts)
        else:
            selfs.append(backward_self(1, info))
        dqs, dkvs, dkv_others = zip(*selfs)
        dkv_others = list(dkv_others)
        if direct:
            dkv_others[1] = after(dkv_others[1], (column_middle, row_feed))
        dkv_gots = [swap(a) for a in dkv_others]
        first_grad, last_grad, vectors, *packed_input = project_backward(
            info,
            work_tokens,
            normed_first,
            dqs,
            dkvs,
            dkv_gots,
            dsecond,
            mods,
            (ggain_second, ggain_third),
            embedded,
            genc,
            input_weight,
            packing,
        )
        gtokens = (first_grad, last_grad)
        if direct:
            got_row = after(direct.cross(row_feed, 2), gtokens)
            row_middle = after(direct.cross(column_middle, 1), gtokens)
            away = after(packed_input[1], (got_row, row_middle))
            chip = direct.core_sum(packed_input[0], away)
            row_middle = direct.add(column_middle, row_middle)
            gots = direct.z_parts(chip)
            token_parts = after(send_home(after(gtokens, chip)), gots)
            ready = after(info, token_parts)
            reduced_feed = row_feed.astype(F32) + got_row.astype(F32)
            size = chip[0].shape[0] - VECTORS
            joined = join_columns(ready, [chip[0]] + gots)
            middle_got = direct.cross(after(row_middle, joined), 2)
            parts = [joined] + [direct.cross(joined, turn) for turn in (1, 2, 3)]
            reduced_middle = row_middle.astype(F32) + middle_got.astype(F32)
            reduced_input, gtime, ggains = finish(info, parts, size, shard)
        else:

            def reduce(packed):
                part = lax.psum_scatter(packed[0], "fsdp", scatter_dimension=0, tiled=True)
                return lax.psum(part[0], "seq").astype(F32)

            reduced_input = reduce(packed_input)
            reduced_input = unpack_rows(reduced_input, 0, shard, 3 * width)
            reduced_middle = reduce(packed_middle)
            reduced_feed = reduce(packed_feed)
            token_parts = send_home(gtokens)
            ggains = lax.psum(vectors[:3], AXES)
            ggains = lax.dynamic_slice_in_dim(ggains, fsdp * shard, shard, 1)
            by_group = lax.all_gather(vectors[3:5], AXES, axis=0)
            by_group = by_group.reshape(seq_count, columns, 2, 2 * width).sum(axis=2)
            by_group = by_group.transpose(1, 0, 2).reshape(-1, 2 * width)
            every = time_embedding(gather(timesteps), width)
            own_columns = lax.dynamic_slice_in_dim(every, fsdp * shard, shard, 1)
            gtime = exact_dot(own_columns.astype(F32), by_group)

        tall = narrow_weight.shape[0]
        return (
            at_home(out_parts, BF16),
            at_home([part[:token_rows] for part in token_parts], F32),
            at_home([part[token_rows:] for part in token_parts], F32),
            gtime,
            reduced_input,
            unpack_rows(reduced_middle, shard, shard, width),
            unpack_rows(reduced_middle, 0, shard, width),
            unpack_rows(reduced_middle, 2 * shard, shard, 2 * width),
            unpack_rows(reduced_feed, 0, shard, width),
            unpack_rows(reduced_feed, shard, shard, hidden),
            unpack_rows(reduced_feed, shard * (1 + hidden // width), tall, width),
            ggains,
        )

    return on_device


def solution(mesh):
    rows = P("fsdp", "seq", None)
    weight = P("fsdp", None)
    in_specs = (rows, rows, P("fsdp", None), P("fsdp")) + (weight,) * 8 + (P(None, "fsdp"), rows)
    out_specs = (rows,) * 3 + (weight,) * 8 + (P(None, "fsdp"),)
    return jax.shard_map(
        make(mesh.shape["seq"], mesh.shape["fsdp"]),
        mesh=mesh,
        in_specs=in_specs,
        out_specs=out_specs,
        check_vma=False,
    )
```

```python
import math

import jax
import jax.numpy as jnp
from jax import lax
from jax.experimental import pallas as pl
from jax.experimental.pallas import tpu as pltpu
from jax.sharding import PartitionSpec as P


HEAD_DIM = 64
PAIR = 2 * HEAD_DIM
EPS = 1e-05
NEG = -1e30
F32 = jnp.float32
BF16 = jnp.bfloat16
AXES = ("seq", "fsdp")
VMEM_LIMIT = 60 * 2**20
BLOCK = 256
WIDE = 512


def dot(left, right, left_dim=1, right_dim=0):
    return lax.dot_general(
        left, right, (((left_dim,), (right_dim,)), ((), ())), preferred_element_type=F32
    )


def whole(shape):
    return pl.BlockSpec(shape, lambda *_: (0,) * len(shape))


def rows_of(width, block=BLOCK):
    return pl.BlockSpec((block, width), lambda i, *_: (i, 0))


def params():
    return pltpu.CompilerParams(vmem_limit_bytes=VMEM_LIMIT)


def cost(flops, moved, transcendentals=0):
    return pl.CostEstimate(
        flops=int(flops), bytes_accessed=int(moved), transcendentals=int(transcendentals)
    )


def normalized(values):
    average = jnp.mean(values, axis=-1, keepdims=True)
    centred = values - average
    spread = jnp.mean(centred * centred, axis=-1, keepdims=True)
    scale = lax.rsqrt(spread + EPS)
    return centred * scale, scale


def norm_backward(upstream, normed, scale):
    mean_up = jnp.mean(upstream, axis=-1, keepdims=True)
    mean_both = jnp.mean(upstream * normed, axis=-1, keepdims=True)
    return (upstream - mean_up - normed * mean_both) * scale


def lane_is(part):
    lane = lax.broadcasted_iota(jnp.int32, (1, PAIR), 1)
    return lane < HEAD_DIM if part == 0 else lane >= HEAD_DIM


def half_of(values, part):
    return jnp.where(lane_is(part), values, jnp.zeros_like(values))


def pair_at(index):
    return pl.ds(pl.multiple_of(index * PAIR, PAIR), PAIR)


def first_step(dims=1):
    first = pl.program_id(0) == 0
    return first if dims == 1 else first & (pl.program_id(1) == 0)


class Weight:
    def __init__(self, pieces, start, width):
        self.arrays = pieces
        self.start = start
        self.width = width

    @property
    def split(self):
        return len(self.arrays) > 1

    @property
    def rows(self):
        return len(self.arrays) * self.arrays[0].shape[0]

    @property
    def aligned(self):
        return self.start % self.width == 0

    def inputs(self):
        if not self.aligned:
            return [(array, whole(array.shape)) for array in self.arrays]
        place = self.start // self.width
        shape = (self.arrays[0].shape[0], self.width)
        return [(array, pl.BlockSpec(shape, lambda *_: (0, place))) for array in self.arrays]

    def scratch(self):
        return pltpu.VMEM((self.rows, self.width) if self.split else (16, 128), BF16)

    def load(self, info, refs, scratch, dims=1):
        if not self.split:
            return refs[0]
        columns = slice(0, self.width) if self.aligned else slice(self.start, self.start + self.width)

        @pl.when(first_step(dims))
        def _():
            count = len(refs) // 2
            shard = refs[0].shape[0]
            for index, ref in enumerate(refs):
                turn, shift = divmod(index, count)
                core = info[2] if turn == 0 else 1 - info[2]
                owner = lax.rem(info[4] - shift + count, count)
                start = pl.multiple_of((2 * owner + core) * shard, shard)
                scratch[pl.ds(start, shard), :] = ref[:, columns]

        return scratch


class Halves:
    def __init__(self, arrays, start, rows):
        self.arrays = arrays
        self.start = start
        self.rows = rows
        self.shape = (2 * rows, arrays[0].shape[1])

    def inputs(self, block):
        width = self.shape[1]
        count = self.rows // block
        base = self.start // block
        return [
            (
                self.arrays[0],
                pl.BlockSpec((block, width), lambda i, *_: (base + jnp.minimum(i, count - 1), 0)),
            ),
            (
                self.arrays[1],
                pl.BlockSpec((block, width), lambda i, *_: (base + jnp.maximum(i - count, 0), 0)),
            ),
        ]

    def resident(self):
        place = self.start // self.rows
        spec = pl.BlockSpec((self.rows, self.shape[1]), lambda *_: (place, 0))
        return [(array, spec) for array in self.arrays]

    def load(self, first_ref, second_ref):
        half = pl.num_programs(0) // 2
        return jnp.where(pl.program_id(0) < half, first_ref[...], second_ref[...])


def half_outputs(rows, width, block):
    count = rows // block // 2
    half = (rows // 2, width)
    return [
        (half, BF16, pl.BlockSpec((block, width), lambda i, *_: (jnp.minimum(i, count - 1), 0))),
        (half, BF16, pl.BlockSpec((block, width), lambda i, *_: (jnp.maximum(i - count, 0), 0))),
    ]


def store_half(refs, value):
    first = pl.program_id(0) < pl.num_programs(0) // 2

    @pl.when(first)
    def _():
        refs[0][...] = value

    @pl.when(jnp.logical_not(first))
    def _():
        refs[1][...] = value


class FeedWeights:
    def __init__(self, arrays, hidden):
        self.arrays = arrays
        self.hidden = hidden

    @property
    def split(self):
        return len(self.arrays) > 2

    def inputs(self):
        return [(array, whole(array.shape)) for array in self.arrays]

    def scratch(self):
        if not self.split:
            return [pltpu.VMEM((16, 128), BF16)] * 2
        width = self.arrays[0].shape[1]
        return [pltpu.VMEM((width, self.hidden), BF16), pltpu.VMEM((self.hidden, width), BF16)]

    def load(self, info, refs, scratch):
        if not self.split:
            return refs
        widen, narrow = scratch

        @pl.when(pl.program_id(0) == 0)
        def _():
            count = len(refs) // 2
            rows, width = refs[0].shape
            blocks = self.hidden // width
            tall = rows // 2
            short = tall // blocks
            for index, ref in enumerate(refs):
                turn, shift = divmod(index, count)
                core = info[2] if turn == 0 else 1 - info[2]
                owner = 2 * lax.rem(info[4] - shift + count, count) + core
                start = pl.multiple_of(owner * short, short)
                for block in range(blocks):
                    widen[pl.ds(start, short), block * width : (block + 1) * width] = ref[
                        block * short : (block + 1) * short, :
                    ]
                start = pl.multiple_of(owner * tall, tall)
                narrow[pl.ds(start, tall), :] = ref[tall:, :]

        return widen, narrow


class Packing:
    def __init__(self, shards, direct, width):
        self.shards = shards
        self.direct = direct
        self.width = width

    def outputs(self, elements, extra=0):
        rows = elements // (self.shards * self.width)
        if self.direct:
            rows += extra
        if self.direct:
            shape = (self.shards // 2, rows, self.width)
            return [(shape, BF16, whole(shape))] * 2
        shape = (self.shards, rows, self.width)
        return [(shape, BF16, whole(shape))]

    def store(self, info, packed, grads, vectors=None, unroll=False):
        def put(ref, slot, owner):
            offset = 0
            for grad in grads:
                rows = grad.shape[0] // self.shards
                start = owner * rows
                if not isinstance(owner, int):
                    start = pl.multiple_of(start, rows)
                for block in range(grad.shape[1] // self.width):
                    columns = slice(block * self.width, (block + 1) * self.width)
                    ref[slot, offset : offset + rows, :] = grad[pl.ds(start, rows), columns].astype(
                        BF16
                    )
                    offset += rows
            if vectors is not None and self.direct:
                ref[slot, offset:, :] = vectors.astype(BF16)

        if self.direct:
            count = self.shards // 2
            for ref, core in ((packed[0], info[2]), (packed[1], 1 - info[2])):

                def one(shift, carry, ref=ref, core=core):
                    put(ref, shift, 2 * lax.rem(info[4] + shift, count) + core)
                    return carry

                if unroll:
                    for shift in range(count):
                        one(shift, 0)
                else:
                    lax.fori_loop(0, count, one, 0)
        else:
            for shard in range(self.shards):
                put(packed[0], shard, shard)


def unpack_rows(packed, offset, rows, columns):
    width = packed.shape[1]
    blocks = columns // width
    parts = [packed[offset + b * rows : offset + (b + 1) * rows] for b in range(blocks)]
    return jnp.concatenate(parts, axis=1) if blocks > 1 else parts[0]


def call(body, name, info, grid, inputs, outputs, scratch, estimate):
    return pl.pallas_call(
        body,
        name=name,
        grid_spec=pltpu.PrefetchScalarGridSpec(
            num_scalar_prefetch=1,
            grid=grid if isinstance(grid, tuple) else (grid,),
            in_specs=[spec for _, spec in inputs],
            out_specs=[spec for _, _, spec in outputs],
            scratch_shapes=scratch,
        ),
        out_shape=[jax.ShapeDtypeStruct(shape, kind) for shape, kind, _ in outputs],
        compiler_params=params(),
        cost_estimate=estimate,
    )(info, *[array for array, _ in inputs])


def block_start(info, block_index, block, quarter):
    per_quarter = quarter // block
    first = block_index < per_quarter
    place = jnp.where(first, info[3], 1 - info[3])
    return (2 * info[2] + place) * quarter + lax.rem(block_index, per_quarter) * block


def forbidden(info, start, block, half, queries_dim):
    keys_dim = 1 - queries_dim
    qshape = [1, 1]
    qshape[queries_dim] = block
    kshape = [1, 1]
    kshape[keys_dim] = half
    qpos = start + lax.broadcasted_iota(jnp.int32, tuple(qshape), queries_dim)
    kpos = half + lax.broadcasted_iota(jnp.int32, tuple(kshape), keys_dim)
    first, second = info[0], info[1]
    low = jnp.where((qpos >= first) & (qpos < second), second, first)
    high = jnp.where(qpos >= second, second, 2 * half)
    return jnp.where((kpos >= low) & (kpos < high), NEG, 0.0)


def key_specs(array, lanes, split, width):
    rows = array.shape[0]
    count = width // lanes
    return [
        (array, pl.BlockSpec((rows, lanes), lambda *_: (0, split))),
        (array, pl.BlockSpec((rows, lanes), lambda *_: (0, count + split))),
    ]


def attention_sums(low, high):
    return (low > 1e-20) & (high < 1e30)


def attend_pair(qq, keys_at, turned_values, free, bias, att_ref, inverse_ref, probs_ref):
    count = probs_ref.shape[1]
    row_head = lax.broadcasted_iota(jnp.int32, (PAIR, 1), 0) // HEAD_DIM
    lane_head = lax.broadcasted_iota(jnp.int32, (1, PAIR), 1) // HEAD_DIM
    turned_at = turned_values(slice(0, count))

    def head(part):
        qe = jnp.where(lane_head == part, qq, jnp.zeros_like(qq))
        total = None
        out = None
        for piece in (slice(0, free), slice(free, count)):
            if piece.start == piece.stop:
                continue
            s = dot(keys_at(piece), qe, 1, 1)
            p = jnp.exp(s if piece.start == 0 else s + bias[...])
            low = p.astype(BF16)
            probs_ref[part, piece, :] = low
            term = jnp.sum(p, axis=0, keepdims=True)
            attended = dot(turned_at[:, piece], low)
            total = term if total is None else total + term
            out = attended if out is None else out + attended
        return out, total

    def one(part, carry):
        out, total = head(part)
        inverse = 1.0 / total
        inverse_ref[0, pl.ds(part, 1), :] = inverse
        joined, low, high = carry
        joined = joined + jnp.where(row_head == part, out * inverse, 0.0)
        return joined, jnp.minimum(low, total), jnp.maximum(high, total)

    ones = jnp.ones((1, qq.shape[0]), F32)
    out, low, high = lax.fori_loop(0, 2, one, (jnp.zeros((PAIR, qq.shape[0]), F32), ones, ones))
    att_ref[...] = out.T.astype(BF16)
    low, high = jnp.min(low), jnp.max(high)

    @pl.when(jnp.logical_not((low > 1e-20) & (high < 1e30)))
    def _():
        chunk = BLOCK // 2
        queries = qq.shape[0]

        def again(part, carry):
            qe = jnp.where(lane_head == part, qq, jnp.zeros_like(qq))

            def scores(index):
                at = pl.ds(pl.multiple_of(index * chunk, chunk), chunk)
                s = dot(keys_at(at), qe, 1, 1)
                if free == count:
                    return at, s
                begin = jnp.maximum(index * chunk - free, 0)
                part_bias = bias[pl.ds(pl.multiple_of(begin, chunk), chunk), :]
                return at, s + jnp.where(index * chunk >= free, part_bias, 0.0)

            def largest(index, top):
                return jnp.maximum(top, jnp.max(scores(index)[1], axis=0, keepdims=True))

            top = lax.fori_loop(
                0, count // chunk, largest, jnp.full((1, queries), -jnp.inf, F32)
            )

            def add(index, sums):
                at, s = scores(index)
                p = jnp.exp(s - top)
                low = p.astype(BF16)
                probs_ref[part, at, :] = low
                return (
                    sums[0] + jnp.sum(p, axis=0, keepdims=True),
                    sums[1] + dot(turned_values(at), low),
                )

            total, out = lax.fori_loop(
                0,
                count // chunk,
                add,
                (jnp.zeros((1, queries), F32), jnp.zeros((PAIR, queries), F32)),
            )
            inverse = 1.0 / total
            inverse_ref[0, pl.ds(part, 1), :] = inverse
            return carry + jnp.where(row_head == part, out * inverse, 0.0)

        out = lax.fori_loop(0, 2, again, jnp.zeros((PAIR, queries), F32))
        att_ref[...] = out.T.astype(BF16)


def attention_outputs(rows, width, count):
    pairs = width // PAIR
    return [
        ((rows, width), BF16, pl.BlockSpec((WIDE, PAIR), lambda i, h, *_: (i, h))),
        ((pairs, 2, rows), F32, pl.BlockSpec((1, 2, WIDE), lambda i, h, *_: (h, 0, i))),
        ((2 * pairs, count, rows), BF16, pl.BlockSpec((2, count, WIDE), lambda i, h, *_: (h, 0, i))),
    ]


def place_of(info, core, part):
    return 2 * core + (info[3] if part == 0 else 1 - info[3])


def self_forward(info, own, other, embedded, weight):
    rows, width = own.shape
    pairs = width // PAIR
    quarter = rows // 2
    pieces = len(weight.arrays)

    def body(info_ref, embedded_ref, *refs):
        token_refs, refs = refs[:4], refs[4:]
        weight_refs, refs = refs[:pieces], refs[pieces:]
        (
            mod_ref,
            q_out,
            kv_out,
            normed_out,
            att_ref,
            inverse_ref,
            probs_ref,
            queries,
            keys,
            normed,
            turned_values,
            staged,
            bias,
            scratch,
            sems,
        ) = refs
        step = pl.program_id(0)
        index = pl.program_id(1)
        full = weight.load(info_ref, weight_refs, scratch, 2)
        time_at = slice(3 * width, 5 * width)
        copies = [
            pltpu.make_async_copy(queries, q_out, sems.at[0]),
            pltpu.make_async_copy(keys, kv_out, sems.at[1]),
            pltpu.make_async_copy(normed, normed_out, sems.at[2]),
        ]

        @pl.when(first_step(2))
        def _():
            modulation = dot(embedded_ref[...], full[:, time_at])
            gains = full[:, 5 * width :].astype(F32).T[:3, :]
            plus = 1.0 + modulation[0:1, :width]
            shift = modulation[0:1, width:]
            mod_ref[...] = jnp.concatenate(
                [gains[0:1] * plus, shift, plus, gains, jnp.zeros((2, width), F32)], axis=0
            )
            for number, ref in enumerate(token_refs):
                turn, part = divmod(number, 2)
                holder = info_ref[2] if turn == 0 else 1 - info_ref[2]
                begin = place_of(info_ref, holder, part) * quarter
                staged[pl.ds(pl.multiple_of(begin, quarter), quarter), :] = ref[...]

            def project(block, carry):
                at = pl.ds(pl.multiple_of(block * BLOCK, BLOCK), BLOCK)
                unit, _ = normalized(staged[at, :].astype(F32))
                first = (unit * mod_ref[0:1, :] + mod_ref[1:2, :]).astype(BF16)
                keys[at, :] = dot(first, full[:, width : 3 * width]).astype(BF16)
                per_quarter = quarter // BLOCK
                place = block // per_quarter

                @pl.when(place // 2 == info_ref[2])
                def _():
                    part = lax.bitwise_xor(lax.rem(place, 2), info_ref[3])
                    begin = part * quarter + lax.rem(block, per_quarter) * BLOCK
                    here = pl.ds(pl.multiple_of(begin, BLOCK), BLOCK)
                    normed[here, :] = first
                    queries[here, :] = (dot(first, full[:, :width]) * HEAD_DIM**-0.5).astype(BF16)

                return carry

            lax.fori_loop(0, 2 * rows // BLOCK, project, 0)
            for copy in copies:
                copy.start()

            turned_values[...] = keys[:, width:].T

        @pl.when(index == 0)
        def _():
            start = block_start(info_ref, step, WIDE, quarter)
            bias[...] = forbidden(info_ref, start, WIDE, rows, 1)

        mine = pl.ds(pl.multiple_of(step * WIDE, WIDE), WIDE)
        at = pair_at(index)
        attend_pair(
            queries[mine, at],
            lambda piece: keys[piece, at],
            lambda piece: turned_values[at, piece],
            rows,
            bias,
            att_ref,
            inverse_ref,
            probs_ref,
        )

        @pl.when((step == pl.num_programs(0) - 1) & (index == pairs - 1))
        def _():
            for copy in copies:
                copy.wait()

    anywhere = pl.BlockSpec(memory_space=pl.ANY)
    return call(
        body,
        "self_forward",
        info,
        (rows // WIDE, pairs),
        [(embedded, whole(embedded.shape))]
        + own.resident()
        + other.resident()
        + weight.inputs(),
        [
            ((8, width), F32, whole((8, width))),
            ((rows, width), BF16, anywhere),
            ((2 * rows, 2 * width), BF16, anywhere),
            ((rows, width), BF16, anywhere),
        ]
        + attention_outputs(rows, width, 2 * rows),
        [
            pltpu.VMEM((rows, width), BF16),
            pltpu.VMEM((2 * rows, 2 * width), BF16),
            pltpu.VMEM((rows, width), BF16),
            pltpu.VMEM((width, 2 * rows), BF16),
            pltpu.VMEM((2 * rows, width), BF16),
            pltpu.VMEM((rows, WIDE), F32),
            weight.scratch(),
            pltpu.SemaphoreType.DMA((3,)),
        ],
        cost(32 * rows * rows * width, 12 * rows * width, 2 * rows * rows * width // HEAD_DIM),
    )


def cross_forward(info, att, tokens, own, other, weight, gains):
    rows, width = att.shape
    pairs = width // PAIR
    count = own.rows
    pieces = len(weight.arrays)

    def body(info_ref, att_ref, first_ref, last_ref, gain_ref, *refs):
        enc_refs, refs = refs[:4], refs[4:]
        weight_refs, refs = refs[:pieces], refs[pieces:]
        second_ref, cq_ref, ckv_out, catt_ref, inverse_ref, probs_ref, *refs = refs
        memory, turned_values, staged, scratch, sem = refs
        full = weight.load(info_ref, weight_refs, scratch, 2)
        step = pl.program_id(0)
        index = pl.program_id(1)
        copy = pltpu.make_async_copy(memory, ckv_out, sem)

        @pl.when(first_step(2))
        def _():
            for part, ref in enumerate(enc_refs):
                staged[part * count : (part + 1) * count, :] = ref[...]

            def project(part, carry):
                at = pl.ds(pl.multiple_of(part * count, count), count)
                memory[at, :] = dot(staged[at, :], full[:, 2 * width :]).astype(BF16)
                return carry

            lax.fori_loop(0, 4, project, 0)
            copy.start()
            turned_values[...] = memory[:, width:].T

        @pl.when(index == 0)
        def _():
            second_in = tokens.load(first_ref, last_ref).astype(F32) + dot(
                att_ref[...], full[:, :width]
            )
            second_ref[...] = second_in
            normed, _ = normalized(second_in)
            normed = (normed * gain_ref[4:5, :]).astype(BF16)
            cq_ref[...] = (dot(normed, full[:, width : 2 * width]) * HEAD_DIM**-0.5).astype(BF16)

        at = pair_at(index)
        attend_pair(
            cq_ref[:, at],
            lambda piece: memory[piece, at],
            lambda piece: turned_values[at, piece],
            4 * count,
            None,
            catt_ref,
            inverse_ref,
            probs_ref,
        )

        @pl.when((step == pl.num_programs(0) - 1) & (index == pairs - 1))
        def _():
            copy.wait()

    return call(
        body,
        "cross_forward",
        info,
        (rows // WIDE, pairs),
        [(att, rows_of(width, WIDE))]
        + tokens.inputs(WIDE)
        + [(gains, whole(gains.shape))]
        + own.resident()
        + other.resident()
        + weight.inputs(),
        [
            ((rows, width), F32, rows_of(width, WIDE)),
            ((rows, width), BF16, rows_of(width, WIDE)),
            ((4 * count, 2 * width), BF16, pl.BlockSpec(memory_space=pl.ANY)),
        ]
        + attention_outputs(rows, width, 4 * count),
        [
            pltpu.VMEM((4 * count, 2 * width), BF16),
            pltpu.VMEM((width, 4 * count), BF16),
            pltpu.VMEM((4 * count, width), BF16),
            weight.scratch(),
            pltpu.SemaphoreType.DMA,
        ],
        cost(16 * rows * rows * width, 12 * rows * width, rows * rows * width // HEAD_DIM),
    )


def backward_pair(qq, dd, oo, keys, values, turned_keys, inverses, probs, size, add_keys, add_values):
    products = (oo.astype(F32) * dd.astype(F32)).T
    row_head = lax.broadcasted_iota(jnp.int32, (PAIR, 1), 0) // HEAD_DIM
    lane_head = lax.broadcasted_iota(jnp.int32, (1, PAIR), 1) // HEAD_DIM

    def head(part, total_grad):
        qe = jnp.where(lane_head == part, qq, jnp.zeros_like(qq))
        de = jnp.where(lane_head == part, dd, jnp.zeros_like(dd))
        inner = jnp.sum(jnp.where(row_head == part, products, 0.0), axis=0, keepdims=True)
        inverse = inverses(part)
        column = jnp.broadcast_to(inverse, (8, inverse.shape[1])).T[:, 0:1]
        scaled = (de.astype(F32) * column).astype(BF16)
        grad = None
        for begin in range(0, keys.shape[0], size):
            into = slice(begin, min(begin + size, keys.shape[0]))
            p = probs(part, into)
            dprobs = dot(values[into, :], de, 1, 1)
            dscores = (p.astype(F32) * ((dprobs - inner) * inverse)).astype(BF16)
            add_values(into, dot(p, scaled))
            add_keys(into, dot(dscores, qe))
            term = dot(turned_keys[:, into], dscores)
            grad = term if grad is None else grad + term
        return total_grad + jnp.where(row_head == part, grad, 0.0)

    grad = lax.fori_loop(0, 2, head, jnp.zeros((PAIR, qq.shape[0]), F32))
    return (grad.T * HEAD_DIM**-0.5).astype(BF16)


def attention_backward(name, info, q, kv, att, datt, inverses, probs, splits, split, stores):
    rows, width = q.shape
    count = kv.shape[0]
    lanes = width // splits
    pairs = lanes // PAIR
    all_pairs = width // PAIR
    base = split * pairs

    def body(info_ref, q_ref, k_ref, v_ref, att_ref, datt_ref, inverse_ref, probs_ref, *refs):
        dq_ref, down_ref, dother_ref, turned_keys, acc = refs
        step = pl.program_id(0)
        index = pl.program_id(1)
        at = pair_at(index)
        vat = pair_at(index + pairs)

        @pl.when(step == 0)
        def _():
            turned_keys[at, :] = k_ref[...].T
            acc[:, at] = jnp.zeros((count, PAIR), F32)
            acc[:, vat] = jnp.zeros((count, PAIR), F32)

        def add_keys(into, value):
            acc[into, at] += value

        def add_values(into, value):
            acc[into, vat] += value

        dq_ref[...] = backward_pair(
            q_ref[...],
            datt_ref[...],
            att_ref[...],
            k_ref,
            v_ref,
            turned_keys[at, :],
            lambda part: inverse_ref[0, pl.ds(part, 1), :],
            lambda part, into: probs_ref[part, into, :],
            2048,
            add_keys,
            add_values,
        )

        @pl.when((step == pl.num_programs(0) - 1) & (index == pairs - 1))
        def _():
            stores(info_ref, acc, down_ref, dother_ref)

    pair_rows = pl.BlockSpec((WIDE, PAIR), lambda i, h, *_: (i, base + h))
    half = (count // 2, 2 * lanes)
    return call(
        body,
        name,
        info,
        (rows // WIDE, pairs),
        [
            (q, pair_rows),
            (kv, pl.BlockSpec((count, PAIR), lambda i, h, *_: (0, base + h))),
            (kv, pl.BlockSpec((count, PAIR), lambda i, h, *_: (0, all_pairs + base + h))),
            (att, pair_rows),
            (datt, pair_rows),
            (inverses, pl.BlockSpec((1, 2, WIDE), lambda i, h, *_: (base + h, 0, i))),
            (probs, pl.BlockSpec((2, count, WIDE), lambda i, h, *_: (base + h, 0, i))),
        ],
        [
            ((rows, lanes), BF16, pl.BlockSpec((WIDE, PAIR), lambda i, h, *_: (i, h))),
            (half, BF16, whole(half)),
            (half, BF16, whole(half)),
        ],
        [pltpu.VMEM((lanes, count), BF16), pltpu.VMEM((count, 2 * lanes), F32)],
        cost(32 * rows * count * lanes, 20 * rows * lanes + 2 * rows * count),
    )


def self_backward(info, q, kv, att, dat, inverses, probs, splits, split):
    quarter = q.shape[0] // 2

    def stores(info_ref, acc, down_ref, dother_ref):
        for target, core in ((down_ref, info_ref[2]), (dother_ref, 1 - info_ref[2])):
            for part in range(2):
                begin = pl.multiple_of(place_of(info_ref, core, part) * quarter, quarter)
                target[part * quarter : (part + 1) * quarter, :] = acc[
                    pl.ds(begin, quarter), :
                ].astype(BF16)

    return attention_backward(
        "self_backward", info, q, kv, att, dat, inverses, probs, splits, split, stores
    )


def cross_backward(info, cq, ckv, catt, dca, inverses, probs, splits, split):
    count = ckv.shape[0]

    def stores(info_ref, acc, down_ref, dother_ref):
        down_ref[...] = acc[: count // 2, :].astype(BF16)
        dother_ref[...] = acc[count // 2 :, :].astype(BF16)

    return attention_backward(
        "cross_backward", info, cq, ckv, catt, dca, inverses, probs, splits, split, stores
    )


def feed(info, catt, second_in, dy, cout, weights, gains, packing):
    rows, width = catt.shape
    hidden = weights.hidden
    cout_count = len(cout.arrays)
    feed_count = len(weights.arrays)
    packed = packing.outputs(width * width + 2 * width * hidden)

    def body(info_ref, catt_ref, second_ref, dy_first, dy_last, gain_ref, *refs):
        cout_refs, refs = refs[:cout_count], refs[cout_count:]
        feed_refs, refs = refs[:feed_count], refs[feed_count:]
        (
            out_first,
            out_last,
            dthird_ref,
            dca_ref,
            ggain_ref,
            *packed_refs,
            acc_cout,
            acc_widen,
            acc_narrow,
            cout_scratch,
            widen_scratch,
            narrow_scratch,
        ) = refs
        cout_full = cout.load(info_ref, cout_refs, cout_scratch)
        widen_full, narrow_full = weights.load(info_ref, feed_refs, (widen_scratch, narrow_scratch))
        step = pl.program_id(0)

        @pl.when(step == 0)
        def _():
            acc_cout[...] = jnp.zeros_like(acc_cout)
            acc_widen[...] = jnp.zeros_like(acc_widen)
            acc_narrow[...] = jnp.zeros_like(acc_narrow)
            ggain_ref[...] = jnp.zeros_like(ggain_ref)

        catt = catt_ref[...]
        dy_low = dy.load(dy_first, dy_last)
        gain = gain_ref[5:6, :]
        third = second_ref[...] + dot(catt, cout_full[...])
        normed, scale = normalized(third)
        normed_low = (normed * gain).astype(BF16)
        pre = dot(normed_low, widen_full[...])
        below = 0.5 * (1.0 + lax.erf(pre * math.sqrt(0.5)))
        bell = jnp.exp(-0.5 * pre * pre) * (1.0 / math.sqrt(2.0 * math.pi))
        act = (pre * below).astype(BF16)
        out = (third + dot(act, narrow_full[...])).astype(BF16)
        dact = dot(dy_low, narrow_full[...], 1, 1)
        dpre = (dact * (below + pre * bell)).astype(BF16)
        acc_narrow[...] += dot(act, dy_low, 0, 0)
        acc_widen[...] += dot(normed_low, dpre, 0, 0)
        dnormed = dot(dpre, widen_full[...], 1, 1)
        ggain_ref[...] += jnp.sum(dnormed * normed, axis=0, keepdims=True)
        dthird = dy_low.astype(F32) + norm_backward(dnormed * gain, normed, scale)
        dthird_ref[...] = dthird
        dc = dthird.astype(BF16)
        dca_ref[...] = dot(dc, cout_full[...], 1, 1).astype(BF16)
        acc_cout[...] += dot(catt, dc, 0, 0)
        store_half((out_first, out_last), out)

        @pl.when(step == pl.num_programs(0) - 1)
        def _():
            packing.store(
                info_ref, packed_refs, (acc_cout, acc_widen, acc_narrow), unroll=True
            )

    return call(
        body,
        "feed",
        info,
        rows // BLOCK,
        [(catt, rows_of(width)), (second_in, rows_of(width))]
        + dy.inputs(BLOCK)
        + [(gains, whole(gains.shape))]
        + cout.inputs()
        + weights.inputs(),
        half_outputs(rows, width, BLOCK)
        + [
            ((rows, width), F32, rows_of(width)),
            ((rows, width), BF16, rows_of(width)),
            ((1, width), F32, whole((1, width))),
        ]
        + packed,
        [
            pltpu.VMEM((width, width), F32),
            pltpu.VMEM((width, hidden), F32),
            pltpu.VMEM((hidden, width), F32),
            cout.scratch(),
        ]
        + weights.scratch(),
        cost(
            12 * rows * width * hidden, 24 * rows * width + 8 * width * hidden, 2 * rows * hidden
        ),
    )


def sum_low(own_ref, got_ref):
    return (own_ref[...].astype(F32) + got_ref[...].astype(F32)).astype(BF16)


def middle_backward(
    info, dcqs, second_in, dthird, att, owns, gots, encoder, weight, gains, packing
):
    rows, width = second_in.shape
    count = len(dcqs)
    lanes = width // count
    packed = packing.outputs(4 * width * width)
    pieces = len(weight.arrays)
    short = encoder.shape[0] // (rows // BLOCK)

    def body(info_ref, att_ref, second_ref, dthird_ref, gain_ref, enc_first, enc_last, *refs):
        dcq_refs, refs = refs[:count], refs[count:]
        own_refs, refs = refs[:count], refs[count:]
        got_refs, refs = refs[:count], refs[count:]
        weight_refs, refs = refs[:pieces], refs[pieces:]
        dsecond_ref, dat_ref, ggain_ref, *genc_refs = refs[:5]
        refs = refs[5:]
        packed_refs, refs = refs[: len(packed)], refs[len(packed) :]
        acc_query, acc_out, acc_memory, scratch = refs
        full = weight.load(info_ref, weight_refs, scratch)
        step = pl.program_id(0)

        @pl.when(step == 0)
        def _():
            acc_query[...] = jnp.zeros_like(acc_query)
            acc_out[...] = jnp.zeros_like(acc_out)
            acc_memory[...] = jnp.zeros_like(acc_memory)
            ggain_ref[...] = jnp.zeros_like(ggain_ref)

        dcq = jnp.concatenate([ref[...] for ref in dcq_refs], axis=1)
        gain = gain_ref[4:5, :]
        normed, scale = normalized(second_ref[...])
        normed_low = (normed * gain).astype(BF16)
        dnormed = dot(dcq, full[:, width : 2 * width], 1, 1)
        acc_query[...] += dot(normed_low, dcq, 0, 0)
        ggain_ref[...] += jnp.sum(dnormed * normed, axis=0, keepdims=True)
        dsecond = dthird_ref[...] + norm_backward(dnormed * gain, normed, scale)
        dsecond_ref[...] = dsecond
        da = dsecond.astype(BF16)
        dat_ref[...] = dot(da, full[:, :width], 1, 1).astype(BF16)
        acc_out[...] += dot(att_ref[...], da, 0, 0)

        turned = encoder.load(enc_first, enc_last).T
        grads = [sum_low(own, got) for own, got in zip(own_refs, got_refs)]
        dckv = jnp.concatenate(
            [g[:, :lanes] for g in grads] + [g[:, lanes:] for g in grads], axis=1
        )
        genc = dot(dckv, full[:, 2 * width :], 1, 1).astype(BF16)
        acc_memory[...] += dot(turned, dckv)
        store_half(genc_refs, genc)

        @pl.when(step == pl.num_programs(0) - 1)
        def _():
            packing.store(info_ref, packed_refs, (acc_query, acc_out, acc_memory))

    return call(
        body,
        "middle_backward",
        info,
        rows // BLOCK,
        [
            (att, rows_of(width)),
            (second_in, rows_of(width)),
            (dthird, rows_of(width)),
            (gains, whole(gains.shape)),
        ]
        + encoder.inputs(short)
        + [(a, rows_of(lanes)) for a in dcqs]
        + [(a, rows_of(2 * lanes, short)) for a in owns]
        + [(a, rows_of(2 * lanes, short)) for a in gots]
        + weight.inputs(),
        [
            ((rows, width), F32, rows_of(width)),
            ((rows, width), BF16, rows_of(width)),
            ((1, width), F32, whole((1, width))),
        ]
        + half_outputs(encoder.shape[0], width, short)
        + packed,
        [
            pltpu.VMEM((width, width), F32),
            pltpu.VMEM((width, width), F32),
            pltpu.VMEM((width, 2 * width), F32),
            weight.scratch(),
        ],
        cost(16 * rows * width * width, 20 * rows * width),
    )


VECTORS = 8


def project_backward(
    info, tokens, normed, dqs, owns, gots, dsecond, mods, ggains, embedded, gencs, weight, packing
):
    rows, width = tokens.shape
    count = len(dqs)
    lanes = width // count
    packed = packing.outputs(3 * width * width, VECTORS)
    sent = (rows // 2 + gencs[0].shape[0], width)
    pieces = len(weight.arrays)

    def body(info_ref, first_ref, last_ref, normed_ref, dsecond_ref, mod_ref, *refs):
        second_gain, third_gain, embedded_ref, *genc_refs = refs[:5]
        refs = refs[5:]
        dq_refs, refs = refs[:count], refs[count:]
        own_refs, refs = refs[:count], refs[count:]
        got_refs, refs = refs[:count], refs[count:]
        weight_refs, refs = refs[:pieces], refs[pieces:]
        gfirst_ref, glast_ref, vectors_ref, *packed_refs, acc, sums, scratch = refs
        full = weight.load(info_ref, weight_refs, scratch)
        step = pl.program_id(0)

        @pl.when(step == 0)
        def _():
            acc[...] = jnp.zeros_like(acc)
            sums[...] = jnp.zeros_like(sums)

        turned = normed_ref[...].T
        dkvs = [sum_low(own, got) for own, got in zip(own_refs, got_refs)]
        grads = jnp.concatenate(
            [ref[...] for ref in dq_refs]
            + [dkv[:, :lanes] for dkv in dkvs]
            + [dkv[:, lanes:] for dkv in dkvs],
            axis=1,
        )
        acc[...] += dot(turned, grads)
        dnormed = dot(grads, full[...], 1, 1)
        unit, scale = normalized(tokens.load(first_ref, last_ref).astype(F32))
        sums[0:1, :] += jnp.sum(dnormed * unit, axis=0, keepdims=True)
        sums[1:2, :] += jnp.sum(dnormed, axis=0, keepdims=True)
        gtokens = (
            dsecond_ref[...] + norm_backward(dnormed * mod_ref[0:1, :], unit, scale)
        ).astype(BF16)
        steps = rows // BLOCK // 2
        at = pl.ds(pl.multiple_of(lax.rem(step, steps) * BLOCK, BLOCK), BLOCK)
        for half, ref in enumerate((gfirst_ref, glast_ref)):

            @pl.when(step // steps == half)
            def _(half=half, ref=ref):
                ref[at, :] = gtokens
                ref[rows // 2 :, :] = genc_refs[half][...]

        @pl.when(step == pl.num_programs(0) - 1)
        def _():
            vectors = jnp.concatenate(
                [
                    sums[0:1, :] * mod_ref[2:3, :],
                    second_gain[...],
                    third_gain[...],
                    sums[0:1, :] * mod_ref[3:4, :],
                    sums[1:2, :],
                    embedded_ref[0:1, :].astype(F32),
                    jnp.zeros((VECTORS - 6, width), F32),
                ],
                axis=0,
            )
            vectors_ref[...] = vectors
            packing.store(info_ref, packed_refs, (acc,), vectors)

    return call(
        body,
        "project_backward",
        info,
        rows // BLOCK,
        tokens.inputs(BLOCK)
        + [
            (normed, rows_of(width)),
            (dsecond, rows_of(width)),
            (mods, whole(mods.shape)),
            (ggains[0], whole((1, width))),
            (ggains[1], whole((1, width))),
            (embedded, whole(embedded.shape)),
            (gencs[0], whole(gencs[0].shape)),
            (gencs[1], whole(gencs[1].shape)),
        ]
        + [(a, rows_of(lanes)) for a in dqs]
        + [(a, rows_of(2 * lanes)) for a in owns]
        + [(a, rows_of(2 * lanes)) for a in gots]
        + weight.inputs(),
        [(sent, BF16, whole(sent))] * 2
        + [((VECTORS, width), F32, whole((VECTORS, width)))]
        + packed,
        [pltpu.VMEM((width, 3 * width), F32), pltpu.VMEM((8, width), F32), weight.scratch()],
        cost(12 * rows * width * width, 20 * rows * width),
    )


def join_columns(info, parts):
    size = parts[0].shape[0] - VECTORS
    shape = (size + len(parts) * VECTORS, parts[0].shape[1])

    def body(info_ref, *refs):
        *part_refs, out_ref = refs
        total = part_refs[0][:size, :].astype(F32)
        for ref in part_refs[1:]:
            total = total + ref[:size, :].astype(F32)
        out_ref[:size, :] = total.astype(BF16)
        for index, ref in enumerate(part_refs):
            begin = size + index * VECTORS
            out_ref[begin : begin + VECTORS, :] = ref[size:, :]

    return call(
        body,
        "join_columns",
        info,
        1,
        [(part, whole(part.shape)) for part in parts],
        [(shape, BF16, whole(shape))],
        [],
        cost(0, 4 * size * shape[1]),
    )[0]


def finish(info, parts, size, shard):
    width = parts[0].shape[1]
    count = parts[0].shape[0] - size
    devices = len(parts) * count // VECTORS

    def body(info_ref, *refs):
        part_refs = refs[: len(parts)]
        ginput_ref, gtime_ref, ggains_ref, listed, turned = refs[len(parts) :]
        for block in range(size // shard):
            rows = slice(block * shard, (block + 1) * shard)
            terms = [ref[rows, :].astype(F32) for ref in part_refs]
            ginput_ref[:, block * width : (block + 1) * width] = (terms[0] + terms[1]) + (
                terms[2] + terms[3]
            )
        for turn, ref in enumerate(part_refs):
            place = lax.bitwise_xor(info_ref[5], turn)
            listed[pl.ds(pl.multiple_of(place * count, count), count), :] = ref[size:, :]
        vectors = listed[...]
        column = lax.broadcasted_iota(jnp.int32, (devices, devices * VECTORS), 1)
        row = lax.broadcasted_iota(jnp.int32, (devices, devices * VECTORS), 0)

        def pick(kind):
            chosen = jnp.where(column == row * VECTORS + kind, 1.0, 0.0).astype(BF16)
            return dot(chosen, vectors)

        chosen = jnp.where(lax.rem(column, VECTORS) == row, 1.0, 0.0).astype(BF16)
        turned[...] = jnp.concatenate([0.5 * pick(5), dot(chosen, vectors)], axis=0).T
        place = (2 * info_ref[4] + info_ref[2]) * shard
        part = turned[pl.ds(pl.multiple_of(place, shard), shard), :]
        grads = jnp.concatenate([pick(3), pick(4)], axis=1).astype(BF16)
        gtime_ref[...] = dot(part[:, :devices].astype(BF16), grads)
        ggains_ref[...] = part.T[devices : devices + 3, :]

    return call(
        body,
        "finish",
        info,
        1,
        [(part, whole(part.shape)) for part in parts],
        [
            ((shard, 3 * width), F32, whole((shard, 3 * width))),
            ((shard, 2 * width), F32, whole((shard, 2 * width))),
            ((3, shard), F32, whole((3, shard))),
        ],
        [pltpu.VMEM((devices * VECTORS, width), BF16), pltpu.VMEM((width, 2 * devices), F32)],
        cost(8 * devices * count * width, 12 * size * width),
    )


def permutations(seq_count, fsdp_count):
    columns = fsdp_count // 2

    def at(seq, fsdp):
        return seq * fsdp_count + fsdp

    def pairs(move):
        return [
            (at(seq, fsdp), at(*move(seq, fsdp)))
            for seq in range(seq_count)
            for fsdp in range(fsdp_count)
        ]

    def home(turn):
        def move(seq, fsdp):
            y, x = divmod(seq, 2)
            column, core = divmod(fsdp, 2)
            return 2 * core + (x ^ turn), 2 * column + y

        return move

    shift = {
        r: pairs(lambda seq, fsdp, r=r: (seq, (fsdp + 2 * r) % fsdp_count))
        for r in range(1, columns)
    }
    cross = {t: pairs(lambda seq, fsdp, t=t: (seq ^ t, fsdp)) for t in range(1, seq_count)}
    swap = pairs(lambda seq, fsdp: (seq, fsdp ^ 1))
    return pairs(home(0)), pairs(home(1)), swap, shift, cross


def reverse(pairs):
    return [(target, source) for source, target in pairs]


def after(values, signal):
    return lax.optimization_barrier((values, signal))[0]


class Direct:
    def __init__(self, perms, seq, fsdp, columns):
        self.same, self.crossed, self.swap_pairs, self.shifts, self.crosses = perms
        self.seq = seq
        self.core = fsdp % 2
        self.z = fsdp // 2
        self.columns = columns

    def permute(self, values, pairs):
        return lax.ppermute(values, AXES, pairs)

    def swap(self, values):
        return self.permute(values, self.swap_pairs)

    def along_z(self, values):
        return [values] + [
            self.permute(values, self.shifts[r]) for r in range(1, self.columns)
        ]

    def both_cores(self, pieces):
        return pieces + [self.swap(piece) for piece in pieces]

    def core_sum(self, mine, away, signal=()):
        got = after(self.swap(away), signal)
        return [
            (mine[r].astype(F32) + got[r].astype(F32)).astype(BF16) for r in range(self.columns)
        ]

    def z_parts(self, shards):
        return [self.permute(shards[r], self.shifts[r]) for r in range(1, self.columns)]

    def z_sum(self, shards, got, signal=()):
        total = shards[0].astype(F32)
        for part in after(got, signal):
            total = total + part.astype(F32)
        return lax.optimization_barrier(total.astype(BF16))

    def add(self, first, second):
        return lax.optimization_barrier((first.astype(F32) + second.astype(F32)).astype(BF16))

    def cross(self, values, turn):
        return self.permute(values, self.crosses[turn])


SPLITS = 2


def time_embedding(step_values, model_width):
    half_width = model_width // 2
    frequency = jnp.exp(-math.log(10000.0) * jnp.arange(half_width, dtype=F32) / half_width)
    angles = step_values.astype(F32)[:, None] * frequency[None, :]
    return jnp.concatenate([jnp.sin(angles), jnp.cos(angles)], axis=-1).astype(BF16)


def exact_dot(left, right):
    return lax.dot_general(
        left,
        right,
        (((0,), (0,)), ((), ())),
        precision=lax.Precision.HIGHEST,
        preferred_element_type=F32,
    )


def make(seq_count, fsdp_count):
    perms = permutations(seq_count, fsdp_count)
    same, crossed = perms[:2]
    columns = fsdp_count // 2

    def on_device(
        tokens,
        encoder_states,
        lengths,
        timesteps,
        time_weight,
        self_input,
        self_output,
        cross_query,
        cross_memory,
        cross_output,
        widen_weight,
        narrow_weight,
        norm_gains,
        cotangent,
    ):
        width = tokens.shape[2]
        hidden = widen_weight.shape[1]
        shard = time_weight.shape[0]
        seq = lax.axis_index("seq")
        fsdp = lax.axis_index("fsdp")
        core = fsdp % 2
        side = seq % 2
        direct = Direct(perms, seq, fsdp, columns) if columns == 4 else None

        def send_work(values):
            mine = lax.dynamic_index_in_dim(values, side, 0, keepdims=False)
            others = lax.dynamic_index_in_dim(values, 1 - side, 0, keepdims=False)
            return [lax.ppermute(mine, AXES, same), lax.ppermute(others, AXES, crossed)]

        def send_home(halves):
            return [
                lax.ppermute(halves[0], AXES, reverse(same)),
                lax.ppermute(halves[1], AXES, reverse(crossed)),
            ]

        def at_home(parts, kind):
            first = jnp.where(side == 0, parts[0], parts[1])
            second = jnp.where(side == 0, parts[1], parts[0])
            return jnp.stack([first, second], axis=0).astype(kind)

        def gather(weight, axis=0):
            return lax.all_gather(weight, "fsdp", axis=axis, tiled=True)

        def swap(values):
            return lax.ppermute(values, AXES, perms[2])

        packing = Packing(fsdp_count, direct is not None, width)
        token_rows, encoder_rows = tokens.shape[1], encoder_states.shape[1]
        numbers = jnp.concatenate([lengths, timesteps[:, None]], axis=1)
        numbers_other = swap(numbers)
        own_row = jnp.where(core == seq // 2, numbers, numbers_other)
        own_row = lax.dynamic_slice_in_dim(own_row, side, 1, 0)
        step_value = own_row[0, 3:4]
        place = lax.broadcasted_iota(jnp.int32, (8,), 0)
        info = jnp.where(place == 1, own_row[0, 1], 0) + jnp.where(place <= 1, own_row[0, 0], 0)
        for index, value in enumerate((core, side, fsdp // 2, seq)):
            info = jnp.where(place == index + 2, value, info)
        embedded = jnp.pad(time_embedding(step_value, width), ((0, 15), (0, 0)))

        turned = jnp.pad(norm_gains.T, ((0, 0), (0, 128 - norm_gains.shape[0])))
        first = jnp.concatenate([self_input, time_weight, turned], axis=1)
        first_mine = direct.along_z(first) if direct else [(), ()]
        own = send_work(jnp.concatenate([tokens, encoder_states], axis=1))
        other = [swap(part) for part in after(own, first_mine[1:])]
        work_tokens = Halves(own, 0, token_rows)
        other_tokens = Halves(other, 0, token_rows)
        work_encoder = Halves(own, token_rows, encoder_rows)
        other_encoder = Halves(other, token_rows, encoder_rows)

        ready = info
        rest = jnp.concatenate([self_output, cross_query, cross_memory, cross_output], axis=1)
        if direct:
            first = direct.both_cores(first_mine)
            wide = widen_weight.reshape(shard, hidden // width, width).transpose(1, 0, 2)
            large = jnp.concatenate([wide.reshape(-1, width), narrow_weight], axis=0)
            rest, large = after((rest, large), (own, info, embedded))
            rest_mine = direct.along_z(rest)
            small_other = [swap(rest)]
            large_mine = direct.along_z(large)
            large_other = [swap(large)]
            ready = after(info, (small_other, large_other))
        else:
            first = [gather(first)]
            rest = [gather(rest)]
            feed_weights = FeedWeights([gather(widen_weight), gather(narrow_weight)], hidden)

        mods, q, kv, normed_first, att, inverses, probs = self_forward(
            ready, work_tokens, other_tokens, embedded, Weight(first, 0, first[0].shape[1])
        )
        ready = info
        if direct:
            rest_mine[1:], large_mine[:2] = after((rest_mine[1:], large_mine[:2]), att)
            small_other += [swap(part) for part in rest_mine[1:]]
            rest = rest_mine + small_other
            large_other.append(swap(large_mine[1]))
            ready = after(info, large_other)
        input_weight = Weight(first, 0, 3 * width)
        cross_weight = Weight(rest, 0, 4 * width)
        cout_weight = Weight(rest, 4 * width, width)
        dy_parts = send_work(after(cotangent, att))
        second_in, cq, ckv, catt, cross_inverses, cross_probs = cross_forward(
            ready, att, work_tokens, work_encoder, other_encoder, cross_weight, mods
        )
        work_dy = Halves(after(dy_parts, catt), 0, token_rows)
        if direct:
            large_mine[2:] = after(large_mine[2:], catt)
            large_other += [swap(part) for part in large_mine[2:]]
            feed_weights = FeedWeights(large_mine + large_other, hidden)
        out_first, out_last, dthird, dca, ggain_third, *packed_feed = feed(
            info, catt, second_in, work_dy, cout_weight, feed_weights, mods, packing
        )
        layer_out = (out_first, out_last)
        out_parts = send_home(layer_out)

        def backward_cross(split, ready):
            return cross_backward(
                ready, cq, ckv, catt, dca, cross_inverses, cross_probs, SPLITS, split
            )

        def backward_self(split, ready):
            return self_backward(ready, q, kv, att, dat, inverses, probs, SPLITS, split)

        crosses = [backward_cross(0, info)]
        out_parts = after(out_parts, crosses[0][0])
        chip_feed = direct.core_sum(*packed_feed, crosses[0][0]) if direct else ()
        crosses.append(backward_cross(1, after(info, (chip_feed, out_parts))))
        dcqs, dckvs, dckv_others = zip(*crosses)
        dckv_gots = [swap(a) for a in dckv_others]
        feed_parts = direct.z_parts(chip_feed) if direct else [()]
        dsecond, dat, ggain_second, *genc = middle_backward(
            after(info, (feed_parts[0], dcqs)),
            dcqs,
            second_in,
            dthird,
            att,
            dckvs,
            dckv_gots,
            work_encoder,
            cross_weight,
            mods,
            packing,
        )
        genc, packed_middle = genc[:2], genc[2:]
        selfs = [backward_self(0, after(info, packed_middle))]
        if direct:
            column_feed = direct.z_sum(chip_feed, feed_parts, selfs[0][0])
            chip_middle = direct.core_sum(*packed_middle, selfs[0][0])
            selfs.append(backward_self(1, after(info, (column_feed, chip_middle))))
            middle_parts = after(direct.z_parts(chip_middle), selfs[1][0])
            row_feed = after(direct.cross(column_feed, 1), selfs[1][0])
            row_feed = direct.add(column_feed, row_feed)
            column_middle = direct.z_sum(chip_middle, middle_parts)
        else:
            selfs.append(backward_self(1, info))
        dqs, dkvs, dkv_others = zip(*selfs)
        dkv_others = list(dkv_others)
        if direct:
            dkv_others[1] = after(dkv_others[1], (column_middle, row_feed))
        dkv_gots = [swap(a) for a in dkv_others]
        first_grad, last_grad, vectors, *packed_input = project_backward(
            info,
            work_tokens,
            normed_first,
            dqs,
            dkvs,
            dkv_gots,
            dsecond,
            mods,
            (ggain_second, ggain_third),
            embedded,
            genc,
            input_weight,
            packing,
        )
        gtokens = (first_grad, last_grad)
        if direct:
            got_row = after(direct.cross(row_feed, 2), gtokens)
            row_middle = after(direct.cross(column_middle, 1), gtokens)
            away = after(packed_input[1], (got_row, row_middle))
            chip = direct.core_sum(packed_input[0], away)
            row_middle = direct.add(column_middle, row_middle)
            gots = direct.z_parts(chip)
            token_parts = after(send_home(after(gtokens, chip)), gots)
            ready = after(info, token_parts)
            reduced_feed = row_feed.astype(F32) + got_row.astype(F32)
            size = chip[0].shape[0] - VECTORS
            joined = join_columns(ready, [chip[0]] + gots)
            middle_got = direct.cross(after(row_middle, joined), 2)
            parts = [joined] + [direct.cross(joined, turn) for turn in (1, 2, 3)]
            reduced_middle = row_middle.astype(F32) + middle_got.astype(F32)
            reduced_input, gtime, ggains = finish(info, parts, size, shard)
        else:

            def reduce(packed):
                part = lax.psum_scatter(packed[0], "fsdp", scatter_dimension=0, tiled=True)
                return lax.psum(part[0], "seq").astype(F32)

            reduced_input = reduce(packed_input)
            reduced_input = unpack_rows(reduced_input, 0, shard, 3 * width)
            reduced_middle = reduce(packed_middle)
            reduced_feed = reduce(packed_feed)
            token_parts = send_home(gtokens)
            ggains = lax.psum(vectors[:3], AXES)
            ggains = lax.dynamic_slice_in_dim(ggains, fsdp * shard, shard, 1)
            by_group = lax.all_gather(vectors[3:5], AXES, axis=0)
            by_group = by_group.reshape(seq_count, columns, 2, 2 * width).sum(axis=2)
            by_group = by_group.transpose(1, 0, 2).reshape(-1, 2 * width)
            every = time_embedding(gather(timesteps), width)
            own_columns = lax.dynamic_slice_in_dim(every, fsdp * shard, shard, 1)
            gtime = exact_dot(own_columns.astype(F32), by_group)

        tall = narrow_weight.shape[0]
        return (
            at_home(out_parts, BF16),
            at_home([part[:token_rows] for part in token_parts], F32),
            at_home([part[token_rows:] for part in token_parts], F32),
            gtime,
            reduced_input,
            unpack_rows(reduced_middle, shard, shard, width),
            unpack_rows(reduced_middle, 0, shard, width),
            unpack_rows(reduced_middle, 2 * shard, shard, 2 * width),
            unpack_rows(reduced_feed, 0, shard, width),
            unpack_rows(reduced_feed, shard, shard, hidden),
            unpack_rows(reduced_feed, shard * (1 + hidden // width), tall, width),
            ggains,
        )

    return on_device


def solution(mesh):
    rows = P("fsdp", "seq", None)
    weight = P("fsdp", None)
    in_specs = (rows, rows, P("fsdp", None), P("fsdp")) + (weight,) * 8 + (P(None, "fsdp"), rows)
    out_specs = (rows,) * 3 + (weight,) * 8 + (P(None, "fsdp"),)
    return jax.shard_map(
        make(mesh.shape["seq"], mesh.shape["fsdp"]),
        mesh=mesh,
        in_specs=in_specs,
        out_specs=out_specs,
        check_vma=False,
    )
```

```python
import math

import jax
import jax.numpy as jnp
from jax import lax
from jax.experimental import pallas as pl
from jax.experimental.pallas import tpu as pltpu
from jax.sharding import PartitionSpec as P


HEAD_DIM = 64
PAIR = 2 * HEAD_DIM
EPS = 1e-05
NEG = -1e30
F32 = jnp.float32
BF16 = jnp.bfloat16
AXES = ("seq", "fsdp")
VMEM_LIMIT = 60 * 2**20
BLOCK = 256
WIDE = 512


def dot(left, right, left_dim=1, right_dim=0):
    return lax.dot_general(
        left, right, (((left_dim,), (right_dim,)), ((), ())), preferred_element_type=F32
    )


def whole(shape):
    return pl.BlockSpec(shape, lambda *_: (0,) * len(shape))


def rows_of(width, block=BLOCK):
    return pl.BlockSpec((block, width), lambda i, *_: (i, 0))


def params():
    return pltpu.CompilerParams(vmem_limit_bytes=VMEM_LIMIT)


def cost(flops, moved, transcendentals=0):
    return pl.CostEstimate(
        flops=int(flops), bytes_accessed=int(moved), transcendentals=int(transcendentals)
    )


def normalized(values):
    average = jnp.mean(values, axis=-1, keepdims=True)
    centred = values - average
    spread = jnp.mean(centred * centred, axis=-1, keepdims=True)
    scale = lax.rsqrt(spread + EPS)
    return centred * scale, scale


def norm_backward(upstream, normed, scale):
    mean_up = jnp.mean(upstream, axis=-1, keepdims=True)
    mean_both = jnp.mean(upstream * normed, axis=-1, keepdims=True)
    return (upstream - mean_up - normed * mean_both) * scale


def lane_is(part):
    lane = lax.broadcasted_iota(jnp.int32, (1, PAIR), 1)
    return lane < HEAD_DIM if part == 0 else lane >= HEAD_DIM


def half_of(values, part):
    return jnp.where(lane_is(part), values, jnp.zeros_like(values))


def pair_at(index):
    return pl.ds(pl.multiple_of(index * PAIR, PAIR), PAIR)


def first_step(dims=1):
    first = pl.program_id(0) == 0
    return first if dims == 1 else first & (pl.program_id(1) == 0)


class Weight:
    def __init__(self, pieces, start, width):
        self.arrays = pieces
        self.start = start
        self.width = width

    @property
    def split(self):
        return len(self.arrays) > 1

    @property
    def rows(self):
        return len(self.arrays) * self.arrays[0].shape[0]

    @property
    def aligned(self):
        return self.start % self.width == 0

    def inputs(self):
        if not self.aligned:
            return [(array, whole(array.shape)) for array in self.arrays]
        place = self.start // self.width
        shape = (self.arrays[0].shape[0], self.width)
        return [(array, pl.BlockSpec(shape, lambda *_: (0, place))) for array in self.arrays]

    def scratch(self):
        return pltpu.VMEM((self.rows, self.width) if self.split else (16, 128), BF16)

    def load(self, info, refs, scratch, dims=1):
        if not self.split:
            return refs[0]
        columns = slice(0, self.width) if self.aligned else slice(self.start, self.start + self.width)

        @pl.when(first_step(dims))
        def _():
            count = len(refs) // 2
            shard = refs[0].shape[0]
            for index, ref in enumerate(refs):
                turn, shift = divmod(index, count)
                core = info[2] if turn == 0 else 1 - info[2]
                owner = lax.rem(info[4] - shift + count, count)
                start = pl.multiple_of((2 * owner + core) * shard, shard)
                scratch[pl.ds(start, shard), :] = ref[:, columns]

        return scratch


class Halves:
    def __init__(self, arrays, start, rows):
        self.arrays = arrays
        self.start = start
        self.rows = rows
        self.shape = (2 * rows, arrays[0].shape[1])

    def inputs(self, block):
        width = self.shape[1]
        count = self.rows // block
        base = self.start // block
        return [
            (
                self.arrays[0],
                pl.BlockSpec((block, width), lambda i, *_: (base + jnp.minimum(i, count - 1), 0)),
            ),
            (
                self.arrays[1],
                pl.BlockSpec((block, width), lambda i, *_: (base + jnp.maximum(i - count, 0), 0)),
            ),
        ]

    def resident(self):
        place = self.start // self.rows
        spec = pl.BlockSpec((self.rows, self.shape[1]), lambda *_: (place, 0))
        return [(array, spec) for array in self.arrays]

    def load(self, first_ref, second_ref):
        half = pl.num_programs(0) // 2
        return jnp.where(pl.program_id(0) < half, first_ref[...], second_ref[...])


def half_outputs(rows, width, block):
    count = rows // block // 2
    half = (rows // 2, width)
    return [
        (half, BF16, pl.BlockSpec((block, width), lambda i, *_: (jnp.minimum(i, count - 1), 0))),
        (half, BF16, pl.BlockSpec((block, width), lambda i, *_: (jnp.maximum(i - count, 0), 0))),
    ]


def store_half(refs, value):
    first = pl.program_id(0) < pl.num_programs(0) // 2

    @pl.when(first)
    def _():
        refs[0][...] = value

    @pl.when(jnp.logical_not(first))
    def _():
        refs[1][...] = value


class FeedWeights:
    def __init__(self, arrays, hidden):
        self.arrays = arrays
        self.hidden = hidden

    @property
    def split(self):
        return len(self.arrays) > 2

    def inputs(self):
        return [(array, whole(array.shape)) for array in self.arrays]

    def scratch(self):
        if not self.split:
            return [pltpu.VMEM((16, 128), BF16)] * 2
        width = self.arrays[0].shape[1]
        return [pltpu.VMEM((width, self.hidden), BF16), pltpu.VMEM((self.hidden, width), BF16)]

    def load(self, info, refs, scratch):
        if not self.split:
            return refs
        widen, narrow = scratch

        @pl.when(pl.program_id(0) == 0)
        def _():
            count = len(refs) // 2
            rows, width = refs[0].shape
            blocks = self.hidden // width
            tall = rows // 2
            short = tall // blocks
            for index, ref in enumerate(refs):
                turn, shift = divmod(index, count)
                core = info[2] if turn == 0 else 1 - info[2]
                owner = 2 * lax.rem(info[4] - shift + count, count) + core
                start = pl.multiple_of(owner * short, short)
                for block in range(blocks):
                    widen[pl.ds(start, short), block * width : (block + 1) * width] = ref[
                        block * short : (block + 1) * short, :
                    ]
                start = pl.multiple_of(owner * tall, tall)
                narrow[pl.ds(start, tall), :] = ref[tall:, :]

        return widen, narrow


class Packing:
    def __init__(self, shards, direct, width):
        self.shards = shards
        self.direct = direct
        self.width = width

    def outputs(self, elements, extra=0):
        rows = elements // (self.shards * self.width)
        if self.direct:
            rows += extra
        if self.direct:
            shape = (self.shards // 2, rows, self.width)
            return [(shape, BF16, whole(shape))] * 2
        shape = (self.shards, rows, self.width)
        return [(shape, BF16, whole(shape))]

    def store(self, info, packed, grads, vectors=None, unroll=False):
        def put(ref, slot, owner):
            offset = 0
            for grad in grads:
                rows = grad.shape[0] // self.shards
                start = owner * rows
                if not isinstance(owner, int):
                    start = pl.multiple_of(start, rows)
                for block in range(grad.shape[1] // self.width):
                    columns = slice(block * self.width, (block + 1) * self.width)
                    ref[slot, offset : offset + rows, :] = grad[pl.ds(start, rows), columns].astype(
                        BF16
                    )
                    offset += rows
            if vectors is not None and self.direct:
                ref[slot, offset:, :] = vectors.astype(BF16)

        if self.direct:
            count = self.shards // 2
            for ref, core in ((packed[0], info[2]), (packed[1], 1 - info[2])):

                def one(shift, carry, ref=ref, core=core):
                    put(ref, shift, 2 * lax.rem(info[4] + shift, count) + core)
                    return carry

                if unroll:
                    for shift in range(count):
                        one(shift, 0)
                else:
                    lax.fori_loop(0, count, one, 0)
        else:
            for shard in range(self.shards):
                put(packed[0], shard, shard)


def unpack_rows(packed, offset, rows, columns):
    width = packed.shape[1]
    blocks = columns // width
    parts = [packed[offset + b * rows : offset + (b + 1) * rows] for b in range(blocks)]
    return jnp.concatenate(parts, axis=1) if blocks > 1 else parts[0]


def call(body, name, info, grid, inputs, outputs, scratch, estimate):
    return pl.pallas_call(
        body,
        name=name,
        grid_spec=pltpu.PrefetchScalarGridSpec(
            num_scalar_prefetch=1,
            grid=grid if isinstance(grid, tuple) else (grid,),
            in_specs=[spec for _, spec in inputs],
            out_specs=[spec for _, _, spec in outputs],
            scratch_shapes=scratch,
        ),
        out_shape=[jax.ShapeDtypeStruct(shape, kind) for shape, kind, _ in outputs],
        compiler_params=params(),
        cost_estimate=estimate,
    )(info, *[array for array, _ in inputs])


def block_start(info, block_index, block, quarter):
    per_quarter = quarter // block
    first = block_index < per_quarter
    place = jnp.where(first, info[3], 1 - info[3])
    return (2 * info[2] + place) * quarter + lax.rem(block_index, per_quarter) * block


def forbidden(info, start, block, half, queries_dim):
    keys_dim = 1 - queries_dim
    qshape = [1, 1]
    qshape[queries_dim] = block
    kshape = [1, 1]
    kshape[keys_dim] = half
    qpos = start + lax.broadcasted_iota(jnp.int32, tuple(qshape), queries_dim)
    kpos = half + lax.broadcasted_iota(jnp.int32, tuple(kshape), keys_dim)
    first, second = info[0], info[1]
    low = jnp.where((qpos >= first) & (qpos < second), second, first)
    high = jnp.where(qpos >= second, second, 2 * half)
    return jnp.where((kpos >= low) & (kpos < high), NEG, 0.0)


def key_specs(array, lanes, split, width):
    rows = array.shape[0]
    count = width // lanes
    return [
        (array, pl.BlockSpec((rows, lanes), lambda *_: (0, split))),
        (array, pl.BlockSpec((rows, lanes), lambda *_: (0, count + split))),
    ]


def attention_sums(low, high):
    return (low > 1e-20) & (high < 1e30)


def attend_pair(qq, keys_at, turned_values, free, bias, att_ref, inverse_ref, probs_ref):
    count = probs_ref.shape[1]
    row_head = lax.broadcasted_iota(jnp.int32, (PAIR, 1), 0) // HEAD_DIM
    lane_head = lax.broadcasted_iota(jnp.int32, (1, PAIR), 1) // HEAD_DIM
    turned_at = turned_values(slice(0, count))

    def head(part):
        qe = jnp.where(lane_head == part, qq, jnp.zeros_like(qq))
        total = None
        out = None
        for piece in (slice(0, free), slice(free, count)):
            if piece.start == piece.stop:
                continue
            s = dot(keys_at(piece), qe, 1, 1)
            p = jnp.exp(s if piece.start == 0 else s + bias[...])
            low = p.astype(BF16)
            probs_ref[part, piece, :] = low
            term = jnp.sum(p, axis=0, keepdims=True)
            attended = dot(turned_at[:, piece], low)
            total = term if total is None else total + term
            out = attended if out is None else out + attended
        return out, total

    def one(part, carry):
        out, total = head(part)
        inverse = 1.0 / total
        inverse_ref[0, pl.ds(part, 1), :] = inverse
        joined, low, high = carry
        joined = joined + jnp.where(row_head == part, out * inverse, 0.0)
        return joined, jnp.minimum(low, total), jnp.maximum(high, total)

    ones = jnp.ones((1, qq.shape[0]), F32)
    out, low, high = lax.fori_loop(0, 2, one, (jnp.zeros((PAIR, qq.shape[0]), F32), ones, ones))
    att_ref[...] = out.T.astype(BF16)
    low, high = jnp.min(low), jnp.max(high)

    @pl.when(jnp.logical_not((low > 1e-20) & (high < 1e30)))
    def _():
        chunk = BLOCK // 2
        queries = qq.shape[0]

        def again(part, carry):
            qe = jnp.where(lane_head == part, qq, jnp.zeros_like(qq))

            def scores(index):
                at = pl.ds(pl.multiple_of(index * chunk, chunk), chunk)
                s = dot(keys_at(at), qe, 1, 1)
                if free == count:
                    return at, s
                begin = jnp.maximum(index * chunk - free, 0)
                part_bias = bias[pl.ds(pl.multiple_of(begin, chunk), chunk), :]
                return at, s + jnp.where(index * chunk >= free, part_bias, 0.0)

            def largest(index, top):
                return jnp.maximum(top, jnp.max(scores(index)[1], axis=0, keepdims=True))

            top = lax.fori_loop(
                0, count // chunk, largest, jnp.full((1, queries), -jnp.inf, F32)
            )

            def add(index, sums):
                at, s = scores(index)
                p = jnp.exp(s - top)
                low = p.astype(BF16)
                probs_ref[part, at, :] = low
                return (
                    sums[0] + jnp.sum(p, axis=0, keepdims=True),
                    sums[1] + dot(turned_values(at), low),
                )

            total, out = lax.fori_loop(
                0,
                count // chunk,
                add,
                (jnp.zeros((1, queries), F32), jnp.zeros((PAIR, queries), F32)),
            )
            inverse = 1.0 / total
            inverse_ref[0, pl.ds(part, 1), :] = inverse
            return carry + jnp.where(row_head == part, out * inverse, 0.0)

        out = lax.fori_loop(0, 2, again, jnp.zeros((PAIR, queries), F32))
        att_ref[...] = out.T.astype(BF16)


def attention_outputs(rows, width, count):
    pairs = width // PAIR
    return [
        ((rows, width), BF16, pl.BlockSpec((WIDE, PAIR), lambda i, h, *_: (i, h))),
        ((pairs, 2, rows), F32, pl.BlockSpec((1, 2, WIDE), lambda i, h, *_: (h, 0, i))),
        ((2 * pairs, count, rows), BF16, pl.BlockSpec((2, count, WIDE), lambda i, h, *_: (h, 0, i))),
    ]


def place_of(info, core, part):
    return 2 * core + (info[3] if part == 0 else 1 - info[3])


def self_forward(info, own, other, embedded, weight):
    rows, width = own.shape
    pairs = width // PAIR
    quarter = rows // 2
    pieces = len(weight.arrays)

    def body(info_ref, embedded_ref, *refs):
        token_refs, refs = refs[:4], refs[4:]
        weight_refs, refs = refs[:pieces], refs[pieces:]
        (
            mod_ref,
            q_out,
            kv_out,
            normed_out,
            att_ref,
            inverse_ref,
            probs_ref,
            queries,
            keys,
            normed,
            turned_values,
            staged,
            bias,
            scratch,
            sems,
        ) = refs
        step = pl.program_id(0)
        index = pl.program_id(1)
        full = weight.load(info_ref, weight_refs, scratch, 2)
        time_at = slice(3 * width, 5 * width)
        copies = [
            pltpu.make_async_copy(queries, q_out, sems.at[0]),
            pltpu.make_async_copy(keys, kv_out, sems.at[1]),
            pltpu.make_async_copy(normed, normed_out, sems.at[2]),
        ]

        @pl.when(first_step(2))
        def _():
            modulation = dot(embedded_ref[...], full[:, time_at])
            gains = full[:, 5 * width :].astype(F32).T[:3, :]
            plus = 1.0 + modulation[0:1, :width]
            shift = modulation[0:1, width:]
            mod_ref[...] = jnp.concatenate(
                [gains[0:1] * plus, shift, plus, gains, jnp.zeros((2, width), F32)], axis=0
            )
            for number, ref in enumerate(token_refs):
                turn, part = divmod(number, 2)
                holder = info_ref[2] if turn == 0 else 1 - info_ref[2]
                begin = place_of(info_ref, holder, part) * quarter
                staged[pl.ds(pl.multiple_of(begin, quarter), quarter), :] = ref[...]

            def project(block, carry):
                at = pl.ds(pl.multiple_of(block * BLOCK, BLOCK), BLOCK)
                unit, _ = normalized(staged[at, :].astype(F32))
                first = (unit * mod_ref[0:1, :] + mod_ref[1:2, :]).astype(BF16)
                keys[at, :] = dot(first, full[:, width : 3 * width]).astype(BF16)
                per_quarter = quarter // BLOCK
                place = block // per_quarter

                @pl.when(place // 2 == info_ref[2])
                def _():
                    part = lax.bitwise_xor(lax.rem(place, 2), info_ref[3])
                    begin = part * quarter + lax.rem(block, per_quarter) * BLOCK
                    here = pl.ds(pl.multiple_of(begin, BLOCK), BLOCK)
                    normed[here, :] = first
                    queries[here, :] = (dot(first, full[:, :width]) * HEAD_DIM**-0.5).astype(BF16)

                return carry

            lax.fori_loop(0, 2 * rows // BLOCK, project, 0)
            for copy in copies:
                copy.start()

            turned_values[...] = keys[:, width:].T

        @pl.when(index == 0)
        def _():
            start = block_start(info_ref, step, WIDE, quarter)
            bias[...] = forbidden(info_ref, start, WIDE, rows, 1)

        mine = pl.ds(pl.multiple_of(step * WIDE, WIDE), WIDE)
        at = pair_at(index)
        attend_pair(
            queries[mine, at],
            lambda piece: keys[piece, at],
            lambda piece: turned_values[at, piece],
            rows,
            bias,
            att_ref,
            inverse_ref,
            probs_ref,
        )

        @pl.when((step == pl.num_programs(0) - 1) & (index == pairs - 1))
        def _():
            for copy in copies:
                copy.wait()

    anywhere = pl.BlockSpec(memory_space=pl.ANY)
    return call(
        body,
        "self_forward",
        info,
        (rows // WIDE, pairs),
        [(embedded, whole(embedded.shape))]
        + own.resident()
        + other.resident()
        + weight.inputs(),
        [
            ((8, width), F32, whole((8, width))),
            ((rows, width), BF16, anywhere),
            ((2 * rows, 2 * width), BF16, anywhere),
            ((rows, width), BF16, anywhere),
        ]
        + attention_outputs(rows, width, 2 * rows),
        [
            pltpu.VMEM((rows, width), BF16),
            pltpu.VMEM((2 * rows, 2 * width), BF16),
            pltpu.VMEM((rows, width), BF16),
            pltpu.VMEM((width, 2 * rows), BF16),
            pltpu.VMEM((2 * rows, width), BF16),
            pltpu.VMEM((rows, WIDE), F32),
            weight.scratch(),
            pltpu.SemaphoreType.DMA((3,)),
        ],
        cost(32 * rows * rows * width, 12 * rows * width, 2 * rows * rows * width // HEAD_DIM),
    )


def cross_forward(info, att, tokens, own, other, weight, gains):
    rows, width = att.shape
    pairs = width // PAIR
    count = own.rows
    pieces = len(weight.arrays)

    def body(info_ref, att_ref, first_ref, last_ref, gain_ref, *refs):
        enc_refs, refs = refs[:4], refs[4:]
        weight_refs, refs = refs[:pieces], refs[pieces:]
        second_ref, cq_ref, ckv_out, catt_ref, inverse_ref, probs_ref, *refs = refs
        memory, turned_values, staged, scratch, sem = refs
        full = weight.load(info_ref, weight_refs, scratch, 2)
        step = pl.program_id(0)
        index = pl.program_id(1)
        copy = pltpu.make_async_copy(memory, ckv_out, sem)

        @pl.when(first_step(2))
        def _():
            for part, ref in enumerate(enc_refs):
                staged[part * count : (part + 1) * count, :] = ref[...]

            def project(part, carry):
                at = pl.ds(pl.multiple_of(part * count, count), count)
                memory[at, :] = dot(staged[at, :], full[:, 2 * width :]).astype(BF16)
                return carry

            lax.fori_loop(0, 4, project, 0)
            copy.start()
            turned_values[...] = memory[:, width:].T

        @pl.when(index == 0)
        def _():
            second_in = tokens.load(first_ref, last_ref).astype(F32) + dot(
                att_ref[...], full[:, :width]
            )
            second_ref[...] = second_in
            normed, _ = normalized(second_in)
            normed = (normed * gain_ref[4:5, :]).astype(BF16)
            cq_ref[...] = (dot(normed, full[:, width : 2 * width]) * HEAD_DIM**-0.5).astype(BF16)

        at = pair_at(index)
        attend_pair(
            cq_ref[:, at],
            lambda piece: memory[piece, at],
            lambda piece: turned_values[at, piece],
            4 * count,
            None,
            catt_ref,
            inverse_ref,
            probs_ref,
        )

        @pl.when((step == pl.num_programs(0) - 1) & (index == pairs - 1))
        def _():
            copy.wait()

    return call(
        body,
        "cross_forward",
        info,
        (rows // WIDE, pairs),
        [(att, rows_of(width, WIDE))]
        + tokens.inputs(WIDE)
        + [(gains, whole(gains.shape))]
        + own.resident()
        + other.resident()
        + weight.inputs(),
        [
            ((rows, width), F32, rows_of(width, WIDE)),
            ((rows, width), BF16, rows_of(width, WIDE)),
            ((4 * count, 2 * width), BF16, pl.BlockSpec(memory_space=pl.ANY)),
        ]
        + attention_outputs(rows, width, 4 * count),
        [
            pltpu.VMEM((4 * count, 2 * width), BF16),
            pltpu.VMEM((width, 4 * count), BF16),
            pltpu.VMEM((4 * count, width), BF16),
            weight.scratch(),
            pltpu.SemaphoreType.DMA,
        ],
        cost(16 * rows * rows * width, 12 * rows * width, rows * rows * width // HEAD_DIM),
    )


def backward_pair(qq, dd, oo, keys, values, turned_keys, inverses, probs, size, add_keys, add_values):
    products = (oo.astype(F32) * dd.astype(F32)).T
    row_head = lax.broadcasted_iota(jnp.int32, (PAIR, 1), 0) // HEAD_DIM
    lane_head = lax.broadcasted_iota(jnp.int32, (1, PAIR), 1) // HEAD_DIM

    def head(part, total_grad):
        qe = jnp.where(lane_head == part, qq, jnp.zeros_like(qq))
        de = jnp.where(lane_head == part, dd, jnp.zeros_like(dd))
        inner = jnp.sum(jnp.where(row_head == part, products, 0.0), axis=0, keepdims=True)
        inverse = inverses(part)
        column = jnp.broadcast_to(inverse, (8, inverse.shape[1])).T[:, 0:1]
        scaled = (de.astype(F32) * column).astype(BF16)
        grad = None
        for begin in range(0, keys.shape[0], size):
            into = slice(begin, min(begin + size, keys.shape[0]))
            p = probs(part, into)
            dprobs = dot(values[into, :], de, 1, 1)
            dscores = (p.astype(F32) * ((dprobs - inner) * inverse)).astype(BF16)
            add_values(into, dot(p, scaled))
            add_keys(into, dot(dscores, qe))
            term = dot(turned_keys[:, into], dscores)
            grad = term if grad is None else grad + term
        return total_grad + jnp.where(row_head == part, grad, 0.0)

    grad = lax.fori_loop(0, 2, head, jnp.zeros((PAIR, qq.shape[0]), F32))
    return (grad.T * HEAD_DIM**-0.5).astype(BF16)


def attention_backward(name, info, q, kv, att, datt, inverses, probs, splits, split, stores):
    rows, width = q.shape
    count = kv.shape[0]
    lanes = width // splits
    pairs = lanes // PAIR
    all_pairs = width // PAIR
    base = split * pairs

    def body(info_ref, q_ref, k_ref, v_ref, att_ref, datt_ref, inverse_ref, probs_ref, *refs):
        dq_ref, down_ref, dother_ref, turned_keys, acc = refs
        step = pl.program_id(0)
        index = pl.program_id(1)
        at = pair_at(index)
        vat = pair_at(index + pairs)

        @pl.when(step == 0)
        def _():
            turned_keys[at, :] = k_ref[...].T
            acc[:, at] = jnp.zeros((count, PAIR), F32)
            acc[:, vat] = jnp.zeros((count, PAIR), F32)

        def add_keys(into, value):
            acc[into, at] += value

        def add_values(into, value):
            acc[into, vat] += value

        dq_ref[...] = backward_pair(
            q_ref[...],
            datt_ref[...],
            att_ref[...],
            k_ref,
            v_ref,
            turned_keys[at, :],
            lambda part: inverse_ref[0, pl.ds(part, 1), :],
            lambda part, into: probs_ref[part, into, :],
            2048,
            add_keys,
            add_values,
        )

        @pl.when((step == pl.num_programs(0) - 1) & (index == pairs - 1))
        def _():
            stores(info_ref, acc, down_ref, dother_ref)

    pair_rows = pl.BlockSpec((WIDE, PAIR), lambda i, h, *_: (i, base + h))
    half = (count // 2, 2 * lanes)
    return call(
        body,
        name,
        info,
        (rows // WIDE, pairs),
        [
            (q, pair_rows),
            (kv, pl.BlockSpec((count, PAIR), lambda i, h, *_: (0, base + h))),
            (kv, pl.BlockSpec((count, PAIR), lambda i, h, *_: (0, all_pairs + base + h))),
            (att, pair_rows),
            (datt, pair_rows),
            (inverses, pl.BlockSpec((1, 2, WIDE), lambda i, h, *_: (base + h, 0, i))),
            (probs, pl.BlockSpec((2, count, WIDE), lambda i, h, *_: (base + h, 0, i))),
        ],
        [
            ((rows, lanes), BF16, pl.BlockSpec((WIDE, PAIR), lambda i, h, *_: (i, h))),
            (half, BF16, whole(half)),
            (half, BF16, whole(half)),
        ],
        [pltpu.VMEM((lanes, count), BF16), pltpu.VMEM((count, 2 * lanes), F32)],
        cost(32 * rows * count * lanes, 20 * rows * lanes + 2 * rows * count),
    )


def self_backward(info, q, kv, att, dat, inverses, probs, splits, split):
    quarter = q.shape[0] // 2

    def stores(info_ref, acc, down_ref, dother_ref):
        for target, core in ((down_ref, info_ref[2]), (dother_ref, 1 - info_ref[2])):
            for part in range(2):
                begin = pl.multiple_of(place_of(info_ref, core, part) * quarter, quarter)
                target[part * quarter : (part + 1) * quarter, :] = acc[
                    pl.ds(begin, quarter), :
                ].astype(BF16)

    return attention_backward(
        "self_backward", info, q, kv, att, dat, inverses, probs, splits, split, stores
    )


def cross_backward(info, cq, ckv, catt, dca, inverses, probs, splits, split):
    count = ckv.shape[0]

    def stores(info_ref, acc, down_ref, dother_ref):
        down_ref[...] = acc[: count // 2, :].astype(BF16)
        dother_ref[...] = acc[count // 2 :, :].astype(BF16)

    return attention_backward(
        "cross_backward", info, cq, ckv, catt, dca, inverses, probs, splits, split, stores
    )


def feed(info, catt, second_in, dy, cout, weights, gains, packing):
    rows, width = catt.shape
    hidden = weights.hidden
    cout_count = len(cout.arrays)
    feed_count = len(weights.arrays)
    packed = packing.outputs(width * width + 2 * width * hidden)

    def body(info_ref, catt_ref, second_ref, dy_first, dy_last, gain_ref, *refs):
        cout_refs, refs = refs[:cout_count], refs[cout_count:]
        feed_refs, refs = refs[:feed_count], refs[feed_count:]
        (
            out_first,
            out_last,
            dthird_ref,
            dca_ref,
            ggain_ref,
            *packed_refs,
            acc_cout,
            acc_widen,
            acc_narrow,
            cout_scratch,
            widen_scratch,
            narrow_scratch,
        ) = refs
        cout_full = cout.load(info_ref, cout_refs, cout_scratch)
        widen_full, narrow_full = weights.load(info_ref, feed_refs, (widen_scratch, narrow_scratch))
        step = pl.program_id(0)

        @pl.when(step == 0)
        def _():
            acc_cout[...] = jnp.zeros_like(acc_cout)
            acc_widen[...] = jnp.zeros_like(acc_widen)
            acc_narrow[...] = jnp.zeros_like(acc_narrow)
            ggain_ref[...] = jnp.zeros_like(ggain_ref)

        catt = catt_ref[...]
        dy_low = dy.load(dy_first, dy_last)
        gain = gain_ref[5:6, :]
        third = second_ref[...] + dot(catt, cout_full[...])
        normed, scale = normalized(third)
        normed_low = (normed * gain).astype(BF16)
        pre = dot(normed_low, widen_full[...])
        below = 0.5 * (1.0 + lax.erf(pre * math.sqrt(0.5)))
        bell = jnp.exp(-0.5 * pre * pre) * (1.0 / math.sqrt(2.0 * math.pi))
        act = (pre * below).astype(BF16)
        out = (third + dot(act, narrow_full[...])).astype(BF16)
        dact = dot(dy_low, narrow_full[...], 1, 1)
        dpre = (dact * (below + pre * bell)).astype(BF16)
        acc_narrow[...] += dot(act, dy_low, 0, 0)
        acc_widen[...] += dot(normed_low, dpre, 0, 0)
        dnormed = dot(dpre, widen_full[...], 1, 1)
        ggain_ref[...] += jnp.sum(dnormed * normed, axis=0, keepdims=True)
        dthird = dy_low.astype(F32) + norm_backward(dnormed * gain, normed, scale)
        dthird_ref[...] = dthird
        dc = dthird.astype(BF16)
        dca_ref[...] = dot(dc, cout_full[...], 1, 1).astype(BF16)
        acc_cout[...] += dot(catt, dc, 0, 0)
        store_half((out_first, out_last), out)

        @pl.when(step == pl.num_programs(0) - 1)
        def _():
            packing.store(
                info_ref, packed_refs, (acc_cout, acc_widen, acc_narrow), unroll=True
            )

    return call(
        body,
        "feed",
        info,
        rows // BLOCK,
        [(catt, rows_of(width)), (second_in, rows_of(width))]
        + dy.inputs(BLOCK)
        + [(gains, whole(gains.shape))]
        + cout.inputs()
        + weights.inputs(),
        half_outputs(rows, width, BLOCK)
        + [
            ((rows, width), F32, rows_of(width)),
            ((rows, width), BF16, rows_of(width)),
            ((1, width), F32, whole((1, width))),
        ]
        + packed,
        [
            pltpu.VMEM((width, width), F32),
            pltpu.VMEM((width, hidden), F32),
            pltpu.VMEM((hidden, width), F32),
            cout.scratch(),
        ]
        + weights.scratch(),
        cost(
            12 * rows * width * hidden, 24 * rows * width + 8 * width * hidden, 2 * rows * hidden
        ),
    )


def sum_low(own_ref, got_ref):
    return (own_ref[...].astype(F32) + got_ref[...].astype(F32)).astype(BF16)


def middle_backward(
    info, dcqs, second_in, dthird, att, owns, gots, encoder, weight, gains, packing
):
    rows, width = second_in.shape
    count = len(dcqs)
    lanes = width // count
    packed = packing.outputs(4 * width * width)
    pieces = len(weight.arrays)
    short = encoder.shape[0] // (rows // BLOCK)

    def body(info_ref, att_ref, second_ref, dthird_ref, gain_ref, enc_first, enc_last, *refs):
        dcq_refs, refs = refs[:count], refs[count:]
        own_refs, refs = refs[:count], refs[count:]
        got_refs, refs = refs[:count], refs[count:]
        weight_refs, refs = refs[:pieces], refs[pieces:]
        dsecond_ref, dat_ref, ggain_ref, *genc_refs = refs[:5]
        refs = refs[5:]
        packed_refs, refs = refs[: len(packed)], refs[len(packed) :]
        acc_query, acc_out, acc_memory, scratch = refs
        full = weight.load(info_ref, weight_refs, scratch)
        step = pl.program_id(0)

        @pl.when(step == 0)
        def _():
            acc_query[...] = jnp.zeros_like(acc_query)
            acc_out[...] = jnp.zeros_like(acc_out)
            acc_memory[...] = jnp.zeros_like(acc_memory)
            ggain_ref[...] = jnp.zeros_like(ggain_ref)

        dcq = jnp.concatenate([ref[...] for ref in dcq_refs], axis=1)
        gain = gain_ref[4:5, :]
        normed, scale = normalized(second_ref[...])
        normed_low = (normed * gain).astype(BF16)
        dnormed = dot(dcq, full[:, width : 2 * width], 1, 1)
        acc_query[...] += dot(normed_low, dcq, 0, 0)
        ggain_ref[...] += jnp.sum(dnormed * normed, axis=0, keepdims=True)
        dsecond = dthird_ref[...] + norm_backward(dnormed * gain, normed, scale)
        dsecond_ref[...] = dsecond
        da = dsecond.astype(BF16)
        dat_ref[...] = dot(da, full[:, :width], 1, 1).astype(BF16)
        acc_out[...] += dot(att_ref[...], da, 0, 0)

        turned = encoder.load(enc_first, enc_last).T
        grads = [sum_low(own, got) for own, got in zip(own_refs, got_refs)]
        dckv = jnp.concatenate(
            [g[:, :lanes] for g in grads] + [g[:, lanes:] for g in grads], axis=1
        )
        genc = dot(dckv, full[:, 2 * width :], 1, 1).astype(BF16)
        acc_memory[...] += dot(turned, dckv)
        store_half(genc_refs, genc)

        @pl.when(step == pl.num_programs(0) - 1)
        def _():
            packing.store(info_ref, packed_refs, (acc_query, acc_out, acc_memory))

    return call(
        body,
        "middle_backward",
        info,
        rows // BLOCK,
        [
            (att, rows_of(width)),
            (second_in, rows_of(width)),
            (dthird, rows_of(width)),
            (gains, whole(gains.shape)),
        ]
        + encoder.inputs(short)
        + [(a, rows_of(lanes)) for a in dcqs]
        + [(a, rows_of(2 * lanes, short)) for a in owns]
        + [(a, rows_of(2 * lanes, short)) for a in gots]
        + weight.inputs(),
        [
            ((rows, width), F32, rows_of(width)),
            ((rows, width), BF16, rows_of(width)),
            ((1, width), F32, whole((1, width))),
        ]
        + half_outputs(encoder.shape[0], width, short)
        + packed,
        [
            pltpu.VMEM((width, width), F32),
            pltpu.VMEM((width, width), F32),
            pltpu.VMEM((width, 2 * width), F32),
            weight.scratch(),
        ],
        cost(16 * rows * width * width, 20 * rows * width),
    )


VECTORS = 8


def project_backward(
    info, tokens, normed, dqs, owns, gots, dsecond, mods, ggains, embedded, gencs, weight, packing
):
    rows, width = tokens.shape
    count = len(dqs)
    lanes = width // count
    packed = packing.outputs(3 * width * width, VECTORS)
    sent = (rows // 2 + gencs[0].shape[0], width)
    pieces = len(weight.arrays)

    def body(info_ref, first_ref, last_ref, normed_ref, dsecond_ref, mod_ref, *refs):
        second_gain, third_gain, embedded_ref, *genc_refs = refs[:5]
        refs = refs[5:]
        dq_refs, refs = refs[:count], refs[count:]
        own_refs, refs = refs[:count], refs[count:]
        got_refs, refs = refs[:count], refs[count:]
        weight_refs, refs = refs[:pieces], refs[pieces:]
        gfirst_ref, glast_ref, vectors_ref, *packed_refs, acc, sums, scratch = refs
        full = weight.load(info_ref, weight_refs, scratch)
        step = pl.program_id(0)

        @pl.when(step == 0)
        def _():
            acc[...] = jnp.zeros_like(acc)
            sums[...] = jnp.zeros_like(sums)

        turned = normed_ref[...].T
        dkvs = [sum_low(own, got) for own, got in zip(own_refs, got_refs)]
        grads = jnp.concatenate(
            [ref[...] for ref in dq_refs]
            + [dkv[:, :lanes] for dkv in dkvs]
            + [dkv[:, lanes:] for dkv in dkvs],
            axis=1,
        )
        acc[...] += dot(turned, grads)
        dnormed = dot(grads, full[...], 1, 1)
        unit, scale = normalized(tokens.load(first_ref, last_ref).astype(F32))
        sums[0:1, :] += jnp.sum(dnormed * unit, axis=0, keepdims=True)
        sums[1:2, :] += jnp.sum(dnormed, axis=0, keepdims=True)
        gtokens = (
            dsecond_ref[...] + norm_backward(dnormed * mod_ref[0:1, :], unit, scale)
        ).astype(BF16)
        steps = rows // BLOCK // 2
        at = pl.ds(pl.multiple_of(lax.rem(step, steps) * BLOCK, BLOCK), BLOCK)
        for half, ref in enumerate((gfirst_ref, glast_ref)):

            @pl.when(step // steps == half)
            def _(half=half, ref=ref):
                ref[at, :] = gtokens
                ref[rows // 2 :, :] = genc_refs[half][...]

        @pl.when(step == pl.num_programs(0) - 1)
        def _():
            vectors = jnp.concatenate(
                [
                    sums[0:1, :] * mod_ref[2:3, :],
                    second_gain[...],
                    third_gain[...],
                    sums[0:1, :] * mod_ref[3:4, :],
                    sums[1:2, :],
                    embedded_ref[0:1, :].astype(F32),
                    jnp.zeros((VECTORS - 6, width), F32),
                ],
                axis=0,
            )
            vectors_ref[...] = vectors
            packing.store(info_ref, packed_refs, (acc,), vectors)

    return call(
        body,
        "project_backward",
        info,
        rows // BLOCK,
        tokens.inputs(BLOCK)
        + [
            (normed, rows_of(width)),
            (dsecond, rows_of(width)),
            (mods, whole(mods.shape)),
            (ggains[0], whole((1, width))),
            (ggains[1], whole((1, width))),
            (embedded, whole(embedded.shape)),
            (gencs[0], whole(gencs[0].shape)),
            (gencs[1], whole(gencs[1].shape)),
        ]
        + [(a, rows_of(lanes)) for a in dqs]
        + [(a, rows_of(2 * lanes)) for a in owns]
        + [(a, rows_of(2 * lanes)) for a in gots]
        + weight.inputs(),
        [(sent, BF16, whole(sent))] * 2
        + [((VECTORS, width), F32, whole((VECTORS, width)))]
        + packed,
        [pltpu.VMEM((width, 3 * width), F32), pltpu.VMEM((8, width), F32), weight.scratch()],
        cost(12 * rows * width * width, 20 * rows * width),
    )


def join_columns(info, parts):
    size = parts[0].shape[0] - VECTORS
    shape = (size + len(parts) * VECTORS, parts[0].shape[1])

    def body(info_ref, *refs):
        *part_refs, out_ref = refs
        total = part_refs[0][:size, :].astype(F32)
        for ref in part_refs[1:]:
            total = total + ref[:size, :].astype(F32)
        out_ref[:size, :] = total.astype(BF16)
        for index, ref in enumerate(part_refs):
            begin = size + index * VECTORS
            out_ref[begin : begin + VECTORS, :] = ref[size:, :]

    return call(
        body,
        "join_columns",
        info,
        1,
        [(part, whole(part.shape)) for part in parts],
        [(shape, BF16, whole(shape))],
        [],
        cost(0, 4 * size * shape[1]),
    )[0]


def finish(info, parts, size, shard):
    width = parts[0].shape[1]
    count = parts[0].shape[0] - size
    devices = len(parts) * count // VECTORS

    def body(info_ref, *refs):
        part_refs = refs[: len(parts)]
        ginput_ref, gtime_ref, ggains_ref, listed, turned = refs[len(parts) :]
        for block in range(size // shard):
            rows = slice(block * shard, (block + 1) * shard)
            terms = [ref[rows, :].astype(F32) for ref in part_refs]
            ginput_ref[:, block * width : (block + 1) * width] = (terms[0] + terms[1]) + (
                terms[2] + terms[3]
            )
        for turn, ref in enumerate(part_refs):
            place = lax.bitwise_xor(info_ref[5], turn)
            listed[pl.ds(pl.multiple_of(place * count, count), count), :] = ref[size:, :]
        vectors = listed[...]
        column = lax.broadcasted_iota(jnp.int32, (devices, devices * VECTORS), 1)
        row = lax.broadcasted_iota(jnp.int32, (devices, devices * VECTORS), 0)

        def pick(kind):
            chosen = jnp.where(column == row * VECTORS + kind, 1.0, 0.0).astype(BF16)
            return dot(chosen, vectors)

        chosen = jnp.where(lax.rem(column, VECTORS) == row, 1.0, 0.0).astype(BF16)
        turned[...] = jnp.concatenate([0.5 * pick(5), dot(chosen, vectors)], axis=0).T
        place = (2 * info_ref[4] + info_ref[2]) * shard
        part = turned[pl.ds(pl.multiple_of(place, shard), shard), :]
        grads = jnp.concatenate([pick(3), pick(4)], axis=1).astype(BF16)
        gtime_ref[...] = dot(part[:, :devices].astype(BF16), grads)
        ggains_ref[...] = part.T[devices : devices + 3, :]

    return call(
        body,
        "finish",
        info,
        1,
        [(part, whole(part.shape)) for part in parts],
        [
            ((shard, 3 * width), F32, whole((shard, 3 * width))),
            ((shard, 2 * width), F32, whole((shard, 2 * width))),
            ((3, shard), F32, whole((3, shard))),
        ],
        [pltpu.VMEM((devices * VECTORS, width), BF16), pltpu.VMEM((width, 2 * devices), F32)],
        cost(8 * devices * count * width, 12 * size * width),
    )


def permutations(seq_count, fsdp_count):
    columns = fsdp_count // 2

    def at(seq, fsdp):
        return seq * fsdp_count + fsdp

    def pairs(move):
        return [
            (at(seq, fsdp), at(*move(seq, fsdp)))
            for seq in range(seq_count)
            for fsdp in range(fsdp_count)
        ]

    def home(turn):
        def move(seq, fsdp):
            y, x = divmod(seq, 2)
            column, core = divmod(fsdp, 2)
            return 2 * core + (x ^ turn), 2 * column + y

        return move

    shift = {
        r: pairs(lambda seq, fsdp, r=r: (seq, (fsdp + 2 * r) % fsdp_count))
        for r in range(1, columns)
    }
    cross = {t: pairs(lambda seq, fsdp, t=t: (seq ^ t, fsdp)) for t in range(1, seq_count)}
    swap = pairs(lambda seq, fsdp: (seq, fsdp ^ 1))
    return pairs(home(0)), pairs(home(1)), swap, shift, cross


def reverse(pairs):
    return [(target, source) for source, target in pairs]


def after(values, signal):
    return lax.optimization_barrier((values, signal))[0]


class Direct:
    def __init__(self, perms, seq, fsdp, columns):
        self.same, self.crossed, self.swap_pairs, self.shifts, self.crosses = perms
        self.seq = seq
        self.core = fsdp % 2
        self.z = fsdp // 2
        self.columns = columns

    def permute(self, values, pairs):
        return lax.ppermute(values, AXES, pairs)

    def swap(self, values):
        return self.permute(values, self.swap_pairs)

    def along_z(self, values):
        return [values] + [
            self.permute(values, self.shifts[r]) for r in range(1, self.columns)
        ]

    def both_cores(self, pieces):
        return pieces + [self.swap(piece) for piece in pieces]

    def core_sum(self, mine, away, signal=()):
        got = after(self.swap(away), signal)
        return [
            (mine[r].astype(F32) + got[r].astype(F32)).astype(BF16) for r in range(self.columns)
        ]

    def z_parts(self, shards):
        return [self.permute(shards[r], self.shifts[r]) for r in range(1, self.columns)]

    def z_sum(self, shards, got, signal=()):
        total = shards[0].astype(F32)
        for part in after(got, signal):
            total = total + part.astype(F32)
        return lax.optimization_barrier(total.astype(BF16))

    def add(self, first, second):
        return lax.optimization_barrier((first.astype(F32) + second.astype(F32)).astype(BF16))

    def cross(self, values, turn):
        return self.permute(values, self.crosses[turn])


SPLITS = 2


def time_embedding(step_values, model_width):
    half_width = model_width // 2
    frequency = jnp.exp(-math.log(10000.0) * jnp.arange(half_width, dtype=F32) / half_width)
    angles = step_values.astype(F32)[:, None] * frequency[None, :]
    return jnp.concatenate([jnp.sin(angles), jnp.cos(angles)], axis=-1).astype(BF16)


def exact_dot(left, right):
    return lax.dot_general(
        left,
        right,
        (((0,), (0,)), ((), ())),
        precision=lax.Precision.HIGHEST,
        preferred_element_type=F32,
    )


def make(seq_count, fsdp_count):
    perms = permutations(seq_count, fsdp_count)
    same, crossed = perms[:2]
    columns = fsdp_count // 2

    def on_device(
        tokens,
        encoder_states,
        lengths,
        timesteps,
        time_weight,
        self_input,
        self_output,
        cross_query,
        cross_memory,
        cross_output,
        widen_weight,
        narrow_weight,
        norm_gains,
        cotangent,
    ):
        width = tokens.shape[2]
        hidden = widen_weight.shape[1]
        shard = time_weight.shape[0]
        seq = lax.axis_index("seq")
        fsdp = lax.axis_index("fsdp")
        core = fsdp % 2
        side = seq % 2
        direct = Direct(perms, seq, fsdp, columns) if columns == 4 else None

        def send_work(values):
            mine = lax.dynamic_index_in_dim(values, side, 0, keepdims=False)
            others = lax.dynamic_index_in_dim(values, 1 - side, 0, keepdims=False)
            return [lax.ppermute(mine, AXES, same), lax.ppermute(others, AXES, crossed)]

        def send_home(halves):
            return [
                lax.ppermute(halves[0], AXES, reverse(same)),
                lax.ppermute(halves[1], AXES, reverse(crossed)),
            ]

        def at_home(parts, kind):
            first = jnp.where(side == 0, parts[0], parts[1])
            second = jnp.where(side == 0, parts[1], parts[0])
            return jnp.stack([first, second], axis=0).astype(kind)

        def gather(weight, axis=0):
            return lax.all_gather(weight, "fsdp", axis=axis, tiled=True)

        def swap(values):
            return lax.ppermute(values, AXES, perms[2])

        packing = Packing(fsdp_count, direct is not None, width)
        token_rows, encoder_rows = tokens.shape[1], encoder_states.shape[1]
        numbers = jnp.concatenate([lengths, timesteps[:, None]], axis=1)
        numbers_other = swap(numbers)
        own_row = jnp.where(core == seq // 2, numbers, numbers_other)
        own_row = lax.dynamic_slice_in_dim(own_row, side, 1, 0)
        step_value = own_row[0, 3:4]
        place = lax.broadcasted_iota(jnp.int32, (8,), 0)
        info = jnp.where(place == 1, own_row[0, 1], 0) + jnp.where(place <= 1, own_row[0, 0], 0)
        for index, value in enumerate((core, side, fsdp // 2, seq)):
            info = jnp.where(place == index + 2, value, info)
        embedded = jnp.pad(time_embedding(step_value, width), ((0, 15), (0, 0)))

        turned = jnp.pad(norm_gains.T, ((0, 0), (0, 128 - norm_gains.shape[0])))
        first = jnp.concatenate([self_input, time_weight, turned], axis=1)
        first_mine = direct.along_z(first) if direct else [(), ()]
        own = send_work(jnp.concatenate([tokens, encoder_states], axis=1))
        other = [swap(part) for part in after(own, first_mine[1:])]
        work_tokens = Halves(own, 0, token_rows)
        other_tokens = Halves(other, 0, token_rows)
        work_encoder = Halves(own, token_rows, encoder_rows)
        other_encoder = Halves(other, token_rows, encoder_rows)

        ready = info
        rest = jnp.concatenate([self_output, cross_query, cross_memory, cross_output], axis=1)
        if direct:
            first = direct.both_cores(first_mine)
            wide = widen_weight.reshape(shard, hidden // width, width).transpose(1, 0, 2)
            large = jnp.concatenate([wide.reshape(-1, width), narrow_weight], axis=0)
            rest, large = after((rest, large), (own, info, embedded))
            rest_mine = direct.along_z(rest)
            small_other = [swap(rest)]
            large_mine = direct.along_z(large)
            large_other = [swap(large)]
            ready = after(info, (small_other, large_other))
        else:
            first = [gather(first)]
            rest = [gather(rest)]
            feed_weights = FeedWeights([gather(widen_weight), gather(narrow_weight)], hidden)

        mods, q, kv, normed_first, att, inverses, probs = self_forward(
            ready, work_tokens, other_tokens, embedded, Weight(first, 0, first[0].shape[1])
        )
        ready = info
        if direct:
            rest_mine[1:], large_mine[:2] = after((rest_mine[1:], large_mine[:2]), att)
            small_other += [swap(part) for part in rest_mine[1:]]
            rest = rest_mine + small_other
            large_other.append(swap(large_mine[1]))
            ready = after(info, large_other)
        input_weight = Weight(first, 0, 3 * width)
        cross_weight = Weight(rest, 0, 4 * width)
        cout_weight = Weight(rest, 4 * width, width)
        dy_parts = send_work(after(cotangent, att))
        second_in, cq, ckv, catt, cross_inverses, cross_probs = cross_forward(
            ready, att, work_tokens, work_encoder, other_encoder, cross_weight, mods
        )
        work_dy = Halves(after(dy_parts, catt), 0, token_rows)
        if direct:
            large_mine[2:] = after(large_mine[2:], catt)
            large_other += [swap(part) for part in large_mine[2:]]
            feed_weights = FeedWeights(large_mine + large_other, hidden)
        out_first, out_last, dthird, dca, ggain_third, *packed_feed = feed(
            info, catt, second_in, work_dy, cout_weight, feed_weights, mods, packing
        )
        layer_out = (out_first, out_last)
        out_parts = send_home(layer_out)

        def backward_cross(split, ready):
            return cross_backward(
                ready, cq, ckv, catt, dca, cross_inverses, cross_probs, SPLITS, split
            )

        def backward_self(split, ready):
            return self_backward(ready, q, kv, att, dat, inverses, probs, SPLITS, split)

        crosses = [backward_cross(0, info)]
        out_parts = after(out_parts, crosses[0][0])
        chip_feed = direct.core_sum(*packed_feed, crosses[0][0]) if direct else ()
        crosses.append(backward_cross(1, after(info, (chip_feed, out_parts))))
        dcqs, dckvs, dckv_others = zip(*crosses)
        dckv_gots = [swap(a) for a in dckv_others]
        feed_parts = direct.z_parts(chip_feed) if direct else [()]
        dsecond, dat, ggain_second, *genc = middle_backward(
            after(info, (feed_parts[0], dcqs)),
            dcqs,
            second_in,
            dthird,
            att,
            dckvs,
            dckv_gots,
            work_encoder,
            cross_weight,
            mods,
            packing,
        )
        genc, packed_middle = genc[:2], genc[2:]
        selfs = [backward_self(0, after(info, packed_middle))]
        if direct:
            column_feed = direct.z_sum(chip_feed, feed_parts, selfs[0][0])
            chip_middle = direct.core_sum(*packed_middle, selfs[0][0])
            selfs.append(backward_self(1, after(info, (column_feed, chip_middle))))
            middle_parts = after(direct.z_parts(chip_middle), selfs[1][0])
            row_feed = after(direct.cross(column_feed, 1), selfs[1][0])
            row_feed = direct.add(column_feed, row_feed)
            column_middle = direct.z_sum(chip_middle, middle_parts)
        else:
            selfs.append(backward_self(1, info))
        dqs, dkvs, dkv_others = zip(*selfs)
        dkv_others = list(dkv_others)
        if direct:
            dkv_others[1] = after(dkv_others[1], (column_middle, row_feed))
        dkv_gots = [swap(a) for a in dkv_others]
        first_grad, last_grad, vectors, *packed_input = project_backward(
            info,
            work_tokens,
            normed_first,
            dqs,
            dkvs,
            dkv_gots,
            dsecond,
            mods,
            (ggain_second, ggain_third),
            embedded,
            genc,
            input_weight,
            packing,
        )
        gtokens = (first_grad, last_grad)
        if direct:
            got_row = after(direct.cross(row_feed, 2), gtokens)
            row_middle = after(direct.cross(column_middle, 1), gtokens)
            away = after(packed_input[1], (got_row, row_middle))
            chip = direct.core_sum(packed_input[0], away)
            row_middle = direct.add(column_middle, row_middle)
            gots = direct.z_parts(chip)
            middle_got = direct.cross(row_middle, 2)
            token_parts = after(send_home(after(gtokens, chip)), gots)
            ready = after(info, (token_parts, middle_got))
            size = chip[0].shape[0] - VECTORS
            joined = join_columns(ready, [chip[0]] + gots)
            parts = [joined] + [direct.cross(joined, turn) for turn in (1, 2, 3)]
            late = after((row_feed, got_row, row_middle, middle_got), joined)
            reduced_feed = late[0].astype(F32) + late[1].astype(F32)
            reduced_middle = late[2].astype(F32) + late[3].astype(F32)
            reduced_input, gtime, ggains = finish(info, parts, size, shard)
        else:

            def reduce(packed):
                part = lax.psum_scatter(packed[0], "fsdp", scatter_dimension=0, tiled=True)
                return lax.psum(part[0], "seq").astype(F32)

            reduced_input = reduce(packed_input)
            reduced_input = unpack_rows(reduced_input, 0, shard, 3 * width)
            reduced_middle = reduce(packed_middle)
            reduced_feed = reduce(packed_feed)
            token_parts = send_home(gtokens)
            ggains = lax.psum(vectors[:3], AXES)
            ggains = lax.dynamic_slice_in_dim(ggains, fsdp * shard, shard, 1)
            by_group = lax.all_gather(vectors[3:5], AXES, axis=0)
            by_group = by_group.reshape(seq_count, columns, 2, 2 * width).sum(axis=2)
            by_group = by_group.transpose(1, 0, 2).reshape(-1, 2 * width)
            every = time_embedding(gather(timesteps), width)
            own_columns = lax.dynamic_slice_in_dim(every, fsdp * shard, shard, 1)
            gtime = exact_dot(own_columns.astype(F32), by_group)

        tall = narrow_weight.shape[0]
        return (
            at_home(out_parts, BF16),
            at_home([part[:token_rows] for part in token_parts], F32),
            at_home([part[token_rows:] for part in token_parts], F32),
            gtime,
            reduced_input,
            unpack_rows(reduced_middle, shard, shard, width),
            unpack_rows(reduced_middle, 0, shard, width),
            unpack_rows(reduced_middle, 2 * shard, shard, 2 * width),
            unpack_rows(reduced_feed, 0, shard, width),
            unpack_rows(reduced_feed, shard, shard, hidden),
            unpack_rows(reduced_feed, shard * (1 + hidden // width), tall, width),
            ggains,
        )

    return on_device


def solution(mesh):
    rows = P("fsdp", "seq", None)
    weight = P("fsdp", None)
    in_specs = (rows, rows, P("fsdp", None), P("fsdp")) + (weight,) * 8 + (P(None, "fsdp"), rows)
    out_specs = (rows,) * 3 + (weight,) * 8 + (P(None, "fsdp"),)
    return jax.shard_map(
        make(mesh.shape["seq"], mesh.shape["fsdp"]),
        mesh=mesh,
        in_specs=in_specs,
        out_specs=out_specs,
        check_vma=False,
    )
```

```python
import math

import jax
import jax.numpy as jnp
from jax import lax
from jax.experimental import pallas as pl
from jax.experimental.pallas import tpu as pltpu
from jax.sharding import PartitionSpec as P


HEAD_DIM = 64
PAIR = 2 * HEAD_DIM
EPS = 1e-05
NEG = -1e30
F32 = jnp.float32
BF16 = jnp.bfloat16
AXES = ("seq", "fsdp")
VMEM_LIMIT = 60 * 2**20
BLOCK = 256
WIDE = 512


def dot(left, right, left_dim=1, right_dim=0):
    return lax.dot_general(
        left, right, (((left_dim,), (right_dim,)), ((), ())), preferred_element_type=F32
    )


def whole(shape):
    return pl.BlockSpec(shape, lambda *_: (0,) * len(shape))


def rows_of(width, block=BLOCK):
    return pl.BlockSpec((block, width), lambda i, *_: (i, 0))


def params():
    return pltpu.CompilerParams(vmem_limit_bytes=VMEM_LIMIT)


def cost(flops, moved, transcendentals=0):
    return pl.CostEstimate(
        flops=int(flops), bytes_accessed=int(moved), transcendentals=int(transcendentals)
    )


def normalized(values):
    average = jnp.mean(values, axis=-1, keepdims=True)
    centred = values - average
    spread = jnp.mean(centred * centred, axis=-1, keepdims=True)
    scale = lax.rsqrt(spread + EPS)
    return centred * scale, scale


def norm_backward(upstream, normed, scale):
    mean_up = jnp.mean(upstream, axis=-1, keepdims=True)
    mean_both = jnp.mean(upstream * normed, axis=-1, keepdims=True)
    return (upstream - mean_up - normed * mean_both) * scale


def lane_is(part):
    lane = lax.broadcasted_iota(jnp.int32, (1, PAIR), 1)
    return lane < HEAD_DIM if part == 0 else lane >= HEAD_DIM


def half_of(values, part):
    return jnp.where(lane_is(part), values, jnp.zeros_like(values))


def pair_at(index):
    return pl.ds(pl.multiple_of(index * PAIR, PAIR), PAIR)


def first_step(dims=1):
    first = pl.program_id(0) == 0
    return first if dims == 1 else first & (pl.program_id(1) == 0)


class Weight:
    def __init__(self, pieces, start, width):
        self.arrays = pieces
        self.start = start
        self.width = width

    @property
    def split(self):
        return len(self.arrays) > 1

    @property
    def rows(self):
        return len(self.arrays) * self.arrays[0].shape[0]

    @property
    def aligned(self):
        return self.start % self.width == 0

    def inputs(self):
        if not self.aligned:
            return [(array, whole(array.shape)) for array in self.arrays]
        place = self.start // self.width
        shape = (self.arrays[0].shape[0], self.width)
        return [(array, pl.BlockSpec(shape, lambda *_: (0, place))) for array in self.arrays]

    def scratch(self):
        return pltpu.VMEM((self.rows, self.width) if self.split else (16, 128), BF16)

    def load(self, info, refs, scratch, dims=1):
        if not self.split:
            return refs[0]
        columns = slice(0, self.width) if self.aligned else slice(self.start, self.start + self.width)

        @pl.when(first_step(dims))
        def _():
            count = len(refs) // 2
            shard = refs[0].shape[0]
            for index, ref in enumerate(refs):
                turn, shift = divmod(index, count)
                core = info[2] if turn == 0 else 1 - info[2]
                owner = lax.rem(info[4] - shift + count, count)
                start = pl.multiple_of((2 * owner + core) * shard, shard)
                scratch[pl.ds(start, shard), :] = ref[:, columns]

        return scratch


class Halves:
    def __init__(self, arrays, start, rows):
        self.arrays = arrays
        self.start = start
        self.rows = rows
        self.shape = (2 * rows, arrays[0].shape[1])

    def inputs(self, block):
        width = self.shape[1]
        count = self.rows // block
        base = self.start // block
        return [
            (
                self.arrays[0],
                pl.BlockSpec((block, width), lambda i, *_: (base + jnp.minimum(i, count - 1), 0)),
            ),
            (
                self.arrays[1],
                pl.BlockSpec((block, width), lambda i, *_: (base + jnp.maximum(i - count, 0), 0)),
            ),
        ]

    def resident(self):
        place = self.start // self.rows
        spec = pl.BlockSpec((self.rows, self.shape[1]), lambda *_: (place, 0))
        return [(array, spec) for array in self.arrays]

    def load(self, first_ref, second_ref):
        half = pl.num_programs(0) // 2
        return jnp.where(pl.program_id(0) < half, first_ref[...], second_ref[...])


def half_outputs(rows, width, block):
    count = rows // block // 2
    half = (rows // 2, width)
    return [
        (half, BF16, pl.BlockSpec((block, width), lambda i, *_: (jnp.minimum(i, count - 1), 0))),
        (half, BF16, pl.BlockSpec((block, width), lambda i, *_: (jnp.maximum(i - count, 0), 0))),
    ]


def store_half(refs, value):
    first = pl.program_id(0) < pl.num_programs(0) // 2

    @pl.when(first)
    def _():
        refs[0][...] = value

    @pl.when(jnp.logical_not(first))
    def _():
        refs[1][...] = value


class FeedWeights:
    def __init__(self, arrays, hidden):
        self.arrays = arrays
        self.hidden = hidden

    @property
    def split(self):
        return len(self.arrays) > 2

    def inputs(self):
        return [(array, whole(array.shape)) for array in self.arrays]

    def scratch(self):
        if not self.split:
            return [pltpu.VMEM((16, 128), BF16)] * 2
        width = self.arrays[0].shape[1]
        return [pltpu.VMEM((width, self.hidden), BF16), pltpu.VMEM((self.hidden, width), BF16)]

    def load(self, info, refs, scratch):
        if not self.split:
            return refs
        widen, narrow = scratch

        @pl.when(pl.program_id(0) == 0)
        def _():
            count = len(refs) // 2
            rows, width = refs[0].shape
            blocks = self.hidden // width
            tall = rows // 2
            short = tall // blocks
            for index, ref in enumerate(refs):
                turn, shift = divmod(index, count)
                core = info[2] if turn == 0 else 1 - info[2]
                owner = 2 * lax.rem(info[4] - shift + count, count) + core
                start = pl.multiple_of(owner * short, short)
                for block in range(blocks):
                    widen[pl.ds(start, short), block * width : (block + 1) * width] = ref[
                        block * short : (block + 1) * short, :
                    ]
                start = pl.multiple_of(owner * tall, tall)
                narrow[pl.ds(start, tall), :] = ref[tall:, :]

        return widen, narrow


class Packing:
    def __init__(self, shards, direct, width):
        self.shards = shards
        self.direct = direct
        self.width = width

    def outputs(self, elements, extra=0):
        rows = elements // (self.shards * self.width)
        if self.direct:
            rows += extra
        if self.direct:
            shape = (self.shards // 2, rows, self.width)
            return [(shape, BF16, whole(shape))] * 2
        shape = (self.shards, rows, self.width)
        return [(shape, BF16, whole(shape))]

    def store(self, info, packed, grads, vectors=None, unroll=False):
        def put(ref, slot, owner):
            offset = 0
            for grad in grads:
                rows = grad.shape[0] // self.shards
                start = owner * rows
                if not isinstance(owner, int):
                    start = pl.multiple_of(start, rows)
                for block in range(grad.shape[1] // self.width):
                    columns = slice(block * self.width, (block + 1) * self.width)
                    ref[slot, offset : offset + rows, :] = grad[pl.ds(start, rows), columns].astype(
                        BF16
                    )
                    offset += rows
            if vectors is not None and self.direct:
                ref[slot, offset:, :] = vectors.astype(BF16)

        if self.direct:
            count = self.shards // 2
            for ref, core in ((packed[0], info[2]), (packed[1], 1 - info[2])):

                def one(shift, carry, ref=ref, core=core):
                    put(ref, shift, 2 * lax.rem(info[4] + shift, count) + core)
                    return carry

                if unroll:
                    for shift in range(count):
                        one(shift, 0)
                else:
                    lax.fori_loop(0, count, one, 0)
        else:
            for shard in range(self.shards):
                put(packed[0], shard, shard)


def unpack_rows(packed, offset, rows, columns):
    width = packed.shape[1]
    blocks = columns // width
    parts = [packed[offset + b * rows : offset + (b + 1) * rows] for b in range(blocks)]
    return jnp.concatenate(parts, axis=1) if blocks > 1 else parts[0]


def call(body, name, info, grid, inputs, outputs, scratch, estimate):
    return pl.pallas_call(
        body,
        name=name,
        grid_spec=pltpu.PrefetchScalarGridSpec(
            num_scalar_prefetch=1,
            grid=grid if isinstance(grid, tuple) else (grid,),
            in_specs=[spec for _, spec in inputs],
            out_specs=[spec for _, _, spec in outputs],
            scratch_shapes=scratch,
        ),
        out_shape=[jax.ShapeDtypeStruct(shape, kind) for shape, kind, _ in outputs],
        compiler_params=params(),
        cost_estimate=estimate,
    )(info, *[array for array, _ in inputs])


def block_start(info, block_index, block, quarter):
    per_quarter = quarter // block
    first = block_index < per_quarter
    place = jnp.where(first, info[3], 1 - info[3])
    return (2 * info[2] + place) * quarter + lax.rem(block_index, per_quarter) * block


def forbidden(info, start, block, half, queries_dim):
    keys_dim = 1 - queries_dim
    qshape = [1, 1]
    qshape[queries_dim] = block
    kshape = [1, 1]
    kshape[keys_dim] = half
    qpos = start + lax.broadcasted_iota(jnp.int32, tuple(qshape), queries_dim)
    kpos = half + lax.broadcasted_iota(jnp.int32, tuple(kshape), keys_dim)
    first, second = info[0], info[1]
    low = jnp.where((qpos >= first) & (qpos < second), second, first)
    high = jnp.where(qpos >= second, second, 2 * half)
    return jnp.where((kpos >= low) & (kpos < high), NEG, 0.0)


def key_specs(array, lanes, split, width):
    rows = array.shape[0]
    count = width // lanes
    return [
        (array, pl.BlockSpec((rows, lanes), lambda *_: (0, split))),
        (array, pl.BlockSpec((rows, lanes), lambda *_: (0, count + split))),
    ]


def attention_sums(low, high):
    return (low > 1e-20) & (high < 1e30)


def attend_pair(qq, keys_at, turned_values, free, bias, att_ref, inverse_ref, probs_ref):
    count = probs_ref.shape[1]
    row_head = lax.broadcasted_iota(jnp.int32, (PAIR, 1), 0) // HEAD_DIM
    lane_head = lax.broadcasted_iota(jnp.int32, (1, PAIR), 1) // HEAD_DIM
    turned_at = turned_values(slice(0, count))

    def head(part):
        qe = jnp.where(lane_head == part, qq, jnp.zeros_like(qq))
        total = None
        out = None
        for piece in (slice(0, free), slice(free, count)):
            if piece.start == piece.stop:
                continue
            s = dot(keys_at(piece), qe, 1, 1)
            p = jnp.exp(s if piece.start == 0 else s + bias[...])
            low = p.astype(BF16)
            probs_ref[part, piece, :] = low
            term = jnp.sum(p, axis=0, keepdims=True)
            attended = dot(turned_at[:, piece], low)
            total = term if total is None else total + term
            out = attended if out is None else out + attended
        return out, total

    def one(part, carry):
        out, total = head(part)
        inverse = 1.0 / total
        inverse_ref[0, pl.ds(part, 1), :] = inverse
        joined, low, high = carry
        joined = joined + jnp.where(row_head == part, out * inverse, 0.0)
        return joined, jnp.minimum(low, total), jnp.maximum(high, total)

    ones = jnp.ones((1, qq.shape[0]), F32)
    start = (jnp.zeros((PAIR, qq.shape[0]), F32), ones, ones)
    out, low, high = lax.fori_loop(0, 2, one, start, unroll=True)
    att_ref[...] = out.T.astype(BF16)
    low, high = jnp.min(low), jnp.max(high)

    @pl.when(jnp.logical_not((low > 1e-20) & (high < 1e30)))
    def _():
        chunk = BLOCK // 2
        queries = qq.shape[0]

        def again(part, carry):
            qe = jnp.where(lane_head == part, qq, jnp.zeros_like(qq))

            def scores(index):
                at = pl.ds(pl.multiple_of(index * chunk, chunk), chunk)
                s = dot(keys_at(at), qe, 1, 1)
                if free == count:
                    return at, s
                begin = jnp.maximum(index * chunk - free, 0)
                part_bias = bias[pl.ds(pl.multiple_of(begin, chunk), chunk), :]
                return at, s + jnp.where(index * chunk >= free, part_bias, 0.0)

            def largest(index, top):
                return jnp.maximum(top, jnp.max(scores(index)[1], axis=0, keepdims=True))

            top = lax.fori_loop(
                0, count // chunk, largest, jnp.full((1, queries), -jnp.inf, F32)
            )

            def add(index, sums):
                at, s = scores(index)
                p = jnp.exp(s - top)
                low = p.astype(BF16)
                probs_ref[part, at, :] = low
                return (
                    sums[0] + jnp.sum(p, axis=0, keepdims=True),
                    sums[1] + dot(turned_values(at), low),
                )

            total, out = lax.fori_loop(
                0,
                count // chunk,
                add,
                (jnp.zeros((1, queries), F32), jnp.zeros((PAIR, queries), F32)),
            )
            inverse = 1.0 / total
            inverse_ref[0, pl.ds(part, 1), :] = inverse
            return carry + jnp.where(row_head == part, out * inverse, 0.0)

        out = lax.fori_loop(0, 2, again, jnp.zeros((PAIR, queries), F32))
        att_ref[...] = out.T.astype(BF16)


def attention_outputs(rows, width, count):
    pairs = width // PAIR
    return [
        ((rows, width), BF16, pl.BlockSpec((WIDE, PAIR), lambda i, h, *_: (i, h))),
        ((pairs, 2, rows), F32, pl.BlockSpec((1, 2, WIDE), lambda i, h, *_: (h, 0, i))),
        ((2 * pairs, count, rows), BF16, pl.BlockSpec((2, count, WIDE), lambda i, h, *_: (h, 0, i))),
    ]


def place_of(info, core, part):
    return 2 * core + (info[3] if part == 0 else 1 - info[3])


def self_forward(info, own, other, embedded, weight):
    rows, width = own.shape
    pairs = width // PAIR
    quarter = rows // 2
    pieces = len(weight.arrays)

    def body(info_ref, embedded_ref, *refs):
        token_refs, refs = refs[:4], refs[4:]
        weight_refs, refs = refs[:pieces], refs[pieces:]
        (
            mod_ref,
            q_out,
            kv_out,
            normed_out,
            att_ref,
            inverse_ref,
            probs_ref,
            queries,
            keys,
            normed,
            turned_values,
            staged,
            bias,
            scratch,
            sems,
        ) = refs
        step = pl.program_id(0)
        index = pl.program_id(1)
        full = weight.load(info_ref, weight_refs, scratch, 2)
        time_at = slice(3 * width, 5 * width)
        copies = [
            pltpu.make_async_copy(queries, q_out, sems.at[0]),
            pltpu.make_async_copy(keys, kv_out, sems.at[1]),
            pltpu.make_async_copy(normed, normed_out, sems.at[2]),
        ]

        @pl.when(first_step(2))
        def _():
            modulation = dot(embedded_ref[...], full[:, time_at])
            gains = full[:, 5 * width :].astype(F32).T[:3, :]
            plus = 1.0 + modulation[0:1, :width]
            shift = modulation[0:1, width:]
            mod_ref[...] = jnp.concatenate(
                [gains[0:1] * plus, shift, plus, gains, jnp.zeros((2, width), F32)], axis=0
            )
            for number, ref in enumerate(token_refs):
                turn, part = divmod(number, 2)
                holder = info_ref[2] if turn == 0 else 1 - info_ref[2]
                begin = place_of(info_ref, holder, part) * quarter
                staged[pl.ds(pl.multiple_of(begin, quarter), quarter), :] = ref[...]

            def project(block, carry):
                at = pl.ds(pl.multiple_of(block * BLOCK, BLOCK), BLOCK)
                unit, _ = normalized(staged[at, :].astype(F32))
                first = (unit * mod_ref[0:1, :] + mod_ref[1:2, :]).astype(BF16)
                keys[at, :] = dot(first, full[:, width : 3 * width]).astype(BF16)
                per_quarter = quarter // BLOCK
                place = block // per_quarter

                @pl.when(place // 2 == info_ref[2])
                def _():
                    part = lax.bitwise_xor(lax.rem(place, 2), info_ref[3])
                    begin = part * quarter + lax.rem(block, per_quarter) * BLOCK
                    here = pl.ds(pl.multiple_of(begin, BLOCK), BLOCK)
                    normed[here, :] = first
                    queries[here, :] = (dot(first, full[:, :width]) * HEAD_DIM**-0.5).astype(BF16)

                return carry

            lax.fori_loop(0, 2 * rows // BLOCK, project, 0)
            for copy in copies:
                copy.start()

            turned_values[...] = keys[:, width:].T

        @pl.when(index == 0)
        def _():
            start = block_start(info_ref, step, WIDE, quarter)
            bias[...] = forbidden(info_ref, start, WIDE, rows, 1)

        mine = pl.ds(pl.multiple_of(step * WIDE, WIDE), WIDE)
        at = pair_at(index)
        attend_pair(
            queries[mine, at],
            lambda piece: keys[piece, at],
            lambda piece: turned_values[at, piece],
            rows,
            bias,
            att_ref,
            inverse_ref,
            probs_ref,
        )

        @pl.when((step == pl.num_programs(0) - 1) & (index == pairs - 1))
        def _():
            for copy in copies:
                copy.wait()

    anywhere = pl.BlockSpec(memory_space=pl.ANY)
    return call(
        body,
        "self_forward",
        info,
        (rows // WIDE, pairs),
        [(embedded, whole(embedded.shape))]
        + own.resident()
        + other.resident()
        + weight.inputs(),
        [
            ((8, width), F32, whole((8, width))),
            ((rows, width), BF16, anywhere),
            ((2 * rows, 2 * width), BF16, anywhere),
            ((rows, width), BF16, anywhere),
        ]
        + attention_outputs(rows, width, 2 * rows),
        [
            pltpu.VMEM((rows, width), BF16),
            pltpu.VMEM((2 * rows, 2 * width), BF16),
            pltpu.VMEM((rows, width), BF16),
            pltpu.VMEM((width, 2 * rows), BF16),
            pltpu.VMEM((2 * rows, width), BF16),
            pltpu.VMEM((rows, WIDE), F32),
            weight.scratch(),
            pltpu.SemaphoreType.DMA((3,)),
        ],
        cost(32 * rows * rows * width, 12 * rows * width, 2 * rows * rows * width // HEAD_DIM),
    )


def cross_forward(info, att, tokens, own, other, weight, gains):
    rows, width = att.shape
    pairs = width // PAIR
    count = own.rows
    pieces = len(weight.arrays)

    def body(info_ref, att_ref, first_ref, last_ref, gain_ref, *refs):
        enc_refs, refs = refs[:4], refs[4:]
        weight_refs, refs = refs[:pieces], refs[pieces:]
        second_ref, cq_ref, ckv_out, catt_ref, inverse_ref, probs_ref, *refs = refs
        memory, turned_values, staged, scratch, sem = refs
        full = weight.load(info_ref, weight_refs, scratch, 2)
        step = pl.program_id(0)
        index = pl.program_id(1)
        copy = pltpu.make_async_copy(memory, ckv_out, sem)

        @pl.when(first_step(2))
        def _():
            for part, ref in enumerate(enc_refs):
                staged[part * count : (part + 1) * count, :] = ref[...]

            def project(part, carry):
                at = pl.ds(pl.multiple_of(part * count, count), count)
                memory[at, :] = dot(staged[at, :], full[:, 2 * width :]).astype(BF16)
                return carry

            lax.fori_loop(0, 4, project, 0)
            copy.start()
            turned_values[...] = memory[:, width:].T

        @pl.when(index == 0)
        def _():
            second_in = tokens.load(first_ref, last_ref).astype(F32) + dot(
                att_ref[...], full[:, :width]
            )
            second_ref[...] = second_in
            normed, _ = normalized(second_in)
            normed = (normed * gain_ref[4:5, :]).astype(BF16)
            cq_ref[...] = (dot(normed, full[:, width : 2 * width]) * HEAD_DIM**-0.5).astype(BF16)

        at = pair_at(index)
        attend_pair(
            cq_ref[:, at],
            lambda piece: memory[piece, at],
            lambda piece: turned_values[at, piece],
            4 * count,
            None,
            catt_ref,
            inverse_ref,
            probs_ref,
        )

        @pl.when((step == pl.num_programs(0) - 1) & (index == pairs - 1))
        def _():
            copy.wait()

    return call(
        body,
        "cross_forward",
        info,
        (rows // WIDE, pairs),
        [(att, rows_of(width, WIDE))]
        + tokens.inputs(WIDE)
        + [(gains, whole(gains.shape))]
        + own.resident()
        + other.resident()
        + weight.inputs(),
        [
            ((rows, width), F32, rows_of(width, WIDE)),
            ((rows, width), BF16, rows_of(width, WIDE)),
            ((4 * count, 2 * width), BF16, pl.BlockSpec(memory_space=pl.ANY)),
        ]
        + attention_outputs(rows, width, 4 * count),
        [
            pltpu.VMEM((4 * count, 2 * width), BF16),
            pltpu.VMEM((width, 4 * count), BF16),
            pltpu.VMEM((4 * count, width), BF16),
            weight.scratch(),
            pltpu.SemaphoreType.DMA,
        ],
        cost(16 * rows * rows * width, 12 * rows * width, rows * rows * width // HEAD_DIM),
    )


def backward_pair(qq, dd, oo, keys, values, turned_keys, inverses, probs, size, add_keys, add_values):
    products = (oo.astype(F32) * dd.astype(F32)).T
    row_head = lax.broadcasted_iota(jnp.int32, (PAIR, 1), 0) // HEAD_DIM
    lane_head = lax.broadcasted_iota(jnp.int32, (1, PAIR), 1) // HEAD_DIM

    def head(part, total_grad):
        qe = jnp.where(lane_head == part, qq, jnp.zeros_like(qq))
        de = jnp.where(lane_head == part, dd, jnp.zeros_like(dd))
        inner = jnp.sum(jnp.where(row_head == part, products, 0.0), axis=0, keepdims=True)
        inverse = inverses(part)
        column = jnp.broadcast_to(inverse, (8, inverse.shape[1])).T[:, 0:1]
        scaled = (de.astype(F32) * column).astype(BF16)
        grad = None
        for begin in range(0, keys.shape[0], size):
            into = slice(begin, min(begin + size, keys.shape[0]))
            p = probs(part, into)
            dprobs = dot(values[into, :], de, 1, 1)
            dscores = (p.astype(F32) * ((dprobs - inner) * inverse)).astype(BF16)
            add_values(into, dot(p, scaled))
            add_keys(into, dot(dscores, qe))
            term = dot(turned_keys[:, into], dscores)
            grad = term if grad is None else grad + term
        return total_grad + jnp.where(row_head == part, grad, 0.0)

    grad = lax.fori_loop(0, 2, head, jnp.zeros((PAIR, qq.shape[0]), F32))
    return (grad.T * HEAD_DIM**-0.5).astype(BF16)


def attention_backward(name, info, q, kv, att, datt, inverses, probs, splits, split, stores):
    rows, width = q.shape
    count = kv.shape[0]
    lanes = width // splits
    pairs = lanes // PAIR
    all_pairs = width // PAIR
    base = split * pairs

    def body(info_ref, q_ref, k_ref, v_ref, att_ref, datt_ref, inverse_ref, probs_ref, *refs):
        dq_ref, down_ref, dother_ref, turned_keys, acc = refs
        step = pl.program_id(0)
        index = pl.program_id(1)
        at = pair_at(index)
        vat = pair_at(index + pairs)

        @pl.when(step == 0)
        def _():
            turned_keys[at, :] = k_ref[...].T
            acc[:, at] = jnp.zeros((count, PAIR), F32)
            acc[:, vat] = jnp.zeros((count, PAIR), F32)

        def add_keys(into, value):
            acc[into, at] += value

        def add_values(into, value):
            acc[into, vat] += value

        dq_ref[...] = backward_pair(
            q_ref[...],
            datt_ref[...],
            att_ref[...],
            k_ref,
            v_ref,
            turned_keys[at, :],
            lambda part: inverse_ref[0, pl.ds(part, 1), :],
            lambda part, into: probs_ref[part, into, :],
            2048,
            add_keys,
            add_values,
        )

        @pl.when((step == pl.num_programs(0) - 1) & (index == pairs - 1))
        def _():
            stores(info_ref, acc, down_ref, dother_ref)

    pair_rows = pl.BlockSpec((WIDE, PAIR), lambda i, h, *_: (i, base + h))
    half = (count // 2, 2 * lanes)
    return call(
        body,
        name,
        info,
        (rows // WIDE, pairs),
        [
            (q, pair_rows),
            (kv, pl.BlockSpec((count, PAIR), lambda i, h, *_: (0, base + h))),
            (kv, pl.BlockSpec((count, PAIR), lambda i, h, *_: (0, all_pairs + base + h))),
            (att, pair_rows),
            (datt, pair_rows),
            (inverses, pl.BlockSpec((1, 2, WIDE), lambda i, h, *_: (base + h, 0, i))),
            (probs, pl.BlockSpec((2, count, WIDE), lambda i, h, *_: (base + h, 0, i))),
        ],
        [
            ((rows, lanes), BF16, pl.BlockSpec((WIDE, PAIR), lambda i, h, *_: (i, h))),
            (half, BF16, whole(half)),
            (half, BF16, whole(half)),
        ],
        [pltpu.VMEM((lanes, count), BF16), pltpu.VMEM((count, 2 * lanes), F32)],
        cost(32 * rows * count * lanes, 20 * rows * lanes + 2 * rows * count),
    )


def self_backward(info, q, kv, att, dat, inverses, probs, splits, split):
    quarter = q.shape[0] // 2

    def stores(info_ref, acc, down_ref, dother_ref):
        for target, core in ((down_ref, info_ref[2]), (dother_ref, 1 - info_ref[2])):
            for part in range(2):
                begin = pl.multiple_of(place_of(info_ref, core, part) * quarter, quarter)
                target[part * quarter : (part + 1) * quarter, :] = acc[
                    pl.ds(begin, quarter), :
                ].astype(BF16)

    return attention_backward(
        "self_backward", info, q, kv, att, dat, inverses, probs, splits, split, stores
    )


def cross_backward(info, cq, ckv, catt, dca, inverses, probs, splits, split):
    count = ckv.shape[0]

    def stores(info_ref, acc, down_ref, dother_ref):
        down_ref[...] = acc[: count // 2, :].astype(BF16)
        dother_ref[...] = acc[count // 2 :, :].astype(BF16)

    return attention_backward(
        "cross_backward", info, cq, ckv, catt, dca, inverses, probs, splits, split, stores
    )


def feed(info, catt, second_in, dy, cout, weights, gains, packing):
    rows, width = catt.shape
    hidden = weights.hidden
    cout_count = len(cout.arrays)
    feed_count = len(weights.arrays)
    packed = packing.outputs(width * width + 2 * width * hidden)

    def body(info_ref, catt_ref, second_ref, dy_first, dy_last, gain_ref, *refs):
        cout_refs, refs = refs[:cout_count], refs[cout_count:]
        feed_refs, refs = refs[:feed_count], refs[feed_count:]
        (
            out_first,
            out_last,
            dthird_ref,
            dca_ref,
            ggain_ref,
            *packed_refs,
            acc_cout,
            acc_widen,
            acc_narrow,
            cout_scratch,
            widen_scratch,
            narrow_scratch,
        ) = refs
        cout_full = cout.load(info_ref, cout_refs, cout_scratch)
        widen_full, narrow_full = weights.load(info_ref, feed_refs, (widen_scratch, narrow_scratch))
        step = pl.program_id(0)

        @pl.when(step == 0)
        def _():
            acc_cout[...] = jnp.zeros_like(acc_cout)
            acc_widen[...] = jnp.zeros_like(acc_widen)
            acc_narrow[...] = jnp.zeros_like(acc_narrow)
            ggain_ref[...] = jnp.zeros_like(ggain_ref)

        catt = catt_ref[...]
        dy_low = dy.load(dy_first, dy_last)
        gain = gain_ref[5:6, :]
        third = second_ref[...] + dot(catt, cout_full[...])
        normed, scale = normalized(third)
        normed_low = (normed * gain).astype(BF16)
        pre = dot(normed_low, widen_full[...])
        below = 0.5 * (1.0 + lax.erf(pre * math.sqrt(0.5)))
        bell = jnp.exp(-0.5 * pre * pre) * (1.0 / math.sqrt(2.0 * math.pi))
        act = (pre * below).astype(BF16)
        out = (third + dot(act, narrow_full[...])).astype(BF16)
        dact = dot(dy_low, narrow_full[...], 1, 1)
        dpre = (dact * (below + pre * bell)).astype(BF16)
        acc_narrow[...] += dot(act, dy_low, 0, 0)
        acc_widen[...] += dot(normed_low, dpre, 0, 0)
        dnormed = dot(dpre, widen_full[...], 1, 1)
        ggain_ref[...] += jnp.sum(dnormed * normed, axis=0, keepdims=True)
        dthird = dy_low.astype(F32) + norm_backward(dnormed * gain, normed, scale)
        dthird_ref[...] = dthird
        dc = dthird.astype(BF16)
        dca_ref[...] = dot(dc, cout_full[...], 1, 1).astype(BF16)
        acc_cout[...] += dot(catt, dc, 0, 0)
        store_half((out_first, out_last), out)

        @pl.when(step == pl.num_programs(0) - 1)
        def _():
            packing.store(
                info_ref, packed_refs, (acc_cout, acc_widen, acc_narrow), unroll=True
            )

    return call(
        body,
        "feed",
        info,
        rows // BLOCK,
        [(catt, rows_of(width)), (second_in, rows_of(width))]
        + dy.inputs(BLOCK)
        + [(gains, whole(gains.shape))]
        + cout.inputs()
        + weights.inputs(),
        half_outputs(rows, width, BLOCK)
        + [
            ((rows, width), F32, rows_of(width)),
            ((rows, width), BF16, rows_of(width)),
            ((1, width), F32, whole((1, width))),
        ]
        + packed,
        [
            pltpu.VMEM((width, width), F32),
            pltpu.VMEM((width, hidden), F32),
            pltpu.VMEM((hidden, width), F32),
            cout.scratch(),
        ]
        + weights.scratch(),
        cost(
            12 * rows * width * hidden, 24 * rows * width + 8 * width * hidden, 2 * rows * hidden
        ),
    )


def sum_low(own_ref, got_ref):
    return (own_ref[...].astype(F32) + got_ref[...].astype(F32)).astype(BF16)


def middle_backward(
    info, dcqs, second_in, dthird, att, owns, gots, encoder, weight, gains, packing
):
    rows, width = second_in.shape
    count = len(dcqs)
    lanes = width // count
    packed = packing.outputs(4 * width * width)
    pieces = len(weight.arrays)
    short = encoder.shape[0] // (rows // BLOCK)

    def body(info_ref, att_ref, second_ref, dthird_ref, gain_ref, enc_first, enc_last, *refs):
        dcq_refs, refs = refs[:count], refs[count:]
        own_refs, refs = refs[:count], refs[count:]
        got_refs, refs = refs[:count], refs[count:]
        weight_refs, refs = refs[:pieces], refs[pieces:]
        dsecond_ref, dat_ref, ggain_ref, *genc_refs = refs[:5]
        refs = refs[5:]
        packed_refs, refs = refs[: len(packed)], refs[len(packed) :]
        acc_query, acc_out, acc_memory, scratch = refs
        full = weight.load(info_ref, weight_refs, scratch)
        step = pl.program_id(0)

        @pl.when(step == 0)
        def _():
            acc_query[...] = jnp.zeros_like(acc_query)
            acc_out[...] = jnp.zeros_like(acc_out)
            acc_memory[...] = jnp.zeros_like(acc_memory)
            ggain_ref[...] = jnp.zeros_like(ggain_ref)

        dcq = jnp.concatenate([ref[...] for ref in dcq_refs], axis=1)
        gain = gain_ref[4:5, :]
        normed, scale = normalized(second_ref[...])
        normed_low = (normed * gain).astype(BF16)
        dnormed = dot(dcq, full[:, width : 2 * width], 1, 1)
        acc_query[...] += dot(normed_low, dcq, 0, 0)
        ggain_ref[...] += jnp.sum(dnormed * normed, axis=0, keepdims=True)
        dsecond = dthird_ref[...] + norm_backward(dnormed * gain, normed, scale)
        dsecond_ref[...] = dsecond
        da = dsecond.astype(BF16)
        dat_ref[...] = dot(da, full[:, :width], 1, 1).astype(BF16)
        acc_out[...] += dot(att_ref[...], da, 0, 0)

        turned = encoder.load(enc_first, enc_last).T
        grads = [sum_low(own, got) for own, got in zip(own_refs, got_refs)]
        dckv = jnp.concatenate(
            [g[:, :lanes] for g in grads] + [g[:, lanes:] for g in grads], axis=1
        )
        genc = dot(dckv, full[:, 2 * width :], 1, 1).astype(BF16)
        acc_memory[...] += dot(turned, dckv)
        store_half(genc_refs, genc)

        @pl.when(step == pl.num_programs(0) - 1)
        def _():
            packing.store(info_ref, packed_refs, (acc_query, acc_out, acc_memory))

    return call(
        body,
        "middle_backward",
        info,
        rows // BLOCK,
        [
            (att, rows_of(width)),
            (second_in, rows_of(width)),
            (dthird, rows_of(width)),
            (gains, whole(gains.shape)),
        ]
        + encoder.inputs(short)
        + [(a, rows_of(lanes)) for a in dcqs]
        + [(a, rows_of(2 * lanes, short)) for a in owns]
        + [(a, rows_of(2 * lanes, short)) for a in gots]
        + weight.inputs(),
        [
            ((rows, width), F32, rows_of(width)),
            ((rows, width), BF16, rows_of(width)),
            ((1, width), F32, whole((1, width))),
        ]
        + half_outputs(encoder.shape[0], width, short)
        + packed,
        [
            pltpu.VMEM((width, width), F32),
            pltpu.VMEM((width, width), F32),
            pltpu.VMEM((width, 2 * width), F32),
            weight.scratch(),
        ],
        cost(16 * rows * width * width, 20 * rows * width),
    )


VECTORS = 8


def project_backward(
    info, tokens, normed, dqs, owns, gots, dsecond, mods, ggains, embedded, gencs, weight, packing
):
    rows, width = tokens.shape
    count = len(dqs)
    lanes = width // count
    packed = packing.outputs(3 * width * width, VECTORS)
    sent = (rows // 2 + gencs[0].shape[0], width)
    pieces = len(weight.arrays)

    def body(info_ref, first_ref, last_ref, normed_ref, dsecond_ref, mod_ref, *refs):
        second_gain, third_gain, embedded_ref, *genc_refs = refs[:5]
        refs = refs[5:]
        dq_refs, refs = refs[:count], refs[count:]
        own_refs, refs = refs[:count], refs[count:]
        got_refs, refs = refs[:count], refs[count:]
        weight_refs, refs = refs[:pieces], refs[pieces:]
        gfirst_ref, glast_ref, vectors_ref, *packed_refs, acc, sums, scratch = refs
        full = weight.load(info_ref, weight_refs, scratch)
        step = pl.program_id(0)

        @pl.when(step == 0)
        def _():
            acc[...] = jnp.zeros_like(acc)
            sums[...] = jnp.zeros_like(sums)

        turned = normed_ref[...].T
        dkvs = [sum_low(own, got) for own, got in zip(own_refs, got_refs)]
        grads = jnp.concatenate(
            [ref[...] for ref in dq_refs]
            + [dkv[:, :lanes] for dkv in dkvs]
            + [dkv[:, lanes:] for dkv in dkvs],
            axis=1,
        )
        acc[...] += dot(turned, grads)
        dnormed = dot(grads, full[...], 1, 1)
        unit, scale = normalized(tokens.load(first_ref, last_ref).astype(F32))
        sums[0:1, :] += jnp.sum(dnormed * unit, axis=0, keepdims=True)
        sums[1:2, :] += jnp.sum(dnormed, axis=0, keepdims=True)
        gtokens = (
            dsecond_ref[...] + norm_backward(dnormed * mod_ref[0:1, :], unit, scale)
        ).astype(BF16)
        steps = rows // BLOCK // 2
        at = pl.ds(pl.multiple_of(lax.rem(step, steps) * BLOCK, BLOCK), BLOCK)
        for half, ref in enumerate((gfirst_ref, glast_ref)):

            @pl.when(step // steps == half)
            def _(half=half, ref=ref):
                ref[at, :] = gtokens
                ref[rows // 2 :, :] = genc_refs[half][...]

        @pl.when(step == pl.num_programs(0) - 1)
        def _():
            vectors = jnp.concatenate(
                [
                    sums[0:1, :] * mod_ref[2:3, :],
                    second_gain[...],
                    third_gain[...],
                    sums[0:1, :] * mod_ref[3:4, :],
                    sums[1:2, :],
                    embedded_ref[0:1, :].astype(F32),
                    jnp.zeros((VECTORS - 6, width), F32),
                ],
                axis=0,
            )
            vectors_ref[...] = vectors
            packing.store(info_ref, packed_refs, (acc,), vectors)

    return call(
        body,
        "project_backward",
        info,
        rows // BLOCK,
        tokens.inputs(BLOCK)
        + [
            (normed, rows_of(width)),
            (dsecond, rows_of(width)),
            (mods, whole(mods.shape)),
            (ggains[0], whole((1, width))),
            (ggains[1], whole((1, width))),
            (embedded, whole(embedded.shape)),
            (gencs[0], whole(gencs[0].shape)),
            (gencs[1], whole(gencs[1].shape)),
        ]
        + [(a, rows_of(lanes)) for a in dqs]
        + [(a, rows_of(2 * lanes)) for a in owns]
        + [(a, rows_of(2 * lanes)) for a in gots]
        + weight.inputs(),
        [(sent, BF16, whole(sent))] * 2
        + [((VECTORS, width), F32, whole((VECTORS, width)))]
        + packed,
        [pltpu.VMEM((width, 3 * width), F32), pltpu.VMEM((8, width), F32), weight.scratch()],
        cost(12 * rows * width * width, 20 * rows * width),
    )


def join_columns(info, parts):
    size = parts[0].shape[0] - VECTORS
    shape = (size + len(parts) * VECTORS, parts[0].shape[1])

    def body(info_ref, *refs):
        *part_refs, out_ref = refs
        total = part_refs[0][:size, :].astype(F32)
        for ref in part_refs[1:]:
            total = total + ref[:size, :].astype(F32)
        out_ref[:size, :] = total.astype(BF16)
        for index, ref in enumerate(part_refs):
            begin = size + index * VECTORS
            out_ref[begin : begin + VECTORS, :] = ref[size:, :]

    return call(
        body,
        "join_columns",
        info,
        1,
        [(part, whole(part.shape)) for part in parts],
        [(shape, BF16, whole(shape))],
        [],
        cost(0, 4 * size * shape[1]),
    )[0]


def finish(info, parts, size, shard):
    width = parts[0].shape[1]
    count = parts[0].shape[0] - size
    devices = len(parts) * count // VECTORS

    def body(info_ref, *refs):
        part_refs = refs[: len(parts)]
        ginput_ref, gtime_ref, ggains_ref, listed, turned = refs[len(parts) :]
        for block in range(size // shard):
            rows = slice(block * shard, (block + 1) * shard)
            terms = [ref[rows, :].astype(F32) for ref in part_refs]
            ginput_ref[:, block * width : (block + 1) * width] = (terms[0] + terms[1]) + (
                terms[2] + terms[3]
            )
        for turn, ref in enumerate(part_refs):
            place = lax.bitwise_xor(info_ref[5], turn)
            listed[pl.ds(pl.multiple_of(place * count, count), count), :] = ref[size:, :]
        vectors = listed[...]
        column = lax.broadcasted_iota(jnp.int32, (devices, devices * VECTORS), 1)
        row = lax.broadcasted_iota(jnp.int32, (devices, devices * VECTORS), 0)

        def pick(kind):
            chosen = jnp.where(column == row * VECTORS + kind, 1.0, 0.0).astype(BF16)
            return dot(chosen, vectors)

        chosen = jnp.where(lax.rem(column, VECTORS) == row, 1.0, 0.0).astype(BF16)
        turned[...] = jnp.concatenate([0.5 * pick(5), dot(chosen, vectors)], axis=0).T
        place = (2 * info_ref[4] + info_ref[2]) * shard
        part = turned[pl.ds(pl.multiple_of(place, shard), shard), :]
        grads = jnp.concatenate([pick(3), pick(4)], axis=1).astype(BF16)
        gtime_ref[...] = dot(part[:, :devices].astype(BF16), grads)
        ggains_ref[...] = part.T[devices : devices + 3, :]

    return call(
        body,
        "finish",
        info,
        1,
        [(part, whole(part.shape)) for part in parts],
        [
            ((shard, 3 * width), F32, whole((shard, 3 * width))),
            ((shard, 2 * width), F32, whole((shard, 2 * width))),
            ((3, shard), F32, whole((3, shard))),
        ],
        [pltpu.VMEM((devices * VECTORS, width), BF16), pltpu.VMEM((width, 2 * devices), F32)],
        cost(8 * devices * count * width, 12 * size * width),
    )


def permutations(seq_count, fsdp_count):
    columns = fsdp_count // 2

    def at(seq, fsdp):
        return seq * fsdp_count + fsdp

    def pairs(move):
        return [
            (at(seq, fsdp), at(*move(seq, fsdp)))
            for seq in range(seq_count)
            for fsdp in range(fsdp_count)
        ]

    def home(turn):
        def move(seq, fsdp):
            y, x = divmod(seq, 2)
            column, core = divmod(fsdp, 2)
            return 2 * core + (x ^ turn), 2 * column + y

        return move

    shift = {
        r: pairs(lambda seq, fsdp, r=r: (seq, (fsdp + 2 * r) % fsdp_count))
        for r in range(1, columns)
    }
    cross = {t: pairs(lambda seq, fsdp, t=t: (seq ^ t, fsdp)) for t in range(1, seq_count)}
    swap = pairs(lambda seq, fsdp: (seq, fsdp ^ 1))
    return pairs(home(0)), pairs(home(1)), swap, shift, cross


def reverse(pairs):
    return [(target, source) for source, target in pairs]


def after(values, signal):
    return lax.optimization_barrier((values, signal))[0]


class Direct:
    def __init__(self, perms, seq, fsdp, columns):
        self.same, self.crossed, self.swap_pairs, self.shifts, self.crosses = perms
        self.seq = seq
        self.core = fsdp % 2
        self.z = fsdp // 2
        self.columns = columns

    def permute(self, values, pairs):
        return lax.ppermute(values, AXES, pairs)

    def swap(self, values):
        return self.permute(values, self.swap_pairs)

    def along_z(self, values):
        return [values] + [
            self.permute(values, self.shifts[r]) for r in range(1, self.columns)
        ]

    def both_cores(self, pieces):
        return pieces + [self.swap(piece) for piece in pieces]

    def core_sum(self, mine, away, signal=()):
        got = after(self.swap(away), signal)
        return [
            (mine[r].astype(F32) + got[r].astype(F32)).astype(BF16) for r in range(self.columns)
        ]

    def z_parts(self, shards):
        return [self.permute(shards[r], self.shifts[r]) for r in range(1, self.columns)]

    def z_sum(self, shards, got, signal=()):
        total = shards[0].astype(F32)
        for part in after(got, signal):
            total = total + part.astype(F32)
        return lax.optimization_barrier(total.astype(BF16))

    def add(self, first, second):
        return lax.optimization_barrier((first.astype(F32) + second.astype(F32)).astype(BF16))

    def cross(self, values, turn):
        return self.permute(values, self.crosses[turn])


SPLITS = 2


def time_embedding(step_values, model_width):
    half_width = model_width // 2
    frequency = jnp.exp(-math.log(10000.0) * jnp.arange(half_width, dtype=F32) / half_width)
    angles = step_values.astype(F32)[:, None] * frequency[None, :]
    return jnp.concatenate([jnp.sin(angles), jnp.cos(angles)], axis=-1).astype(BF16)


def exact_dot(left, right):
    return lax.dot_general(
        left,
        right,
        (((0,), (0,)), ((), ())),
        precision=lax.Precision.HIGHEST,
        preferred_element_type=F32,
    )


def make(seq_count, fsdp_count):
    perms = permutations(seq_count, fsdp_count)
    same, crossed = perms[:2]
    columns = fsdp_count // 2

    def on_device(
        tokens,
        encoder_states,
        lengths,
        timesteps,
        time_weight,
        self_input,
        self_output,
        cross_query,
        cross_memory,
        cross_output,
        widen_weight,
        narrow_weight,
        norm_gains,
        cotangent,
    ):
        width = tokens.shape[2]
        hidden = widen_weight.shape[1]
        shard = time_weight.shape[0]
        seq = lax.axis_index("seq")
        fsdp = lax.axis_index("fsdp")
        core = fsdp % 2
        side = seq % 2
        direct = Direct(perms, seq, fsdp, columns) if columns == 4 else None

        def send_work(values):
            mine = lax.dynamic_index_in_dim(values, side, 0, keepdims=False)
            others = lax.dynamic_index_in_dim(values, 1 - side, 0, keepdims=False)
            return [lax.ppermute(mine, AXES, same), lax.ppermute(others, AXES, crossed)]

        def send_home(halves):
            return [
                lax.ppermute(halves[0], AXES, reverse(same)),
                lax.ppermute(halves[1], AXES, reverse(crossed)),
            ]

        def at_home(parts, kind):
            first = jnp.where(side == 0, parts[0], parts[1])
            second = jnp.where(side == 0, parts[1], parts[0])
            return jnp.stack([first, second], axis=0).astype(kind)

        def gather(weight, axis=0):
            return lax.all_gather(weight, "fsdp", axis=axis, tiled=True)

        def swap(values):
            return lax.ppermute(values, AXES, perms[2])

        packing = Packing(fsdp_count, direct is not None, width)
        token_rows, encoder_rows = tokens.shape[1], encoder_states.shape[1]
        numbers = jnp.concatenate([lengths, timesteps[:, None]], axis=1)
        numbers_other = swap(numbers)
        own_row = jnp.where(core == seq // 2, numbers, numbers_other)
        own_row = lax.dynamic_slice_in_dim(own_row, side, 1, 0)
        step_value = own_row[0, 3:4]
        place = lax.broadcasted_iota(jnp.int32, (8,), 0)
        info = jnp.where(place == 1, own_row[0, 1], 0) + jnp.where(place <= 1, own_row[0, 0], 0)
        for index, value in enumerate((core, side, fsdp // 2, seq)):
            info = jnp.where(place == index + 2, value, info)
        embedded = jnp.pad(time_embedding(step_value, width), ((0, 15), (0, 0)))

        turned = jnp.pad(norm_gains.T, ((0, 0), (0, 128 - norm_gains.shape[0])))
        first = jnp.concatenate([self_input, time_weight, turned], axis=1)
        first_mine = direct.along_z(first) if direct else [(), ()]
        own = send_work(jnp.concatenate([tokens, encoder_states], axis=1))
        other = [swap(part) for part in after(own, first_mine[1:])]
        work_tokens = Halves(own, 0, token_rows)
        other_tokens = Halves(other, 0, token_rows)
        work_encoder = Halves(own, token_rows, encoder_rows)
        other_encoder = Halves(other, token_rows, encoder_rows)

        ready = info
        rest = jnp.concatenate([self_output, cross_query, cross_memory, cross_output], axis=1)
        if direct:
            first = direct.both_cores(first_mine)
            wide = widen_weight.reshape(shard, hidden // width, width).transpose(1, 0, 2)
            large = jnp.concatenate([wide.reshape(-1, width), narrow_weight], axis=0)
            rest, large = after((rest, large), (own, info, embedded))
            rest_mine = direct.along_z(rest)
            small_other = [swap(rest)]
            large_mine = direct.along_z(large)
            large_other = [swap(large)]
            ready = after(info, (small_other, large_other))
        else:
            first = [gather(first)]
            rest = [gather(rest)]
            feed_weights = FeedWeights([gather(widen_weight), gather(narrow_weight)], hidden)

        mods, q, kv, normed_first, att, inverses, probs = self_forward(
            ready, work_tokens, other_tokens, embedded, Weight(first, 0, first[0].shape[1])
        )
        ready = info
        if direct:
            rest_mine[1:], large_mine[:2] = after((rest_mine[1:], large_mine[:2]), att)
            small_other += [swap(part) for part in rest_mine[1:]]
            rest = rest_mine + small_other
            large_other.append(swap(large_mine[1]))
            ready = after(info, large_other)
        input_weight = Weight(first, 0, 3 * width)
        cross_weight = Weight(rest, 0, 4 * width)
        cout_weight = Weight(rest, 4 * width, width)
        dy_parts = send_work(after(cotangent, att))
        second_in, cq, ckv, catt, cross_inverses, cross_probs = cross_forward(
            ready, att, work_tokens, work_encoder, other_encoder, cross_weight, mods
        )
        work_dy = Halves(after(dy_parts, catt), 0, token_rows)
        if direct:
            large_mine[2:] = after(large_mine[2:], catt)
            large_other += [swap(part) for part in large_mine[2:]]
            feed_weights = FeedWeights(large_mine + large_other, hidden)
        out_first, out_last, dthird, dca, ggain_third, *packed_feed = feed(
            info, catt, second_in, work_dy, cout_weight, feed_weights, mods, packing
        )
        layer_out = (out_first, out_last)
        out_parts = send_home(layer_out)

        def backward_cross(split, ready):
            return cross_backward(
                ready, cq, ckv, catt, dca, cross_inverses, cross_probs, SPLITS, split
            )

        def backward_self(split, ready):
            return self_backward(ready, q, kv, att, dat, inverses, probs, SPLITS, split)

        crosses = [backward_cross(0, info)]
        out_parts = after(out_parts, crosses[0][0])
        chip_feed = direct.core_sum(*packed_feed, crosses[0][0]) if direct else ()
        crosses.append(backward_cross(1, after(info, (chip_feed, out_parts))))
        dcqs, dckvs, dckv_others = zip(*crosses)
        dckv_gots = [swap(a) for a in dckv_others]
        feed_parts = direct.z_parts(chip_feed) if direct else [()]
        dsecond, dat, ggain_second, *genc = middle_backward(
            after(info, (feed_parts[0], dcqs)),
            dcqs,
            second_in,
            dthird,
            att,
            dckvs,
            dckv_gots,
            work_encoder,
            cross_weight,
            mods,
            packing,
        )
        genc, packed_middle = genc[:2], genc[2:]
        selfs = [backward_self(0, after(info, packed_middle))]
        if direct:
            column_feed = direct.z_sum(chip_feed, feed_parts, selfs[0][0])
            chip_middle = direct.core_sum(*packed_middle, selfs[0][0])
            selfs.append(backward_self(1, after(info, (column_feed, chip_middle))))
            middle_parts = after(direct.z_parts(chip_middle), selfs[1][0])
            row_feed = after(direct.cross(column_feed, 1), selfs[1][0])
            row_feed = direct.add(column_feed, row_feed)
            column_middle = direct.z_sum(chip_middle, middle_parts)
        else:
            selfs.append(backward_self(1, info))
        dqs, dkvs, dkv_others = zip(*selfs)
        dkv_others = list(dkv_others)
        if direct:
            dkv_others[1] = after(dkv_others[1], (column_middle, row_feed))
        dkv_gots = [swap(a) for a in dkv_others]
        first_grad, last_grad, vectors, *packed_input = project_backward(
            info,
            work_tokens,
            normed_first,
            dqs,
            dkvs,
            dkv_gots,
            dsecond,
            mods,
            (ggain_second, ggain_third),
            embedded,
            genc,
            input_weight,
            packing,
        )
        gtokens = (first_grad, last_grad)
        if direct:
            got_row = after(direct.cross(row_feed, 2), gtokens)
            row_middle = after(direct.cross(column_middle, 1), gtokens)
            away = after(packed_input[1], (got_row, row_middle))
            chip = direct.core_sum(packed_input[0], away)
            row_middle = direct.add(column_middle, row_middle)
            gots = direct.z_parts(chip)
            middle_got = direct.cross(row_middle, 2)
            token_parts = after(send_home(after(gtokens, chip)), gots)
            ready = after(info, (token_parts, middle_got))
            size = chip[0].shape[0] - VECTORS
            joined = join_columns(ready, [chip[0]] + gots)
            parts = [joined] + [direct.cross(joined, turn) for turn in (1, 2, 3)]
            late = after((row_feed, got_row, row_middle, middle_got), joined)
            reduced_feed = late[0].astype(F32) + late[1].astype(F32)
            reduced_middle = late[2].astype(F32) + late[3].astype(F32)
            reduced_input, gtime, ggains = finish(info, parts, size, shard)
        else:

            def reduce(packed):
                part = lax.psum_scatter(packed[0], "fsdp", scatter_dimension=0, tiled=True)
                return lax.psum(part[0], "seq").astype(F32)

            reduced_input = reduce(packed_input)
            reduced_input = unpack_rows(reduced_input, 0, shard, 3 * width)
            reduced_middle = reduce(packed_middle)
            reduced_feed = reduce(packed_feed)
            token_parts = send_home(gtokens)
            ggains = lax.psum(vectors[:3], AXES)
            ggains = lax.dynamic_slice_in_dim(ggains, fsdp * shard, shard, 1)
            by_group = lax.all_gather(vectors[3:5], AXES, axis=0)
            by_group = by_group.reshape(seq_count, columns, 2, 2 * width).sum(axis=2)
            by_group = by_group.transpose(1, 0, 2).reshape(-1, 2 * width)
            every = time_embedding(gather(timesteps), width)
            own_columns = lax.dynamic_slice_in_dim(every, fsdp * shard, shard, 1)
            gtime = exact_dot(own_columns.astype(F32), by_group)

        tall = narrow_weight.shape[0]
        return (
            at_home(out_parts, BF16),
            at_home([part[:token_rows] for part in token_parts], F32),
            at_home([part[token_rows:] for part in token_parts], F32),
            gtime,
            reduced_input,
            unpack_rows(reduced_middle, shard, shard, width),
            unpack_rows(reduced_middle, 0, shard, width),
            unpack_rows(reduced_middle, 2 * shard, shard, 2 * width),
            unpack_rows(reduced_feed, 0, shard, width),
            unpack_rows(reduced_feed, shard, shard, hidden),
            unpack_rows(reduced_feed, shard * (1 + hidden // width), tall, width),
            ggains,
        )

    return on_device


def solution(mesh):
    rows = P("fsdp", "seq", None)
    weight = P("fsdp", None)
    in_specs = (rows, rows, P("fsdp", None), P("fsdp")) + (weight,) * 8 + (P(None, "fsdp"), rows)
    out_specs = (rows,) * 3 + (weight,) * 8 + (P(None, "fsdp"),)
    return jax.shard_map(
        make(mesh.shape["seq"], mesh.shape["fsdp"]),
        mesh=mesh,
        in_specs=in_specs,
        out_specs=out_specs,
        check_vma=False,
    )
```
